32 devices in a mesh: dp: 4 (over z), seq: 4 (over x, core), tensor: 2 (over y).
Axes of the slice: x: 2, y: 2, z: 4, core: 2. Of those that a mesh axis runs over, the one named last changes fastest.
Arguments:
- layer_in: bfloat16 [1024, 16, 1472], P('tensor', ('dp', 'seq')), may hold values from -6 to 6
- out_grad: bfloat16 [1024, 16, 1472], P('tensor', ('dp', 'seq')), may hold values from -6 to 6
- doc_lengths: int32 [16, 4], P(('dp', 'seq')), may hold values from 1 to 512, 1024 in all within a row
- valid_length: int32 [16], P(('dp', 'seq')), may hold values from 256 to 1024
- gain_attn: bfloat16 [1472], replicated, may hold values from 0.5 to 1.5
- query_weight: bfloat16 [1472, 384], P(None, 'tensor'), may hold values from -0.078125 to 0.078125
- key_weight: bfloat16 [1472, 384], P(None, 'tensor'), may hold values from -0.078125 to 0.078125
- value_weight: bfloat16 [1472, 384], P(None, 'tensor'), may hold values from -0.15625 to 0.15625
- position_bias: float32 [32, 6], P(None, 'tensor'), may hold values from -4 to 4
- output_weight: bfloat16 [384, 1472], P('tensor'), may hold values from -1.75 to 1.75
- gain_ffn: bfloat16 [1472], replicated, may hold values from 0.5 to 1.5
- gate_weight: bfloat16 [1472, 3584], P(None, 'tensor'), may hold values from -0.15625 to 0.15625
- up_weight: bfloat16 [1472, 3584], P(None, 'tensor'), may hold values from -0.15625 to 0.15625
- down_weight: bfloat16 [3584, 1472], P('tensor'), may hold values from -0.09375 to 0.09375
Outputs:
- out_y: bfloat16 [1024, 16, 1472], P('tensor', ('dp', 'seq'))
- grad_layer_in: float32 [1024, 16, 1472], P('tensor', ('dp', 'seq'))
- grad_gain_attn: float32 [1472], replicated
- grad_query_weight: float32 [1472, 384], P('dp', 'tensor')
- grad_key_weight: float32 [1472, 384], P('dp', 'tensor')
- grad_value_weight: float32 [1472, 384], P('dp', 'tensor')
- grad_position_bias: float32 [32, 6], replicated
- grad_output_weight: float32 [384, 1472], P('tensor', 'dp')
- grad_gain_ffn: float32 [1472], replicated
- grad_gate_weight: float32 [1472, 3584], P('dp', 'tensor')
- grad_up_weight: float32 [1472, 3584], P('dp', 'tensor')
- grad_down_weight: float32 [3584, 1472], P('tensor', 'dp')
The draws below stay inside these ranges and needn't reach their ends.
Inputs may be any that keep to these rules, and one draw needn't show every extreme that they name: `doc_lengths`: in each row the 4 lengths sum to 1024.
All inputs are finite; a program needn't handle non-finite values.
Results may differ from the reference program's by a relative error of at most 0.019.
Values may be sent and summed in bfloat16 or wider, within the bound.
A program may use at most 192 MiB of HBM per device.

```python
import math
import jax
import jax.numpy as jnp
import numpy as np
from jax import lax

D = 1472
H = 6
DH = 64
FF = 3584
NB = 32
LEN = 1024
SEGS = 4
HD = 384
ROWS = 16


def touch_ends(entries, rng, least, high):
    index_at = [jax.random.randint(jax.random.fold_in(rng, axis), (), 0, length) for axis, length in enumerate(entries.shape)]
    widest = entries.shape.index(max(entries.shape))
    beside = index_at[:widest] + [(index_at[widest] + 1) % entries.shape[widest]] + index_at[widest + 1:]
    return entries.at[tuple(index_at)].set(least).at[tuple(beside)].set(high)


def with_spikes(values, rng, source, target, parts, factor):
    owner, partner = [(jnp.arange(values.shape[axis_at]) // (values.shape[axis_at] // parts)).reshape([-1 if axis == axis_at else 1 for axis in range(values.ndim)]) for axis_at in (source, target)]
    chosen = jax.random.permutation(rng, parts)[partner]
    strong = (owner == chosen) | (owner == (partner + parts // 2) % parts)
    return jnp.where(strong, factor * values, values)


def level_of(key, extent, split, least, top_value):
    level = 1.0
    for dim, blocks in split:
        draws = jax.random.uniform(jax.random.fold_in(jax.random.fold_in(key, 6), dim), (blocks,), jnp.float32, least / len(split), top_value / len(split))
        level = level * jnp.repeat(jnp.exp(draws), extent[dim] // blocks).reshape((-1,) + (1,) * (len(extent) - 1 - dim))
    return level


def length_profile(number_of, total, reach, lean):
    portions = [(1 << 20) // math.isqrt(grade ** lean) + 1 for grade in range(2, number_of + 1)]
    spare, holding = total - reach - (number_of - 1), [1] * (number_of - 1)
    while spare > 0:
        movable = [i for i in range(number_of - 1) if holding[i] < reach]
        whole, budget = sum([portions[i] for i in movable]), spare
        for i in movable:
            extra = min(reach - holding[i], max(1, budget * portions[i] // whole), spare)
            holding[i] = holding[i] + extra
            spare = spare - extra
    return np.array([reach] + holding)


def ragged(rng, amount, total, limit, lean):
    if amount == 2:
        one = jax.random.randint(rng, (), max(1, total - limit), min(limit, total - 1) + 1)
        return jnp.stack([one, total - one])
    sizes = jnp.asarray(length_profile(amount, total, limit, lean), jnp.int32)
    twos = (amount - 1) // 2
    giver, taker = sizes[1:1 + 2 * twos:2], sizes[2:2 + 2 * twos:2]
    slack = jnp.minimum(giver - 1, limit - taker)
    moved = jax.random.randint(jax.random.fold_in(rng, 1), (twos,), 0, 1 << 20) % (slack + 1)
    sizes = sizes.at[1:1 + 2 * twos:2].set(giver - moved).at[2:2 + 2 * twos:2].set(taker + moved)
    return sizes[jax.random.permutation(jax.random.fold_in(rng, 2), amount)]


def scatter_about(key, dims, scale, bound, pieces=(), kind=jnp.bfloat16):
    drawn = scale * jax.random.normal(key, dims, jnp.float32)
    if pieces:
        drawn = drawn * level_of(key, dims, pieces, -0.22, 0.18)
    return jnp.clip(drawn, -bound, bound).astype(kind)


def heavy_noise(rng, extent, width, reach, pieces, heavy, kind=jnp.bfloat16):
    entries = width * jax.random.normal(rng, extent, jnp.float32)
    if pieces:
        entries = entries * level_of(rng, extent, pieces, -0.22, 0.18)
    return jnp.clip(with_spikes(entries, jax.random.fold_in(rng, 3), *heavy), -reach, reach).astype(kind)


def setup_inputs(seed: int = 0) -> dict:
    key_of = jax.random.split(jax.random.key(seed), 15)
    layer_in = scatter_about(key_of[0], (LEN, ROWS, D), 1.0, 6.0, ((0, 2), (1, 16)))
    out_grad = heavy_noise(key_of[1], (LEN, ROWS, D), 1.0, 6.0, ((0, 2), (1, 16)), (1, 2, 16, 2.0))
    doc_lengths = jax.vmap(lambda own: ragged(own, SEGS, LEN, LEN // 2, 2))(jax.random.split(key_of[2], ROWS)).reshape((ROWS, SEGS)).astype(jnp.int32)
    valid_length = touch_ends(jax.random.randint(key_of[3], (ROWS,), LEN // 4, LEN + 1), jax.random.fold_in(key_of[3], 1), LEN // 4, LEN).astype(jnp.int32)
    gain_attn = jnp.clip(1.0 + 0.1 * jax.random.normal(key_of[4], (D,), jnp.float32), 0.5, 1.5).astype(jnp.bfloat16)
    query_weight = scatter_about(key_of[5], (D, HD), (4 * D) ** -0.5, 0.078125, ((1, 2),))
    key_weight = scatter_about(key_of[6], (D, HD), (4 * D) ** -0.5, 0.078125, ((1, 2),))
    value_weight = scatter_about(key_of[7], (D, HD), D ** -0.5, 0.15625, ((1, 2),))
    position_bias = scatter_about(key_of[8], (NB, H), 1.0, 4.0, ((1, 2),), jnp.float32)
    output_weight = scatter_about(key_of[9], (HD, D), (HD // 32) ** -0.5, 1.75, ((0, 2),))
    gain_ffn = jnp.clip(1.0 + 0.1 * jax.random.normal(key_of[10], (D,), jnp.float32), 0.5, 1.5).astype(jnp.bfloat16)
    gate_weight = scatter_about(key_of[11], (D, FF), D ** -0.5, 0.15625, ((1, 2),))
    up_weight = scatter_about(key_of[12], (D, FF), D ** -0.5, 0.15625, ((1, 2),))
    down_weight = scatter_about(key_of[13], (FF, D), FF ** -0.5, 0.09375, ((0, 2),))
    return dict(layer_in=layer_in, out_grad=out_grad, doc_lengths=doc_lengths, valid_length=valid_length, gain_attn=gain_attn, query_weight=query_weight, key_weight=key_weight, value_weight=value_weight, position_bias=position_bias, output_weight=output_weight, gain_ffn=gain_ffn, gate_weight=gate_weight, up_weight=up_weight, down_weight=down_weight)


@jax.custom_vjp
def low(v):
    return lax.optimization_barrier(v.astype(jnp.bfloat16)).astype(jnp.float32)

@jax.custom_vjp
def low_back(v):
    return v

def low_keep(v):
    return (low(v), None)

def low_pass(kept, grad):
    return (grad,)

def back_keep(v):
    return (v, None)

def back_low(kept, grad):
    return (low(grad),)
low.defvjp(low_keep, low_pass)
low_back.defvjp(back_keep, back_low)
far_steps = (12, 16, 23, 32, 46, 64, 91)
eps_norm = 1e-06
masked_score = -1e+30
highest = lax.Precision.HIGHEST

def bucket_table(first, count, length):
    rows_at = first + jnp.arange(count, dtype=jnp.int32)[:, None]
    cols_at = jnp.arange(length, dtype=jnp.int32)[None, :]
    offset = cols_at - rows_at
    distance = jnp.abs(offset)
    far = 8 + sum(((distance >= step).astype(jnp.int32) for step in far_steps))
    near = jnp.where(distance < 8, distance, far).astype(jnp.int32)
    return (near + jnp.where(offset > 0, 16, 0)).astype(jnp.int32)

def segment_ids(lengths, valid, length):
    ends = jnp.cumsum(lengths, axis=-1).astype(jnp.int32)
    where_at = jnp.arange(length, dtype=jnp.int32)
    counted = lax.optimization_barrier(jnp.sum((where_at[None, :, None] >= ends[:, None, :]).astype(jnp.int32), axis=-1)).astype(jnp.int32)
    padded = jnp.int32(lengths.shape[-1])
    return jnp.where(where_at[None, :] < valid[:, None], counted, padded).astype(jnp.int32)

def rms_scale(values, gain):
    return values * lax.rsqrt(lax.optimization_barrier(jnp.mean(values * values, axis=-1, keepdims=True)) + eps_norm) * gain

def row_forward(params, row_in, allowed, buckets):
    gain_attn, query_weight, key_weight, value_weight, position_bias, output_weight, gain_ffn, gate_weight, up_weight, down_weight = params
    length = row_in.shape[0]
    xn_one = low(rms_scale(row_in, gain_attn))
    query = low(low_back(jnp.dot(xn_one, query_weight, precision=highest))).reshape(length, H, DH)
    keys = low(low_back(jnp.dot(xn_one, key_weight, precision=highest))).reshape(length, H, DH)
    values = low(low_back(jnp.dot(xn_one, value_weight, precision=highest))).reshape(length, H, DH)
    scores = jnp.einsum('qhd,khd->hqk', query, keys, precision=highest)
    scores = low_back(scores + jnp.take(position_bias.T, buckets, axis=1))
    attn_probs = jax.nn.softmax(jnp.where(allowed[None], scores, masked_score), axis=-1)
    mixed = jnp.einsum('hqk,khd->qhd', low(attn_probs), values, precision=highest).reshape(length, HD)
    mixed = low(low_back(mixed))
    hres = row_in + low_back(jnp.dot(mixed, output_weight, precision=highest))
    xn_two = low(rms_scale(hres, gain_ffn))
    gate = low_back(jnp.dot(xn_two, gate_weight, precision=highest))
    up_part = low_back(jnp.dot(xn_two, up_weight, precision=highest))
    hidden = low(jax.nn.gelu(gate, approximate=True) * up_part)
    return hres + low_back(jnp.dot(hidden, down_weight, precision=highest))

def reference(layer_in, out_grad, doc_lengths, valid_length, gain_attn, query_weight, key_weight, value_weight, position_bias, output_weight, gain_ffn, gate_weight, up_weight, down_weight):
    params = tuple((item.astype(jnp.float32) for item in (gain_attn, query_weight, key_weight, value_weight, position_bias, output_weight, gain_ffn, gate_weight, up_weight, down_weight)))
    length = layer_in.shape[0]
    segment = segment_ids(doc_lengths, valid_length, length)
    buckets = bucket_table(0, length, length)
    live = (jnp.arange(length, dtype=jnp.int32)[None, :] < valid_length[:, None]).astype(jnp.float32)
    rows_in = jnp.swapaxes(layer_in.astype(jnp.float32), 0, 1)
    rows_grad = jnp.swapaxes(out_grad.astype(jnp.float32), 0, 1) * live[:, :, None]
    zero_grads = tuple((jnp.zeros_like(item) for item in params))

    def one_row(totals, inputs):
        row_in, row_grad, row_segment = inputs
        allowed = row_segment[:, None] == row_segment[None, :]

        def forward(weights, values):
            return row_forward(weights, values, allowed, buckets)
        row_out, pullback = jax.vjp(forward, params, row_in)
        grad_params, grad_row = pullback(row_grad)
        totals = tuple((total + grad for total, grad in zip(totals, grad_params)))
        return (totals, (row_out, grad_row))
    totals, (outs, grads) = lax.scan(one_row, zero_grads, (rows_in, rows_grad, segment))
    out_y = jnp.swapaxes(outs, 0, 1).astype(jnp.bfloat16)
    grad_layer_in = jnp.swapaxes(grads, 0, 1)
    return (out_y, grad_layer_in, totals[0], totals[1], totals[2], totals[3], totals[4], totals[5], totals[6], totals[7], totals[8], totals[9])
```

```python
import functools
import math

import jax
import jax.numpy as jnp
from jax import lax
from jax.experimental import pallas as pl
from jax.experimental.pallas import tpu as pltpu
from jax.sharding import PartitionSpec as P

steps_at = (1, 2, 3, 4, 5, 6, 7, 8, 12, 16, 23, 32, 46, 64, 91)
eps_norm = 1e-06
masked_score = -1e30
q_block = 256
band_half = 128
low = jnp.bfloat16
wide = jnp.float32


def dot(a, b, ca, cb):
    return lax.dot_general(a, b, (((ca,), (cb,)), ((), ())), preferred_element_type=wide)


def attn_fwd_kernel(length, bias_ref, q_ref, k_ref, v_ref, seg_k_ref, seg_q_ref, p_ref, o_ref, table):
    block = pl.program_id(0)
    head = pl.program_id(1)
    reach = length - q_block

    @pl.when(block == 0)
    def _():
        table[head, : reach - band_half, :] = jnp.full((reach - band_half, q_block), bias_ref[15, head], wide)
        tail = length + reach - (reach + q_block + band_half)
        table[head, reach + q_block + band_half :, :] = jnp.full((tail, q_block), bias_ref[31, head], wide)
        rows = q_block + 2 * band_half
        d = (
            lax.broadcasted_iota(jnp.int32, (rows, q_block), 0)
            - lax.broadcasted_iota(jnp.int32, (rows, q_block), 1)
            - band_half
        )
        n = jnp.abs(d)
        before = jnp.full((rows, q_block), bias_ref[0, head], wide)
        after = jnp.full((rows, q_block), bias_ref[16, head], wide)
        for number, step in enumerate(steps_at):
            reached = n >= step
            before = jnp.where(reached, bias_ref[number + 1, head], before)
            after = jnp.where(reached, bias_ref[number + 17, head], after)
        table[head, reach - band_half : reach + q_block + band_half, :] = jnp.where(d > 0, after, before)

    first = pl.multiple_of(reach - block * q_block, q_block)
    scores = dot(k_ref[...], q_ref[...], 0, 0) + table[head, pl.ds(first, length), :]
    seg_k = jnp.concatenate([seg_k_ref[...]] * (q_block // 128), axis=1)
    scores = jnp.where(seg_k == seg_q_ref[...], scores, masked_score)
    raised = jnp.exp(scores - jnp.max(scores, axis=0, keepdims=True))
    probs = (raised * (1.0 / jnp.sum(raised, axis=0, keepdims=True))).astype(low)
    p_ref[0] = probs
    o_ref[...] = dot(v_ref[...], probs, 1, 0).astype(low)


def attn_forward(qkv, seg, bias):
    width, length = qkv.shape
    heads = bias.shape[1]
    dim = width // (3 * heads)
    seg_k = jnp.broadcast_to(seg[:, None], (length, 128))
    seg_q = seg[None, :]
    blocks = length // q_block
    return pl.pallas_call(
        functools.partial(attn_fwd_kernel, length),
        grid=(blocks, heads),
        in_specs=[
            pl.BlockSpec(memory_space=pltpu.SMEM),
            pl.BlockSpec((dim, q_block), lambda b, h: (h, b)),
            pl.BlockSpec((dim, length), lambda b, h: (heads + h, 0)),
            pl.BlockSpec((dim, length), lambda b, h: (2 * heads + h, 0)),
            pl.BlockSpec((length, 128), lambda b, h: (0, 0)),
            pl.BlockSpec((1, q_block), lambda b, h: (0, b)),
        ],
        out_specs=[
            pl.BlockSpec((1, length, q_block), lambda b, h: (h, 0, b)),
            pl.BlockSpec((dim, q_block), lambda b, h: (h, b)),
        ],
        out_shape=[
            jax.ShapeDtypeStruct((heads, length, length), low),
            jax.ShapeDtypeStruct((heads * dim, length), low),
        ],
        scratch_shapes=[pltpu.VMEM((heads, 2 * length - q_block, q_block), wide)],
        compiler_params=pltpu.CompilerParams(vmem_limit_bytes=48 << 20),
        cost_estimate=pl.CostEstimate(
            flops=4 * heads * length * length * dim * 4,
            bytes_accessed=2 * heads * length * length + 8 * width * length,
            transcendentals=heads * length * length,
        ),
        name="attn_forward",
    )(bias, qkv, qkv, qkv, seg_k, seg_q)


def attn_bwd_kernel(length, q_ref, k_ref, v_ref, go_ref, o_ref, p_ref, gq_ref, gk_ref, gv_ref, gb_ref, k_acc, v_acc, sums):
    block = pl.program_id(1)
    reach = length - q_block

    @pl.when(block == 0)
    def _():
        k_acc[...] = jnp.zeros_like(k_acc)
        v_acc[...] = jnp.zeros_like(v_acc)
        sums[...] = jnp.zeros_like(sums)

    probs = p_ref[0]
    go = go_ref[...]
    inner = jnp.sum(go.astype(wide) * o_ref[...].astype(wide), axis=0, keepdims=True)
    scores = probs.astype(wide) * (dot(v_ref[...], go, 0, 0) - inner)
    first = pl.multiple_of(reach - block * q_block, q_block)
    sums[pl.ds(first, length), :] += scores
    scores = scores.astype(low)
    gq_ref[...] = dot(k_ref[...], scores, 1, 0).astype(low)
    k_acc[...] += dot(q_ref[...], scores, 1, 1)
    v_acc[...] += dot(go, probs, 1, 1)

    @pl.when(block == pl.num_programs(1) - 1)
    def _():
        gk_ref[...] = k_acc[...].astype(low)
        gv_ref[...] = v_acc[...].astype(low)
        rows = q_block + 2 * band_half
        d = (
            lax.broadcasted_iota(jnp.int32, (rows, q_block), 0)
            - lax.broadcasted_iota(jnp.int32, (rows, q_block), 1)
            - band_half
        )
        n = jnp.abs(d)
        near = sums[reach - band_half : reach + q_block + band_half, :]
        far_before = jnp.sum(sums[: reach - band_half, :], axis=0, keepdims=True)
        far_after = jnp.sum(sums[reach + q_block + band_half :, :], axis=0, keepdims=True)
        bucket = jnp.zeros((rows, q_block), jnp.int32)
        for step in steps_at:
            bucket = bucket + jnp.where(n >= step, 1, 0)
        bucket = bucket + jnp.where(d > 0, 16, 0)
        for b in range(32):
            total = jnp.sum(jnp.where(bucket == b, near, 0.0), axis=0, keepdims=True)
            if b == 15:
                total = total + far_before
            if b == 31:
                total = total + far_after
            gb_ref[0, b : b + 1, :] = total


def attn_backward(qkv, grad_mixed, mixed, probs):
    width, length = qkv.shape
    heads = probs.shape[0]
    dim = width // (3 * heads)
    blocks = length // q_block
    half = pl.BlockSpec((dim, q_block), lambda h, b: (h, b))
    whole = pl.BlockSpec((dim, length), lambda h, b: (h, 0))
    gq, gk, gv, gb = pl.pallas_call(
        functools.partial(attn_bwd_kernel, length),
        grid=(heads, blocks),
        in_specs=[
            half,
            pl.BlockSpec((dim, length), lambda h, b: (heads + h, 0)),
            pl.BlockSpec((dim, length), lambda h, b: (2 * heads + h, 0)),
            half,
            half,
            pl.BlockSpec((1, length, q_block), lambda h, b: (h, 0, b)),
        ],
        out_specs=[half, whole, whole, pl.BlockSpec((1, 32, q_block), lambda h, b: (h, 0, 0))],
        out_shape=[
            jax.ShapeDtypeStruct((heads * dim, length), low),
            jax.ShapeDtypeStruct((heads * dim, length), low),
            jax.ShapeDtypeStruct((heads * dim, length), low),
            jax.ShapeDtypeStruct((heads, 32, q_block), wide),
        ],
        scratch_shapes=[
            pltpu.VMEM((dim, length), wide),
            pltpu.VMEM((dim, length), wide),
            pltpu.VMEM((2 * length - q_block, q_block), wide),
        ],
        compiler_params=pltpu.CompilerParams(vmem_limit_bytes=48 << 20),
        cost_estimate=pl.CostEstimate(
            flops=8 * heads * length * length * dim * 4,
            bytes_accessed=2 * heads * length * length + 16 * width * length,
            transcendentals=0,
        ),
        name="attn_backward",
    )(qkv, qkv, qkv, grad_mixed, mixed, probs)
    return jnp.concatenate([gq, gk, gv], axis=0), jnp.sum(gb, axis=2).T


def ffn_kernel(*refs):
    (x_ref, g_ref, gate_w, up_w, down_w), refs = refs[:5], refs[-9:]
    hid_ref, gg_ref, gu_ref, out_ref, gx_ref, xs, gs, out_acc, gx_acc = refs
    step = pl.program_id(0)

    @pl.when(step == 0)
    def _():
        xs[...] = x_ref[...].T
        gs[...] = g_ref[...].T
        out_acc[...] = jnp.zeros_like(out_acc)
        gx_acc[...] = jnp.zeros_like(gx_acc)

    gate = dot(xs[...], gate_w[...], 1, 0)
    up = dot(xs[...], up_w[...], 1, 0)
    grad = dot(gs[...], down_w[...], 1, 0)
    c = math.sqrt(2.0 / math.pi)
    square = gate * gate
    t = jnp.tanh(c * gate * (1.0 + 0.044715 * square))
    half = 0.5 * (1.0 + t)
    gelu = gate * half
    slope = half + 0.5 * gate * (1.0 - t * t) * (c * (1.0 + 3 * 0.044715 * square))
    hid = (gelu * up).astype(low)
    gg = (grad * up * slope).astype(low)
    gu = (grad * gelu).astype(low)
    hid_ref[...] = hid
    gg_ref[...] = gg
    gu_ref[...] = gu
    out_acc[...] += dot(down_w[...], hid, 1, 1)
    gx_acc[...] += dot(gate_w[...], gg, 1, 1) + dot(up_w[...], gu, 1, 1)

    @pl.when(step == pl.num_programs(0) - 1)
    def _():
        out_ref[...] = out_acc[...].astype(out_ref.dtype)
        gx_ref[...] = gx_acc[...].astype(gx_ref.dtype)


def ffn(x, g, gate_w, up_w, down_w, kept, slot, slots, kind):
    width, tokens = x.shape
    hidden = gate_w.shape[1]
    tile = 256
    full = pl.BlockSpec((width, tokens), lambda j: (0, 0), pipeline_mode=pl.Buffered(1))
    weight = pl.BlockSpec((width, tile), lambda j: (0, j))
    act = pl.BlockSpec((tokens, tile), lambda j: (slot, j))
    act_shape = jax.ShapeDtypeStruct((slots * tokens, hidden), low)
    args = [x, g, gate_w, up_w, down_w]
    specs = [full, full, weight, weight, weight]
    alias = {}
    if kept is not None:
        args += list(kept)
        specs += [pl.BlockSpec(memory_space=pl.ANY)] * 3
        alias = {5: 0, 6: 1, 7: 2}
    hid, gg, gu, out, gx = pl.pallas_call(
        ffn_kernel,
        grid=(hidden // tile,),
        in_specs=specs,
        out_specs=[act, act, act, full, full],
        out_shape=[act_shape, act_shape, act_shape]
        + [jax.ShapeDtypeStruct((width, tokens), kind)] * 2,
        scratch_shapes=[
            pltpu.VMEM((tokens, width), low),
            pltpu.VMEM((tokens, width), low),
            pltpu.VMEM((width, tokens), wide),
            pltpu.VMEM((width, tokens), wide),
        ],
        input_output_aliases=alias,
        compiler_params=pltpu.CompilerParams(vmem_limit_bytes=56 << 20),
        cost_estimate=pl.CostEstimate(
            flops=12 * tokens * width * hidden,
            bytes_accessed=6 * width * hidden + 8 * width * tokens + 6 * tokens * hidden,
            transcendentals=tokens * hidden,
        ),
        name="ffn_both_ways",
    )(*args)
    return (hid, gg, gu), out, gx


def norm_of(values, gain):
    scale = lax.rsqrt(jnp.mean(values * values, axis=0, keepdims=True) + eps_norm)
    return values * scale * gain, scale


def norm_back(values, scale, gain, grad):
    normed = values * scale
    pushed = gain * grad
    mean = jnp.mean(normed * pushed, axis=0, keepdims=True)
    return scale * (pushed - normed * mean), jnp.sum(grad * normed, axis=1)


class Moves:
    def __init__(self, mesh):
        self.nz = mesh.shape["dp"]
        self.nseq = mesh.shape["seq"]
        self.ny = mesh.shape["tensor"]
        self.nx = self.nseq // 2
        both = [(m, c, y) for m in range(self.nx) for c in range(2) for y in range(2)]
        at = lambda m, c, y: (m * 2 + c) * 2 + y
        self.swap_pairs = [(at(m, c, y), at(m, y, c)) for m, c, y in both]
        self.second_pairs = [(at(m, c, y), at(m, y, 1 - c)) for m, c, y in both]
        self.back_pairs = [(b, a) for a, b in self.second_pairs]
        self.core_pairs = [(m * 2 + c, m * 2 + 1 - c) for m in range(self.nx) for c in range(2)]
        self.ring_x = [(m * 2 + c, (m + 1) % self.nx * 2 + c) for m in range(self.nx) for c in range(2)]
        self.ring_z = [(z, (z + 1) % self.nz) for z in range(self.nz)]

    def swap(self, a):
        return lax.ppermute(a, ("seq", "tensor"), self.swap_pairs)

    def second(self, a):
        return lax.ppermute(a, ("seq", "tensor"), self.second_pairs)

    def back(self, a):
        return lax.ppermute(a, ("seq", "tensor"), self.back_pairs)

    def core(self, a):
        return lax.ppermute(a, "seq", self.core_pairs)

    def over_y(self, a):
        return lax.ppermute(a, "tensor", [(0, 1), (1, 0)])

    def ring(self, take, me, n, axis, pairs):
        if n == 1:
            return take(me)
        held = take((me + n - 1) % n)
        for t in range(1, n):
            got = lax.ppermute(held.astype(low), axis, pairs)
            held = got.astype(wide) + take((me + 2 * n - 1 - t) % n).astype(wide)
        return held.astype(low)

    def over_x_then_z(self, a, m, z):
        a = self.ring(lambda i: lax.dynamic_index_in_dim(a, i, 1, False), m, self.nx, "seq", self.ring_x)
        return self.ring(lambda i: lax.dynamic_index_in_dim(a, i, 0, False), z, self.nz, "dp", self.ring_z)

    def over_z_then_x(self, a, m, z):
        a = self.ring(lambda i: lax.dynamic_index_in_dim(a, i, 0, False), z, self.nz, "dp", self.ring_z)
        return self.ring(lambda i: lax.dynamic_index_in_dim(a, i, 0, False), m, self.nx, "seq", self.ring_x)

    def gather_x_core(self, piece, m, c):
        rows, columns = piece.shape
        if self.nx == 2:
            over = lax.ppermute(piece, "seq", self.ring_x)
            here = jnp.where(m == 0, jnp.concatenate([piece, over], 0), jnp.concatenate([over, piece], 0))
            there = self.core(here)
            return jnp.where(
                c == 0, jnp.concatenate([here, there], 1), jnp.concatenate([there, here], 1)
            )
        got = lax.all_gather(piece, "seq").reshape(self.nx, 2, rows, columns)
        return got.transpose(0, 2, 1, 3).reshape(self.nx * rows, 2 * columns)


def segment_ids(lengths, valid, length):
    ends = jnp.sum(jnp.where(jnp.arange(4)[None, :] <= jnp.arange(4)[:, None], lengths[None, :], 0), axis=1)
    where_at = jnp.arange(length, dtype=jnp.int32)
    counted = jnp.sum((where_at[:, None] >= ends[None, :]).astype(jnp.int32), axis=1)
    return jnp.where(where_at < valid, counted, 4)


def local(
    mesh,
    layer_in,
    out_grad,
    doc_lengths,
    valid_length,
    gain_attn,
    query_weight,
    key_weight,
    value_weight,
    position_bias,
    output_weight,
    gain_ffn,
    gate_weight,
    up_weight,
    down_weight,
):
    moves = Moves(mesh)
    half_len, _, width = layer_in.shape
    length = 2 * half_len
    heads = position_bias.shape[1]
    inner_width = query_weight.shape[1]
    s = lax.axis_index("seq")
    y = lax.axis_index("tensor")
    z = lax.axis_index("dp")
    c = s % 2
    m = s // 2

    x_in = moves.swap(layer_in.reshape(half_len, width).T)
    qkv_w = jnp.concatenate([query_weight.T, key_weight.T, value_weight.T], axis=0)
    qkv_w = moves.swap(qkv_w)
    facts = moves.swap(jnp.concatenate([doc_lengths[0], valid_length]))
    bias = moves.swap(position_bias)
    out_w = moves.swap(output_weight)
    positions = y * half_len + jnp.arange(half_len, dtype=jnp.int32)
    g_in = jnp.where((positions < valid_length[0])[None, :], out_grad.reshape(half_len, width).T, 0)
    g_in = g_in.astype(low)
    g_own = moves.swap(g_in)
    g_oth = moves.second(g_in)
    segment = segment_ids(facts[:4], facts[4], length)
    gain_one = gain_attn.astype(wide)[:, None]
    gain_two = gain_ffn.astype(wide)[:, None]

    def both_halves(own):
        other = moves.core(own)
        return jnp.where(
            c == 0, jnp.concatenate([own, other], 1), jnp.concatenate([other, own], 1)
        )

    def my_half(a):
        return lax.dynamic_slice_in_dim(a, c * half_len, half_len, 1)

    def other_half(a):
        return lax.dynamic_slice_in_dim(a, (1 - c) * half_len, half_len, 1)

    x_wide = x_in.astype(wide)
    normed, scale_one = norm_of(x_wide, gain_one)
    xn_one = both_halves(normed.astype(low))
    qkv = dot(qkv_w, xn_one, 1, 0).astype(low)
    probs, mixed = attn_forward(qkv, segment, bias)
    sent = dot(out_w, other_half(mixed), 0, 0).astype(low)
    hres = x_wide + dot(out_w, my_half(mixed), 0, 0) + moves.core(sent).astype(wide)

    normed, scale_two = norm_of(hres, gain_two)
    xn_own = normed.astype(low)
    xn_oth = moves.over_y(xn_own)
    down_t = down_weight.T
    kept, out_own, gx_own = ffn(xn_own, g_own, gate_weight, up_weight, down_t, None, 0, 2, wide)
    kept, out_oth, gx_oth = ffn(xn_oth, g_oth, gate_weight, up_weight, down_t, kept, 1, 2, low)
    hid, grad_gate, grad_up = kept
    gx = gx_own + moves.over_y(gx_oth).astype(wide)
    out_y = moves.swap((hres + out_own).astype(low)).astype(wide) + moves.back(out_oth).astype(wide)
    out_y = out_y.astype(low)

    def ffn_weight_grad(left_own, left_oth, right, x_first):
        left = jnp.concatenate([left_own, left_oth], axis=1)
        columns = right.shape[1] // 2
        send = dot(left, lax.dynamic_slice_in_dim(right, (1 - c) * columns, columns, 1), 1, 0)
        got = moves.core(send.astype(low))
        keep = dot(left, lax.dynamic_slice_in_dim(right, c * columns, columns, 1), 1, 0)
        total = (keep + got.astype(wide)).astype(low)
        total = total.reshape(moves.nz, moves.nx, -1, columns)
        piece = (moves.over_x_then_z if x_first else moves.over_z_then_x)(total, m, z)
        return moves.gather_x_core(piece, m, c).astype(wide)

    sum_d = ffn_weight_grad(g_own, g_oth, hid, False)
    sum_g = ffn_weight_grad(xn_own, xn_oth, grad_gate, True)
    sum_u = ffn_weight_grad(xn_own, xn_oth, grad_up, True)

    back, grad_gain_two = norm_back(hres, scale_two, gain_two, gx)
    grad_hres = g_own.astype(wide) + back
    branch = both_halves(grad_hres.astype(low))

    grad_mixed = dot(out_w, branch, 1, 0).astype(low)
    grad_qkv, grad_bias = attn_backward(qkv, grad_mixed, mixed, probs)
    grad_attn_w = jnp.concatenate(
        [dot(xn_one, grad_qkv, 1, 1).astype(low), dot(branch, mixed, 1, 1).astype(low)], axis=1
    )
    sent = dot(qkv_w, other_half(grad_qkv), 0, 0).astype(low)
    gx = dot(qkv_w, my_half(grad_qkv), 0, 0) + moves.core(sent).astype(wide)
    back, grad_gain_one = norm_back(x_wide, scale_one, gain_one, gx)
    grad_in = moves.swap((grad_hres + back).astype(low)).astype(wide)

    columns = grad_attn_w.shape[1] // 2
    got = moves.over_y(lax.dynamic_slice_in_dim(grad_attn_w, (1 - y) * columns, columns, 1))
    total = lax.dynamic_slice_in_dim(grad_attn_w, y * columns, columns, 1).astype(wide) + got.astype(wide)
    total = total.astype(low).reshape(moves.nz, moves.nx, -1, columns)
    piece = moves.over_x_then_z(total, m, z)
    pieces = lax.all_gather(piece, ("seq", "tensor")).reshape(moves.nx, 2, 2, -1, columns)
    pieces = lax.dynamic_index_in_dim(pieces, y, 1, False)
    sums = pieces.transpose(0, 2, 1, 3).reshape(-1, 2 * columns).astype(wide)
    sum_q, sum_k, sum_v, sum_o = (
        sums[:, i * inner_width : (i + 1) * inner_width] for i in range(4)
    )

    bias_full = jnp.zeros((grad_bias.shape[0], 2 * heads), wide)
    bias_full = lax.dynamic_update_slice(bias_full, grad_bias, (jnp.int32(0), c * heads))
    gain_one_sum, gain_two_sum, bias_sum = lax.psum(
        (grad_gain_one, grad_gain_two, bias_full), ("dp", "seq", "tensor")
    )
    return (
        out_y.T.reshape(half_len, 1, width),
        grad_in.T.reshape(half_len, 1, width),
        gain_one_sum,
        sum_q,
        sum_k,
        sum_v,
        bias_sum,
        sum_o.T,
        gain_two_sum,
        sum_g,
        sum_u,
        sum_d.T,
    )


def solution(mesh):
    rows = P("tensor", ("dp", "seq"), None)
    columns = P(None, "tensor")
    return jax.shard_map(
        functools.partial(local, mesh),
        mesh=mesh,
        in_specs=(
            rows,
            rows,
            P(("dp", "seq"), None),
            P(("dp", "seq")),
            P(),
            columns,
            columns,
            columns,
            columns,
            P("tensor", None),
            P(),
            columns,
            columns,
            P("tensor", None),
        ),
        out_specs=(
            rows,
            rows,
            P(),
            P("dp", "tensor"),
            P("dp", "tensor"),
            P("dp", "tensor"),
            P(),
            P("tensor", "dp"),
            P(),
            P("dp", "tensor"),
            P("dp", "tensor"),
            P("tensor", "dp"),
        ),
        check_vma=False,
    )
```

```python
import functools
import math

import jax
import jax.numpy as jnp
from jax import lax
from jax.experimental import pallas as pl
from jax.experimental.pallas import tpu as pltpu
from jax.sharding import PartitionSpec as P

steps_at = (1, 2, 3, 4, 5, 6, 7, 8, 12, 16, 23, 32, 46, 64, 91)
eps_norm = 1e-06
masked_score = -1e30
q_block = 256
band_half = 128
low = jnp.bfloat16
wide = jnp.float32
hint = pl.CostEstimate(flops=1000, bytes_accessed=1000, transcendentals=0)


def dot(a, b, ca, cb):
    return lax.dot_general(a, b, (((ca,), (cb,)), ((), ())), preferred_element_type=wide)


def after(value, *first):
    return lax.optimization_barrier((value, *first))[0]


def attn_fwd_kernel(length, bias_ref, q_ref, k_ref, v_ref, seg_k_ref, seg_q_ref, p_ref, o_ref, table):
    block = pl.program_id(0)
    head = pl.program_id(1)
    reach = length - q_block

    @pl.when(block == 0)
    def _():
        table[head, : reach - band_half, :] = jnp.full((reach - band_half, q_block), bias_ref[15, head], wide)
        tail = length + reach - (reach + q_block + band_half)
        table[head, reach + q_block + band_half :, :] = jnp.full((tail, q_block), bias_ref[31, head], wide)
        rows = q_block + 2 * band_half
        d = (
            lax.broadcasted_iota(jnp.int32, (rows, q_block), 0)
            - lax.broadcasted_iota(jnp.int32, (rows, q_block), 1)
            - band_half
        )
        n = jnp.abs(d)
        before = jnp.full((rows, q_block), bias_ref[0, head], wide)
        after = jnp.full((rows, q_block), bias_ref[16, head], wide)
        for number, step in enumerate(steps_at):
            reached = n >= step
            before = jnp.where(reached, bias_ref[number + 1, head], before)
            after = jnp.where(reached, bias_ref[number + 17, head], after)
        table[head, reach - band_half : reach + q_block + band_half, :] = jnp.where(d > 0, after, before)

    first = pl.multiple_of(reach - block * q_block, q_block)
    scores = dot(k_ref[...], q_ref[...], 0, 0) + table[head, pl.ds(first, length), :]
    seg_k = jnp.concatenate([seg_k_ref[...]] * (q_block // 128), axis=1)
    scores = jnp.where(seg_k == seg_q_ref[...], scores, masked_score)
    raised = jnp.exp(scores - jnp.max(scores, axis=0, keepdims=True))
    probs = (raised * (1.0 / jnp.sum(raised, axis=0, keepdims=True))).astype(low)
    p_ref[0] = probs
    o_ref[...] = dot(v_ref[...], probs, 1, 0).astype(low)


def attn_forward(qkv, seg, bias):
    width, length = qkv.shape
    heads = bias.shape[1]
    dim = width // (3 * heads)
    seg_k = jnp.broadcast_to(seg[:, None], (length, 128))
    seg_q = seg[None, :]
    blocks = length // q_block
    return pl.pallas_call(
        functools.partial(attn_fwd_kernel, length),
        grid=(blocks, heads),
        in_specs=[
            pl.BlockSpec(memory_space=pltpu.SMEM),
            pl.BlockSpec((dim, q_block), lambda b, h: (h, b)),
            pl.BlockSpec((dim, length), lambda b, h: (heads + h, 0)),
            pl.BlockSpec((dim, length), lambda b, h: (2 * heads + h, 0)),
            pl.BlockSpec((length, 128), lambda b, h: (0, 0)),
            pl.BlockSpec((1, q_block), lambda b, h: (0, b)),
        ],
        out_specs=[
            pl.BlockSpec((1, length, q_block), lambda b, h: (h, 0, b)),
            pl.BlockSpec((dim, q_block), lambda b, h: (h, b)),
        ],
        out_shape=[
            jax.ShapeDtypeStruct((heads, length, length), low),
            jax.ShapeDtypeStruct((heads * dim, length), low),
        ],
        scratch_shapes=[pltpu.VMEM((heads, 2 * length - q_block, q_block), wide)],
        compiler_params=pltpu.CompilerParams(vmem_limit_bytes=48 << 20),
        cost_estimate=hint,
        name="attn_forward",
    )(bias, qkv, qkv, qkv, seg_k, seg_q)


def attn_bwd_kernel(length, q_ref, k_ref, v_ref, go_ref, o_ref, p_ref, gq_ref, gk_ref, gv_ref, gb_ref, k_acc, v_acc, sums):
    block = pl.program_id(1)
    reach = length - q_block

    @pl.when(block == 0)
    def _():
        k_acc[...] = jnp.zeros_like(k_acc)
        v_acc[...] = jnp.zeros_like(v_acc)
        sums[...] = jnp.zeros_like(sums)

    probs = p_ref[0]
    go = go_ref[...]
    inner = jnp.sum(go.astype(wide) * o_ref[...].astype(wide), axis=0, keepdims=True)
    scores = probs.astype(wide) * (dot(v_ref[...], go, 0, 0) - inner)
    first = pl.multiple_of(reach - block * q_block, q_block)
    sums[pl.ds(first, length), :] += scores
    scores = scores.astype(low)
    gq_ref[...] = dot(k_ref[...], scores, 1, 0).astype(low)
    k_acc[...] += dot(q_ref[...], scores, 1, 1)
    v_acc[...] += dot(go, probs, 1, 1)

    @pl.when(block == pl.num_programs(1) - 1)
    def _():
        gk_ref[...] = k_acc[...].astype(low)
        gv_ref[...] = v_acc[...].astype(low)
        rows = q_block + 2 * band_half
        d = (
            lax.broadcasted_iota(jnp.int32, (rows, q_block), 0)
            - lax.broadcasted_iota(jnp.int32, (rows, q_block), 1)
            - band_half
        )
        n = jnp.abs(d)
        near = sums[reach - band_half : reach + q_block + band_half, :]
        far_before = jnp.sum(sums[: reach - band_half, :], axis=0, keepdims=True)
        far_after = jnp.sum(sums[reach + q_block + band_half :, :], axis=0, keepdims=True)
        bucket = jnp.zeros((rows, q_block), jnp.int32)
        for step in steps_at:
            bucket = bucket + jnp.where(n >= step, 1, 0)
        bucket = bucket + jnp.where(d > 0, 16, 0)
        for b in range(32):
            total = jnp.sum(jnp.where(bucket == b, near, 0.0), axis=0, keepdims=True)
            if b == 15:
                total = total + far_before
            if b == 31:
                total = total + far_after
            gb_ref[0, b : b + 1, :] = total


def attn_backward(qkv, grad_mixed, mixed, probs):
    width, length = qkv.shape
    heads = probs.shape[0]
    dim = width // (3 * heads)
    blocks = length // q_block
    half = pl.BlockSpec((dim, q_block), lambda h, b: (h, b))
    whole = pl.BlockSpec((dim, length), lambda h, b: (h, 0))
    gq, gk, gv, gb = pl.pallas_call(
        functools.partial(attn_bwd_kernel, length),
        grid=(heads, blocks),
        in_specs=[
            half,
            pl.BlockSpec((dim, length), lambda h, b: (heads + h, 0)),
            pl.BlockSpec((dim, length), lambda h, b: (2 * heads + h, 0)),
            half,
            half,
            pl.BlockSpec((1, length, q_block), lambda h, b: (h, 0, b)),
        ],
        out_specs=[half, whole, whole, pl.BlockSpec((1, 32, q_block), lambda h, b: (h, 0, 0))],
        out_shape=[
            jax.ShapeDtypeStruct((heads * dim, length), low),
            jax.ShapeDtypeStruct((heads * dim, length), low),
            jax.ShapeDtypeStruct((heads * dim, length), low),
            jax.ShapeDtypeStruct((heads, 32, q_block), wide),
        ],
        scratch_shapes=[
            pltpu.VMEM((dim, length), wide),
            pltpu.VMEM((dim, length), wide),
            pltpu.VMEM((2 * length - q_block, q_block), wide),
        ],
        compiler_params=pltpu.CompilerParams(vmem_limit_bytes=48 << 20),
        cost_estimate=hint,
        name="attn_backward",
    )(qkv, qkv, qkv, grad_mixed, mixed, probs)
    return jnp.concatenate([gq, gk, gv], axis=0), jnp.sum(gb, axis=2).T


def ffn_kernel(
    x_ref, go_ref, gr_ref, gate_w, up_w, down_w,
    hid_ref, gg_ref, gu_ref, xr_ref, out_ref, out_r_ref, gx_ref,
    xs, gs, out_acc, gx_acc, x_in, gx_out, gx_in, sems,
):
    chunk = pl.program_id(0)
    tile = pl.program_id(1)
    size = xs.shape[0]
    there = {"tensor": 1 - lax.axis_index("tensor")}
    half = [pl.ds(0, size), pl.ds(size, size)]

    def send_x(h):
        return pltpu.make_async_remote_copy(
            src_ref=x_ref.at[:, half[h]], dst_ref=x_in.at[h], send_sem=sems.at[h], recv_sem=sems.at[2 + h],
            device_id=there, device_id_type=pl.DeviceIdType.MESH,
        )

    def send_gx(h):
        return pltpu.make_async_remote_copy(
            src_ref=gx_out.at[h], dst_ref=gx_in.at[h], send_sem=sems.at[4 + h], recv_sem=sems.at[6 + h],
            device_id=there, device_id_type=pl.DeviceIdType.MESH,
        )

    @pl.when(tile == 0)
    def _():
        out_acc[...] = jnp.zeros_like(out_acc)
        gx_acc[...] = jnp.zeros_like(gx_acc)

    @pl.when((tile == 0) & (chunk == 0))
    def _():
        barrier = pltpu.get_barrier_semaphore()
        pl.semaphore_signal(barrier, inc=1, device_id=there, device_id_type=pl.DeviceIdType.MESH)
        pl.semaphore_wait(barrier, 1)
        send_x(0).start()
        send_x(1).start()
        xs[...] = x_ref[:, half[1]].T
        gs[...] = go_ref[:, half[1]].T

    for h in range(2):

        @pl.when((tile == 0) & (chunk == 1 + h))
        def _(h=h):
            send_x(h).wait_recv()
            xs[...] = x_in[h].T
            gs[...] = gr_ref[:, half[h]].T
            xr_ref[:, half[h]] = x_in[h]

    @pl.when((tile == 0) & (chunk == 3))
    def _():
        xs[...] = x_ref[:, half[0]].T
        gs[...] = go_ref[:, half[0]].T

    gate = dot(xs[...], gate_w[...], 1, 0)
    up = dot(xs[...], up_w[...], 1, 0)
    grad = dot(gs[...], down_w[...], 1, 0)
    c = math.sqrt(2.0 / math.pi)
    square = gate * gate
    t = jnp.tanh(c * gate * (1.0 + 0.044715 * square))
    part = 0.5 * (1.0 + t)
    gelu = gate * part
    slope = part + 0.5 * gate * (1.0 - t * t) * (c * (1.0 + 3 * 0.044715 * square))
    hid = (gelu * up).astype(low)
    gg = (grad * up * slope).astype(low)
    gu = (grad * gelu).astype(low)
    hid_ref[...] = hid
    gg_ref[...] = gg
    gu_ref[...] = gu
    out_acc[...] += dot(down_w[...], hid, 1, 1)
    gx_acc[...] += dot(gate_w[...], gg, 1, 1) + dot(up_w[...], gu, 1, 1)

    last = tile == pl.num_programs(1) - 1
    for at, h in ((0, 1), (3, 0)):

        @pl.when(last & (chunk == at))
        def _(h=h):
            out_ref[:, half[h]] = out_acc[...]
            gx_ref[:, half[h]] = gx_acc[...]

    for h in range(2):

        @pl.when(last & (chunk == 1 + h))
        def _(h=h):
            out_r_ref[:, half[h]] = out_acc[...].astype(low)
            gx_out[h] = gx_acc[...].astype(low)
            send_gx(h).start()

    @pl.when(last & (chunk == 3))
    def _():
        for h in range(2):
            send_gx(h).wait_recv()
            gx_ref[:, half[h]] += gx_in[h].astype(wide)
        for h in range(2):
            send_x(h).wait_send()
            send_gx(h).wait_send()


def ffn(x, g_own, g_oth, gate_w, up_w, down_w):
    width, tokens = x.shape
    hidden = gate_w.shape[1]
    tile, size = 256, tokens // 2
    full = pl.BlockSpec((width, tokens), lambda s, j: (0, 0), pipeline_mode=pl.Buffered(1))
    weight = pl.BlockSpec((width, tile), lambda s, j: (0, j))
    act = pl.BlockSpec((size, tile), lambda s, j: ((s + 1) % 4, j))
    act_shape = jax.ShapeDtypeStruct((2 * tokens, hidden), low)
    tokens_of = lambda kind: jax.ShapeDtypeStruct((width, tokens), kind)
    part = pltpu.VMEM((2, width, size), low)
    return pl.pallas_call(
        ffn_kernel,
        grid=(4, hidden // tile),
        in_specs=[full, full, full, weight, weight, weight],
        out_specs=[act, act, act, full, full, full, full],
        out_shape=[act_shape, act_shape, act_shape, tokens_of(low), tokens_of(wide), tokens_of(low), tokens_of(wide)],
        scratch_shapes=[
            pltpu.VMEM((size, width), low),
            pltpu.VMEM((size, width), low),
            pltpu.VMEM((width, size), wide),
            pltpu.VMEM((width, size), wide),
            part,
            part,
            part,
            pltpu.SemaphoreType.DMA((8,)),
        ],
        compiler_params=pltpu.CompilerParams(vmem_limit_bytes=56 << 20, collective_id=0, has_side_effects=True),
        cost_estimate=hint,
        name="ffn_both_ways",
    )(x, g_own, g_oth, gate_w, up_w, down_w)


def weight_grad_kernel(core_ref, own_ref, oth_ref, right_ref, *refs):
    tokens = own_ref.shape[1]
    total = dot(own_ref[...], right_ref[:tokens, :], 1, 0) + dot(oth_ref[...], right_ref[tokens:, :], 1, 0)
    if len(refs) == 2:
        total = total + refs[0][...].astype(wide)
    refs[-1][...] = total.astype(low)


def weight_grad(own, oth, right, core, got=None):
    width, tokens = own.shape
    columns = right.shape[1] // 2
    blocks = 4
    rows = width // blocks
    left = pl.BlockSpec((rows, tokens), lambda i, core_ref: (i, 0))
    out = pl.BlockSpec((rows, columns), lambda i, core_ref: (i, 0))
    args = [own, oth, right] + ([] if got is None else [got])
    return pl.pallas_call(
        weight_grad_kernel,
        grid_spec=pltpu.PrefetchScalarGridSpec(
            num_scalar_prefetch=1,
            grid=(blocks,),
            in_specs=[
                left,
                left,
                pl.BlockSpec((2 * tokens, columns), lambda i, core_ref: (0, core_ref[0]), pipeline_mode=pl.Buffered(1)),
            ]
            + ([] if got is None else [out]),
            out_specs=out,
        ),
        out_shape=jax.ShapeDtypeStruct((width, columns), low),
        compiler_params=pltpu.CompilerParams(vmem_limit_bytes=40 << 20),
        cost_estimate=hint,
        name="weight_grad",
    )(core.reshape(1), *args)


def norm_of(values, gain):
    scale = lax.rsqrt(jnp.mean(values * values, axis=0, keepdims=True) + eps_norm)
    return values * scale * gain, scale


def norm_back(values, scale, gain, grad):
    normed = values * scale
    pushed = gain * grad
    mean = jnp.mean(normed * pushed, axis=0, keepdims=True)
    return scale * (pushed - normed * mean), jnp.sum(grad * normed, axis=1)


class Moves:
    def __init__(self, mesh):
        self.nz = mesh.shape["dp"]
        self.nx = mesh.shape["seq"] // 2
        both = [(m, c, y) for m in range(self.nx) for c in range(2) for y in range(2)]
        at = lambda m, c, y: (m * 2 + c) * 2 + y
        self.swap_pairs = [(at(m, c, y), at(m, y, c)) for m, c, y in both if c != y]
        self.second_pairs = [(at(m, c, y), at(m, y, 1 - c)) for m, c, y in both]
        self.back_pairs = [(b, a) for a, b in self.second_pairs]
        self.ring_x = [(m * 2 + c, (m + 1) % self.nx * 2 + c) for m in range(self.nx) for c in range(2)]
        self.y = lax.axis_index("tensor")
        self.z = lax.axis_index("dp")
        s = lax.axis_index("seq")
        self.c = s % 2
        self.m = s // 2

    def swap(self, a):
        got = lax.ppermute(a, ("seq", "tensor"), self.swap_pairs)
        return jnp.where(self.c == self.y, a, got)

    def second(self, a):
        return lax.ppermute(a, ("seq", "tensor"), self.second_pairs)

    def back(self, a):
        return lax.ppermute(a, ("seq", "tensor"), self.back_pairs)

    def core(self, a):
        return lax.ppermute(a, "seq", [(s, s ^ 1) for s in range(2 * self.nx)])

    def over_y(self, a):
        return lax.ppermute(a, "tensor", [(0, 1), (1, 0)])

    def over_x(self, a):
        return lax.ppermute(a, "seq", self.ring_x)

    def start_x(self, a):
        take = lax.dynamic_index_in_dim(a, (self.m + self.nx - 1) % self.nx, 1, False)
        return a, self.over_x(take)

    def finish_x(self, a, got, *first):
        take = lambda i: lax.dynamic_index_in_dim(a, i % self.nx, 1, False)
        got = after(got, *first)
        held = (got.astype(wide) + take(self.m + 2 * self.nx - 2).astype(wide)).astype(low)
        for t in range(2, self.nx):
            held = (self.over_x(held).astype(wide) + take(self.m + 2 * self.nx - 1 - t).astype(wide)).astype(low)
        return held

    def scatter_x(self, a):
        take = lambda i: lax.dynamic_index_in_dim(a, i % self.nx, 1, False)
        held = take(self.m + self.nx - 1)
        for t in range(1, self.nx):
            held = (self.over_x(held).astype(wide) + take(self.m + 2 * self.nx - 1 - t).astype(wide)).astype(low)
        return held

    def scatter_z(self, a):
        return lax.psum_scatter(a, "dp", scatter_dimension=0, tiled=True)

    def gather_x(self, piece):
        if self.nx == 2:
            over = self.over_x(piece)
            return jnp.where(
                self.m == 0, jnp.concatenate([piece, over], 0), jnp.concatenate([over, piece], 0)
            )
        groups = [[m * 2 + c for m in range(self.nx)] for c in range(2)]
        return lax.all_gather(piece, "seq", axis=0, tiled=True, axis_index_groups=groups)

    def gather_core(self, piece):
        there = self.core(piece)
        return jnp.where(
            self.c == 0, jnp.concatenate([piece, there], 1), jnp.concatenate([there, piece], 1)
        )

    def sum_everywhere(self, a):
        a = a + self.core(a)
        a = a + self.over_y(a)
        step = 1
        while step < self.nx:
            a = a + lax.ppermute(a, "seq", [(s, s ^ (2 * step)) for s in range(2 * self.nx)])
            step *= 2
        step = 1
        while step < self.nz:
            a = a + lax.ppermute(a, "dp", [(z, z ^ step) for z in range(self.nz)])
            step *= 2
        return a


def segment_ids(lengths, valid, length):
    ends = jnp.sum(jnp.where(jnp.arange(4)[None, :] <= jnp.arange(4)[:, None], lengths[None, :], 0), axis=1)
    where_at = jnp.arange(length, dtype=jnp.int32)
    counted = jnp.sum((where_at[:, None] >= ends[None, :]).astype(jnp.int32), axis=1)
    return jnp.where(where_at < valid, counted, 4)


def local(
    mesh,
    layer_in,
    out_grad,
    doc_lengths,
    valid_length,
    gain_attn,
    query_weight,
    key_weight,
    value_weight,
    position_bias,
    output_weight,
    gain_ffn,
    gate_weight,
    up_weight,
    down_weight,
):
    moves = Moves(mesh)
    half_len, _, width = layer_in.shape
    length = 2 * half_len
    heads = position_bias.shape[1]
    inner_width = query_weight.shape[1]
    y, c, m = moves.y, moves.c, moves.m

    facts = jnp.concatenate([doc_lengths[0].astype(wide), valid_length.astype(wide), position_bias.reshape(-1)])
    facts = moves.swap(facts)
    bias = facts[5:].reshape(position_bias.shape)
    facts = facts[:5].astype(jnp.int32)
    x_in = moves.swap(layer_in.reshape(half_len, width).T)
    qkv_w = jnp.concatenate([query_weight.T, key_weight.T, value_weight.T], axis=0)
    qkv_w = moves.swap(qkv_w)
    positions = y * half_len + jnp.arange(half_len, dtype=jnp.int32)
    g_in = jnp.where((positions < valid_length[0])[None, :], out_grad.reshape(half_len, width).T, 0)
    g_in, out_w, x_in, facts = lax.optimization_barrier((g_in.astype(low), output_weight, x_in, facts))
    out_w = moves.swap(out_w)
    g_own = moves.swap(g_in)
    g_oth = moves.second(g_in)
    segment = segment_ids(facts[:4], facts[4], length)
    gain_one = gain_attn.astype(wide)[:, None]
    gain_two = gain_ffn.astype(wide)[:, None]

    def both_halves(own):
        other = moves.core(own)
        return jnp.where(
            c == 0, jnp.concatenate([own, other], 1), jnp.concatenate([other, own], 1)
        )

    def my_half(a):
        return lax.dynamic_slice_in_dim(a, c * half_len, half_len, 1)

    def other_half(a):
        return lax.dynamic_slice_in_dim(a, (1 - c) * half_len, half_len, 1)

    x_wide = x_in.astype(wide)
    normed, scale_one = norm_of(x_wide, gain_one)
    xn_one = both_halves(normed.astype(low))
    qkv = dot(qkv_w, xn_one, 1, 0).astype(low)
    probs, mixed = attn_forward(qkv, segment, bias)
    sent = dot(out_w, other_half(mixed), 0, 0).astype(low)
    hres = x_wide + dot(out_w, my_half(mixed), 0, 0) + moves.core(sent).astype(wide)

    normed, scale_two = norm_of(hres, gain_two)
    xn_own = normed.astype(low)
    hid, grad_gate, grad_up, xn_oth, out_own, out_oth, gx = ffn(
        xn_own, g_own, g_oth, gate_weight, up_weight, down_weight.T
    )

    columns = hid.shape[1] // 2
    send_d = weight_grad(g_own, g_oth, hid, 1 - c)
    got_d = moves.core(send_d)
    send_g = weight_grad(xn_own, xn_oth, after(grad_gate, send_d), 1 - c)
    got_g = moves.core(send_g)
    send_u = weight_grad(xn_own, xn_oth, after(grad_up, send_g), 1 - c)
    got_u = moves.core(send_u)
    total_d = weight_grad(g_own, g_oth, after(hid, send_u), c, got_d)
    total_g = weight_grad(xn_own, xn_oth, after(grad_gate, total_d), c, got_g)
    total_u = weight_grad(xn_own, xn_oth, after(grad_up, total_g), c, got_u)
    part_d = moves.scatter_z(total_d)
    x_sent = [moves.start_x(t.reshape(moves.nz, moves.nx, -1, columns)) for t in (total_g, total_u)]

    gx = after(gx, total_u)
    out_y = moves.swap((hres + out_own).astype(low)).astype(wide) + moves.back(out_oth).astype(wide)

    back, grad_gain_two = norm_back(hres, scale_two, gain_two, gx)
    grad_hres = g_own.astype(wide) + back
    branch = both_halves(grad_hres.astype(low))

    grad_mixed = dot(out_w, branch, 1, 0).astype(low)
    grad_qkv, grad_bias = attn_backward(qkv, grad_mixed, mixed, probs)

    part_g = moves.finish_x(*x_sent[0], grad_qkv).reshape(-1, columns)
    sent = dot(qkv_w, other_half(after(grad_qkv, part_g)), 0, 0).astype(low)
    part_g = moves.scatter_z(part_g)
    got_x = moves.core(sent)
    grad_attn_w = jnp.concatenate(
        [dot(xn_one, after(grad_qkv, sent), 1, 1).astype(low), dot(branch, mixed, 1, 1).astype(low)], axis=1
    )
    gx = dot(qkv_w, my_half(after(grad_qkv, grad_attn_w)), 0, 0) + got_x.astype(wide)
    back, grad_gain_one = norm_back(x_wide, scale_one, gain_one, gx)
    grad_in = (grad_hres + back).astype(low)
    part_u = moves.scatter_z(moves.finish_x(*x_sent[1], grad_in).reshape(-1, columns))

    a_columns = grad_attn_w.shape[1] // 2
    chunks = grad_attn_w.reshape(moves.nz, moves.nx, -1, 2 * a_columns)

    def scatter_y(a):
        got = moves.over_y(lax.dynamic_slice_in_dim(a, (1 - y) * a_columns, a_columns, a.ndim - 1))
        kept = lax.dynamic_slice_in_dim(a, y * a_columns, a_columns, a.ndim - 1)
        return (kept.astype(wide) + got.astype(wide)).astype(low)

    half_z = moves.nz // 2
    part = jnp.concatenate(
        [moves.scatter_x(scatter_y(chunks[:half_z])), scatter_y(moves.scatter_x(chunks[half_z:]))], 0
    )
    piece = moves.gather_x(moves.scatter_z(part.reshape(-1, a_columns)))
    there = moves.over_y(piece)
    group = jnp.where(y == 0, jnp.concatenate([piece, there], 1), jnp.concatenate([there, piece], 1))
    sums = jnp.where(c == y, group, moves.core(group)).astype(wide)
    sum_q, sum_k, sum_v, sum_o = (
        sums[:, i * inner_width : (i + 1) * inner_width] for i in range(4)
    )
    grad_in = moves.swap(grad_in).astype(wide)

    if moves.nx == 2:
        part_d = (part_d.astype(wide) + moves.over_x(part_d).astype(wide)).astype(low)
    else:
        part_d = moves.gather_x(moves.scatter_x(part_d.reshape(1, moves.nx, -1, columns))[0])
    sum_d = moves.gather_core(part_d).astype(wide)
    sum_g = moves.gather_core(moves.gather_x(part_g)).astype(wide)
    sum_u = moves.gather_core(moves.gather_x(part_u)).astype(wide)

    bias_full = jnp.zeros((grad_bias.shape[0], 2 * heads), wide)
    bias_full = lax.dynamic_update_slice(bias_full, grad_bias, (jnp.int32(0), c * heads))
    early = moves.sum_everywhere(jnp.concatenate([grad_gain_two, bias_full.reshape(-1)]))
    gain_two_sum, bias_sum = early[:width], early[width:].reshape(bias_full.shape)
    gain_one_sum = moves.sum_everywhere(grad_gain_one)
    return (
        out_y.astype(low).T.reshape(half_len, 1, width),
        grad_in.T.reshape(half_len, 1, width),
        gain_one_sum,
        sum_q,
        sum_k,
        sum_v,
        bias_sum,
        sum_o.T,
        gain_two_sum,
        sum_g,
        sum_u,
        sum_d.T,
    )


def solution(mesh):
    rows = P("tensor", ("dp", "seq"), None)
    columns = P(None, "tensor")
    return jax.shard_map(
        functools.partial(local, mesh),
        mesh=mesh,
        in_specs=(
            rows,
            rows,
            P(("dp", "seq"), None),
            P(("dp", "seq")),
            P(),
            columns,
            columns,
            columns,
            columns,
            P("tensor", None),
            P(),
            columns,
            columns,
            P("tensor", None),
        ),
        out_specs=(
            rows,
            rows,
            P(),
            P("dp", "tensor"),
            P("dp", "tensor"),
            P("dp", "tensor"),
            P(),
            P("tensor", "dp"),
            P(),
            P("dp", "tensor"),
            P("dp", "tensor"),
            P("tensor", "dp"),
        ),
        check_vma=False,
    )
```

```python
import functools
import math

import jax
import jax.numpy as jnp
from jax import lax
from jax.experimental import pallas as pl
from jax.experimental.pallas import tpu as pltpu
from jax.sharding import PartitionSpec as P

steps_at = (1, 2, 3, 4, 5, 6, 7, 8, 12, 16, 23, 32, 46, 64, 91)
eps_norm = 1e-06
masked_score = -1e30
q_block = 256
band_half = 128
low = jnp.bfloat16
wide = jnp.float32
hint = pl.CostEstimate(flops=1000, bytes_accessed=1000, transcendentals=0)


def dot(a, b, ca, cb):
    return lax.dot_general(a, b, (((ca,), (cb,)), ((), ())), preferred_element_type=wide)


def after(value, *first):
    return lax.optimization_barrier((value, *first))[0]


def attn_fwd_kernel(length, bias_ref, q_ref, k_ref, v_ref, seg_k_ref, seg_q_ref, p_ref, o_ref, table):
    block = pl.program_id(0)
    head = pl.program_id(1)
    reach = length - q_block

    @pl.when(block == 0)
    def _():
        table[head, : reach - band_half, :] = jnp.full((reach - band_half, q_block), bias_ref[15, head], wide)
        tail = length + reach - (reach + q_block + band_half)
        table[head, reach + q_block + band_half :, :] = jnp.full((tail, q_block), bias_ref[31, head], wide)
        rows = q_block + 2 * band_half
        d = (
            lax.broadcasted_iota(jnp.int32, (rows, q_block), 0)
            - lax.broadcasted_iota(jnp.int32, (rows, q_block), 1)
            - band_half
        )
        n = jnp.abs(d)
        before = jnp.full((rows, q_block), bias_ref[0, head], wide)
        after = jnp.full((rows, q_block), bias_ref[16, head], wide)
        for number, step in enumerate(steps_at):
            reached = n >= step
            before = jnp.where(reached, bias_ref[number + 1, head], before)
            after = jnp.where(reached, bias_ref[number + 17, head], after)
        table[head, reach - band_half : reach + q_block + band_half, :] = jnp.where(d > 0, after, before)

    first = pl.multiple_of(reach - block * q_block, q_block)
    scores = dot(k_ref[...], q_ref[...], 0, 0) + table[head, pl.ds(first, length), :]
    seg_k = jnp.concatenate([seg_k_ref[...]] * (q_block // 128), axis=1)
    scores = jnp.where(seg_k == seg_q_ref[...], scores, masked_score)
    raised = jnp.exp(scores - jnp.max(scores, axis=0, keepdims=True))
    probs = (raised * (1.0 / jnp.sum(raised, axis=0, keepdims=True))).astype(low)
    p_ref[0] = probs
    o_ref[...] = dot(v_ref[...], probs, 1, 0).astype(low)


def attn_forward(qkv, seg, bias):
    width, length = qkv.shape
    heads = bias.shape[1]
    dim = width // (3 * heads)
    seg_k = jnp.broadcast_to(seg[:, None], (length, 128))
    seg_q = seg[None, :]
    blocks = length // q_block
    return pl.pallas_call(
        functools.partial(attn_fwd_kernel, length),
        grid=(blocks, heads),
        in_specs=[
            pl.BlockSpec(memory_space=pltpu.SMEM),
            pl.BlockSpec((dim, q_block), lambda b, h: (h, b)),
            pl.BlockSpec((dim, length), lambda b, h: (heads + h, 0)),
            pl.BlockSpec((dim, length), lambda b, h: (2 * heads + h, 0)),
            pl.BlockSpec((length, 128), lambda b, h: (0, 0)),
            pl.BlockSpec((1, q_block), lambda b, h: (0, b)),
        ],
        out_specs=[
            pl.BlockSpec((1, length, q_block), lambda b, h: (h, 0, b)),
            pl.BlockSpec((dim, q_block), lambda b, h: (h, b)),
        ],
        out_shape=[
            jax.ShapeDtypeStruct((heads, length, length), low),
            jax.ShapeDtypeStruct((heads * dim, length), low),
        ],
        scratch_shapes=[pltpu.VMEM((heads, 2 * length - q_block, q_block), wide)],
        compiler_params=pltpu.CompilerParams(vmem_limit_bytes=48 << 20),
        cost_estimate=hint,
        name="attn_forward",
    )(bias, qkv, qkv, qkv, seg_k, seg_q)


def attn_bwd_kernel(length, q_ref, k_ref, v_ref, go_ref, o_ref, p_ref, gq_ref, gk_ref, gv_ref, gb_ref, k_acc, v_acc, sums):
    block = pl.program_id(1)
    reach = length - q_block

    @pl.when(block == 0)
    def _():
        k_acc[...] = jnp.zeros_like(k_acc)
        v_acc[...] = jnp.zeros_like(v_acc)
        sums[...] = jnp.zeros_like(sums)

    probs = p_ref[0]
    go = go_ref[...]
    inner = jnp.sum(go.astype(wide) * o_ref[...].astype(wide), axis=0, keepdims=True)
    scores = probs.astype(wide) * (dot(v_ref[...], go, 0, 0) - inner)
    first = pl.multiple_of(reach - block * q_block, q_block)
    sums[pl.ds(first, length), :] += scores
    scores = scores.astype(low)
    gq_ref[...] = dot(k_ref[...], scores, 1, 0).astype(low)
    k_acc[...] += dot(q_ref[...], scores, 1, 1)
    v_acc[...] += dot(go, probs, 1, 1)

    @pl.when(block == pl.num_programs(1) - 1)
    def _():
        gk_ref[...] = k_acc[...].astype(low)
        gv_ref[...] = v_acc[...].astype(low)
        rows = q_block + 2 * band_half
        d = (
            lax.broadcasted_iota(jnp.int32, (rows, q_block), 0)
            - lax.broadcasted_iota(jnp.int32, (rows, q_block), 1)
            - band_half
        )
        n = jnp.abs(d)
        near = sums[reach - band_half : reach + q_block + band_half, :]
        far_before = jnp.sum(sums[: reach - band_half, :], axis=0, keepdims=True)
        far_after = jnp.sum(sums[reach + q_block + band_half :, :], axis=0, keepdims=True)
        bucket = jnp.zeros((rows, q_block), jnp.int32)
        for step in steps_at:
            bucket = bucket + jnp.where(n >= step, 1, 0)
        bucket = bucket + jnp.where(d > 0, 16, 0)
        for b in range(32):
            total = jnp.sum(jnp.where(bucket == b, near, 0.0), axis=0, keepdims=True)
            if b == 15:
                total = total + far_before
            if b == 31:
                total = total + far_after
            gb_ref[0, b : b + 1, :] = total


def attn_backward(qkv, grad_mixed, mixed, probs):
    width, length = qkv.shape
    heads = probs.shape[0]
    dim = width // (3 * heads)
    blocks = length // q_block
    half = pl.BlockSpec((dim, q_block), lambda h, b: (h, b))
    whole = pl.BlockSpec((dim, length), lambda h, b: (h, 0))
    gq, gk, gv, gb = pl.pallas_call(
        functools.partial(attn_bwd_kernel, length),
        grid=(heads, blocks),
        in_specs=[
            half,
            pl.BlockSpec((dim, length), lambda h, b: (heads + h, 0)),
            pl.BlockSpec((dim, length), lambda h, b: (2 * heads + h, 0)),
            half,
            half,
            pl.BlockSpec((1, length, q_block), lambda h, b: (h, 0, b)),
        ],
        out_specs=[half, whole, whole, pl.BlockSpec((1, 32, q_block), lambda h, b: (h, 0, 0))],
        out_shape=[
            jax.ShapeDtypeStruct((heads * dim, length), low),
            jax.ShapeDtypeStruct((heads * dim, length), low),
            jax.ShapeDtypeStruct((heads * dim, length), low),
            jax.ShapeDtypeStruct((heads, 32, q_block), wide),
        ],
        scratch_shapes=[
            pltpu.VMEM((dim, length), wide),
            pltpu.VMEM((dim, length), wide),
            pltpu.VMEM((2 * length - q_block, q_block), wide),
        ],
        compiler_params=pltpu.CompilerParams(vmem_limit_bytes=48 << 20),
        cost_estimate=hint,
        name="attn_backward",
    )(qkv, qkv, qkv, grad_mixed, mixed, probs)
    return jnp.concatenate([gq, gk, gv], axis=0), jnp.sum(gb, axis=2).T


def ffn_kernel(
    x_ref, go_ref, gr_ref, gate_w, up_w, down_w,
    hid_ref, pair_ref, xr_ref, out_ref, out_r_ref, gx_ref,
    xs, gs, out_acc, gx_acc, x_in, gx_out, gx_in, sems,
):
    chunk = pl.program_id(0)
    tile = pl.program_id(1)
    size = xs.shape[0]
    there = {"tensor": 1 - lax.axis_index("tensor")}
    half = [pl.ds(0, size), pl.ds(size, size)]

    def send_x(h):
        return pltpu.make_async_remote_copy(
            src_ref=x_ref.at[:, half[h]], dst_ref=x_in.at[h], send_sem=sems.at[h], recv_sem=sems.at[2 + h],
            device_id=there, device_id_type=pl.DeviceIdType.MESH,
        )

    def send_gx(h):
        return pltpu.make_async_remote_copy(
            src_ref=gx_out.at[h], dst_ref=gx_in.at[h], send_sem=sems.at[4 + h], recv_sem=sems.at[6 + h],
            device_id=there, device_id_type=pl.DeviceIdType.MESH,
        )

    @pl.when(tile == 0)
    def _():
        out_acc[...] = jnp.zeros_like(out_acc)
        gx_acc[...] = jnp.zeros_like(gx_acc)

    @pl.when((tile == 0) & (chunk == 0))
    def _():
        barrier = pltpu.get_barrier_semaphore()
        pl.semaphore_signal(barrier, inc=1, device_id=there, device_id_type=pl.DeviceIdType.MESH)
        pl.semaphore_wait(barrier, 1)
        send_x(0).start()
        send_x(1).start()
        xs[...] = x_ref[:, half[1]].T
        gs[...] = go_ref[:, half[1]].T

    for h in range(2):

        @pl.when((tile == 0) & (chunk == 1 + h))
        def _(h=h):
            send_x(h).wait_recv()
            xs[...] = x_in[h].T
            gs[...] = gr_ref[:, half[h]].T
            xr_ref[:, half[h]] = x_in[h]

    @pl.when((tile == 0) & (chunk == 3))
    def _():
        xs[...] = x_ref[:, half[0]].T
        gs[...] = go_ref[:, half[0]].T

    gate = dot(xs[...], gate_w[...], 1, 0)
    up = dot(xs[...], up_w[...], 1, 0)
    grad = dot(gs[...], down_w[...], 1, 0)
    c = math.sqrt(2.0 / math.pi)
    square = gate * gate
    t = jnp.tanh(c * gate * (1.0 + 0.044715 * square))
    part = 0.5 * (1.0 + t)
    gelu = gate * part
    slope = part + 0.5 * gate * (1.0 - t * t) * (c * (1.0 + 3 * 0.044715 * square))
    hid = (gelu * up).astype(low)
    gg = (grad * up * slope).astype(low)
    gu = (grad * gelu).astype(low)
    hid_ref[...] = hid
    pair_ref[0] = gg
    pair_ref[1] = gu
    out_acc[...] += dot(down_w[...], hid, 1, 1)
    gx_acc[...] += dot(gate_w[...], gg, 1, 1) + dot(up_w[...], gu, 1, 1)

    last = tile == pl.num_programs(1) - 1
    for at, h in ((0, 1), (3, 0)):

        @pl.when(last & (chunk == at))
        def _(h=h):
            out_ref[:, half[h]] = out_acc[...]
            gx_ref[:, half[h]] = gx_acc[...]

    for h in range(2):

        @pl.when(last & (chunk == 1 + h))
        def _(h=h):
            out_r_ref[:, half[h]] = out_acc[...].astype(low)
            gx_out[h] = gx_acc[...].astype(low)
            send_gx(h).start()

    @pl.when(last & (chunk == 3))
    def _():
        for h in range(2):
            send_gx(h).wait_recv()
            gx_ref[:, half[h]] += gx_in[h].astype(wide)
        for h in range(2):
            send_x(h).wait_send()
            send_gx(h).wait_send()


def ffn(x, g_own, g_oth, gate_w, up_w, down_w):
    width, tokens = x.shape
    hidden = gate_w.shape[1]
    tile, size = 256, tokens // 2
    full = pl.BlockSpec((width, tokens), lambda s, j: (0, 0), pipeline_mode=pl.Buffered(1))
    weight = pl.BlockSpec((width, tile), lambda s, j: (0, j))
    act = pl.BlockSpec((size, tile), lambda s, j: ((s + 1) % 4, j))
    act_shape = jax.ShapeDtypeStruct((2 * tokens, hidden), low)
    tokens_of = lambda kind: jax.ShapeDtypeStruct((width, tokens), kind)
    part = pltpu.VMEM((2, width, size), low)
    return pl.pallas_call(
        ffn_kernel,
        grid=(4, hidden // tile),
        in_specs=[full, full, full, weight, weight, weight],
        out_specs=[act, pl.BlockSpec((2, size, tile), lambda s, j: (0, (s + 1) % 4, j)), full, full, full, full],
        out_shape=[act_shape, jax.ShapeDtypeStruct((2, 2 * tokens, hidden), low), tokens_of(low), tokens_of(wide), tokens_of(low), tokens_of(wide)],
        scratch_shapes=[
            pltpu.VMEM((size, width), low),
            pltpu.VMEM((size, width), low),
            pltpu.VMEM((width, size), wide),
            pltpu.VMEM((width, size), wide),
            part,
            part,
            part,
            pltpu.SemaphoreType.DMA((8,)),
        ],
        compiler_params=pltpu.CompilerParams(vmem_limit_bytes=56 << 20, collective_id=0, has_side_effects=True),
        cost_estimate=hint,
        name="ffn_both_ways",
    )(x, g_own, g_oth, gate_w, up_w, down_w)


def weight_grad_kernel(core_ref, own_ref, oth_ref, right_ref, *refs):
    tokens = own_ref.shape[1]
    total = dot(own_ref[...], right_ref[:tokens, :], 1, 0) + dot(oth_ref[...], right_ref[tokens:, :], 1, 0)
    if len(refs) == 2:
        total = total + refs[0][...].astype(wide)
    refs[-1][...] = total.astype(low)


def weight_grad(own, oth, right, core, got=None):
    width, tokens = own.shape
    columns = right.shape[1] // 2
    blocks = 4
    rows = width // blocks
    left = pl.BlockSpec((rows, tokens), lambda i, core_ref: (i, 0))
    out = pl.BlockSpec((rows, columns), lambda i, core_ref: (i, 0))
    args = [own, oth, right] + ([] if got is None else [got])
    return pl.pallas_call(
        weight_grad_kernel,
        grid_spec=pltpu.PrefetchScalarGridSpec(
            num_scalar_prefetch=1,
            grid=(blocks,),
            in_specs=[
                left,
                left,
                pl.BlockSpec((2 * tokens, columns), lambda i, core_ref: (0, core_ref[0]), pipeline_mode=pl.Buffered(1)),
            ]
            + ([] if got is None else [out]),
            out_specs=out,
        ),
        out_shape=jax.ShapeDtypeStruct((width, columns), low),
        compiler_params=pltpu.CompilerParams(vmem_limit_bytes=40 << 20),
        cost_estimate=hint,
        name="weight_grad",
    )(core.reshape(1), *args)


def back_kernel(
    hid_h, pair_h, go_h, gr_h, xo_h, xr_h, gx_h, hres_h, xin_h, probs_h, xn1_h, outp_h, outr_h,
    out_w, w_t, qkv, mixed, gain2, gain1, scale2, scale1,
    got_p, got_r, got_in, d_out, p_out, a_out, gin, small,
    r_core, xp, zd, zp, dx, px, bf, rx, ya, xa, za, ab, ab2, sm_src, sm_in, send_sems, recv_sems, load_sems,
):
    s = lax.axis_index("seq")
    y = lax.axis_index("tensor")
    z = lax.axis_index("dp")
    c = s % 2
    m = s // 2
    width = xp.shape[0]
    rows = d_out.shape[0]
    columns = xp.shape[1]
    half_len = rx.shape[1]
    length = 2 * half_len
    heads = probs_h.shape[0]
    dim = mixed.shape[0] // heads
    zs = width // rows
    mesh_id = dict(device_id_type=pl.DeviceIdType.MESH)
    to_core = {"seq": 2 * m + 1 - c}
    to_x = {"seq": 2 * (1 - m) + c}
    to_y = {"tensor": 1 - y}
    to_z = {"dp": (z + 1) % zs}
    to_swap = {"seq": 2 * m + y, "tensor": c}
    to_back = {"seq": 2 * m + 1 - y, "tensor": c}

    barrier = pltpu.get_barrier_semaphore()
    greet = [to_core, to_y, {"seq": 2 * m + 1 - c, "tensor": 1 - y}, to_x] + [{"dp": (z + i) % zs} for i in range(1, zs)]
    for who in greet:
        pl.semaphore_signal(barrier, inc=1, device_id=who, **mesh_id)
    pl.semaphore_wait(barrier, len(greet))

    def move(k, src, dst, who):
        return pltpu.make_async_remote_copy(
            src_ref=src, dst_ref=dst, send_sem=send_sems.at[k], recv_sem=recv_sems.at[k], device_id=who, **mesh_id
        )

    def load(k, src, dst):
        return pltpu.make_async_copy(src, dst, load_sems.at[k])

    def chunk(j):
        return pl.ds(pl.multiple_of(j * rows, rows), rows)

    def side(i, size):
        return pl.ds(pl.multiple_of(i * size, 128), size)

    order = [(z + zs - 1 - k) % zs for k in range(zs)]
    mine = side(c, columns)
    my_half = side(c, half_len)
    other_half = side(1 - c, half_len)

    swap_out = move(35, outp_h, got_p, to_swap)
    back_out = move(36, outr_h, got_r, to_back)
    z_down = [move(3, r_core.at[0, chunk(order[0])], zd.at[0], to_z)] + [
        move(3 + t, zd.at[t - 1], zd.at[t], to_z) for t in range(1, zs - 1)
    ]
    x_down = move(6, zd.at[zs - 2], dx, to_x)
    core_down = move(7, d_out.at[:, mine], d_out.at[:, mine], to_core)
    x_pair = [move(8 + k, r_core.at[1, chunk(j)], xp.at[chunk(j)], to_x) for k, j in enumerate(order)]
    z_pair = [move(12, r_core.at[2, chunk(order[0])], zp.at[0], to_z)] + [
        move(12 + t, zp.at[t - 1], zp.at[t], to_z) for t in range(1, zs - 1)
    ]
    x_pair_back = move(15, zp.at[zs - 2], px, to_x)
    core_pair = move(16, p_out.at[m, :, mine], p_out.at[m, :, mine], to_core)
    core_pair_back = move(17, p_out.at[1 - m, :, mine], p_out.at[1 - m, :, mine], to_core)
    core_branch = move(18, bf.at[:, my_half], bf.at[:, my_half], to_core)
    a_cols = ya.shape[2]
    a_rows = xa.shape[1]
    my_cols = side(y, a_cols)
    my_rows = pl.ds(pl.multiple_of(m * a_rows, a_rows), a_rows)
    x_rows = pl.ds(pl.multiple_of((1 - m) * a_rows, a_rows), a_rows)
    x_attn = [move(24 + k, ya.at[j, x_rows], xa.at[j], to_x) for k, j in enumerate(order)]
    z_attn = [move(28, ya.at[order[0], my_rows], za.at[0], to_z)] + [
        move(28 + t, za.at[t - 1], za.at[t], to_z) for t in range(1, zs - 1)
    ]
    x_attn_back = move(31, ab.at[my_rows], ab.at[my_rows], to_x)
    y_attn_back = move(32, ab2.at[:, my_cols], ab2.at[:, my_cols], to_y)
    core_attn = move(33, ab2, a_out, to_core)
    swap_in = move(34, gin, got_in, to_swap)

    @pl.when(c != y)
    def _():
        swap_out.start()

    back_out.start()

    def step_z_down(t):
        z_down[t - 1].wait_recv()
        zd[t - 1] = (zd[t - 1].astype(wide) + r_core[0, chunk(order[t]), :].astype(wide)).astype(low)
        if t < zs - 1:
            z_down[t].start()

    def step_z_pair(t):
        x_pair[t].wait_recv()
        term = r_core[2, chunk(order[t]), :].astype(wide) + xp[chunk(order[t]), :].astype(wide)
        if t:
            z_pair[t - 1].wait_recv()
            zp[t - 1] = (zp[t - 1].astype(wide) + term).astype(low)
        else:
            r_core[2, chunk(order[0]), :] = term.astype(low)
        if t < zs - 1:
            z_pair[t].start()

    def weights(r_buf, l_go, l_gr, l_xo, l_xr, s_buf):
        loads = [
            load(0, hid_h, r_buf.at[0]),
            load(1, go_h, l_go),
            load(2, gr_h, l_gr),
            load(3, pair_h.at[1 - m], r_buf.at[1]),
            load(4, xo_h, l_xo),
            load(5, xr_h, l_xr),
        ]
        load_own = load(6, pair_h.at[m], r_buf.at[0])
        for each in loads:
            each.start()
        core = [move(k, s_buf.at[k % 2], r_core.at[k], to_core) for k in range(3)]

        def product(left_o, left_r, right, col, out, add):
            def block(i, carry):
                at = chunk(i)
                total = dot(left_o[at, :], right[:half_len, col], 1, 0)
                total = total + dot(left_r[at, :], right[half_len:, col], 1, 0)
                if add:
                    total = total + out[at, :].astype(wide)
                out[at, :] = total.astype(low)
                return carry

            lax.fori_loop(0, zs, block, 0)

        theirs = side(1 - c, columns)
        for each in loads[:3]:
            each.wait()
        product(l_go, l_gr, r_buf.at[0], theirs, s_buf.at[0], False)
        core[0].start()
        for each in loads[3:]:
            each.wait()
        product(l_xo, l_xr, r_buf.at[1], theirs, s_buf.at[1], False)
        core[1].start()
        core[0].wait_recv()
        product(l_go, l_gr, r_buf.at[0], mine, r_core.at[0], True)
        z_down[0].start()
        load_own.start()
        core[1].wait_recv()
        product(l_xo, l_xr, r_buf.at[1], mine, r_core.at[1], True)
        for each in x_pair:
            each.start()
        load_own.wait()
        core[0].wait_send()
        product(l_xo, l_xr, r_buf.at[0], theirs, s_buf.at[0], False)
        core[2].start()
        step_z_down(1)
        core[2].wait_recv()
        product(l_xo, l_xr, r_buf.at[0], mine, r_core.at[2], True)
        core[1].wait_send()
        core[2].wait_send()

    hidden = hid_h.shape[1]
    left = pltpu.VMEM((width, half_len), low)
    pl.run_scoped(
        weights,
        pltpu.VMEM((2, length, hidden), low),
        left,
        left,
        left,
        left,
        pltpu.VMEM((2, width, columns), low),
    )

    def attention(gxv, hv, gov, p_buf, k_acc, v_acc, sums, gqkv, gm, xn1, sx, ga):
        loads = [load(7, gx_h, gxv), load(8, hres_h, hv), load(9, go_h, gov), load(10, xn1_h, xn1)]
        load_x = load(11, xin_h, gov)
        for each in loads:
            each.start()

        def probs_load(h, b, slot):
            return load(12 + slot, probs_h.at[h, :, side(b, q_block)], p_buf.at[slot])

        probs_load(0, 0, 0).start()
        lanes = half_len // 128
        piece = 64
        pieces = width // piece

        def fold(a):
            return sum(a[:, i * 128 : (i + 1) * 128] for i in range(lanes))

        def spread(a):
            return jnp.concatenate([a] * lanes, axis=1)

        def norm_backward(values, gain, scale, grad, store, row):
            def first(i, total):
                at = pl.ds(pl.multiple_of(i * piece, piece), piece)
                return total + jnp.sum(values(at) * (spread(gain[at, :]) * grad(at)), axis=0, keepdims=True)

            total = lax.fori_loop(0, pieces, first, jnp.zeros((1, half_len), wide))
            mean = total * scale[...] * (1.0 / width)

            def second(i, carry):
                at = pl.ds(pl.multiple_of(i * piece, piece), piece)
                g = grad(at)
                normed = values(at) * scale[...]
                store(at, scale[...] * (spread(gain[at, :]) * g - normed * mean))
                ga_part[at, :] = fold(g * normed)
                return carry

            lax.fori_loop(0, pieces, second, 0)
            small[row : row + 1, :] = jnp.sum(ga_part[...].T, axis=0, keepdims=True)

        ga_part = sums.at[:width, :128]
        small[...] = jnp.zeros_like(small)
        for each in loads[:3]:
            each.wait()

        def store_hres(at, back):
            total = gov[at, :].astype(wide) + back
            gxv[at, :] = total
            bf[at, my_half] = total.astype(low)

        norm_backward(lambda at: hv[at, :], gain2, scale2, lambda at: gxv[at, :], store_hres, 0)
        core_branch.start()
        load_x.start()
        step_z_down(2)
        core_branch.wait_recv()
        gm[...] = dot(out_w[...], bf[...], 1, 0).astype(low)

        reach = length - q_block
        blocks = length // q_block
        near_rows = q_block + 2 * band_half
        d = (
            lax.broadcasted_iota(jnp.int32, (near_rows, q_block), 0)
            - lax.broadcasted_iota(jnp.int32, (near_rows, q_block), 1)
            - band_half
        )
        for h in range(heads):
            head = pl.ds(h * dim, dim)
            k_rows = pl.ds((heads + h) * dim, dim)
            v_rows = pl.ds((2 * heads + h) * dim, dim)
            k_acc[...] = jnp.zeros_like(k_acc)
            v_acc[...] = jnp.zeros_like(v_acc)
            sums[...] = jnp.zeros_like(sums)

            def block(b, carry):
                slot = b % 2
                at = side(b, q_block)
                probs_load(h, b, slot).wait()

                @pl.when(b < blocks - 1)
                def _():
                    probs_load(h, b + 1, 1 - slot).start()

                if h < heads - 1:

                    @pl.when(b == blocks - 1)
                    def _():
                        probs_load(h + 1, 0, 1 - slot).start()

                probs = p_buf[slot]
                go = gm[head, at]
                inner = jnp.sum(go.astype(wide) * mixed[head, at].astype(wide), axis=0, keepdims=True)
                scores = probs.astype(wide) * (dot(qkv[v_rows, :], go, 0, 0) - inner)
                first = pl.multiple_of(reach - b * q_block, q_block)
                sums[pl.ds(first, length), :] += scores
                scores = scores.astype(low)
                gqkv[head, at] = dot(qkv[k_rows, :], scores, 1, 0).astype(low)
                k_acc[...] += dot(qkv[head, at], scores, 1, 1)
                v_acc[...] += dot(go, probs, 1, 1)
                return carry

            lax.fori_loop(0, blocks, block, 0)
            gqkv[k_rows, :] = k_acc[...].astype(low)
            gqkv[v_rows, :] = v_acc[...].astype(low)
            near = sums[reach - band_half : reach + q_block + band_half, :]
            n = jnp.abs(d)
            bucket = jnp.zeros((near_rows, q_block), jnp.int32)
            for step in steps_at:
                bucket = bucket + jnp.where(n >= step, 1, 0)
            bucket = bucket + jnp.where(d > 0, 16, 0)
            totals = []
            for b in range(32):
                total = jnp.sum(jnp.where(bucket == b, near, 0.0), axis=0, keepdims=True)
                if b == 15:
                    total = total + jnp.sum(sums[: reach - band_half, :], axis=0, keepdims=True)
                if b == 31:
                    total = total + jnp.sum(sums[reach + q_block + band_half :, :], axis=0, keepdims=True)
                totals.append(total)
            totals = jnp.concatenate(totals, axis=0)
            totals = jnp.concatenate([totals, jnp.zeros((96, q_block), wide)], axis=0)
            line = jnp.sum(totals.T, axis=0, keepdims=True)
            for side_c in range(2):
                row = 8 + side_c * heads + h
                small[row : row + 1, :128] = jnp.where(c == side_c, line, 0.0)
            if h == 0:
                step_z_down(3)
            if h == 1:
                step_z_pair(0)

        def input_grad(half, store):
            def block(i, carry):
                at = chunk(i)
                store(at, dot(w_t[at, :], gqkv[:, half], 1, 0))
                return carry

            lax.fori_loop(0, zs, block, 0)

        def store_sent(at, value):
            sx[at, :] = value.astype(low)

        input_grad(other_half, store_sent)
        core_x = move(19, sx, rx, to_core)
        core_x.start()
        loads[3].wait()
        y_attn = [
            move(20 + k, ga.at[j, :, side(1 - y, a_cols)], ya.at[j], to_y) for k, j in enumerate(order)
        ]
        wide_cols = gqkv.shape[0]
        for k, j in enumerate(order):
            ga[j, :rows, :wide_cols] = dot(xn1[chunk(j), :], gqkv[...], 1, 1).astype(low)
            ga[j, :rows, wide_cols:] = dot(bf[chunk(j), :], mixed[...], 1, 1).astype(low)
            ga[j, rows:, :] = jnp.zeros((ga.shape[1] - rows, ga.shape[2]), low)
            y_attn[k].start()
        step_z_pair(1)

        def store_own(at, value):
            hv[at, :] = value

        input_grad(my_half, store_own)
        load_x.wait()
        core_x.wait_recv()

        def store_in(at, back):
            gin[at, :] = (gxv[at, :] + back).astype(low)

        norm_backward(
            lambda at: gov[at, :].astype(wide),
            gain1,
            scale1,
            lambda at: hv[at, :] + rx[at, :].astype(wide),
            store_in,
            1,
        )

        @pl.when(c != y)
        def _():
            swap_in.start()

        for k, j in enumerate(order):
            y_attn[k].wait_recv()
            ya[j] = (ya[j].astype(wide) + ga[j, :, my_cols].astype(wide)).astype(low)
            x_attn[k].start()
        step_z_pair(2)
        x_down.start()
        core_x.wait_send()
        for each in y_attn:
            each.wait_send()

    f32 = lambda *shape: pltpu.VMEM(shape, wide)
    b16 = lambda *shape: pltpu.VMEM(shape, low)
    pl.run_scoped(
        attention,
        f32(width, half_len),
        f32(width, half_len),
        b16(width, half_len),
        b16(2, length, q_block),
        f32(dim, length),
        f32(dim, length),
        f32(2 * length - q_block, q_block),
        b16(3 * heads * dim, length),
        b16(heads * dim, length),
        b16(width, length),
        b16(width, half_len),
        b16(zs, ya.shape[1], 2 * ya.shape[2]),
    )

    def step_attn(t):
        x_attn[t].wait_recv()
        term = ya[order[t], my_rows, :].astype(wide) + xa[order[t]].astype(wide)
        if t:
            z_attn[t - 1].wait_recv()
            za[t - 1] = (za[t - 1].astype(wide) + term).astype(low)
        else:
            x_attn[0].wait_send()
            ya[order[0], my_rows, :] = term.astype(low)
        if t < zs - 1:
            z_attn[t].start()

    hops = [to_core, to_y, to_x, {"dp": z + 1 - 2 * (z % 2)}, {"dp": (z + 2) % zs}]
    exchange = [move(37 + i, sm_src.at[i], sm_in.at[i], who) for i, who in enumerate(hops)]

    def start_sum(i):
        sm_src[i] = small[...]
        exchange[i].start()

    def end_sum(i):
        exchange[i].wait_recv()
        small[...] = sm_src[i] + sm_in[i]

    start_sum(0)
    step_attn(0)
    end_sum(0)
    start_sum(1)
    step_attn(1)
    end_sum(1)
    start_sum(2)
    step_attn(2)
    step_attn(3)
    ab[my_rows, :] = za[zs - 2]
    x_attn_back.start()
    step_z_pair(3)
    p_out[m, :, mine] = zp[zs - 2]
    x_pair_back.start()
    core_pair.start()
    end_sum(2)
    start_sum(3)
    x_down.wait_recv()
    d_out[:, mine] = (zd[zs - 2].astype(wide) + dx[...].astype(wide)).astype(low)
    core_down.start()
    end_sum(3)
    start_sum(4)
    x_attn_back.wait_recv()
    ab2[:, my_cols] = ab[...]
    y_attn_back.start()
    end_sum(4)
    y_attn_back.wait_recv()

    @pl.when(c == y)
    def _():
        core_attn.start()
        a_out[...] = ab2[...]
        core_attn.wait_send()

    x_pair_back.wait_recv()
    p_out[1 - m, :, mine] = px[...]
    core_pair_back.start()

    @pl.when(c != y)
    def _():
        core_attn.wait_recv()
        swap_out.wait()
        swap_in.wait()

    back_out.wait()
    for each in (core_down, core_pair, core_pair_back):
        each.wait()
    core_branch.wait_send()
    x_down.wait_send()
    x_pair_back.wait_send()
    x_attn_back.wait_send()
    y_attn_back.wait_send()
    for each in z_down + x_pair + z_pair + x_attn[1:] + z_attn + exchange:
        each.wait_send()


def back_all(
    hid, pair, g_own, g_oth, x_own, x_oth, gx, hres, x_in, probs, xn_one, out_first, out_oth,
    out_w, qkv_w, qkv, mixed, gain_two, gain_one, scale_two, scale_one, zs,
):
    width, half_len = g_own.shape
    length = 2 * half_len
    rows = width // zs
    columns = hid.shape[1] // 2
    heads = probs.shape[0]
    a_cols = 2 * (qkv_w.shape[0] + out_w.shape[0]) // 4
    a_len = -(-rows // 32) * 32
    hbm = pl.BlockSpec(memory_space=pl.ANY)
    vmem = pl.BlockSpec(memory_space=pltpu.VMEM)
    sds = lambda kind, *shape: jax.ShapeDtypeStruct(shape, kind)
    b16 = lambda *shape: pltpu.VMEM(shape, low)
    spread = lambda gain: jnp.broadcast_to(gain, (width, 128))
    return pl.pallas_call(
        back_kernel,
        in_specs=[hbm] * 13 + [vmem] * 8,
        out_specs=[hbm] * 3 + [vmem] * 5,
        out_shape=[
            sds(low, width, half_len),
            sds(low, width, half_len),
            sds(low, width, half_len),
            sds(low, rows, 2 * columns),
            sds(low, 2, rows, 2 * columns),
            sds(low, a_len, 2 * a_cols),
            sds(low, width, half_len),
            sds(wide, 16, width),
        ],
        scratch_shapes=[
            b16(3, width, columns),
            b16(width, columns),
            b16(zs - 1, rows, columns),
            b16(zs - 1, rows, columns),
            b16(rows, columns),
            b16(rows, columns),
            b16(width, length),
            b16(width, half_len),
            b16(zs, a_len, a_cols),
            b16(zs, a_len // 2, a_cols),
            b16(zs - 1, a_len // 2, a_cols),
            b16(a_len, a_cols),
            b16(a_len, 2 * a_cols),
            pltpu.VMEM((5, 16, width), wide),
            pltpu.VMEM((5, 16, width), wide),
            pltpu.SemaphoreType.DMA((42,)),
            pltpu.SemaphoreType.DMA((42,)),
            pltpu.SemaphoreType.DMA((14,)),
        ],
        compiler_params=pltpu.CompilerParams(vmem_limit_bytes=61 << 20, collective_id=1, has_side_effects=True),
        cost_estimate=hint,
        name="back_all",
    )(
        hid, pair, g_own, g_oth, x_own, x_oth, gx, hres, x_in, probs, xn_one, out_first, out_oth,
        out_w, qkv_w.T, qkv, mixed, spread(gain_two), spread(gain_one), scale_two, scale_one,
    )


def norm_of(values, gain):
    scale = lax.rsqrt(jnp.mean(values * values, axis=0, keepdims=True) + eps_norm)
    return values * scale * gain, scale


def norm_back(values, scale, gain, grad):
    normed = values * scale
    pushed = gain * grad
    mean = jnp.mean(normed * pushed, axis=0, keepdims=True)
    return scale * (pushed - normed * mean), jnp.sum(grad * normed, axis=1)


class Moves:
    def __init__(self, mesh):
        self.nz = mesh.shape["dp"]
        self.nx = mesh.shape["seq"] // 2
        both = [(m, c, y) for m in range(self.nx) for c in range(2) for y in range(2)]
        at = lambda m, c, y: (m * 2 + c) * 2 + y
        self.swap_pairs = [(at(m, c, y), at(m, y, c)) for m, c, y in both if c != y]
        self.second_pairs = [(at(m, c, y), at(m, y, 1 - c)) for m, c, y in both]
        self.back_pairs = [(b, a) for a, b in self.second_pairs]
        self.ring_x = [(m * 2 + c, (m + 1) % self.nx * 2 + c) for m in range(self.nx) for c in range(2)]
        self.y = lax.axis_index("tensor")
        self.z = lax.axis_index("dp")
        s = lax.axis_index("seq")
        self.c = s % 2
        self.m = s // 2

    def swap(self, a):
        got = lax.ppermute(a, ("seq", "tensor"), self.swap_pairs)
        return jnp.where(self.c == self.y, a, got)

    def second(self, a):
        return lax.ppermute(a, ("seq", "tensor"), self.second_pairs)

    def back(self, a):
        return lax.ppermute(a, ("seq", "tensor"), self.back_pairs)

    def core(self, a):
        return lax.ppermute(a, "seq", [(s, s ^ 1) for s in range(2 * self.nx)])

    def over_y(self, a):
        return lax.ppermute(a, "tensor", [(0, 1), (1, 0)])

    def over_x(self, a):
        return lax.ppermute(a, "seq", self.ring_x)

    def start_x(self, a):
        take = lax.dynamic_index_in_dim(a, (self.m + self.nx - 1) % self.nx, 1, False)
        return a, self.over_x(take)

    def finish_x(self, a, got, *first):
        take = lambda i: lax.dynamic_index_in_dim(a, i % self.nx, 1, False)
        got = after(got, *first)
        held = (got.astype(wide) + take(self.m + 2 * self.nx - 2).astype(wide)).astype(low)
        for t in range(2, self.nx):
            held = (self.over_x(held).astype(wide) + take(self.m + 2 * self.nx - 1 - t).astype(wide)).astype(low)
        return held

    def scatter_x(self, a):
        take = lambda i: lax.dynamic_index_in_dim(a, i % self.nx, 1, False)
        held = take(self.m + self.nx - 1)
        for t in range(1, self.nx):
            held = (self.over_x(held).astype(wide) + take(self.m + 2 * self.nx - 1 - t).astype(wide)).astype(low)
        return held

    def scatter_z(self, a):
        return lax.psum_scatter(a, "dp", scatter_dimension=0, tiled=True)

    def gather_x(self, piece):
        if self.nx == 2:
            over = self.over_x(piece)
            return jnp.where(
                self.m == 0, jnp.concatenate([piece, over], 0), jnp.concatenate([over, piece], 0)
            )
        groups = [[m * 2 + c for m in range(self.nx)] for c in range(2)]
        return lax.all_gather(piece, "seq", axis=0, tiled=True, axis_index_groups=groups)

    def gather_core(self, piece):
        there = self.core(piece)
        return jnp.where(
            self.c == 0, jnp.concatenate([piece, there], 1), jnp.concatenate([there, piece], 1)
        )

    def sum_everywhere(self, a):
        a = a + self.core(a)
        a = a + self.over_y(a)
        step = 1
        while step < self.nx:
            a = a + lax.ppermute(a, "seq", [(s, s ^ (2 * step)) for s in range(2 * self.nx)])
            step *= 2
        step = 1
        while step < self.nz:
            a = a + lax.ppermute(a, "dp", [(z, z ^ step) for z in range(self.nz)])
            step *= 2
        return a


def segment_ids(lengths, valid, length):
    ends = jnp.sum(jnp.where(jnp.arange(4)[None, :] <= jnp.arange(4)[:, None], lengths[None, :], 0), axis=1)
    where_at = jnp.arange(length, dtype=jnp.int32)
    counted = jnp.sum((where_at[:, None] >= ends[None, :]).astype(jnp.int32), axis=1)
    return jnp.where(where_at < valid, counted, 4)


def local(
    mesh,
    layer_in,
    out_grad,
    doc_lengths,
    valid_length,
    gain_attn,
    query_weight,
    key_weight,
    value_weight,
    position_bias,
    output_weight,
    gain_ffn,
    gate_weight,
    up_weight,
    down_weight,
):
    moves = Moves(mesh)
    half_len, _, width = layer_in.shape
    length = 2 * half_len
    heads = position_bias.shape[1]
    inner_width = query_weight.shape[1]
    y, c, m = moves.y, moves.c, moves.m

    facts = jnp.concatenate([doc_lengths[0].astype(wide), valid_length.astype(wide), position_bias.reshape(-1)])
    facts = moves.swap(facts)
    bias = facts[5:].reshape(position_bias.shape)
    facts = facts[:5].astype(jnp.int32)
    x_in = moves.swap(layer_in.reshape(half_len, width).T)
    qkv_w = jnp.concatenate([query_weight.T, key_weight.T, value_weight.T], axis=0)
    qkv_w = moves.swap(qkv_w)
    positions = y * half_len + jnp.arange(half_len, dtype=jnp.int32)
    g_in = jnp.where((positions < valid_length[0])[None, :], out_grad.reshape(half_len, width).T, 0)
    g_in, out_w, x_in, facts = lax.optimization_barrier((g_in.astype(low), output_weight, x_in, facts))
    out_w = moves.swap(out_w)
    g_own = moves.swap(g_in)
    g_oth = moves.second(g_in)
    segment = segment_ids(facts[:4], facts[4], length)
    gain_one = gain_attn.astype(wide)[:, None]
    gain_two = gain_ffn.astype(wide)[:, None]

    def both_halves(own):
        other = moves.core(own)
        return jnp.where(
            c == 0, jnp.concatenate([own, other], 1), jnp.concatenate([other, own], 1)
        )

    def my_half(a):
        return lax.dynamic_slice_in_dim(a, c * half_len, half_len, 1)

    def other_half(a):
        return lax.dynamic_slice_in_dim(a, (1 - c) * half_len, half_len, 1)

    x_wide = x_in.astype(wide)
    normed, scale_one = norm_of(x_wide, gain_one)
    xn_one = both_halves(normed.astype(low))
    qkv = dot(qkv_w, xn_one, 1, 0).astype(low)
    probs, mixed = attn_forward(qkv, segment, bias)
    sent = dot(out_w, other_half(mixed), 0, 0).astype(low)
    hres = x_wide + dot(out_w, my_half(mixed), 0, 0) + moves.core(sent).astype(wide)

    normed, scale_two = norm_of(hres, gain_two)
    xn_own = normed.astype(low)
    hid, pair, xn_oth, out_own, out_oth, gx = ffn(
        xn_own, g_own, g_oth, gate_weight, up_weight, down_weight.T
    )
    if moves.nx == 2 and moves.nz == 4:
        out_first = (hres + out_own).astype(low)
        got_first, got_oth, got_in, sum_d, sum_p, sums, grad_in, small = back_all(
            hid, pair, g_own, g_oth, xn_own, xn_oth, gx, hres, x_in, probs, xn_one, out_first, out_oth,
            out_w, qkv_w, qkv, mixed, gain_two, gain_one, scale_two, scale_one, moves.nz,
        )
        out_y = jnp.where(c == y, out_first, got_first).astype(wide) + got_oth.astype(wide)
        grad_in = jnp.where(c == y, grad_in, got_in).astype(wide)
        sums = sums[: width // moves.nz].astype(wide)
        sum_q, sum_k, sum_v, sum_o = (
            sums[:, i * inner_width : (i + 1) * inner_width] for i in range(4)
        )
        return (
            out_y.astype(low).T.reshape(half_len, 1, width),
            grad_in.T.reshape(half_len, 1, width),
            small[1],
            sum_q,
            sum_k,
            sum_v,
            small[8 : 8 + 2 * heads, : position_bias.shape[0]].T,
            sum_o.T,
            small[0],
            sum_p[0].astype(wide),
            sum_p[1].astype(wide),
            sum_d.astype(wide).T,
        )
    grad_gate, grad_up = pair[0], pair[1]

    columns = hid.shape[1] // 2
    send_d = weight_grad(g_own, g_oth, hid, 1 - c)
    got_d = moves.core(send_d)
    send_g = weight_grad(xn_own, xn_oth, after(grad_gate, send_d), 1 - c)
    got_g = moves.core(send_g)
    send_u = weight_grad(xn_own, xn_oth, after(grad_up, send_g), 1 - c)
    got_u = moves.core(send_u)
    total_d = weight_grad(g_own, g_oth, after(hid, send_u), c, got_d)
    total_g = weight_grad(xn_own, xn_oth, after(grad_gate, total_d), c, got_g)
    total_u = weight_grad(xn_own, xn_oth, after(grad_up, total_g), c, got_u)
    part_d = moves.scatter_z(total_d)
    x_sent = [moves.start_x(t.reshape(moves.nz, moves.nx, -1, columns)) for t in (total_g, total_u)]

    gx = after(gx, total_u)
    out_y = moves.swap((hres + out_own).astype(low)).astype(wide) + moves.back(out_oth).astype(wide)

    back, grad_gain_two = norm_back(hres, scale_two, gain_two, gx)
    grad_hres = g_own.astype(wide) + back
    branch = both_halves(grad_hres.astype(low))

    grad_mixed = dot(out_w, branch, 1, 0).astype(low)
    grad_qkv, grad_bias = attn_backward(qkv, grad_mixed, mixed, probs)

    part_g = moves.finish_x(*x_sent[0], grad_qkv).reshape(-1, columns)
    sent = dot(qkv_w, other_half(after(grad_qkv, part_g)), 0, 0).astype(low)
    part_g = moves.scatter_z(part_g)
    got_x = moves.core(sent)
    grad_attn_w = jnp.concatenate(
        [dot(xn_one, after(grad_qkv, sent), 1, 1).astype(low), dot(branch, mixed, 1, 1).astype(low)], axis=1
    )
    gx = dot(qkv_w, my_half(after(grad_qkv, grad_attn_w)), 0, 0) + got_x.astype(wide)
    back, grad_gain_one = norm_back(x_wide, scale_one, gain_one, gx)
    grad_in = (grad_hres + back).astype(low)
    part_u = moves.scatter_z(moves.finish_x(*x_sent[1], grad_in).reshape(-1, columns))

    a_columns = grad_attn_w.shape[1] // 2
    chunks = grad_attn_w.reshape(moves.nz, moves.nx, -1, 2 * a_columns)

    def scatter_y(a):
        got = moves.over_y(lax.dynamic_slice_in_dim(a, (1 - y) * a_columns, a_columns, a.ndim - 1))
        kept = lax.dynamic_slice_in_dim(a, y * a_columns, a_columns, a.ndim - 1)
        return (kept.astype(wide) + got.astype(wide)).astype(low)

    half_z = moves.nz // 2
    part = jnp.concatenate(
        [moves.scatter_x(scatter_y(chunks[:half_z])), scatter_y(moves.scatter_x(chunks[half_z:]))], 0
    )
    piece = moves.gather_x(moves.scatter_z(part.reshape(-1, a_columns)))
    there = moves.over_y(piece)
    group = jnp.where(y == 0, jnp.concatenate([piece, there], 1), jnp.concatenate([there, piece], 1))
    sums = jnp.where(c == y, group, moves.core(group)).astype(wide)
    sum_q, sum_k, sum_v, sum_o = (
        sums[:, i * inner_width : (i + 1) * inner_width] for i in range(4)
    )
    grad_in = moves.swap(grad_in).astype(wide)

    if moves.nx == 2:
        part_d = (part_d.astype(wide) + moves.over_x(part_d).astype(wide)).astype(low)
    else:
        part_d = moves.gather_x(moves.scatter_x(part_d.reshape(1, moves.nx, -1, columns))[0])
    sum_d = moves.gather_core(part_d).astype(wide)
    sum_g = moves.gather_core(moves.gather_x(part_g)).astype(wide)
    sum_u = moves.gather_core(moves.gather_x(part_u)).astype(wide)

    bias_full = jnp.zeros((grad_bias.shape[0], 2 * heads), wide)
    bias_full = lax.dynamic_update_slice(bias_full, grad_bias, (jnp.int32(0), c * heads))
    early = moves.sum_everywhere(jnp.concatenate([grad_gain_two, bias_full.reshape(-1)]))
    gain_two_sum, bias_sum = early[:width], early[width:].reshape(bias_full.shape)
    gain_one_sum = moves.sum_everywhere(grad_gain_one)
    return (
        out_y.astype(low).T.reshape(half_len, 1, width),
        grad_in.T.reshape(half_len, 1, width),
        gain_one_sum,
        sum_q,
        sum_k,
        sum_v,
        bias_sum,
        sum_o.T,
        gain_two_sum,
        sum_g,
        sum_u,
        sum_d.T,
    )


def solution(mesh):
    rows = P("tensor", ("dp", "seq"), None)
    columns = P(None, "tensor")
    return jax.shard_map(
        functools.partial(local, mesh),
        mesh=mesh,
        in_specs=(
            rows,
            rows,
            P(("dp", "seq"), None),
            P(("dp", "seq")),
            P(),
            columns,
            columns,
            columns,
            columns,
            P("tensor", None),
            P(),
            columns,
            columns,
            P("tensor", None),
        ),
        out_specs=(
            rows,
            rows,
            P(),
            P("dp", "tensor"),
            P("dp", "tensor"),
            P("dp", "tensor"),
            P(),
            P("tensor", "dp"),
            P(),
            P("dp", "tensor"),
            P("dp", "tensor"),
            P("tensor", "dp"),
        ),
        check_vma=False,
    )
```

```python
import functools
import math

import jax
import jax.numpy as jnp
from jax import lax
from jax.experimental import pallas as pl
from jax.experimental.pallas import tpu as pltpu
from jax.sharding import PartitionSpec as P

steps_at = (1, 2, 3, 4, 5, 6, 7, 8, 12, 16, 23, 32, 46, 64, 91)
eps_norm = 1e-06
masked_score = -1e30
q_block = 256
band_half = 128
low = jnp.bfloat16
wide = jnp.float32
hint = pl.CostEstimate(flops=1000, bytes_accessed=1000, transcendentals=0)


def dot(a, b, ca, cb):
    return lax.dot_general(a, b, (((ca,), (cb,)), ((), ())), preferred_element_type=wide)


def after(value, *first):
    return lax.optimization_barrier((value, *first))[0]


def attn_fwd_kernel(length, bias_ref, q_ref, k_ref, v_ref, seg_k_ref, seg_q_ref, p_ref, o_ref, table):
    block = pl.program_id(0)
    head = pl.program_id(1)
    reach = length - q_block

    @pl.when(block == 0)
    def _():
        table[head, : reach - band_half, :] = jnp.full((reach - band_half, q_block), bias_ref[15, head], wide)
        tail = length + reach - (reach + q_block + band_half)
        table[head, reach + q_block + band_half :, :] = jnp.full((tail, q_block), bias_ref[31, head], wide)
        rows = q_block + 2 * band_half
        d = (
            lax.broadcasted_iota(jnp.int32, (rows, q_block), 0)
            - lax.broadcasted_iota(jnp.int32, (rows, q_block), 1)
            - band_half
        )
        n = jnp.abs(d)
        before = jnp.full((rows, q_block), bias_ref[0, head], wide)
        after = jnp.full((rows, q_block), bias_ref[16, head], wide)
        for number, step in enumerate(steps_at):
            reached = n >= step
            before = jnp.where(reached, bias_ref[number + 1, head], before)
            after = jnp.where(reached, bias_ref[number + 17, head], after)
        table[head, reach - band_half : reach + q_block + band_half, :] = jnp.where(d > 0, after, before)

    first = pl.multiple_of(reach - block * q_block, q_block)
    scores = dot(k_ref[...], q_ref[...], 0, 0) + table[head, pl.ds(first, length), :]
    seg_k = jnp.concatenate([seg_k_ref[...]] * (q_block // 128), axis=1)
    scores = jnp.where(seg_k == seg_q_ref[...], scores, masked_score)
    raised = jnp.exp(scores - jnp.max(scores, axis=0, keepdims=True))
    probs = (raised * (1.0 / jnp.sum(raised, axis=0, keepdims=True))).astype(low)
    p_ref[0] = probs
    o_ref[...] = dot(v_ref[...], probs, 1, 0).astype(low)


def attn_forward(qkv, seg, bias):
    width, length = qkv.shape
    heads = bias.shape[1]
    dim = width // (3 * heads)
    seg_k = jnp.broadcast_to(seg[:, None], (length, 128))
    seg_q = seg[None, :]
    blocks = length // q_block
    return pl.pallas_call(
        functools.partial(attn_fwd_kernel, length),
        grid=(blocks, heads),
        in_specs=[
            pl.BlockSpec(memory_space=pltpu.SMEM),
            pl.BlockSpec((dim, q_block), lambda b, h: (h, b)),
            pl.BlockSpec((dim, length), lambda b, h: (heads + h, 0)),
            pl.BlockSpec((dim, length), lambda b, h: (2 * heads + h, 0)),
            pl.BlockSpec((length, 128), lambda b, h: (0, 0)),
            pl.BlockSpec((1, q_block), lambda b, h: (0, b)),
        ],
        out_specs=[
            pl.BlockSpec((1, length, q_block), lambda b, h: (h, 0, b)),
            pl.BlockSpec((dim, q_block), lambda b, h: (h, b)),
        ],
        out_shape=[
            jax.ShapeDtypeStruct((heads, length, length), low),
            jax.ShapeDtypeStruct((heads * dim, length), low),
        ],
        scratch_shapes=[pltpu.VMEM((heads, 2 * length - q_block, q_block), wide)],
        compiler_params=pltpu.CompilerParams(vmem_limit_bytes=48 << 20),
        cost_estimate=hint,
        name="attn_forward",
    )(bias, qkv, qkv, qkv, seg_k, seg_q)


def attn_bwd_kernel(length, q_ref, k_ref, v_ref, go_ref, o_ref, p_ref, gq_ref, gk_ref, gv_ref, gb_ref, k_acc, v_acc, sums):
    block = pl.program_id(1)
    reach = length - q_block

    @pl.when(block == 0)
    def _():
        k_acc[...] = jnp.zeros_like(k_acc)
        v_acc[...] = jnp.zeros_like(v_acc)
        sums[...] = jnp.zeros_like(sums)

    probs = p_ref[0]
    go = go_ref[...]
    inner = jnp.sum(go.astype(wide) * o_ref[...].astype(wide), axis=0, keepdims=True)
    scores = probs.astype(wide) * (dot(v_ref[...], go, 0, 0) - inner)
    first = pl.multiple_of(reach - block * q_block, q_block)
    sums[pl.ds(first, length), :] += scores
    scores = scores.astype(low)
    gq_ref[...] = dot(k_ref[...], scores, 1, 0).astype(low)
    k_acc[...] += dot(q_ref[...], scores, 1, 1)
    v_acc[...] += dot(go, probs, 1, 1)

    @pl.when(block == pl.num_programs(1) - 1)
    def _():
        gk_ref[...] = k_acc[...].astype(low)
        gv_ref[...] = v_acc[...].astype(low)
        rows = q_block + 2 * band_half
        d = (
            lax.broadcasted_iota(jnp.int32, (rows, q_block), 0)
            - lax.broadcasted_iota(jnp.int32, (rows, q_block), 1)
            - band_half
        )
        n = jnp.abs(d)
        near = sums[reach - band_half : reach + q_block + band_half, :]
        far_before = jnp.sum(sums[: reach - band_half, :], axis=0, keepdims=True)
        far_after = jnp.sum(sums[reach + q_block + band_half :, :], axis=0, keepdims=True)
        bucket = jnp.zeros((rows, q_block), jnp.int32)
        for step in steps_at:
            bucket = bucket + jnp.where(n >= step, 1, 0)
        bucket = bucket + jnp.where(d > 0, 16, 0)
        for b in range(32):
            total = jnp.sum(jnp.where(bucket == b, near, 0.0), axis=0, keepdims=True)
            if b == 15:
                total = total + far_before
            if b == 31:
                total = total + far_after
            gb_ref[0, b : b + 1, :] = total


def attn_backward(qkv, grad_mixed, mixed, probs):
    width, length = qkv.shape
    heads = probs.shape[0]
    dim = width // (3 * heads)
    blocks = length // q_block
    half = pl.BlockSpec((dim, q_block), lambda h, b: (h, b))
    whole = pl.BlockSpec((dim, length), lambda h, b: (h, 0))
    gq, gk, gv, gb = pl.pallas_call(
        functools.partial(attn_bwd_kernel, length),
        grid=(heads, blocks),
        in_specs=[
            half,
            pl.BlockSpec((dim, length), lambda h, b: (heads + h, 0)),
            pl.BlockSpec((dim, length), lambda h, b: (2 * heads + h, 0)),
            half,
            half,
            pl.BlockSpec((1, length, q_block), lambda h, b: (h, 0, b)),
        ],
        out_specs=[half, whole, whole, pl.BlockSpec((1, 32, q_block), lambda h, b: (h, 0, 0))],
        out_shape=[
            jax.ShapeDtypeStruct((heads * dim, length), low),
            jax.ShapeDtypeStruct((heads * dim, length), low),
            jax.ShapeDtypeStruct((heads * dim, length), low),
            jax.ShapeDtypeStruct((heads, 32, q_block), wide),
        ],
        scratch_shapes=[
            pltpu.VMEM((dim, length), wide),
            pltpu.VMEM((dim, length), wide),
            pltpu.VMEM((2 * length - q_block, q_block), wide),
        ],
        compiler_params=pltpu.CompilerParams(vmem_limit_bytes=48 << 20),
        cost_estimate=hint,
        name="attn_backward",
    )(qkv, qkv, qkv, grad_mixed, mixed, probs)
    return jnp.concatenate([gq, gk, gv], axis=0), jnp.sum(gb, axis=2).T


def ffn_kernel(
    x_ref, go_ref, gr_ref, gate_w, up_w, down_w,
    hid_ref, pair_ref, xr_ref, out_ref, out_r_ref, gx_ref, late_ref,
    xs, gs, out_acc, gx_acc, x_in, gx_out, gx_in, sems,
):
    chunk = pl.program_id(0)
    tile = pl.program_id(1)
    size = xs.shape[0]
    there = {"tensor": 1 - lax.axis_index("tensor")}
    half = [pl.ds(0, size), pl.ds(size, size)]

    def send_x(h):
        return pltpu.make_async_remote_copy(
            src_ref=x_ref.at[:, half[h]], dst_ref=x_in.at[h], send_sem=sems.at[h], recv_sem=sems.at[2 + h],
            device_id=there, device_id_type=pl.DeviceIdType.MESH,
        )

    send_gx = pltpu.make_async_remote_copy(
        src_ref=gx_out, dst_ref=gx_in, send_sem=sems.at[4], recv_sem=sems.at[5],
        device_id=there, device_id_type=pl.DeviceIdType.MESH,
    )

    @pl.when(tile == 0)
    def _():
        out_acc[...] = jnp.zeros_like(out_acc)
        gx_acc[...] = jnp.zeros_like(gx_acc)

    @pl.when((tile == 0) & (chunk == 0))
    def _():
        barrier = pltpu.get_barrier_semaphore()
        pl.semaphore_signal(barrier, inc=1, device_id=there, device_id_type=pl.DeviceIdType.MESH)
        pl.semaphore_wait(barrier, 1)
        send_x(0).start()
        send_x(1).start()
        xs[...] = x_ref[:, half[1]].T
        gs[...] = go_ref[:, half[1]].T

    for h in range(2):

        @pl.when((tile == 0) & (chunk == 1 + h))
        def _(h=h):
            send_x(h).wait_recv()
            xs[...] = x_in[h].T
            gs[...] = gr_ref[:, half[h]].T
            xr_ref[:, half[h]] = x_in[h]

    @pl.when((tile == 0) & (chunk == 3))
    def _():
        xs[...] = x_ref[:, half[0]].T
        gs[...] = go_ref[:, half[0]].T

    gate = dot(xs[...], gate_w[...], 1, 0)
    up = dot(xs[...], up_w[...], 1, 0)
    grad = dot(gs[...], down_w[...], 1, 0)
    c = math.sqrt(2.0 / math.pi)
    square = gate * gate
    t = jnp.tanh(c * gate * (1.0 + 0.044715 * square))
    part = 0.5 * (1.0 + t)
    gelu = gate * part
    slope = part + 0.5 * gate * (1.0 - t * t) * (c * (1.0 + 3 * 0.044715 * square))
    hid = (gelu * up).astype(low)
    gg = (grad * up * slope).astype(low)
    gu = (grad * gelu).astype(low)
    hid_ref[...] = hid
    pair_ref[0] = gg
    pair_ref[1] = gu
    out_acc[...] += dot(down_w[...], hid, 1, 1)
    gx_acc[...] += dot(gate_w[...], gg, 1, 1) + dot(up_w[...], gu, 1, 1)

    last = tile == pl.num_programs(1) - 1
    for at, h in ((0, 1), (3, 0)):

        @pl.when(last & (chunk == at))
        def _(h=h):
            out_ref[:, half[h]] = out_acc[...]
            gx_ref[:, half[h]] = gx_acc[...]

    for h in range(2):

        @pl.when(last & (chunk == 1 + h))
        def _(h=h):
            out_r_ref[:, half[h]] = out_acc[...].astype(low)
            if h:
                late_ref[...] = gx_acc[...].astype(low)
            else:
                gx_out[...] = gx_acc[...].astype(low)
                send_gx.start()

    @pl.when(last & (chunk == 3))
    def _():
        send_gx.wait_recv()
        gx_ref[:, half[0]] += gx_in[...].astype(wide)
        for h in range(2):
            send_x(h).wait_send()
        send_gx.wait_send()


def ffn(x, g_own, g_oth, gate_w, up_w, down_w):
    width, tokens = x.shape
    hidden = gate_w.shape[1]
    tile, size = 256, tokens // 2
    full = pl.BlockSpec((width, tokens), lambda s, j: (0, 0), pipeline_mode=pl.Buffered(1))
    weight = pl.BlockSpec((width, tile), lambda s, j: (0, j))
    act = pl.BlockSpec((size, tile), lambda s, j: ((s + 1) % 4, j))
    act_shape = jax.ShapeDtypeStruct((2 * tokens, hidden), low)
    tokens_of = lambda kind: jax.ShapeDtypeStruct((width, tokens), kind)
    part = pltpu.VMEM((width, size), low)
    late = pl.BlockSpec((width, size), lambda s, j: (0, 0), pipeline_mode=pl.Buffered(1))
    return pl.pallas_call(
        ffn_kernel,
        grid=(4, hidden // tile),
        in_specs=[full, full, full, weight, weight, weight],
        out_specs=[act, pl.BlockSpec((2, size, tile), lambda s, j: (0, (s + 1) % 4, j)), full, full, full, full, late],
        out_shape=[act_shape, jax.ShapeDtypeStruct((2, 2 * tokens, hidden), low), tokens_of(low), tokens_of(wide), tokens_of(low), tokens_of(wide)]
        + [jax.ShapeDtypeStruct((width, size), low)],
        scratch_shapes=[
            pltpu.VMEM((size, width), low),
            pltpu.VMEM((size, width), low),
            pltpu.VMEM((width, size), wide),
            pltpu.VMEM((width, size), wide),
            pltpu.VMEM((2, width, size), low),
            part,
            part,
            pltpu.SemaphoreType.DMA((6,)),
        ],
        compiler_params=pltpu.CompilerParams(vmem_limit_bytes=56 << 20, collective_id=0, has_side_effects=True),
        cost_estimate=hint,
        name="ffn_both_ways",
    )(x, g_own, g_oth, gate_w, up_w, down_w)


def weight_grad_kernel(core_ref, own_ref, oth_ref, right_ref, *refs):
    tokens = own_ref.shape[1]
    total = dot(own_ref[...], right_ref[:tokens, :], 1, 0) + dot(oth_ref[...], right_ref[tokens:, :], 1, 0)
    if len(refs) == 2:
        total = total + refs[0][...].astype(wide)
    refs[-1][...] = total.astype(low)


def weight_grad(own, oth, right, core, got=None):
    width, tokens = own.shape
    columns = right.shape[1] // 2
    blocks = 4
    rows = width // blocks
    left = pl.BlockSpec((rows, tokens), lambda i, core_ref: (i, 0))
    out = pl.BlockSpec((rows, columns), lambda i, core_ref: (i, 0))
    args = [own, oth, right] + ([] if got is None else [got])
    return pl.pallas_call(
        weight_grad_kernel,
        grid_spec=pltpu.PrefetchScalarGridSpec(
            num_scalar_prefetch=1,
            grid=(blocks,),
            in_specs=[
                left,
                left,
                pl.BlockSpec((2 * tokens, columns), lambda i, core_ref: (0, core_ref[0]), pipeline_mode=pl.Buffered(1)),
            ]
            + ([] if got is None else [out]),
            out_specs=out,
        ),
        out_shape=jax.ShapeDtypeStruct((width, columns), low),
        compiler_params=pltpu.CompilerParams(vmem_limit_bytes=40 << 20),
        cost_estimate=hint,
        name="weight_grad",
    )(core.reshape(1), *args)


def back_kernel(
    hid_h, pair_h, go_h, gr_h, xo_h, xr_h, gx_h, hres_h, xin_h, probs_h, xn1_h, outp_h, outr_h, late_h,
    out_w, w_t, qkv, mixed, gain2, gain1, scale2, scale1,
    got_p, got_r, got_in, d_out, p_out, a_out, gin, small,
    r_core, xp, zd, zp, dx, px, bf, rx, ya, xa, za, ab, late_in, sm_src, sm_in, send_sems, recv_sems, load_sems,
):
    s = lax.axis_index("seq")
    y = lax.axis_index("tensor")
    z = lax.axis_index("dp")
    c = s % 2
    m = s // 2
    width = xp.shape[0]
    rows = d_out.shape[0]
    columns = xp.shape[1]
    half_len = rx.shape[1]
    length = 2 * half_len
    heads = probs_h.shape[0]
    dim = mixed.shape[0] // heads
    zs = width // rows
    mesh_id = dict(device_id_type=pl.DeviceIdType.MESH)
    to_core = {"seq": 2 * m + 1 - c}
    to_x = {"seq": 2 * (1 - m) + c}
    to_y = {"tensor": 1 - y}
    to_z = {"dp": (z + 1) % zs}
    to_swap = {"seq": 2 * m + y, "tensor": c}
    to_back = {"seq": 2 * m + 1 - y, "tensor": c}

    barrier = pltpu.get_barrier_semaphore()
    greet = [to_core, to_y, {"seq": 2 * m + 1 - c, "tensor": 1 - y}, to_x] + [{"dp": (z + i) % zs} for i in range(1, zs)]
    for who in greet:
        pl.semaphore_signal(barrier, inc=1, device_id=who, **mesh_id)
    pl.semaphore_wait(barrier, len(greet))

    def move(k, src, dst, who):
        return pltpu.make_async_remote_copy(
            src_ref=src, dst_ref=dst, send_sem=send_sems.at[k], recv_sem=recv_sems.at[k], device_id=who, **mesh_id
        )

    def load(k, src, dst):
        return pltpu.make_async_copy(src, dst, load_sems.at[k])

    def chunk(j):
        return pl.ds(pl.multiple_of(j * rows, rows), rows)

    def side(i, size):
        return pl.ds(pl.multiple_of(i * size, 128), size)

    order = [(z + zs - 1 - k) % zs for k in range(zs)]
    mine = side(c, columns)
    my_half = side(c, half_len)
    other_half = side(1 - c, half_len)
    cut = [(0, 192), (192, rows - 192)]

    def part(j, p):
        return pl.ds(pl.multiple_of(j * rows + cut[p][0], 16), cut[p][1])

    parts = [pl.ds(*each) for each in cut]

    late = move(0, late_h, late_in, to_y)
    swap_out = move(1, outp_h, got_p, to_swap)
    back_out = move(2, outr_h, got_r, to_back)
    z_down = [move(3, r_core.at[0, chunk(order[0])], zd.at[0], to_z), move(4, zd.at[0], zd.at[1], to_z)]
    z_down_last = [move(5 + p, zd.at[1, parts[p]], zd.at[2, parts[p]], to_z) for p in range(2)]
    x_down = [move(7 + p, zd.at[2, parts[p]], dx.at[parts[p]], to_x) for p in range(2)]
    core_down = [move(9 + p, d_out.at[parts[p], mine], d_out.at[parts[p], mine], to_core) for p in range(2)]
    z_pair = [move(11, r_core.at[2, chunk(order[0])], zp.at[0], to_z), move(12, zp.at[0], zp.at[1], to_z)]
    z_pair_last = [move(13 + p, zp.at[1, parts[p]], zp.at[2, parts[p]], to_z) for p in range(2)]
    x_pair_back = [move(15 + p, zp.at[2, parts[p]], px.at[parts[p]], to_x) for p in range(2)]
    core_pair = [move(17 + p, p_out.at[m, parts[p], mine], p_out.at[m, parts[p], mine], to_core) for p in range(2)]
    core_pair_back = [
        move(19 + p, p_out.at[1 - m, parts[p], mine], p_out.at[1 - m, parts[p], mine], to_core) for p in range(2)
    ]
    core_branch = move(21, bf.at[:, my_half], bf.at[:, my_half], to_core)
    a_cols = ya.shape[2]
    a_rows = xa.shape[1]
    my_cols = side(y, a_cols)
    my_rows = pl.ds(pl.multiple_of(m * a_rows, a_rows), a_rows)
    x_rows = pl.ds(pl.multiple_of((1 - m) * a_rows, a_rows), a_rows)
    x_attn = [move(22 + k, ya.at[j, x_rows], xa.at[j], to_x) for k, j in enumerate(order)]
    z_attn = [move(26, ya.at[order[0], my_rows], za.at[0], to_z)] + [
        move(26 + t, za.at[t - 1], za.at[t], to_z) for t in range(1, zs - 1)
    ]
    my_piece = ab.at[my_rows, my_cols]
    spread_attn = [
        move(29 + i, my_piece, my_piece, who)
        for i, who in enumerate((to_x, to_y, {"seq": 2 * (1 - m) + c, "tensor": 1 - y}))
    ]
    core_attn = move(32, ab, a_out, to_core)
    swap_in = move(33, gin, got_in, to_swap)

    def x_pair(k):
        at = chunk((z + zs - 1 - k) % zs)
        return move(44 + k, r_core.at[1, at], xp.at[at], to_x)

    late.start()

    def step_z_down(t):
        z_down[t - 1].wait_recv()
        zd[t - 1] = (zd[t - 1].astype(wide) + r_core[0, chunk(order[t]), :].astype(wide)).astype(low)
        for each in z_down_last if t == 2 else [z_down[t]]:
            each.start()

    def last_z_down(p):
        z_down_last[p].wait_recv()
        at = parts[p]
        zd[2, at, :] = (zd[2, at, :].astype(wide) + r_core[0, part(z, p), :].astype(wide)).astype(low)
        x_down[p].start()

    def end_down(p):
        x_down[p].wait_recv()
        at = parts[p]
        d_out[at, mine] = (zd[2, at, :].astype(wide) + dx[at, :].astype(wide)).astype(low)
        core_down[p].start()

    def step_z_pair(t):
        x_pair(t).wait_recv()
        term = r_core[2, chunk(order[t]), :].astype(wide) + xp[chunk(order[t]), :].astype(wide)
        if t:
            z_pair[t - 1].wait_recv()
            zp[t - 1] = (zp[t - 1].astype(wide) + term).astype(low)
        else:
            r_core[2, chunk(order[0]), :] = term.astype(low)
        for each in z_pair_last if t == 2 else [z_pair[t]]:
            each.start()

    def last_z_pair(p):
        if p == 0:
            x_pair(3).wait_recv()
        z_pair_last[p].wait_recv()
        at = parts[p]
        term = r_core[2, part(z, p), :].astype(wide) + xp[part(z, p), :].astype(wide)
        total = (zp[2, at, :].astype(wide) + term).astype(low)
        zp[2, at, :] = total
        x_pair_back[p].start()
        p_out[m, at, mine] = total
        core_pair[p].start()

    def end_pair(p):
        x_pair_back[p].wait_recv()
        at = parts[p]
        p_out[1 - m, at, mine] = px[at, :]
        core_pair_back[p].start()

    def step_attn(t):
        x_attn[t].wait_recv()
        term = ya[order[t], my_rows, :].astype(wide) + xa[order[t]].astype(wide)
        if t:
            z_attn[t - 1].wait_recv()
            za[t - 1] = (za[t - 1].astype(wide) + term).astype(low)
        else:
            x_attn[0].wait_send()
            ya[order[0], my_rows, :] = term.astype(low)
        if t < zs - 1:
            z_attn[t].start()

    hops = [to_core, to_y, to_x, {"dp": z + 1 - 2 * (z % 2)}, {"dp": (z + 2) % zs}]
    exchange = [move(39 + i, sm_src.at[i], sm_in.at[i], who) for i, who in enumerate(hops)]

    def start_sum(i):
        sm_src[i] = small[...]
        exchange[i].start()

    def end_sum(i):
        exchange[i].wait_recv()
        small[...] = sm_src[i] + sm_in[i]

    def weights(r_buf, l_go, l_gr, l_xo, l_xr, s_buf):
        loads = [
            load(0, pair_h.at[1 - m], r_buf.at[0]),
            load(1, xo_h, l_xo),
            load(2, xr_h, l_xr),
            load(3, hid_h, r_buf.at[1]),
            load(4, go_h, l_go),
            load(5, gr_h, l_gr),
        ]
        load_own = load(6, pair_h.at[m], r_buf.at[0])
        for each in loads:
            each.start()
        theirs = side(1 - c, columns)

        def core(i, k):
            at = chunk((z + zs - 1 - k) % zs)
            return move(48 + i * zs + k, s_buf.at[i % 2, at], r_core.at[(1, 0, 2)[i], at], to_core)

        def product(left_o, left_r, right, col, i, extra=None):
            def block(k, carry):
                at = chunk((z + zs - 1 - k) % zs)
                total = dot(left_o[at, :], right[:half_len, col], 1, 0)
                total = total + dot(left_r[at, :], right[half_len:, col], 1, 0)
                if extra is None:
                    s_buf[i % 2, at, :] = total.astype(low)
                    core(i, k).start()
                else:
                    out = (1, 0, 2)[i]
                    core(i, k).wait_recv()
                    r_core[out, at, :] = (total + r_core[out, at, :].astype(wide)).astype(low)
                    extra(k)
                return carry

            lax.fori_loop(0, zs, block, 0)

        def at_first(run):
            def extra(k):
                pl.when(k == 0)(run)

            return extra

        def sent(i):
            def block(k, carry):
                core(i, k).wait_send()
                return carry

            lax.fori_loop(0, zs, block, 0)

        for each in loads[:3]:
            each.wait()
        product(l_xo, l_xr, r_buf.at[0], theirs, 0)
        product(l_xo, l_xr, r_buf.at[0], mine, 0, lambda k: x_pair(k).start())
        load_own.start()

        @pl.when(c != y)
        def _():
            swap_out.start()

        back_out.start()
        for each in loads[3:]:
            each.wait()
        product(l_go, l_gr, r_buf.at[1], theirs, 1)
        product(l_go, l_gr, r_buf.at[1], mine, 1, at_first(z_down[0].start))
        load_own.wait()
        sent(0)
        product(l_xo, l_xr, r_buf.at[0], theirs, 2)
        product(l_xo, l_xr, r_buf.at[0], mine, 2, at_first(lambda: step_z_pair(0)))
        sent(1)
        sent(2)

    hidden = hid_h.shape[1]
    left = pltpu.VMEM((width, half_len), low)
    pl.run_scoped(
        weights,
        pltpu.VMEM((2, length, hidden), low),
        left,
        left,
        left,
        left,
        pltpu.VMEM((2, width, columns), low),
    )

    def attention(gxv, hv, gov, p_buf, k_acc, v_acc, sums, gqkv, gm, xn1, sx, ga):
        loads = [load(7, gx_h, gxv), load(8, hres_h, hv), load(9, go_h, gov), load(10, xn1_h, xn1)]
        load_x = load(11, xin_h, gov)
        for each in loads:
            each.start()

        def probs_load(h, b, slot):
            return load(12 + slot, probs_h.at[h, :, side(b, q_block)], p_buf.at[slot])

        probs_load(0, 0, 0).start()
        lanes = half_len // 128
        piece = 64
        pieces = width // piece

        def fold(a):
            return sum(a[:, i * 128 : (i + 1) * 128] for i in range(lanes))

        def spread(a):
            return jnp.concatenate([a] * lanes, axis=1)

        def norm_backward(values, gain, scale, grad, store, row):
            def first(i, total):
                at = pl.ds(pl.multiple_of(i * piece, piece), piece)
                return total + jnp.sum(values(at) * (spread(gain[at, :]) * grad(at)), axis=0, keepdims=True)

            total = lax.fori_loop(0, pieces, first, jnp.zeros((1, half_len), wide))
            mean = total * scale[...] * (1.0 / width)

            def second(i, carry):
                at = pl.ds(pl.multiple_of(i * piece, piece), piece)
                g = grad(at)
                normed = values(at) * scale[...]
                store(at, scale[...] * (spread(gain[at, :]) * g - normed * mean))
                ga_part[at, :] = fold(g * normed)
                return carry

            lax.fori_loop(0, pieces, second, 0)
            small[row : row + 1, :] = jnp.sum(ga_part[...].T, axis=0, keepdims=True)

        ga_part = sums.at[:width, :128]
        small[...] = jnp.zeros_like(small)
        for each in loads[:3]:
            each.wait()
        late.wait_recv()
        gxv[:, late_in.shape[1] :] += late_in[...].astype(wide)

        def store_hres(at, back):
            total = gov[at, :].astype(wide) + back
            gxv[at, :] = total
            bf[at, my_half] = total.astype(low)

        norm_backward(lambda at: hv[at, :], gain2, scale2, lambda at: gxv[at, :], store_hres, 0)
        core_branch.start()
        load_x.start()
        step_z_down(1)
        core_branch.wait_recv()
        gm[...] = dot(out_w[...], bf[...], 1, 0).astype(low)

        reach = length - q_block
        blocks = length // q_block
        near_rows = q_block + 2 * band_half
        d = (
            lax.broadcasted_iota(jnp.int32, (near_rows, q_block), 0)
            - lax.broadcasted_iota(jnp.int32, (near_rows, q_block), 1)
            - band_half
        )
        for h in range(heads):
            head = pl.ds(h * dim, dim)
            k_rows = pl.ds((heads + h) * dim, dim)
            v_rows = pl.ds((2 * heads + h) * dim, dim)
            k_acc[...] = jnp.zeros_like(k_acc)
            v_acc[...] = jnp.zeros_like(v_acc)
            sums[...] = jnp.zeros_like(sums)

            def block(b, carry):
                slot = b % 2
                at = side(b, q_block)
                probs_load(h, b, slot).wait()

                @pl.when(b < blocks - 1)
                def _():
                    probs_load(h, b + 1, 1 - slot).start()

                if h < heads - 1:

                    @pl.when(b == blocks - 1)
                    def _():
                        probs_load(h + 1, 0, 1 - slot).start()

                probs = p_buf[slot]
                go = gm[head, at]
                inner = jnp.sum(go.astype(wide) * mixed[head, at].astype(wide), axis=0, keepdims=True)
                scores = probs.astype(wide) * (dot(qkv[v_rows, :], go, 0, 0) - inner)
                first = pl.multiple_of(reach - b * q_block, q_block)
                sums[pl.ds(first, length), :] += scores
                scores = scores.astype(low)
                gqkv[head, at] = dot(qkv[k_rows, :], scores, 1, 0).astype(low)
                k_acc[...] += dot(qkv[head, at], scores, 1, 1)
                v_acc[...] += dot(go, probs, 1, 1)
                return carry

            lax.fori_loop(0, blocks, block, 0)
            gqkv[k_rows, :] = k_acc[...].astype(low)
            gqkv[v_rows, :] = v_acc[...].astype(low)
            near = sums[reach - band_half : reach + q_block + band_half, :]
            n = jnp.abs(d)
            bucket = jnp.zeros((near_rows, q_block), jnp.int32)
            for step in steps_at:
                bucket = bucket + jnp.where(n >= step, 1, 0)
            bucket = bucket + jnp.where(d > 0, 16, 0)
            totals = []
            for b in range(32):
                total = jnp.sum(jnp.where(bucket == b, near, 0.0), axis=0, keepdims=True)
                if b == 15:
                    total = total + jnp.sum(sums[: reach - band_half, :], axis=0, keepdims=True)
                if b == 31:
                    total = total + jnp.sum(sums[reach + q_block + band_half :, :], axis=0, keepdims=True)
                totals.append(total)
            totals = jnp.concatenate(totals, axis=0)
            totals = jnp.concatenate([totals, jnp.zeros((96, q_block), wide)], axis=0)
            line = jnp.sum(totals.T, axis=0, keepdims=True)
            for side_c in range(2):
                row = 8 + side_c * heads + h
                small[row : row + 1, :128] = jnp.where(c == side_c, line, 0.0)
            if h == 1:
                step_z_pair(1)

        def input_grad(half, store):
            def block(i, carry):
                at = chunk(i)
                store(at, dot(w_t[at, :], gqkv[:, half], 1, 0))
                return carry

            lax.fori_loop(0, zs, block, 0)

        def store_sent(at, value):
            sx[at, :] = value.astype(low)

        input_grad(other_half, store_sent)
        core_x = move(34, sx, rx, to_core)
        core_x.start()
        loads[3].wait()
        y_attn = [
            move(35 + k, ga.at[j, :, side(1 - y, a_cols)], ya.at[j], to_y) for k, j in enumerate(order)
        ]
        wide_cols = gqkv.shape[0]
        for k, j in enumerate(order):
            ga[j, :rows, :wide_cols] = dot(xn1[chunk(j), :], gqkv[...], 1, 1).astype(low)
            ga[j, :rows, wide_cols:] = dot(bf[chunk(j), :], mixed[...], 1, 1).astype(low)
            ga[j, rows:, :] = jnp.zeros((ga.shape[1] - rows, ga.shape[2]), low)
            y_attn[k].start()
        step_z_down(2)

        def store_own(at, value):
            hv[at, :] = value

        input_grad(my_half, store_own)
        load_x.wait()
        core_x.wait_recv()

        def store_in(at, back):
            gin[at, :] = (gxv[at, :] + back).astype(low)

        norm_backward(
            lambda at: gov[at, :].astype(wide),
            gain1,
            scale1,
            lambda at: hv[at, :] + rx[at, :].astype(wide),
            store_in,
            1,
        )

        @pl.when(c != y)
        def _():
            swap_in.start()

        def step_y_attn(k):
            j = order[k]
            y_attn[k].wait_recv()
            ya[j] = (ya[j].astype(wide) + ga[j, :, my_cols].astype(wide)).astype(low)
            x_attn[k].start()

        step_y_attn(0)
        step_z_pair(2)
        start_sum(0)
        step_y_attn(1)
        step_attn(0)
        end_sum(0)
        start_sum(1)
        last_z_down(0)
        step_y_attn(2)
        last_z_down(1)
        step_y_attn(3)
        core_x.wait_send()
        for each in y_attn:
            each.wait_send()

    f32 = lambda *shape: pltpu.VMEM(shape, wide)
    b16 = lambda *shape: pltpu.VMEM(shape, low)
    pl.run_scoped(
        attention,
        f32(width, half_len),
        f32(width, half_len),
        b16(width, half_len),
        b16(2, length, q_block),
        f32(dim, length),
        f32(dim, length),
        f32(2 * length - q_block, q_block),
        b16(3 * heads * dim, length),
        b16(heads * dim, length),
        b16(width, length),
        b16(width, half_len),
        b16(zs, ya.shape[1], 2 * ya.shape[2]),
    )

    end_sum(1)
    start_sum(2)
    end_down(0)
    last_z_pair(0)
    end_down(1)
    last_z_pair(1)
    step_attn(1)
    end_sum(2)
    start_sum(3)
    step_attn(2)
    end_pair(0)
    step_attn(3)
    ab[my_rows, my_cols] = za[zs - 2]
    for each in spread_attn:
        each.start()
    end_sum(3)
    start_sum(4)
    end_pair(1)
    for each in spread_attn:
        each.wait_recv()

    @pl.when(c == y)
    def _():
        core_attn.start()
        a_out[...] = ab[...]
        core_attn.wait_send()

    end_sum(4)

    @pl.when(c != y)
    def _():
        core_attn.wait_recv()
        swap_out.wait()
        swap_in.wait()

    back_out.wait()
    for each in core_down + core_pair + core_pair_back:
        each.wait()
    for each in [late, core_branch] + z_down + z_down_last + x_down + z_pair + z_pair_last + x_pair_back:
        each.wait_send()
    for each in [x_pair(k) for k in range(zs)] + x_attn[1:] + z_attn + spread_attn + exchange:
        each.wait_send()


def back_all(
    hid, pair, g_own, g_oth, x_own, x_oth, gx, hres, x_in, probs, xn_one, out_first, out_oth, late,
    out_w, qkv_w, qkv, mixed, gain_two, gain_one, scale_two, scale_one, zs,
):
    width, half_len = g_own.shape
    length = 2 * half_len
    rows = width // zs
    columns = hid.shape[1] // 2
    heads = probs.shape[0]
    a_cols = 2 * (qkv_w.shape[0] + out_w.shape[0]) // 4
    a_len = -(-rows // 32) * 32
    hbm = pl.BlockSpec(memory_space=pl.ANY)
    vmem = pl.BlockSpec(memory_space=pltpu.VMEM)
    sds = lambda kind, *shape: jax.ShapeDtypeStruct(shape, kind)
    b16 = lambda *shape: pltpu.VMEM(shape, low)
    spread = lambda gain: jnp.broadcast_to(gain, (width, 128))
    return pl.pallas_call(
        back_kernel,
        in_specs=[hbm] * 14 + [vmem] * 8,
        out_specs=[hbm] * 3 + [vmem] * 5,
        out_shape=[
            sds(low, width, half_len),
            sds(low, width, half_len),
            sds(low, width, half_len),
            sds(low, rows, 2 * columns),
            sds(low, 2, rows, 2 * columns),
            sds(low, a_len, 2 * a_cols),
            sds(low, width, half_len),
            sds(wide, 16, width),
        ],
        scratch_shapes=[
            b16(3, width, columns),
            b16(width, columns),
            b16(zs - 1, rows, columns),
            b16(zs - 1, rows, columns),
            b16(rows, columns),
            b16(rows, columns),
            b16(width, length),
            b16(width, half_len),
            b16(zs, a_len, a_cols),
            b16(zs, a_len // 2, a_cols),
            b16(zs - 1, a_len // 2, a_cols),
            b16(a_len, 2 * a_cols),
            b16(width, half_len // 2),
            pltpu.VMEM((5, 16, width), wide),
            pltpu.VMEM((5, 16, width), wide),
            pltpu.SemaphoreType.DMA((60,)),
            pltpu.SemaphoreType.DMA((60,)),
            pltpu.SemaphoreType.DMA((14,)),
        ],
        compiler_params=pltpu.CompilerParams(vmem_limit_bytes=61 << 20, collective_id=1, has_side_effects=True),
        cost_estimate=hint,
        name="back_all",
    )(
        hid, pair, g_own, g_oth, x_own, x_oth, gx, hres, x_in, probs, xn_one, out_first, out_oth, late,
        out_w, qkv_w.T, qkv, mixed, spread(gain_two), spread(gain_one), scale_two, scale_one,
    )


def norm_of(values, gain):
    scale = lax.rsqrt(jnp.mean(values * values, axis=0, keepdims=True) + eps_norm)
    return values * scale * gain, scale


def norm_back(values, scale, gain, grad):
    normed = values * scale
    pushed = gain * grad
    mean = jnp.mean(normed * pushed, axis=0, keepdims=True)
    return scale * (pushed - normed * mean), jnp.sum(grad * normed, axis=1)


class Moves:
    def __init__(self, mesh):
        self.nz = mesh.shape["dp"]
        self.nx = mesh.shape["seq"] // 2
        both = [(m, c, y) for m in range(self.nx) for c in range(2) for y in range(2)]
        at = lambda m, c, y: (m * 2 + c) * 2 + y
        self.swap_pairs = [(at(m, c, y), at(m, y, c)) for m, c, y in both if c != y]
        self.second_pairs = [(at(m, c, y), at(m, y, 1 - c)) for m, c, y in both]
        self.back_pairs = [(b, a) for a, b in self.second_pairs]
        self.ring_x = [(m * 2 + c, (m + 1) % self.nx * 2 + c) for m in range(self.nx) for c in range(2)]
        self.y = lax.axis_index("tensor")
        self.z = lax.axis_index("dp")
        s = lax.axis_index("seq")
        self.c = s % 2
        self.m = s // 2

    def swap(self, a):
        got = lax.ppermute(a, ("seq", "tensor"), self.swap_pairs)
        return jnp.where(self.c == self.y, a, got)

    def second(self, a):
        return lax.ppermute(a, ("seq", "tensor"), self.second_pairs)

    def back(self, a):
        return lax.ppermute(a, ("seq", "tensor"), self.back_pairs)

    def core(self, a):
        return lax.ppermute(a, "seq", [(s, s ^ 1) for s in range(2 * self.nx)])

    def over_y(self, a):
        return lax.ppermute(a, "tensor", [(0, 1), (1, 0)])

    def over_x(self, a):
        return lax.ppermute(a, "seq", self.ring_x)

    def start_x(self, a):
        take = lax.dynamic_index_in_dim(a, (self.m + self.nx - 1) % self.nx, 1, False)
        return a, self.over_x(take)

    def finish_x(self, a, got, *first):
        take = lambda i: lax.dynamic_index_in_dim(a, i % self.nx, 1, False)
        got = after(got, *first)
        held = (got.astype(wide) + take(self.m + 2 * self.nx - 2).astype(wide)).astype(low)
        for t in range(2, self.nx):
            held = (self.over_x(held).astype(wide) + take(self.m + 2 * self.nx - 1 - t).astype(wide)).astype(low)
        return held

    def scatter_x(self, a):
        take = lambda i: lax.dynamic_index_in_dim(a, i % self.nx, 1, False)
        held = take(self.m + self.nx - 1)
        for t in range(1, self.nx):
            held = (self.over_x(held).astype(wide) + take(self.m + 2 * self.nx - 1 - t).astype(wide)).astype(low)
        return held

    def scatter_z(self, a):
        return lax.psum_scatter(a, "dp", scatter_dimension=0, tiled=True)

    def gather_x(self, piece):
        if self.nx == 2:
            over = self.over_x(piece)
            return jnp.where(
                self.m == 0, jnp.concatenate([piece, over], 0), jnp.concatenate([over, piece], 0)
            )
        groups = [[m * 2 + c for m in range(self.nx)] for c in range(2)]
        return lax.all_gather(piece, "seq", axis=0, tiled=True, axis_index_groups=groups)

    def gather_core(self, piece):
        there = self.core(piece)
        return jnp.where(
            self.c == 0, jnp.concatenate([piece, there], 1), jnp.concatenate([there, piece], 1)
        )

    def sum_everywhere(self, a):
        a = a + self.core(a)
        a = a + self.over_y(a)
        step = 1
        while step < self.nx:
            a = a + lax.ppermute(a, "seq", [(s, s ^ (2 * step)) for s in range(2 * self.nx)])
            step *= 2
        step = 1
        while step < self.nz:
            a = a + lax.ppermute(a, "dp", [(z, z ^ step) for z in range(self.nz)])
            step *= 2
        return a


def segment_ids(lengths, valid, length):
    ends = jnp.sum(jnp.where(jnp.arange(4)[None, :] <= jnp.arange(4)[:, None], lengths[None, :], 0), axis=1)
    where_at = jnp.arange(length, dtype=jnp.int32)
    counted = jnp.sum((where_at[:, None] >= ends[None, :]).astype(jnp.int32), axis=1)
    return jnp.where(where_at < valid, counted, 4)


def local(
    mesh,
    layer_in,
    out_grad,
    doc_lengths,
    valid_length,
    gain_attn,
    query_weight,
    key_weight,
    value_weight,
    position_bias,
    output_weight,
    gain_ffn,
    gate_weight,
    up_weight,
    down_weight,
):
    moves = Moves(mesh)
    half_len, _, width = layer_in.shape
    length = 2 * half_len
    heads = position_bias.shape[1]
    inner_width = query_weight.shape[1]
    y, c, m = moves.y, moves.c, moves.m

    facts = jnp.concatenate([doc_lengths[0].astype(wide), valid_length.astype(wide), position_bias.reshape(-1)])
    facts = moves.swap(facts)
    bias = facts[5:].reshape(position_bias.shape)
    facts = facts[:5].astype(jnp.int32)
    x_in = moves.swap(layer_in.reshape(half_len, width).T)
    qkv_w = jnp.concatenate([query_weight.T, key_weight.T, value_weight.T], axis=0)
    qkv_w = moves.swap(qkv_w)
    positions = y * half_len + jnp.arange(half_len, dtype=jnp.int32)
    g_in = jnp.where((positions < valid_length[0])[None, :], out_grad.reshape(half_len, width).T, 0)
    g_in, out_w, x_in, facts = lax.optimization_barrier((g_in.astype(low), output_weight, x_in, facts))
    out_w = moves.swap(out_w)
    g_own = moves.swap(g_in)
    g_oth = moves.second(g_in)
    segment = segment_ids(facts[:4], facts[4], length)
    gain_one = gain_attn.astype(wide)[:, None]
    gain_two = gain_ffn.astype(wide)[:, None]

    def both_halves(own):
        other = moves.core(own)
        return jnp.where(
            c == 0, jnp.concatenate([own, other], 1), jnp.concatenate([other, own], 1)
        )

    def my_half(a):
        return lax.dynamic_slice_in_dim(a, c * half_len, half_len, 1)

    def other_half(a):
        return lax.dynamic_slice_in_dim(a, (1 - c) * half_len, half_len, 1)

    x_wide = x_in.astype(wide)
    normed, scale_one = norm_of(x_wide, gain_one)
    xn_one = both_halves(normed.astype(low))
    qkv = dot(qkv_w, xn_one, 1, 0).astype(low)
    probs, mixed = attn_forward(qkv, segment, bias)
    sent = dot(out_w, other_half(mixed), 0, 0).astype(low)
    hres = x_wide + dot(out_w, my_half(mixed), 0, 0) + moves.core(sent).astype(wide)

    normed, scale_two = norm_of(hres, gain_two)
    xn_own = normed.astype(low)
    hid, pair, xn_oth, out_own, out_oth, gx, late = ffn(
        xn_own, g_own, g_oth, gate_weight, up_weight, down_weight.T
    )
    if moves.nx == 2 and moves.nz == 4:
        out_first = (hres + out_own).astype(low)
        got_first, got_oth, got_in, sum_d, sum_p, sums, grad_in, small = back_all(
            hid, pair, g_own, g_oth, xn_own, xn_oth, gx, hres, x_in, probs, xn_one, out_first, out_oth, late,
            out_w, qkv_w, qkv, mixed, gain_two, gain_one, scale_two, scale_one, moves.nz,
        )
        out_y = jnp.where(c == y, out_first, got_first).astype(wide) + got_oth.astype(wide)
        grad_in = jnp.where(c == y, grad_in, got_in).astype(wide)
        sums = sums[: width // moves.nz].astype(wide)
        sum_q, sum_k, sum_v, sum_o = (
            sums[:, i * inner_width : (i + 1) * inner_width] for i in range(4)
        )
        return (
            out_y.astype(low).T.reshape(half_len, 1, width),
            grad_in.T.reshape(half_len, 1, width),
            small[1],
            sum_q,
            sum_k,
            sum_v,
            small[8 : 8 + 2 * heads, : position_bias.shape[0]].T,
            sum_o.T,
            small[0],
            sum_p[0].astype(wide),
            sum_p[1].astype(wide),
            sum_d.astype(wide).T,
        )
    grad_gate, grad_up = pair[0], pair[1]
    gx = gx.at[:, half_len // 2 :].add(moves.over_y(late).astype(wide))

    columns = hid.shape[1] // 2
    send_d = weight_grad(g_own, g_oth, hid, 1 - c)
    got_d = moves.core(send_d)
    send_g = weight_grad(xn_own, xn_oth, after(grad_gate, send_d), 1 - c)
    got_g = moves.core(send_g)
    send_u = weight_grad(xn_own, xn_oth, after(grad_up, send_g), 1 - c)
    got_u = moves.core(send_u)
    total_d = weight_grad(g_own, g_oth, after(hid, send_u), c, got_d)
    total_g = weight_grad(xn_own, xn_oth, after(grad_gate, total_d), c, got_g)
    total_u = weight_grad(xn_own, xn_oth, after(grad_up, total_g), c, got_u)
    part_d = moves.scatter_z(total_d)
    x_sent = [moves.start_x(t.reshape(moves.nz, moves.nx, -1, columns)) for t in (total_g, total_u)]

    gx = after(gx, total_u)
    out_y = moves.swap((hres + out_own).astype(low)).astype(wide) + moves.back(out_oth).astype(wide)

    back, grad_gain_two = norm_back(hres, scale_two, gain_two, gx)
    grad_hres = g_own.astype(wide) + back
    branch = both_halves(grad_hres.astype(low))

    grad_mixed = dot(out_w, branch, 1, 0).astype(low)
    grad_qkv, grad_bias = attn_backward(qkv, grad_mixed, mixed, probs)

    part_g = moves.finish_x(*x_sent[0], grad_qkv).reshape(-1, columns)
    sent = dot(qkv_w, other_half(after(grad_qkv, part_g)), 0, 0).astype(low)
    part_g = moves.scatter_z(part_g)
    got_x = moves.core(sent)
    grad_attn_w = jnp.concatenate(
        [dot(xn_one, after(grad_qkv, sent), 1, 1).astype(low), dot(branch, mixed, 1, 1).astype(low)], axis=1
    )
    gx = dot(qkv_w, my_half(after(grad_qkv, grad_attn_w)), 0, 0) + got_x.astype(wide)
    back, grad_gain_one = norm_back(x_wide, scale_one, gain_one, gx)
    grad_in = (grad_hres + back).astype(low)
    part_u = moves.scatter_z(moves.finish_x(*x_sent[1], grad_in).reshape(-1, columns))

    a_columns = grad_attn_w.shape[1] // 2
    chunks = grad_attn_w.reshape(moves.nz, moves.nx, -1, 2 * a_columns)

    def scatter_y(a):
        got = moves.over_y(lax.dynamic_slice_in_dim(a, (1 - y) * a_columns, a_columns, a.ndim - 1))
        kept = lax.dynamic_slice_in_dim(a, y * a_columns, a_columns, a.ndim - 1)
        return (kept.astype(wide) + got.astype(wide)).astype(low)

    half_z = moves.nz // 2
    part = jnp.concatenate(
        [moves.scatter_x(scatter_y(chunks[:half_z])), scatter_y(moves.scatter_x(chunks[half_z:]))], 0
    )
    piece = moves.gather_x(moves.scatter_z(part.reshape(-1, a_columns)))
    there = moves.over_y(piece)
    group = jnp.where(y == 0, jnp.concatenate([piece, there], 1), jnp.concatenate([there, piece], 1))
    sums = jnp.where(c == y, group, moves.core(group)).astype(wide)
    sum_q, sum_k, sum_v, sum_o = (
        sums[:, i * inner_width : (i + 1) * inner_width] for i in range(4)
    )
    grad_in = moves.swap(grad_in).astype(wide)

    if moves.nx == 2:
        part_d = (part_d.astype(wide) + moves.over_x(part_d).astype(wide)).astype(low)
    else:
        part_d = moves.gather_x(moves.scatter_x(part_d.reshape(1, moves.nx, -1, columns))[0])
    sum_d = moves.gather_core(part_d).astype(wide)
    sum_g = moves.gather_core(moves.gather_x(part_g)).astype(wide)
    sum_u = moves.gather_core(moves.gather_x(part_u)).astype(wide)

    bias_full = jnp.zeros((grad_bias.shape[0], 2 * heads), wide)
    bias_full = lax.dynamic_update_slice(bias_full, grad_bias, (jnp.int32(0), c * heads))
    early = moves.sum_everywhere(jnp.concatenate([grad_gain_two, bias_full.reshape(-1)]))
    gain_two_sum, bias_sum = early[:width], early[width:].reshape(bias_full.shape)
    gain_one_sum = moves.sum_everywhere(grad_gain_one)
    return (
        out_y.astype(low).T.reshape(half_len, 1, width),
        grad_in.T.reshape(half_len, 1, width),
        gain_one_sum,
        sum_q,
        sum_k,
        sum_v,
        bias_sum,
        sum_o.T,
        gain_two_sum,
        sum_g,
        sum_u,
        sum_d.T,
    )


def solution(mesh):
    rows = P("tensor", ("dp", "seq"), None)
    columns = P(None, "tensor")
    return jax.shard_map(
        functools.partial(local, mesh),
        mesh=mesh,
        in_specs=(
            rows,
            rows,
            P(("dp", "seq"), None),
            P(("dp", "seq")),
            P(),
            columns,
            columns,
            columns,
            columns,
            P("tensor", None),
            P(),
            columns,
            columns,
            P("tensor", None),
        ),
        out_specs=(
            rows,
            rows,
            P(),
            P("dp", "tensor"),
            P("dp", "tensor"),
            P("dp", "tensor"),
            P(),
            P("tensor", "dp"),
            P(),
            P("dp", "tensor"),
            P("dp", "tensor"),
            P("tensor", "dp"),
        ),
        check_vma=False,
    )
```

```python
import functools
import math

import jax
import jax.numpy as jnp
from jax import lax
from jax.experimental import pallas as pl
from jax.experimental.pallas import tpu as pltpu
from jax.sharding import PartitionSpec as P

steps_at = (1, 2, 3, 4, 5, 6, 7, 8, 12, 16, 23, 32, 46, 64, 91)
eps_norm = 1e-06
masked_score = -1e30
q_block = 256
band_half = 128
low = jnp.bfloat16
wide = jnp.float32
hint = pl.CostEstimate(flops=1000, bytes_accessed=1000, transcendentals=0)


def dot(a, b, ca, cb):
    return lax.dot_general(a, b, (((ca,), (cb,)), ((), ())), preferred_element_type=wide)


def after(value, *first):
    return lax.optimization_barrier((value, *first))[0]


def front_kernel(
    x_h, g_h, wq_h, wk_h, wv_h, wo_h, lengths, valid, bias, gain1_row, gain2_row,
    x_in, g_in, g_own, w, w_t, xn1, qkv, mixed, probs_h, hres, xn2, scale1, scale2, gain1, gain2,
    facts_src, facts, p_buf, table, sx, rx, seg_k, seg_q, send_sems, recv_sems, load_sems,
):
    s = lax.axis_index("seq")
    y = lax.axis_index("tensor")
    c = s % 2
    m = s // 2
    width, half_len = x_in.shape
    length = 2 * half_len
    heads, buckets = bias.shape
    inner = mixed.shape[0]
    dim = inner // heads
    piece = 64
    pieces = width // piece
    lanes = half_len // 128
    mesh_id = dict(device_id_type=pl.DeviceIdType.MESH)
    to_core = {"seq": 2 * m + 1 - c}
    to_swap = {"seq": 2 * m + 1 - c, "tensor": 1 - y}

    def side(i, size):
        return pl.ds(pl.multiple_of(i * size, 128), size)

    my_half = side(c, half_len)
    other_half = side(1 - c, half_len)

    def move(k, src, dst, who):
        return pltpu.make_async_remote_copy(
            src_ref=src, dst_ref=dst, send_sem=send_sems.at[k], recv_sem=recv_sems.at[k], device_id=who, **mesh_id
        )

    named = [(x_h, x_in)] + [
        (src, w.at[pl.ds(i * inner, inner)]) for i, src in enumerate((wq_h, wk_h, wv_h, wo_h))
    ]
    moves = [move(1 + i, src, dst, to_swap) for i, (src, dst) in enumerate(named)]
    loads = [pltpu.make_async_copy(src, dst, load_sems.at[1 + i]) for i, (src, dst) in enumerate(named)]
    move_facts = move(0, facts_src, facts, to_swap)
    move_g = move(6, g_in, g_own, to_swap)
    load_g = pltpu.make_async_copy(g_h, g_in, load_sems.at[0])
    keep_g = pltpu.make_async_copy(g_in, g_own, load_sems.at[6])
    core_one = move(7, xn1.at[:, my_half], xn1.at[:, my_half], to_core)
    core_two = move(8, sx, rx, to_core)

    load_g.start()
    for h in range(heads):
        for b in range(buckets):
            at = h * buckets + b
            facts_src[at : at + 1, :] = jnp.full((1, 128), bias[h, b], wide)
    end = jnp.int32(0)
    at = heads * buckets
    for i in range(4):
        end = end + lengths[0, i]
        facts_src[at + i : at + i + 1, :] = jnp.full((1, 128), end.astype(wide), wide)
    facts_src[at + 4 : at + 5, :] = jnp.full((1, 128), valid[0].astype(wide), wide)

    barrier = pltpu.get_barrier_semaphore()
    for who in (to_core, to_swap):
        pl.semaphore_signal(barrier, inc=1, device_id=who, **mesh_id)
    pl.semaphore_wait(barrier, 2)

    @pl.when(c != y)
    def _():
        move_facts.start()
        for each in moves:
            each.start()

    @pl.when(c == y)
    def _():
        for each in loads:
            each.start()
        facts[...] = facts_src[...]

    load_g.wait()
    live = lax.broadcasted_iota(jnp.int32, (piece, half_len), 1) + y * half_len < valid[0]

    def mask(i, carry):
        at = pl.ds(pl.multiple_of(i * piece, piece), piece)
        g_in[at, :] = jnp.where(live, g_in[at, :].astype(wide), 0.0).astype(low)
        return carry

    lax.fori_loop(0, pieces, mask, 0)

    @pl.when(c != y)
    def _():
        move_g.start()

    @pl.when(c == y)
    def _():
        keep_g.start()

    gain1[...] = jnp.broadcast_to(gain1_row[...].astype(wide), (128, width)).T
    gain2[...] = jnp.broadcast_to(gain2_row[...].astype(wide), (128, width)).T

    @pl.when(c != y)
    def _():
        move_facts.wait_recv()

    at = heads * buckets

    def segments(positions):
        count = jnp.zeros(positions.shape, wide)
        for i in range(4):
            count = count + jnp.where(positions >= facts[at + i : at + i + 1, :], 1.0, 0.0)
        return jnp.where(positions < facts[at + 4 : at + 5, :], count, 4.0)

    seg_k[...] = segments(lax.broadcasted_iota(jnp.int32, (length, 128), 0).astype(wide))
    for i in range(length // 128):
        positions = (lax.broadcasted_iota(jnp.int32, (8, 128), 1) + i * 128).astype(wide)
        seg_q[:, i * 128 : (i + 1) * 128] = segments(positions)
    reach = length - q_block
    near_rows = q_block + 2 * band_half
    d = (
        lax.broadcasted_iota(jnp.int32, (near_rows, 128), 0)
        - lax.broadcasted_iota(jnp.int32, (near_rows, 128), 1)
        - band_half
    )
    far_rows = reach - band_half
    for h in range(heads):

        def value(b, h=h):
            return facts[h * buckets + b : h * buckets + b + 1, :]

        for i in range(q_block // 128):
            offset = d - i * 128
            n = jnp.abs(offset)
            before = jnp.broadcast_to(value(0), n.shape)
            later = jnp.broadcast_to(value(16), n.shape)
            for number, step in enumerate(steps_at):
                reached = n >= step
                before = jnp.where(reached, value(number + 1), before)
                later = jnp.where(reached, value(number + 17), later)
            col = pl.ds(i * 128, 128)
            table[h, pl.ds(far_rows, near_rows), col] = jnp.where(offset > 0, later, before)
            table[h, pl.ds(0, far_rows), col] = jnp.broadcast_to(value(15), (far_rows, 128))
            table[h, pl.ds(far_rows + near_rows, far_rows), col] = jnp.broadcast_to(value(31), (far_rows, 128))

    def spread(a):
        return jnp.concatenate([a] * lanes, axis=1)

    def norm(read, gain, scale, write):
        def first(i, total):
            v = read(pl.ds(pl.multiple_of(i * piece, piece), piece))
            return total + jnp.sum(v * v, axis=0, keepdims=True)

        total = lax.fori_loop(0, pieces, first, jnp.zeros((1, half_len), wide))
        scale[...] = lax.rsqrt(total * (1.0 / width) + eps_norm)

        def second(i, carry):
            at = pl.ds(pl.multiple_of(i * piece, piece), piece)
            write(at, (read(at) * scale[...] * spread(gain[at, :])).astype(low))
            return carry

        lax.fori_loop(0, pieces, second, 0)

    def arrived(i):
        @pl.when(c != y)
        def _():
            moves[i].wait_recv()

        @pl.when(c == y)
        def _():
            loads[i].wait()

    arrived(0)

    def write_one(at, value):
        xn1[at, my_half] = value

    norm(lambda at: x_in[at, :].astype(wide), gain1, scale1, write_one)
    core_one.start()
    for i in range(1, 4):
        arrived(i)
    core_one.wait_recv()
    for i in range(3):
        qkv[i * inner : (i + 1) * inner, :] = dot(w[i * inner : (i + 1) * inner, :], xn1[...], 1, 0).astype(low)

    blocks = length // q_block

    def store(i):
        h, b = i // blocks, i % blocks
        return pltpu.make_async_copy(p_buf.at[i % 2], probs_h.at[h, :, side(b, q_block)], load_sems.at[7 + i % 2])

    def block(i, carry):
        h, b = i // blocks, i % blocks
        at = side(b, q_block)
        rows = lambda part: pl.ds(pl.multiple_of((part * heads + h) * dim, dim), dim)
        first = pl.multiple_of(reach - b * q_block, q_block)
        scores = dot(qkv[rows(1), :], qkv[rows(0), at], 0, 0) + table[h, pl.ds(first, length), :]
        keys = jnp.concatenate([seg_k[...]] * (q_block // 128), axis=1)
        scores = jnp.where(keys == seg_q[0:1, at], scores, masked_score)
        raised = jnp.exp(scores - jnp.max(scores, axis=0, keepdims=True))
        probs = (raised * (1.0 / jnp.sum(raised, axis=0, keepdims=True))).astype(low)

        @pl.when(i >= 2)
        def _():
            store(i - 2).wait()

        p_buf[i % 2] = probs
        store(i).start()
        mixed[rows(0), at] = dot(qkv[rows(2), :], probs, 1, 0).astype(low)
        return carry

    lax.fori_loop(0, heads * blocks, block, 0)

    arrived(4)
    out_w = w[3 * inner :, :]
    sx[...] = dot(out_w, mixed[:, other_half], 0, 0).astype(low)
    core_two.start()
    hres[...] = dot(out_w, mixed[:, my_half], 0, 0)
    w_t[...] = w[: 3 * inner, :].T
    core_two.wait_recv()

    def add(i, carry):
        at = pl.ds(pl.multiple_of(i * piece, piece), piece)
        hres[at, :] += x_in[at, :].astype(wide) + rx[at, :].astype(wide)
        return carry

    lax.fori_loop(0, pieces, add, 0)

    def write_two(at, value):
        xn2[at, :] = value

    norm(lambda at: hres[at, :], gain2, scale2, write_two)
    last = heads * blocks
    store(last - 2).wait()
    store(last - 1).wait()
    core_one.wait_send()
    core_two.wait_send()

    @pl.when(c != y)
    def _():
        move_facts.wait_send()
        for each in moves:
            each.wait_send()
        move_g.wait()

    @pl.when(c == y)
    def _():
        keep_g.wait()


def front(x, g, weights, lengths, valid, bias, gain_one, gain_two):
    width, half_len = x.shape
    length = 2 * half_len
    heads = bias.shape[0]
    inner = weights[0].shape[0]
    hbm = pl.BlockSpec(memory_space=pl.ANY)
    vmem = pl.BlockSpec(memory_space=pltpu.VMEM)
    smem = pl.BlockSpec(memory_space=pltpu.SMEM)
    sds = lambda kind, *shape: jax.ShapeDtypeStruct(shape, kind)
    facts = pltpu.VMEM((heads * bias.shape[1] + 8, 128), wide)
    return pl.pallas_call(
        front_kernel,
        in_specs=[hbm] * 6 + [smem] * 3 + [vmem] * 2,
        out_specs=[vmem, vmem, hbm, vmem, vmem, vmem, vmem, vmem, hbm] + [vmem] * 6,
        out_shape=[
            sds(low, width, half_len),
            sds(low, width, half_len),
            sds(low, width, half_len),
            sds(low, 4 * inner, width),
            sds(low, width, 3 * inner),
            sds(low, width, length),
            sds(low, 3 * inner, length),
            sds(low, inner, length),
            sds(low, heads, length, length),
            sds(wide, width, half_len),
            sds(low, width, half_len),
            sds(wide, 1, half_len),
            sds(wide, 1, half_len),
            sds(wide, width, 128),
            sds(wide, width, 128),
        ],
        scratch_shapes=[
            facts,
            facts,
            pltpu.VMEM((2, length, q_block), low),
            pltpu.VMEM((heads, 2 * length - q_block, q_block), wide),
            pltpu.VMEM((width, half_len), low),
            pltpu.VMEM((width, half_len), low),
            pltpu.VMEM((length, 128), wide),
            pltpu.VMEM((8, length), wide),
            pltpu.SemaphoreType.DMA((9,)),
            pltpu.SemaphoreType.DMA((9,)),
            pltpu.SemaphoreType.DMA((9,)),
        ],
        compiler_params=pltpu.CompilerParams(vmem_limit_bytes=60 << 20, collective_id=2, has_side_effects=True),
        cost_estimate=hint,
        name="front_all",
    )(x, g, *weights, lengths, valid, bias, gain_one, gain_two)


def attn_bwd_kernel(length, q_ref, k_ref, v_ref, go_ref, o_ref, p_ref, gq_ref, gk_ref, gv_ref, gb_ref, k_acc, v_acc, sums):
    block = pl.program_id(1)
    reach = length - q_block

    @pl.when(block == 0)
    def _():
        k_acc[...] = jnp.zeros_like(k_acc)
        v_acc[...] = jnp.zeros_like(v_acc)
        sums[...] = jnp.zeros_like(sums)

    probs = p_ref[0]
    go = go_ref[...]
    inner = jnp.sum(go.astype(wide) * o_ref[...].astype(wide), axis=0, keepdims=True)
    scores = probs.astype(wide) * (dot(v_ref[...], go, 0, 0) - inner)
    first = pl.multiple_of(reach - block * q_block, q_block)
    sums[pl.ds(first, length), :] += scores
    scores = scores.astype(low)
    gq_ref[...] = dot(k_ref[...], scores, 1, 0).astype(low)
    k_acc[...] += dot(q_ref[...], scores, 1, 1)
    v_acc[...] += dot(go, probs, 1, 1)

    @pl.when(block == pl.num_programs(1) - 1)
    def _():
        gk_ref[...] = k_acc[...].astype(low)
        gv_ref[...] = v_acc[...].astype(low)
        rows = q_block + 2 * band_half
        d = (
            lax.broadcasted_iota(jnp.int32, (rows, q_block), 0)
            - lax.broadcasted_iota(jnp.int32, (rows, q_block), 1)
            - band_half
        )
        n = jnp.abs(d)
        near = sums[reach - band_half : reach + q_block + band_half, :]
        far_before = jnp.sum(sums[: reach - band_half, :], axis=0, keepdims=True)
        far_after = jnp.sum(sums[reach + q_block + band_half :, :], axis=0, keepdims=True)
        bucket = jnp.zeros((rows, q_block), jnp.int32)
        for step in steps_at:
            bucket = bucket + jnp.where(n >= step, 1, 0)
        bucket = bucket + jnp.where(d > 0, 16, 0)
        for b in range(32):
            total = jnp.sum(jnp.where(bucket == b, near, 0.0), axis=0, keepdims=True)
            if b == 15:
                total = total + far_before
            if b == 31:
                total = total + far_after
            gb_ref[0, b : b + 1, :] = total


def attn_backward(qkv, grad_mixed, mixed, probs):
    width, length = qkv.shape
    heads = probs.shape[0]
    dim = width // (3 * heads)
    blocks = length // q_block
    half = pl.BlockSpec((dim, q_block), lambda h, b: (h, b))
    whole = pl.BlockSpec((dim, length), lambda h, b: (h, 0))
    gq, gk, gv, gb = pl.pallas_call(
        functools.partial(attn_bwd_kernel, length),
        grid=(heads, blocks),
        in_specs=[
            half,
            pl.BlockSpec((dim, length), lambda h, b: (heads + h, 0)),
            pl.BlockSpec((dim, length), lambda h, b: (2 * heads + h, 0)),
            half,
            half,
            pl.BlockSpec((1, length, q_block), lambda h, b: (h, 0, b)),
        ],
        out_specs=[half, whole, whole, pl.BlockSpec((1, 32, q_block), lambda h, b: (h, 0, 0))],
        out_shape=[
            jax.ShapeDtypeStruct((heads * dim, length), low),
            jax.ShapeDtypeStruct((heads * dim, length), low),
            jax.ShapeDtypeStruct((heads * dim, length), low),
            jax.ShapeDtypeStruct((heads, 32, q_block), wide),
        ],
        scratch_shapes=[
            pltpu.VMEM((dim, length), wide),
            pltpu.VMEM((dim, length), wide),
            pltpu.VMEM((2 * length - q_block, q_block), wide),
        ],
        compiler_params=pltpu.CompilerParams(vmem_limit_bytes=48 << 20),
        cost_estimate=hint,
        name="attn_backward",
    )(qkv, qkv, qkv, grad_mixed, mixed, probs)
    return jnp.concatenate([gq, gk, gv], axis=0), jnp.sum(gb, axis=2).T


def ffn_kernel(
    x_ref, go_ref, hres_ref, g_h, gate_w, up_w, down_w,
    hid_ref, pair_ref, xr_ref, gr_ref, out_ref, out_r_ref, gx_ref, late_ref,
    xs, gs, out_acc, gx_acc, x_in, g_in, sems,
):
    chunk = pl.program_id(0)
    tile = pl.program_id(1)
    size = xs.shape[0]
    s = lax.axis_index("seq")
    y = lax.axis_index("tensor")
    c = s % 2
    first = s - c
    mesh_id = dict(device_id_type=pl.DeviceIdType.MESH)
    to_y = {"tensor": 1 - y}
    to_core = {"seq": first + 1 - c}
    to_second = {"seq": first + y, "tensor": 1 - c}
    half = [pl.ds(0, size), pl.ds(size, size)]

    def send_x(h):
        return pltpu.make_async_remote_copy(
            src_ref=x_ref.at[:, half[h]], dst_ref=x_in.at[h], send_sem=sems.at[h], recv_sem=sems.at[2 + h],
            device_id=to_y, **mesh_id,
        )

    def send_g(h):
        return pltpu.make_async_remote_copy(
            src_ref=g_h.at[:, half[h]], dst_ref=g_in.at[h], send_sem=sems.at[4 + h], recv_sem=sems.at[6 + h],
            device_id=to_second, **mesh_id,
        )

    @pl.when(tile == 0)
    def _():
        out_acc[...] = jnp.zeros_like(out_acc)
        gx_acc[...] = jnp.zeros_like(gx_acc)

    @pl.when((tile == 0) & (chunk == 0))
    def _():
        barrier = pltpu.get_barrier_semaphore()
        for who in (to_y, to_core):
            pl.semaphore_signal(barrier, inc=1, device_id=who, **mesh_id)
        pl.semaphore_wait(barrier, 2)
        for h in range(2):
            send_x(h).start()
            send_g(h).start()

    for h in range(2):

        @pl.when((tile == 0) & (chunk == h))
        def _(h=h):
            xs[...] = x_ref[:, half[h]].T
            gs[...] = go_ref[:, half[h]].T

        @pl.when((tile == 0) & (chunk == 2 + h))
        def _(h=h):
            send_x(h).wait_recv()
            xs[...] = x_in[h].T
            xr_ref[:, half[h]] = x_in[h]
            send_g(h).wait_recv()
            gs[...] = g_in[h].T
            gr_ref[:, half[h]] = g_in[h]

    gate = dot(xs[...], gate_w[...], 1, 0)
    up = dot(xs[...], up_w[...], 1, 0)
    grad = dot(gs[...], down_w[...], 1, 0)
    c_gelu = math.sqrt(2.0 / math.pi)
    square = gate * gate
    t = jnp.tanh(c_gelu * gate * (1.0 + 0.044715 * square))
    part = 0.5 * (1.0 + t)
    gelu = gate * part
    slope = part + 0.5 * gate * (1.0 - t * t) * (c_gelu * (1.0 + 3 * 0.044715 * square))
    hid = (gelu * up).astype(low)
    gg = (grad * up * slope).astype(low)
    gu = (grad * gelu).astype(low)
    hid_ref[...] = hid
    pair_ref[0] = gg
    pair_ref[1] = gu
    out_acc[...] += dot(down_w[...], hid, 1, 1)
    gx_acc[...] += dot(gate_w[...], gg, 1, 1) + dot(up_w[...], gu, 1, 1)

    last = tile == pl.num_programs(1) - 1
    for h in range(2):

        @pl.when(last & (chunk == h))
        def _(h=h):
            out_ref[:, half[h]] = (hres_ref[:, half[h]] + out_acc[...]).astype(low)
            gx_ref[:, half[h]] = gx_acc[...]

        @pl.when(last & (chunk == 2 + h))
        def _(h=h):
            out_r_ref[:, half[h]] = out_acc[...].astype(low)
            late_ref[:, half[h]] = gx_acc[...].astype(low)

    @pl.when(last & (chunk == 3))
    def _():
        for h in range(2):
            send_x(h).wait_send()
            send_g(h).wait_send()


def ffn(x, g_own, hres, g_in, gate_w, up_w, down_w):
    width, tokens = x.shape
    hidden = gate_w.shape[1]
    tile, size = 256, tokens // 2
    full = pl.BlockSpec((width, tokens), lambda s, j: (0, 0), pipeline_mode=pl.Buffered(1))
    weight = pl.BlockSpec((width, tile), lambda s, j: (0, j))
    act_shape = jax.ShapeDtypeStruct((2 * tokens, hidden), low)
    tokens_of = lambda kind: jax.ShapeDtypeStruct((width, tokens), kind)
    return pl.pallas_call(
        ffn_kernel,
        grid=(4, hidden // tile),
        in_specs=[full, full, full, pl.BlockSpec(memory_space=pl.ANY), weight, weight, weight],
        out_specs=[
            pl.BlockSpec((size, tile), lambda s, j: (s, j)),
            pl.BlockSpec((2, size, tile), lambda s, j: (0, s, j)),
        ]
        + [full] * 6,
        out_shape=[act_shape, jax.ShapeDtypeStruct((2, 2 * tokens, hidden), low)]
        + [tokens_of(kind) for kind in (low, low, low, low, wide, low)],
        scratch_shapes=[
            pltpu.VMEM((size, width), low),
            pltpu.VMEM((size, width), low),
            pltpu.VMEM((width, size), wide),
            pltpu.VMEM((width, size), wide),
            pltpu.VMEM((2, width, size), low),
            pltpu.VMEM((2, width, size), low),
            pltpu.SemaphoreType.DMA((8,)),
        ],
        compiler_params=pltpu.CompilerParams(vmem_limit_bytes=56 << 20, collective_id=0, has_side_effects=True),
        cost_estimate=hint,
        name="ffn_both_ways",
    )(x, g_own, hres, g_in, gate_w, up_w, down_w)


def weight_grad_kernel(core_ref, own_ref, oth_ref, right_ref, *refs):
    tokens = own_ref.shape[1]
    total = dot(own_ref[...], right_ref[:tokens, :], 1, 0) + dot(oth_ref[...], right_ref[tokens:, :], 1, 0)
    if len(refs) == 2:
        total = total + refs[0][...].astype(wide)
    refs[-1][...] = total.astype(low)


def weight_grad(own, oth, right, core, got=None):
    width, tokens = own.shape
    columns = right.shape[1] // 2
    blocks = 4
    rows = width // blocks
    left = pl.BlockSpec((rows, tokens), lambda i, core_ref: (i, 0))
    out = pl.BlockSpec((rows, columns), lambda i, core_ref: (i, 0))
    args = [own, oth, right] + ([] if got is None else [got])
    return pl.pallas_call(
        weight_grad_kernel,
        grid_spec=pltpu.PrefetchScalarGridSpec(
            num_scalar_prefetch=1,
            grid=(blocks,),
            in_specs=[
                left,
                left,
                pl.BlockSpec((2 * tokens, columns), lambda i, core_ref: (0, core_ref[0]), pipeline_mode=pl.Buffered(1)),
            ]
            + ([] if got is None else [out]),
            out_specs=out,
        ),
        out_shape=jax.ShapeDtypeStruct((width, columns), low),
        compiler_params=pltpu.CompilerParams(vmem_limit_bytes=40 << 20),
        cost_estimate=hint,
        name="weight_grad",
    )(core.reshape(1), *args)


def back_kernel(
    hid_h, pair_h, go_h, gr_h, xo_h, xr_h, gx_h, hres_h, xin_h, probs_h, xn1_h, outp_h, outr_h, late_h,
    out_w, w_t, qkv, mixed, gain2, gain1, scale2, scale1,
    got_p, got_r, got_in, d_out, p_out, a_out, gin, small,
    r_core, xp, zd, zp, dx, px, bf, rx, ya, xa, za, ab, late_in, sm_src, sm_in, send_sems, recv_sems, load_sems,
):
    s = lax.axis_index("seq")
    y = lax.axis_index("tensor")
    z = lax.axis_index("dp")
    c = s % 2
    m = s // 2
    width = xp.shape[0]
    rows = d_out.shape[0]
    columns = xp.shape[1]
    half_len = rx.shape[1]
    length = 2 * half_len
    heads = probs_h.shape[0]
    dim = mixed.shape[0] // heads
    zs = width // rows
    mesh_id = dict(device_id_type=pl.DeviceIdType.MESH)
    to_core = {"seq": 2 * m + 1 - c}
    to_x = {"seq": 2 * (1 - m) + c}
    to_y = {"tensor": 1 - y}
    to_z = {"dp": (z + 1) % zs}
    to_swap = {"seq": 2 * m + y, "tensor": c}
    to_back = {"seq": 2 * m + 1 - y, "tensor": c}

    barrier = pltpu.get_barrier_semaphore()
    greet = [to_core, to_y, {"seq": 2 * m + 1 - c, "tensor": 1 - y}, to_x] + [{"dp": (z + i) % zs} for i in range(1, zs)]
    for who in greet:
        pl.semaphore_signal(barrier, inc=1, device_id=who, **mesh_id)
    pl.semaphore_wait(barrier, len(greet))

    def move(k, src, dst, who):
        return pltpu.make_async_remote_copy(
            src_ref=src, dst_ref=dst, send_sem=send_sems.at[k], recv_sem=recv_sems.at[k], device_id=who, **mesh_id
        )

    def load(k, src, dst):
        return pltpu.make_async_copy(src, dst, load_sems.at[k])

    def chunk(j):
        return pl.ds(pl.multiple_of(j * rows, rows), rows)

    def side(i, size):
        return pl.ds(pl.multiple_of(i * size, 128), size)

    order = [(z + zs - 1 - k) % zs for k in range(zs)]
    mine = side(c, columns)
    my_half = side(c, half_len)
    other_half = side(1 - c, half_len)
    cut = [(0, 192), (192, rows - 192)]

    def part(j, p):
        return pl.ds(pl.multiple_of(j * rows + cut[p][0], 16), cut[p][1])

    parts = [pl.ds(*each) for each in cut]

    late = move(0, late_h, late_in, to_y)
    swap_out = move(1, outp_h, got_p, to_swap)
    back_out = move(2, outr_h, got_r, to_back)
    z_down = [move(3, r_core.at[0, chunk(order[0])], zd.at[0], to_z), move(4, zd.at[0], zd.at[1], to_z)]
    z_down_last = [move(5 + p, zd.at[1, parts[p]], zd.at[2, parts[p]], to_z) for p in range(2)]
    x_down = [move(7 + p, zd.at[2, parts[p]], dx.at[parts[p]], to_x) for p in range(2)]
    core_down = [move(9 + p, d_out.at[parts[p], mine], d_out.at[parts[p], mine], to_core) for p in range(2)]
    z_pair = [move(11, r_core.at[2, chunk(order[0])], zp.at[0], to_z), move(12, zp.at[0], zp.at[1], to_z)]
    z_pair_last = [move(13 + p, zp.at[1, parts[p]], zp.at[2, parts[p]], to_z) for p in range(2)]
    x_pair_back = [move(15 + p, zp.at[2, parts[p]], px.at[parts[p]], to_x) for p in range(2)]
    core_pair = [move(17 + p, p_out.at[m, parts[p], mine], p_out.at[m, parts[p], mine], to_core) for p in range(2)]
    core_pair_back = [
        move(19 + p, p_out.at[1 - m, parts[p], mine], p_out.at[1 - m, parts[p], mine], to_core) for p in range(2)
    ]
    core_branch = move(21, bf.at[:, my_half], bf.at[:, my_half], to_core)
    a_cols = ya.shape[2]
    a_rows = xa.shape[1]
    my_cols = side(y, a_cols)
    my_rows = pl.ds(pl.multiple_of(m * a_rows, a_rows), a_rows)
    x_rows = pl.ds(pl.multiple_of((1 - m) * a_rows, a_rows), a_rows)
    x_attn = [move(22 + k, ya.at[j, x_rows], xa.at[j], to_x) for k, j in enumerate(order)]
    z_attn = [move(26, ya.at[order[0], my_rows], za.at[0], to_z)] + [
        move(26 + t, za.at[t - 1], za.at[t], to_z) for t in range(1, zs - 1)
    ]
    my_piece = ab.at[my_rows, my_cols]
    spread_attn = [
        move(29 + i, my_piece, my_piece, who)
        for i, who in enumerate((to_x, to_y, {"seq": 2 * (1 - m) + c, "tensor": 1 - y}))
    ]
    core_attn = move(32, ab, a_out, to_core)
    swap_in = move(33, gin, got_in, to_swap)

    def x_pair(k):
        at = chunk((z + zs - 1 - k) % zs)
        return move(44 + k, r_core.at[1, at], xp.at[at], to_x)

    late.start()

    def step_z_down(t):
        z_down[t - 1].wait_recv()
        zd[t - 1] = (zd[t - 1].astype(wide) + r_core[0, chunk(order[t]), :].astype(wide)).astype(low)
        for each in z_down_last if t == 2 else [z_down[t]]:
            each.start()

    def last_z_down(p):
        z_down_last[p].wait_recv()
        at = parts[p]
        zd[2, at, :] = (zd[2, at, :].astype(wide) + r_core[0, part(z, p), :].astype(wide)).astype(low)
        x_down[p].start()

    def end_down(p):
        x_down[p].wait_recv()
        at = parts[p]
        d_out[at, mine] = (zd[2, at, :].astype(wide) + dx[at, :].astype(wide)).astype(low)
        core_down[p].start()

    def step_z_pair(t):
        x_pair(t).wait_recv()
        term = r_core[2, chunk(order[t]), :].astype(wide) + xp[chunk(order[t]), :].astype(wide)
        if t:
            z_pair[t - 1].wait_recv()
            zp[t - 1] = (zp[t - 1].astype(wide) + term).astype(low)
        else:
            r_core[2, chunk(order[0]), :] = term.astype(low)
        for each in z_pair_last if t == 2 else [z_pair[t]]:
            each.start()

    def last_z_pair(p):
        if p == 0:
            x_pair(3).wait_recv()
        z_pair_last[p].wait_recv()
        at = parts[p]
        term = r_core[2, part(z, p), :].astype(wide) + xp[part(z, p), :].astype(wide)
        total = (zp[2, at, :].astype(wide) + term).astype(low)
        zp[2, at, :] = total
        x_pair_back[p].start()
        p_out[m, at, mine] = total
        core_pair[p].start()

    def end_pair(p):
        x_pair_back[p].wait_recv()
        at = parts[p]
        p_out[1 - m, at, mine] = px[at, :]
        core_pair_back[p].start()

    def step_attn(t):
        x_attn[t].wait_recv()
        term = ya[order[t], my_rows, :].astype(wide) + xa[order[t]].astype(wide)
        if t:
            z_attn[t - 1].wait_recv()
            za[t - 1] = (za[t - 1].astype(wide) + term).astype(low)
        else:
            x_attn[0].wait_send()
            ya[order[0], my_rows, :] = term.astype(low)
        if t < zs - 1:
            z_attn[t].start()

    hops = [to_core, to_y, to_x, {"dp": z + 1 - 2 * (z % 2)}, {"dp": (z + 2) % zs}]
    exchange = [move(39 + i, sm_src.at[i], sm_in.at[i], who) for i, who in enumerate(hops)]

    def start_sum(i):
        sm_src[i] = small[...]
        exchange[i].start()

    def end_sum(i):
        exchange[i].wait_recv()
        small[...] = sm_src[i] + sm_in[i]

    def weights(r_buf, l_go, l_gr, l_xo, l_xr, s_buf):
        loads = [
            load(0, pair_h.at[1 - m], r_buf.at[0]),
            load(1, xo_h, l_xo),
            load(2, xr_h, l_xr),
            load(3, hid_h, r_buf.at[1]),
            load(4, go_h, l_go),
            load(5, gr_h, l_gr),
        ]
        load_own = load(6, pair_h.at[m], r_buf.at[0])
        for each in loads:
            each.start()
        theirs = side(1 - c, columns)

        def core(i, k):
            at = chunk((z + zs - 1 - k) % zs)
            return move(48 + i * zs + k, s_buf.at[i % 2, at], r_core.at[(1, 0, 2)[i], at], to_core)

        def product(left_o, left_r, right, col, i, extra=None):
            def block(k, carry):
                at = chunk((z + zs - 1 - k) % zs)
                total = dot(left_o[at, :], right[:half_len, col], 1, 0)
                total = total + dot(left_r[at, :], right[half_len:, col], 1, 0)
                if extra is None:
                    s_buf[i % 2, at, :] = total.astype(low)
                    core(i, k).start()
                else:
                    out = (1, 0, 2)[i]
                    core(i, k).wait_recv()
                    r_core[out, at, :] = (total + r_core[out, at, :].astype(wide)).astype(low)
                    extra(k)
                return carry

            lax.fori_loop(0, zs, block, 0)

        def at_first(run):
            def extra(k):
                pl.when(k == 0)(run)

            return extra

        def sent(i):
            def block(k, carry):
                core(i, k).wait_send()
                return carry

            lax.fori_loop(0, zs, block, 0)

        for each in loads[:3]:
            each.wait()
        product(l_xo, l_xr, r_buf.at[0], theirs, 0)
        product(l_xo, l_xr, r_buf.at[0], mine, 0, lambda k: x_pair(k).start())
        load_own.start()

        @pl.when(c != y)
        def _():
            swap_out.start()

        back_out.start()
        for each in loads[3:]:
            each.wait()
        product(l_go, l_gr, r_buf.at[1], theirs, 1)
        product(l_go, l_gr, r_buf.at[1], mine, 1, at_first(z_down[0].start))
        load_own.wait()
        sent(0)
        product(l_xo, l_xr, r_buf.at[0], theirs, 2)
        product(l_xo, l_xr, r_buf.at[0], mine, 2, at_first(lambda: step_z_pair(0)))
        sent(1)
        sent(2)

    hidden = hid_h.shape[1]
    left = pltpu.VMEM((width, half_len), low)
    pl.run_scoped(
        weights,
        pltpu.VMEM((2, length, hidden), low),
        left,
        left,
        left,
        left,
        pltpu.VMEM((2, width, columns), low),
    )

    def attention(gxv, hv, gov, p_buf, k_acc, v_acc, sums, gqkv, gm, xn1, sx, ga):
        loads = [load(7, gx_h, gxv), load(8, hres_h, hv), load(9, go_h, gov), load(10, xn1_h, xn1)]
        load_x = load(11, xin_h, gov)
        for each in loads:
            each.start()

        def probs_load(h, b, slot):
            return load(12 + slot, probs_h.at[h, :, side(b, q_block)], p_buf.at[slot])

        probs_load(0, 0, 0).start()
        lanes = half_len // 128
        piece = 64
        pieces = width // piece

        def fold(a):
            return sum(a[:, i * 128 : (i + 1) * 128] for i in range(lanes))

        def spread(a):
            return jnp.concatenate([a] * lanes, axis=1)

        def norm_backward(values, gain, scale, grad, store, row):
            def first(i, total):
                at = pl.ds(pl.multiple_of(i * piece, piece), piece)
                return total + jnp.sum(values(at) * (spread(gain[at, :]) * grad(at)), axis=0, keepdims=True)

            total = lax.fori_loop(0, pieces, first, jnp.zeros((1, half_len), wide))
            mean = total * scale[...] * (1.0 / width)

            def second(i, carry):
                at = pl.ds(pl.multiple_of(i * piece, piece), piece)
                g = grad(at)
                normed = values(at) * scale[...]
                store(at, scale[...] * (spread(gain[at, :]) * g - normed * mean))
                ga_part[at, :] = fold(g * normed)
                return carry

            lax.fori_loop(0, pieces, second, 0)
            small[row : row + 1, :] = jnp.sum(ga_part[...].T, axis=0, keepdims=True)

        ga_part = sums.at[:width, :128]
        small[...] = jnp.zeros_like(small)
        for each in loads[:3]:
            each.wait()
        late.wait_recv()

        def add_late(i, carry):
            at = pl.ds(pl.multiple_of(i * piece, piece), piece)
            gxv[at, :] += late_in[at, :].astype(wide)
            return carry

        lax.fori_loop(0, pieces, add_late, 0)

        def store_hres(at, back):
            total = gov[at, :].astype(wide) + back
            gxv[at, :] = total
            bf[at, my_half] = total.astype(low)

        norm_backward(lambda at: hv[at, :], gain2, scale2, lambda at: gxv[at, :], store_hres, 0)
        core_branch.start()
        load_x.start()
        step_z_down(1)
        core_branch.wait_recv()
        gm[...] = dot(out_w[...], bf[...], 1, 0).astype(low)

        reach = length - q_block
        blocks = length // q_block
        near_rows = q_block + 2 * band_half
        d = (
            lax.broadcasted_iota(jnp.int32, (near_rows, q_block), 0)
            - lax.broadcasted_iota(jnp.int32, (near_rows, q_block), 1)
            - band_half
        )
        for h in range(heads):
            head = pl.ds(h * dim, dim)
            k_rows = pl.ds((heads + h) * dim, dim)
            v_rows = pl.ds((2 * heads + h) * dim, dim)
            k_acc[...] = jnp.zeros_like(k_acc)
            v_acc[...] = jnp.zeros_like(v_acc)
            sums[...] = jnp.zeros_like(sums)

            def block(b, carry):
                slot = b % 2
                at = side(b, q_block)
                probs_load(h, b, slot).wait()

                @pl.when(b < blocks - 1)
                def _():
                    probs_load(h, b + 1, 1 - slot).start()

                if h < heads - 1:

                    @pl.when(b == blocks - 1)
                    def _():
                        probs_load(h + 1, 0, 1 - slot).start()

                probs = p_buf[slot]
                go = gm[head, at]
                inner = jnp.sum(go.astype(wide) * mixed[head, at].astype(wide), axis=0, keepdims=True)
                scores = probs.astype(wide) * (dot(qkv[v_rows, :], go, 0, 0) - inner)
                first = pl.multiple_of(reach - b * q_block, q_block)
                sums[pl.ds(first, length), :] += scores
                scores = scores.astype(low)
                gqkv[head, at] = dot(qkv[k_rows, :], scores, 1, 0).astype(low)
                k_acc[...] += dot(qkv[head, at], scores, 1, 1)
                v_acc[...] += dot(go, probs, 1, 1)
                return carry

            lax.fori_loop(0, blocks, block, 0)
            gqkv[k_rows, :] = k_acc[...].astype(low)
            gqkv[v_rows, :] = v_acc[...].astype(low)
            near = sums[reach - band_half : reach + q_block + band_half, :]
            n = jnp.abs(d)
            bucket = jnp.zeros((near_rows, q_block), jnp.int32)
            for step in steps_at:
                bucket = bucket + jnp.where(n >= step, 1, 0)
            bucket = bucket + jnp.where(d > 0, 16, 0)
            totals = []
            for b in range(32):
                total = jnp.sum(jnp.where(bucket == b, near, 0.0), axis=0, keepdims=True)
                if b == 15:
                    total = total + jnp.sum(sums[: reach - band_half, :], axis=0, keepdims=True)
                if b == 31:
                    total = total + jnp.sum(sums[reach + q_block + band_half :, :], axis=0, keepdims=True)
                totals.append(total)
            totals = jnp.concatenate(totals, axis=0)
            totals = jnp.concatenate([totals, jnp.zeros((96, q_block), wide)], axis=0)
            line = jnp.sum(totals.T, axis=0, keepdims=True)
            for side_c in range(2):
                row = 8 + side_c * heads + h
                small[row : row + 1, :128] = jnp.where(c == side_c, line, 0.0)
            if h == 1:
                step_z_pair(1)

        def input_grad(half, store):
            def block(i, carry):
                at = chunk(i)
                store(at, dot(w_t[at, :], gqkv[:, half], 1, 0))
                return carry

            lax.fori_loop(0, zs, block, 0)

        def store_sent(at, value):
            sx[at, :] = value.astype(low)

        input_grad(other_half, store_sent)
        core_x = move(34, sx, rx, to_core)
        core_x.start()
        loads[3].wait()
        y_attn = [
            move(35 + k, ga.at[j, :, side(1 - y, a_cols)], ya.at[j], to_y) for k, j in enumerate(order)
        ]
        wide_cols = gqkv.shape[0]
        for k, j in enumerate(order):
            ga[j, :rows, :wide_cols] = dot(xn1[chunk(j), :], gqkv[...], 1, 1).astype(low)
            ga[j, :rows, wide_cols:] = dot(bf[chunk(j), :], mixed[...], 1, 1).astype(low)
            ga[j, rows:, :] = jnp.zeros((ga.shape[1] - rows, ga.shape[2]), low)
            y_attn[k].start()
        step_z_down(2)

        def store_own(at, value):
            hv[at, :] = value

        input_grad(my_half, store_own)
        load_x.wait()
        core_x.wait_recv()

        def store_in(at, back):
            gin[at, :] = (gxv[at, :] + back).astype(low)

        norm_backward(
            lambda at: gov[at, :].astype(wide),
            gain1,
            scale1,
            lambda at: hv[at, :] + rx[at, :].astype(wide),
            store_in,
            1,
        )

        @pl.when(c != y)
        def _():
            swap_in.start()

        def step_y_attn(k):
            j = order[k]
            y_attn[k].wait_recv()
            ya[j] = (ya[j].astype(wide) + ga[j, :, my_cols].astype(wide)).astype(low)
            x_attn[k].start()

        step_y_attn(0)
        step_z_pair(2)
        start_sum(0)
        step_y_attn(1)
        step_attn(0)
        end_sum(0)
        start_sum(1)
        last_z_down(0)
        step_y_attn(2)
        last_z_down(1)
        step_y_attn(3)
        core_x.wait_send()
        for each in y_attn:
            each.wait_send()

    f32 = lambda *shape: pltpu.VMEM(shape, wide)
    b16 = lambda *shape: pltpu.VMEM(shape, low)
    pl.run_scoped(
        attention,
        f32(width, half_len),
        f32(width, half_len),
        b16(width, half_len),
        b16(2, length, q_block),
        f32(dim, length),
        f32(dim, length),
        f32(2 * length - q_block, q_block),
        b16(3 * heads * dim, length),
        b16(heads * dim, length),
        b16(width, length),
        b16(width, half_len),
        b16(zs, ya.shape[1], 2 * ya.shape[2]),
    )

    end_sum(1)
    start_sum(2)
    end_down(0)
    last_z_pair(0)
    end_down(1)
    last_z_pair(1)
    step_attn(1)
    end_sum(2)
    start_sum(3)
    step_attn(2)
    end_pair(0)
    step_attn(3)
    ab[my_rows, my_cols] = za[zs - 2]
    for each in spread_attn:
        each.start()
    end_sum(3)
    start_sum(4)
    end_pair(1)
    for each in spread_attn:
        each.wait_recv()

    @pl.when(c == y)
    def _():
        core_attn.start()
        a_out[...] = ab[...]
        core_attn.wait_send()

    end_sum(4)

    @pl.when(c != y)
    def _():
        core_attn.wait_recv()
        swap_out.wait()
        swap_in.wait()

    back_out.wait()
    for each in core_down + core_pair + core_pair_back:
        each.wait()
    for each in [late, core_branch] + z_down + z_down_last + x_down + z_pair + z_pair_last + x_pair_back:
        each.wait_send()
    for each in [x_pair(k) for k in range(zs)] + x_attn[1:] + z_attn + spread_attn + exchange:
        each.wait_send()


def back_all(
    hid, pair, g_own, g_oth, x_own, x_oth, gx, hres, x_in, probs, xn_one, out_first, out_oth, late,
    out_w, w_t, qkv, mixed, gain_two, gain_one, scale_two, scale_one, zs,
):
    width, half_len = g_own.shape
    length = 2 * half_len
    rows = width // zs
    columns = hid.shape[1] // 2
    heads = probs.shape[0]
    a_cols = (w_t.shape[1] + out_w.shape[0]) // 2
    a_len = -(-rows // 32) * 32
    hbm = pl.BlockSpec(memory_space=pl.ANY)
    vmem = pl.BlockSpec(memory_space=pltpu.VMEM)
    sds = lambda kind, *shape: jax.ShapeDtypeStruct(shape, kind)
    b16 = lambda *shape: pltpu.VMEM(shape, low)
    return pl.pallas_call(
        back_kernel,
        in_specs=[hbm] * 14 + [vmem] * 8,
        out_specs=[hbm] * 3 + [vmem] * 5,
        out_shape=[
            sds(low, width, half_len),
            sds(low, width, half_len),
            sds(low, width, half_len),
            sds(low, rows, 2 * columns),
            sds(low, 2, rows, 2 * columns),
            sds(low, a_len, 2 * a_cols),
            sds(low, width, half_len),
            sds(wide, 16, width),
        ],
        scratch_shapes=[
            b16(3, width, columns),
            b16(width, columns),
            b16(zs - 1, rows, columns),
            b16(zs - 1, rows, columns),
            b16(rows, columns),
            b16(rows, columns),
            b16(width, length),
            b16(width, half_len),
            b16(zs, a_len, a_cols),
            b16(zs, a_len // 2, a_cols),
            b16(zs - 1, a_len // 2, a_cols),
            b16(a_len, 2 * a_cols),
            b16(width, half_len),
            pltpu.VMEM((5, 16, width), wide),
            pltpu.VMEM((5, 16, width), wide),
            pltpu.SemaphoreType.DMA((60,)),
            pltpu.SemaphoreType.DMA((60,)),
            pltpu.SemaphoreType.DMA((14,)),
        ],
        compiler_params=pltpu.CompilerParams(vmem_limit_bytes=61 << 20, collective_id=1, has_side_effects=True),
        cost_estimate=hint,
        name="back_all",
    )(
        hid, pair, g_own, g_oth, x_own, x_oth, gx, hres, x_in, probs, xn_one, out_first, out_oth, late,
        out_w, w_t, qkv, mixed, gain_two, gain_one, scale_two, scale_one,
    )


def norm_back(values, scale, gain, grad):
    normed = values * scale
    pushed = gain * grad
    mean = jnp.mean(normed * pushed, axis=0, keepdims=True)
    return scale * (pushed - normed * mean), jnp.sum(grad * normed, axis=1)


class Moves:
    def __init__(self, mesh):
        self.nz = mesh.shape["dp"]
        self.nx = mesh.shape["seq"] // 2
        both = [(m, c, y) for m in range(self.nx) for c in range(2) for y in range(2)]
        at = lambda m, c, y: (m * 2 + c) * 2 + y
        self.swap_pairs = [(at(m, c, y), at(m, y, c)) for m, c, y in both if c != y]
        self.second_pairs = [(at(m, c, y), at(m, y, 1 - c)) for m, c, y in both]
        self.back_pairs = [(b, a) for a, b in self.second_pairs]
        self.ring_x = [(m * 2 + c, (m + 1) % self.nx * 2 + c) for m in range(self.nx) for c in range(2)]
        self.y = lax.axis_index("tensor")
        self.z = lax.axis_index("dp")
        s = lax.axis_index("seq")
        self.c = s % 2
        self.m = s // 2

    def swap(self, a):
        got = lax.ppermute(a, ("seq", "tensor"), self.swap_pairs)
        return jnp.where(self.c == self.y, a, got)

    def back(self, a):
        return lax.ppermute(a, ("seq", "tensor"), self.back_pairs)

    def core(self, a):
        return lax.ppermute(a, "seq", [(s, s ^ 1) for s in range(2 * self.nx)])

    def over_y(self, a):
        return lax.ppermute(a, "tensor", [(0, 1), (1, 0)])

    def over_x(self, a):
        return lax.ppermute(a, "seq", self.ring_x)

    def start_x(self, a):
        take = lax.dynamic_index_in_dim(a, (self.m + self.nx - 1) % self.nx, 1, False)
        return a, self.over_x(take)

    def finish_x(self, a, got, *first):
        take = lambda i: lax.dynamic_index_in_dim(a, i % self.nx, 1, False)
        got = after(got, *first)
        held = (got.astype(wide) + take(self.m + 2 * self.nx - 2).astype(wide)).astype(low)
        for t in range(2, self.nx):
            held = (self.over_x(held).astype(wide) + take(self.m + 2 * self.nx - 1 - t).astype(wide)).astype(low)
        return held

    def scatter_x(self, a):
        take = lambda i: lax.dynamic_index_in_dim(a, i % self.nx, 1, False)
        held = take(self.m + self.nx - 1)
        for t in range(1, self.nx):
            held = (self.over_x(held).astype(wide) + take(self.m + 2 * self.nx - 1 - t).astype(wide)).astype(low)
        return held

    def scatter_z(self, a):
        return lax.psum_scatter(a, "dp", scatter_dimension=0, tiled=True)

    def gather_x(self, piece):
        if self.nx == 2:
            over = self.over_x(piece)
            return jnp.where(
                self.m == 0, jnp.concatenate([piece, over], 0), jnp.concatenate([over, piece], 0)
            )
        groups = [[m * 2 + c for m in range(self.nx)] for c in range(2)]
        return lax.all_gather(piece, "seq", axis=0, tiled=True, axis_index_groups=groups)

    def gather_core(self, piece):
        there = self.core(piece)
        return jnp.where(
            self.c == 0, jnp.concatenate([piece, there], 1), jnp.concatenate([there, piece], 1)
        )

    def sum_everywhere(self, a):
        a = a + self.core(a)
        a = a + self.over_y(a)
        step = 1
        while step < self.nx:
            a = a + lax.ppermute(a, "seq", [(s, s ^ (2 * step)) for s in range(2 * self.nx)])
            step *= 2
        step = 1
        while step < self.nz:
            a = a + lax.ppermute(a, "dp", [(z, z ^ step) for z in range(self.nz)])
            step *= 2
        return a


def local(
    mesh,
    layer_in,
    out_grad,
    doc_lengths,
    valid_length,
    gain_attn,
    query_weight,
    key_weight,
    value_weight,
    position_bias,
    output_weight,
    gain_ffn,
    gate_weight,
    up_weight,
    down_weight,
):
    moves = Moves(mesh)
    half_len, _, width = layer_in.shape
    length = 2 * half_len
    heads = position_bias.shape[1]
    inner_width = query_weight.shape[1]
    y, c, m = moves.y, moves.c, moves.m

    flat = lambda a: a.reshape(half_len, width).T
    (
        x_in, g_in, g_own, w, w_t, xn_one, qkv, mixed, probs, hres, xn_own, scale_one, scale_two, gain_one, gain_two
    ) = front(
        flat(layer_in),
        flat(out_grad),
        (query_weight.T, key_weight.T, value_weight.T, output_weight),
        doc_lengths,
        valid_length,
        position_bias.T,
        gain_attn[None, :],
        gain_ffn[None, :],
    )
    qkv_w, out_w = w[: 3 * inner_width], w[3 * inner_width :]
    hid, pair, xn_oth, g_oth, out_first, out_oth, gx, late = ffn(
        xn_own, g_own, hres, g_in, gate_weight, up_weight, down_weight.T
    )
    if moves.nx == 2 and moves.nz == 4:
        got_first, got_oth, got_in, sum_d, sum_p, sums, grad_in, small = back_all(
            hid, pair, g_own, g_oth, xn_own, xn_oth, gx, hres, x_in, probs, xn_one, out_first, out_oth, late,
            out_w, w_t, qkv, mixed, gain_two, gain_one, scale_two, scale_one, moves.nz,
        )
        out_y = jnp.where(c == y, out_first, got_first).astype(wide) + got_oth.astype(wide)
        grad_in = jnp.where(c == y, grad_in, got_in).astype(wide)
        sums = sums[: width // moves.nz].astype(wide)
        sum_q, sum_k, sum_v, sum_o = (
            sums[:, i * inner_width : (i + 1) * inner_width] for i in range(4)
        )
        return (
            out_y.astype(low).T.reshape(half_len, 1, width),
            grad_in.T.reshape(half_len, 1, width),
            small[1],
            sum_q,
            sum_k,
            sum_v,
            small[8 : 8 + 2 * heads, : position_bias.shape[0]].T,
            sum_o.T,
            small[0],
            sum_p[0].astype(wide),
            sum_p[1].astype(wide),
            sum_d.astype(wide).T,
        )
    grad_gate, grad_up = pair[0], pair[1]
    gx = gx + moves.over_y(late).astype(wide)
    x_wide = x_in.astype(wide)
    gain_one, gain_two = gain_one[:, :1], gain_two[:, :1]

    def both_halves(own):
        other = moves.core(own)
        return jnp.where(
            c == 0, jnp.concatenate([own, other], 1), jnp.concatenate([other, own], 1)
        )

    def my_half(a):
        return lax.dynamic_slice_in_dim(a, c * half_len, half_len, 1)

    def other_half(a):
        return lax.dynamic_slice_in_dim(a, (1 - c) * half_len, half_len, 1)


    columns = hid.shape[1] // 2
    send_d = weight_grad(g_own, g_oth, hid, 1 - c)
    got_d = moves.core(send_d)
    send_g = weight_grad(xn_own, xn_oth, after(grad_gate, send_d), 1 - c)
    got_g = moves.core(send_g)
    send_u = weight_grad(xn_own, xn_oth, after(grad_up, send_g), 1 - c)
    got_u = moves.core(send_u)
    total_d = weight_grad(g_own, g_oth, after(hid, send_u), c, got_d)
    total_g = weight_grad(xn_own, xn_oth, after(grad_gate, total_d), c, got_g)
    total_u = weight_grad(xn_own, xn_oth, after(grad_up, total_g), c, got_u)
    part_d = moves.scatter_z(total_d)
    x_sent = [moves.start_x(t.reshape(moves.nz, moves.nx, -1, columns)) for t in (total_g, total_u)]

    gx = after(gx, total_u)
    out_y = moves.swap(out_first).astype(wide) + moves.back(out_oth).astype(wide)

    back, grad_gain_two = norm_back(hres, scale_two, gain_two, gx)
    grad_hres = g_own.astype(wide) + back
    branch = both_halves(grad_hres.astype(low))

    grad_mixed = dot(out_w, branch, 1, 0).astype(low)
    grad_qkv, grad_bias = attn_backward(qkv, grad_mixed, mixed, probs)

    part_g = moves.finish_x(*x_sent[0], grad_qkv).reshape(-1, columns)
    sent = dot(qkv_w, other_half(after(grad_qkv, part_g)), 0, 0).astype(low)
    part_g = moves.scatter_z(part_g)
    got_x = moves.core(sent)
    grad_attn_w = jnp.concatenate(
        [dot(xn_one, after(grad_qkv, sent), 1, 1).astype(low), dot(branch, mixed, 1, 1).astype(low)], axis=1
    )
    gx = dot(qkv_w, my_half(after(grad_qkv, grad_attn_w)), 0, 0) + got_x.astype(wide)
    back, grad_gain_one = norm_back(x_wide, scale_one, gain_one, gx)
    grad_in = (grad_hres + back).astype(low)
    part_u = moves.scatter_z(moves.finish_x(*x_sent[1], grad_in).reshape(-1, columns))

    a_columns = grad_attn_w.shape[1] // 2
    chunks = grad_attn_w.reshape(moves.nz, moves.nx, -1, 2 * a_columns)

    def scatter_y(a):
        got = moves.over_y(lax.dynamic_slice_in_dim(a, (1 - y) * a_columns, a_columns, a.ndim - 1))
        kept = lax.dynamic_slice_in_dim(a, y * a_columns, a_columns, a.ndim - 1)
        return (kept.astype(wide) + got.astype(wide)).astype(low)

    half_z = moves.nz // 2
    part = jnp.concatenate(
        [moves.scatter_x(scatter_y(chunks[:half_z])), scatter_y(moves.scatter_x(chunks[half_z:]))], 0
    )
    piece = moves.gather_x(moves.scatter_z(part.reshape(-1, a_columns)))
    there = moves.over_y(piece)
    group = jnp.where(y == 0, jnp.concatenate([piece, there], 1), jnp.concatenate([there, piece], 1))
    sums = jnp.where(c == y, group, moves.core(group)).astype(wide)
    sum_q, sum_k, sum_v, sum_o = (
        sums[:, i * inner_width : (i + 1) * inner_width] for i in range(4)
    )
    grad_in = moves.swap(grad_in).astype(wide)

    if moves.nx == 2:
        part_d = (part_d.astype(wide) + moves.over_x(part_d).astype(wide)).astype(low)
    else:
        part_d = moves.gather_x(moves.scatter_x(part_d.reshape(1, moves.nx, -1, columns))[0])
    sum_d = moves.gather_core(part_d).astype(wide)
    sum_g = moves.gather_core(moves.gather_x(part_g)).astype(wide)
    sum_u = moves.gather_core(moves.gather_x(part_u)).astype(wide)

    bias_full = jnp.zeros((grad_bias.shape[0], 2 * heads), wide)
    bias_full = lax.dynamic_update_slice(bias_full, grad_bias, (jnp.int32(0), c * heads))
    early = moves.sum_everywhere(jnp.concatenate([grad_gain_two, bias_full.reshape(-1)]))
    gain_two_sum, bias_sum = early[:width], early[width:].reshape(bias_full.shape)
    gain_one_sum = moves.sum_everywhere(grad_gain_one)
    return (
        out_y.astype(low).T.reshape(half_len, 1, width),
        grad_in.T.reshape(half_len, 1, width),
        gain_one_sum,
        sum_q,
        sum_k,
        sum_v,
        bias_sum,
        sum_o.T,
        gain_two_sum,
        sum_g,
        sum_u,
        sum_d.T,
    )


def solution(mesh):
    rows = P("tensor", ("dp", "seq"), None)
    columns = P(None, "tensor")
    return jax.shard_map(
        functools.partial(local, mesh),
        mesh=mesh,
        in_specs=(
            rows,
            rows,
            P(("dp", "seq"), None),
            P(("dp", "seq")),
            P(),
            columns,
            columns,
            columns,
            columns,
            P("tensor", None),
            P(),
            columns,
            columns,
            P("tensor", None),
        ),
        out_specs=(
            rows,
            rows,
            P(),
            P("dp", "tensor"),
            P("dp", "tensor"),
            P("dp", "tensor"),
            P(),
            P("tensor", "dp"),
            P(),
            P("dp", "tensor"),
            P("dp", "tensor"),
            P("tensor", "dp"),
        ),
        check_vma=False,
    )
```

```python
import functools
import math

import jax
import jax.numpy as jnp
from jax import lax
from jax.experimental import pallas as pl
from jax.experimental.pallas import tpu as pltpu
from jax.sharding import PartitionSpec as P

steps_at = (1, 2, 3, 4, 5, 6, 7, 8, 12, 16, 23, 32, 46, 64, 91)
eps_norm = 1e-06
masked_score = -1e30
q_block = 256
band_half = 128
low = jnp.bfloat16
wide = jnp.float32
hint = pl.CostEstimate(flops=1000, bytes_accessed=1000, transcendentals=0)


def dot(a, b, ca, cb):
    return lax.dot_general(a, b, (((ca,), (cb,)), ((), ())), preferred_element_type=wide)


def after(value, *first):
    return lax.optimization_barrier((value, *first))[0]


def front_kernel(
    share, x_h, g_h, wq_h, wk_h, wv_h, wo_h, lengths, valid, bias, gain1_row, gain2_row,
    x_out, g_own, g_oth, g_late, wo_out, w_t_out, xn1_out, qkv_out, mixed_out, probs_h, hres_out, xn2,
    scale1, scale2, gain1, gain2,
    x_in, g_in, w, w_t, xn1, qkv, mixed, hres,
    facts_src, facts, p_buf, table, sx, rx, seg_k, seg_q, send_sems, recv_sems, load_sems,
):
    s = lax.axis_index("seq")
    y = lax.axis_index("tensor")
    c = s % 2
    m = s // 2
    width, half_len = x_in.shape
    length = 2 * half_len
    heads, buckets = bias.shape
    inner = mixed.shape[0]
    dim = inner // heads
    piece = 64
    pieces = width // piece
    lanes = half_len // 128
    mesh_id = dict(device_id_type=pl.DeviceIdType.MESH)
    to_core = {"seq": 2 * m + 1 - c}
    to_swap = {"seq": 2 * m + 1 - c, "tensor": 1 - y}

    def side(i, size):
        return pl.ds(pl.multiple_of(i * size, 128), size)

    my_half = side(c, half_len)
    other_half = side(1 - c, half_len)

    def move(k, src, dst, who):
        return pltpu.make_async_remote_copy(
            src_ref=src, dst_ref=dst, send_sem=send_sems.at[k], recv_sem=recv_sems.at[k], device_id=who, **mesh_id
        )

    to_x = {"seq": 2 * (1 - m) + c}
    to_second = {"seq": 2 * m + y, "tensor": 1 - c}

    named = [(x_h, x_in)] + [
        (src, w.at[pl.ds(i * inner, inner)]) for i, src in enumerate((wq_h, wk_h, wv_h, wo_h))
    ]
    moves = [move(1, x_h, x_in, to_swap)]
    passed = []
    for i, src in enumerate((wq_h, wk_h, wv_h, wo_h)):
        if share:
            rows = inner // 2
            dst = w.at[pl.ds(pl.multiple_of(i * inner + m * rows, rows), rows)]
            moves.append(move(2 + i, src.at[pl.ds(pl.multiple_of(m * rows, rows), rows)], dst, to_swap))
            passed.append(move(10 + i, dst, dst, to_x))
        else:
            moves.append(move(2 + i, src, w.at[pl.ds(i * inner, inner)], to_swap))
    loads = [pltpu.make_async_copy(src, dst, load_sems.at[1 + i]) for i, (src, dst) in enumerate(named)]
    move_facts = move(0, facts_src, facts, to_swap)
    move_g = move(6, g_in, g_own, to_swap)
    early = half_len // 2
    second_g = move(9, g_in.at[:, pl.ds(0, early)], g_oth, to_second)
    to = lambda k, src, dst: pltpu.make_async_copy(src, dst, load_sems.at[k])
    keep_late = to(16, g_in.at[:, pl.ds(early, early)], g_late)
    load_g = pltpu.make_async_copy(g_h, g_in, load_sems.at[0])
    keep_g = pltpu.make_async_copy(g_in, g_own, load_sems.at[6])
    stores = [
        pltpu.make_async_copy(src, dst, load_sems.at[9 + i])
        for i, (src, dst) in enumerate(
            ((x_in, x_out), (w.at[pl.ds(3 * inner, inner)], wo_out), (w_t, w_t_out), (xn1, xn1_out), (qkv, qkv_out),
             (mixed, mixed_out), (hres, hres_out))
        )
    ]

    def pass_on(i):
        if share:

            @pl.when(c != y)
            def _():
                moves[1 + i].wait_recv()
                passed[i].start()

    core_one = move(7, xn1.at[:, my_half], xn1.at[:, my_half], to_core)
    core_two = move(8, sx, rx, to_core)

    load_g.start()
    for h in range(heads):
        for b in range(buckets):
            at = h * buckets + b
            facts_src[at : at + 1, :] = jnp.full((1, 128), bias[h, b], wide)
    end = jnp.int32(0)
    at = heads * buckets
    for i in range(4):
        end = end + lengths[0, i]
        facts_src[at + i : at + i + 1, :] = jnp.full((1, 128), end.astype(wide), wide)
    facts_src[at + 4 : at + 5, :] = jnp.full((1, 128), valid[0].astype(wide), wide)

    barrier = pltpu.get_barrier_semaphore()
    greet = [to_core, to_swap, {"tensor": 1 - y}] + ([to_x] if share else [])
    for who in greet:
        pl.semaphore_signal(barrier, inc=1, device_id=who, **mesh_id)
    pl.semaphore_wait(barrier, len(greet))

    @pl.when(c != y)
    def _():
        move_facts.start()
        for i in (1, 2, 3, 0, 4) if share else range(5):
            moves[i].start()

    @pl.when(c == y)
    def _():
        for each in loads:
            each.start()
        facts[...] = facts_src[...]

    load_g.wait()
    live = lax.broadcasted_iota(jnp.int32, (piece, half_len), 1) + y * half_len < valid[0]

    def mask(i, carry):
        at = pl.ds(pl.multiple_of(i * piece, piece), piece)
        g_in[at, :] = jnp.where(live, g_in[at, :].astype(wide), 0.0).astype(low)
        return carry

    lax.fori_loop(0, pieces, mask, 0)

    @pl.when(c != y)
    def _():
        move_g.start()

    @pl.when(c == y)
    def _():
        keep_g.start()

    second_g.start()
    keep_late.start()
    gain1[...] = jnp.broadcast_to(gain1_row[...].astype(wide)[None, :], (128, width)).T
    gain2[...] = jnp.broadcast_to(gain2_row[...].astype(wide)[None, :], (128, width)).T

    @pl.when(c != y)
    def _():
        move_facts.wait_recv()

    at = heads * buckets

    def segments(positions):
        count = jnp.zeros(positions.shape, wide)
        for i in range(4):
            count = count + jnp.where(positions >= facts[at + i : at + i + 1, :], 1.0, 0.0)
        return jnp.where(positions < facts[at + 4 : at + 5, :], count, 4.0)

    seg_k[...] = segments(lax.broadcasted_iota(jnp.int32, (length, 128), 0).astype(wide))
    for i in range(length // 128):
        positions = (lax.broadcasted_iota(jnp.int32, (8, 128), 1) + i * 128).astype(wide)
        seg_q[:, i * 128 : (i + 1) * 128] = segments(positions)
    reach = length - q_block
    near_rows = q_block + 2 * band_half
    d = (
        lax.broadcasted_iota(jnp.int32, (near_rows, 128), 0)
        - lax.broadcasted_iota(jnp.int32, (near_rows, 128), 1)
        - band_half
    )
    far_rows = reach - band_half
    for h in range(heads):

        def value(b, h=h):
            return facts[h * buckets + b : h * buckets + b + 1, :]

        for i in range(q_block // 128):
            offset = d - i * 128
            n = jnp.abs(offset)
            before = jnp.broadcast_to(value(0), n.shape)
            later = jnp.broadcast_to(value(16), n.shape)
            for number, step in enumerate(steps_at):
                reached = n >= step
                before = jnp.where(reached, value(number + 1), before)
                later = jnp.where(reached, value(number + 17), later)
            col = pl.ds(i * 128, 128)
            table[h, pl.ds(far_rows, near_rows), col] = jnp.where(offset > 0, later, before)
            table[h, pl.ds(0, far_rows), col] = jnp.broadcast_to(value(15), (far_rows, 128))
            table[h, pl.ds(far_rows + near_rows, far_rows), col] = jnp.broadcast_to(value(31), (far_rows, 128))

    def spread(a):
        return jnp.concatenate([a] * lanes, axis=1)

    def norm(read, gain, scale, write):
        def first(i, total):
            v = read(pl.ds(pl.multiple_of(i * piece, piece), piece))
            return total + jnp.sum(v * v, axis=0, keepdims=True)

        total = lax.fori_loop(0, pieces, first, jnp.zeros((1, half_len), wide))
        scale[...] = lax.rsqrt(total * (1.0 / width) + eps_norm)

        def second(i, carry):
            at = pl.ds(pl.multiple_of(i * piece, piece), piece)
            write(at, (read(at) * scale[...] * spread(gain[at, :])).astype(low))
            return carry

        lax.fori_loop(0, pieces, second, 0)

    def arrived(i):
        @pl.when(c != y)
        def _():
            (passed[i - 1] if share and i else moves[i]).wait_recv()

        @pl.when(c == y)
        def _():
            loads[i].wait()

    for i in range(3):
        pass_on(i)
    arrived(0)
    stores[0].start()

    def write_one(at, value):
        xn1[at, my_half] = value

    norm(lambda at: x_in[at, :].astype(wide), gain1, scale1, write_one)
    core_one.start()
    pass_on(3)
    for i in range(1, 4):
        arrived(i)
    core_one.wait_recv()
    stores[3].start()
    for i in range(3):
        qkv[i * inner : (i + 1) * inner, :] = dot(w[i * inner : (i + 1) * inner, :], xn1[...], 1, 0).astype(low)

    stores[4].start()

    blocks = length // q_block

    def store(i):
        h, b = i // blocks, i % blocks
        return pltpu.make_async_copy(p_buf.at[i % 2], probs_h.at[h, :, side(b, q_block)], load_sems.at[7 + i % 2])

    def block(i, carry):
        h, b = i // blocks, i % blocks
        at = side(b, q_block)
        rows = lambda part: pl.ds(pl.multiple_of((part * heads + h) * dim, dim), dim)
        first = pl.multiple_of(reach - b * q_block, q_block)
        scores = dot(qkv[rows(1), :], qkv[rows(0), at], 0, 0) + table[h, pl.ds(first, length), :]
        keys = jnp.concatenate([seg_k[...]] * (q_block // 128), axis=1)
        scores = jnp.where(keys == seg_q[0:1, at], scores, masked_score)
        raised = jnp.exp(scores - jnp.max(scores, axis=0, keepdims=True))
        probs = (raised * (1.0 / jnp.sum(raised, axis=0, keepdims=True))).astype(low)

        @pl.when(i >= 2)
        def _():
            store(i - 2).wait()

        p_buf[i % 2] = probs
        store(i).start()
        mixed[rows(0), at] = dot(qkv[rows(2), :], probs, 1, 0).astype(low)
        return carry

    lax.fori_loop(0, heads * blocks, block, 0)

    stores[5].start()
    arrived(4)
    stores[1].start()
    out_w = w[3 * inner :, :]
    sx[...] = dot(out_w, mixed[:, other_half], 0, 0).astype(low)
    core_two.start()
    hres[...] = dot(out_w, mixed[:, my_half], 0, 0)
    w_t[...] = w[: 3 * inner, :].T
    stores[2].start()
    core_two.wait_recv()

    def add(i, carry):
        at = pl.ds(pl.multiple_of(i * piece, piece), piece)
        hres[at, :] += x_in[at, :].astype(wide) + rx[at, :].astype(wide)
        return carry

    lax.fori_loop(0, pieces, add, 0)

    stores[6].start()

    def write_two(at, value):
        xn2[at, :] = value

    norm(lambda at: hres[at, :], gain2, scale2, write_two)
    last = heads * blocks
    store(last - 2).wait()
    store(last - 1).wait()
    core_one.wait_send()
    core_two.wait_send()

    @pl.when(c != y)
    def _():
        move_facts.wait_send()
        for each in moves + passed:
            each.wait_send()
        move_g.wait()

    @pl.when(c == y)
    def _():
        keep_g.wait()

    second_g.wait()
    keep_late.wait()
    for each in stores:
        each.wait()


def front(x, g, weights, lengths, valid, bias, gain_one, gain_two, share):
    width, half_len = x.shape
    length = 2 * half_len
    heads = bias.shape[0]
    inner = weights[0].shape[0]
    hbm = pl.BlockSpec(memory_space=pl.ANY)
    vmem = pl.BlockSpec(memory_space=pltpu.VMEM)
    smem = pl.BlockSpec(memory_space=pltpu.SMEM)
    sds = lambda kind, *shape: jax.ShapeDtypeStruct(shape, kind)
    facts = pltpu.VMEM((heads * bias.shape[1] + 8, 128), wide)
    b16 = lambda *shape: pltpu.VMEM(shape, low)
    return pl.pallas_call(
        functools.partial(front_kernel, share),
        in_specs=[hbm] * 6 + [smem] * 3 + [vmem] * 2,
        out_specs=[hbm] * 11 + [vmem] * 5,
        out_shape=[
            sds(low, width, half_len),
            sds(low, width, half_len),
            sds(low, width, half_len // 2),
            sds(low, width, half_len // 2),
            sds(low, inner, width),
            sds(low, width, 3 * inner),
            sds(low, width, length),
            sds(low, 3 * inner, length),
            sds(low, inner, length),
            sds(low, heads, length, length),
            sds(wide, width, half_len),
            sds(low, width, half_len),
            sds(wide, 1, half_len),
            sds(wide, 1, half_len),
            sds(wide, width, 128),
            sds(wide, width, 128),
        ],
        scratch_shapes=[
            b16(width, half_len),
            b16(width, half_len),
            b16(4 * inner, width),
            b16(width, 3 * inner),
            b16(width, length),
            b16(3 * inner, length),
            b16(inner, length),
            pltpu.VMEM((width, half_len), wide),
            facts,
            facts,
            b16(2, length, q_block),
            pltpu.VMEM((heads, 2 * length - q_block, q_block), wide),
            b16(width, half_len),
            b16(width, half_len),
            pltpu.VMEM((length, 128), wide),
            pltpu.VMEM((8, length), wide),
            pltpu.SemaphoreType.DMA((14,)),
            pltpu.SemaphoreType.DMA((14,)),
            pltpu.SemaphoreType.DMA((17,)),
        ],
        compiler_params=pltpu.CompilerParams(vmem_limit_bytes=60 << 20, collective_id=2, has_side_effects=True),
        cost_estimate=hint,
        name="front_all",
    )(x, g, *weights, lengths, valid, bias, gain_one, gain_two)


def attn_bwd_kernel(length, q_ref, k_ref, v_ref, go_ref, o_ref, p_ref, gq_ref, gk_ref, gv_ref, gb_ref, k_acc, v_acc, sums):
    block = pl.program_id(1)
    reach = length - q_block

    @pl.when(block == 0)
    def _():
        k_acc[...] = jnp.zeros_like(k_acc)
        v_acc[...] = jnp.zeros_like(v_acc)
        sums[...] = jnp.zeros_like(sums)

    probs = p_ref[0]
    go = go_ref[...]
    inner = jnp.sum(go.astype(wide) * o_ref[...].astype(wide), axis=0, keepdims=True)
    scores = probs.astype(wide) * (dot(v_ref[...], go, 0, 0) - inner)
    first = pl.multiple_of(reach - block * q_block, q_block)
    sums[pl.ds(first, length), :] += scores
    scores = scores.astype(low)
    gq_ref[...] = dot(k_ref[...], scores, 1, 0).astype(low)
    k_acc[...] += dot(q_ref[...], scores, 1, 1)
    v_acc[...] += dot(go, probs, 1, 1)

    @pl.when(block == pl.num_programs(1) - 1)
    def _():
        gk_ref[...] = k_acc[...].astype(low)
        gv_ref[...] = v_acc[...].astype(low)
        rows = q_block + 2 * band_half
        d = (
            lax.broadcasted_iota(jnp.int32, (rows, q_block), 0)
            - lax.broadcasted_iota(jnp.int32, (rows, q_block), 1)
            - band_half
        )
        n = jnp.abs(d)
        near = sums[reach - band_half : reach + q_block + band_half, :]
        far_before = jnp.sum(sums[: reach - band_half, :], axis=0, keepdims=True)
        far_after = jnp.sum(sums[reach + q_block + band_half :, :], axis=0, keepdims=True)
        bucket = jnp.zeros((rows, q_block), jnp.int32)
        for step in steps_at:
            bucket = bucket + jnp.where(n >= step, 1, 0)
        bucket = bucket + jnp.where(d > 0, 16, 0)
        for b in range(32):
            total = jnp.sum(jnp.where(bucket == b, near, 0.0), axis=0, keepdims=True)
            if b == 15:
                total = total + far_before
            if b == 31:
                total = total + far_after
            gb_ref[0, b : b + 1, :] = total


def attn_backward(qkv, grad_mixed, mixed, probs):
    width, length = qkv.shape
    heads = probs.shape[0]
    dim = width // (3 * heads)
    blocks = length // q_block
    half = pl.BlockSpec((dim, q_block), lambda h, b: (h, b))
    whole = pl.BlockSpec((dim, length), lambda h, b: (h, 0))
    gq, gk, gv, gb = pl.pallas_call(
        functools.partial(attn_bwd_kernel, length),
        grid=(heads, blocks),
        in_specs=[
            half,
            pl.BlockSpec((dim, length), lambda h, b: (heads + h, 0)),
            pl.BlockSpec((dim, length), lambda h, b: (2 * heads + h, 0)),
            half,
            half,
            pl.BlockSpec((1, length, q_block), lambda h, b: (h, 0, b)),
        ],
        out_specs=[half, whole, whole, pl.BlockSpec((1, 32, q_block), lambda h, b: (h, 0, 0))],
        out_shape=[
            jax.ShapeDtypeStruct((heads * dim, length), low),
            jax.ShapeDtypeStruct((heads * dim, length), low),
            jax.ShapeDtypeStruct((heads * dim, length), low),
            jax.ShapeDtypeStruct((heads, 32, q_block), wide),
        ],
        scratch_shapes=[
            pltpu.VMEM((dim, length), wide),
            pltpu.VMEM((dim, length), wide),
            pltpu.VMEM((2 * length - q_block, q_block), wide),
        ],
        compiler_params=pltpu.CompilerParams(vmem_limit_bytes=48 << 20),
        cost_estimate=hint,
        name="attn_backward",
    )(qkv, qkv, qkv, grad_mixed, mixed, probs)
    return jnp.concatenate([gq, gk, gv], axis=0), jnp.sum(gb, axis=2).T


def ffn_kernel(
    x_ref, go_ref, gr_ref, hres_ref, g_late, gate_w, up_w, down_w,
    hid_ref, pair_ref, xr_h, gr_h, out_h, out_r_h, gx_h, late_h,
    xs, gs, out_acc, gx_acc, x_in, g_in, gx_out, out_v, gx_v, sems, store_sems,
):
    chunk = pl.program_id(0)
    tile = pl.program_id(1)
    size = xs.shape[0]
    mesh_id = dict(device_id_type=pl.DeviceIdType.MESH)
    s = lax.axis_index("seq")
    y = lax.axis_index("tensor")
    c = s % 2
    to_y = {"tensor": 1 - y}
    to_second = {"seq": s - c + y, "tensor": 1 - c}
    half = [pl.ds(0, size), pl.ds(size, size)]

    def move(k, src, dst, who):
        return pltpu.make_async_remote_copy(
            src_ref=src, dst_ref=dst, send_sem=sems.at[k], recv_sem=sems.at[3 + k], device_id=who, **mesh_id
        )

    send_x = [move(h, x_ref.at[:, half[h]], x_in.at[h], to_y) for h in range(2)]
    send_g = move(2, g_late, g_in, to_second)
    to = lambda k, src, dst: pltpu.make_async_copy(src, dst, store_sems.at[k])
    store_x = [to(h, x_in.at[h], xr_h.at[:, half[h]]) for h in range(2)]
    store_out = [to(2 + h, out_v.at[h], out_h.at[:, half[h]]) for h in range(2)]
    store_out_r = [to(4 + h, out_v.at[2 + h], out_r_h.at[:, half[h]]) for h in range(2)]
    store_gx = [to(6 + h, gx_v.at[h], gx_h.at[:, half[h]]) for h in range(2)]
    store_late = [to(8 + h, gx_out.at[h], late_h.at[:, half[h]]) for h in range(2)]
    store_g = to(10, g_in, gr_h)

    @pl.when(tile == 0)
    def _():
        out_acc[...] = jnp.zeros_like(out_acc)
        gx_acc[...] = jnp.zeros_like(gx_acc)

    @pl.when((tile == 0) & (chunk == 0))
    def _():
        barrier = pltpu.get_barrier_semaphore()
        for who in (to_y, {"seq": s + 1 - 2 * c}):
            pl.semaphore_signal(barrier, inc=1, device_id=who, **mesh_id)
        pl.semaphore_wait(barrier, 2)
        for each in (*send_x, send_g):
            each.start()

    for h in range(2):

        @pl.when((tile == 0) & (chunk == h))
        def _(h=h):
            xs[...] = x_ref[:, half[h]].T
            gs[...] = go_ref[:, half[h]].T

        @pl.when((tile == 0) & (chunk == 2 + h))
        def _(h=h):
            send_x[h].wait_recv()
            xs[...] = x_in[h].T
            store_x[h].start()
            if h:
                send_g.wait_recv()
                gs[...] = g_in[...].T
                store_g.start()
            else:
                gs[...] = gr_ref[...].T

    gate = dot(xs[...], gate_w[...], 1, 0)
    up = dot(xs[...], up_w[...], 1, 0)
    grad = dot(gs[...], down_w[...], 1, 0)
    c_gelu = math.sqrt(2.0 / math.pi)
    square = gate * gate
    t = jnp.tanh(c_gelu * gate * (1.0 + 0.044715 * square))
    part = 0.5 * (1.0 + t)
    gelu = gate * part
    slope = part + 0.5 * gate * (1.0 - t * t) * (c_gelu * (1.0 + 3 * 0.044715 * square))
    hid = (gelu * up).astype(low)
    gg = (grad * up * slope).astype(low)
    gu = (grad * gelu).astype(low)
    hid_ref[...] = hid
    pair_ref[0] = gg
    pair_ref[1] = gu
    out_acc[...] += dot(down_w[...], hid, 1, 1)
    gx_acc[...] += dot(gate_w[...], gg, 1, 1) + dot(up_w[...], gu, 1, 1)

    last = tile == pl.num_programs(1) - 1
    for h in range(2):

        @pl.when(last & (chunk == h))
        def _(h=h):
            out_v[h] = (hres_ref[:, half[h]] + out_acc[...]).astype(low)
            store_out[h].start()
            gx_v[h] = gx_acc[...]
            store_gx[h].start()

        @pl.when(last & (chunk == 2 + h))
        def _(h=h):
            out_v[2 + h] = out_acc[...].astype(low)
            store_out_r[h].start()
            gx_out[h] = gx_acc[...].astype(low)
            store_late[h].start()

    @pl.when(last & (chunk == 3))
    def _():
        for each in (*send_x, send_g):
            each.wait_send()
        for each in store_x + store_out + store_out_r + store_gx + store_late + [store_g]:
            each.wait()


def ffn(x, g_own, g_oth, hres, g_late, gate_w, up_w, down_w):
    width, tokens = x.shape
    hidden = gate_w.shape[1]
    tile, size = 256, tokens // 2
    hbm = pl.BlockSpec(memory_space=pl.ANY)
    full = pl.BlockSpec((width, tokens), lambda s, j: (0, 0), pipeline_mode=pl.Buffered(1))
    weight = pl.BlockSpec((width, tile), lambda s, j: (0, j))
    first = pl.BlockSpec((width, size), lambda s, j: (0, 0), pipeline_mode=pl.Buffered(1))
    act_shape = jax.ShapeDtypeStruct((2 * tokens, hidden), low)
    tokens_of = lambda kind: jax.ShapeDtypeStruct((width, tokens), kind)
    return pl.pallas_call(
        ffn_kernel,
        grid=(4, hidden // tile),
        in_specs=[full, full, first, full, hbm, weight, weight, weight],
        out_specs=[
            pl.BlockSpec((size, tile), lambda s, j: (s, j)),
            pl.BlockSpec((2, size, tile), lambda s, j: (0, s, j)),
        ]
        + [hbm] * 6,
        out_shape=[act_shape, jax.ShapeDtypeStruct((2, 2 * tokens, hidden), low)]
        + [tokens_of(low), jax.ShapeDtypeStruct((width, size), low)]
        + [tokens_of(kind) for kind in (low, low, wide, low)],
        scratch_shapes=[
            pltpu.VMEM((size, width), low),
            pltpu.VMEM((size, width), low),
            pltpu.VMEM((width, size), wide),
            pltpu.VMEM((width, size), wide),
            pltpu.VMEM((2, width, size), low),
            pltpu.VMEM((width, size), low),
            pltpu.VMEM((2, width, size), low),
            pltpu.VMEM((4, width, size), low),
            pltpu.VMEM((2, width, size), wide),
            pltpu.SemaphoreType.DMA((6,)),
            pltpu.SemaphoreType.DMA((11,)),
        ],
        compiler_params=pltpu.CompilerParams(vmem_limit_bytes=56 << 20, collective_id=0, has_side_effects=True),
        cost_estimate=hint,
        name="ffn_both_ways",
    )(x, g_own, g_oth, hres, g_late, gate_w, up_w, down_w)


def weight_grad_kernel(core_ref, own_ref, oth_ref, right_ref, *refs):
    tokens = own_ref.shape[1]
    total = dot(own_ref[...], right_ref[:tokens, :], 1, 0) + dot(oth_ref[...], right_ref[tokens:, :], 1, 0)
    if len(refs) == 2:
        total = total + refs[0][...].astype(wide)
    refs[-1][...] = total.astype(low)


def weight_grad(own, oth, right, core, got=None):
    width, tokens = own.shape
    columns = right.shape[1] // 2
    blocks = 4
    rows = width // blocks
    left = pl.BlockSpec((rows, tokens), lambda i, core_ref: (i, 0))
    out = pl.BlockSpec((rows, columns), lambda i, core_ref: (i, 0))
    args = [own, oth, right] + ([] if got is None else [got])
    return pl.pallas_call(
        weight_grad_kernel,
        grid_spec=pltpu.PrefetchScalarGridSpec(
            num_scalar_prefetch=1,
            grid=(blocks,),
            in_specs=[
                left,
                left,
                pl.BlockSpec((2 * tokens, columns), lambda i, core_ref: (0, core_ref[0]), pipeline_mode=pl.Buffered(1)),
            ]
            + ([] if got is None else [out]),
            out_specs=out,
        ),
        out_shape=jax.ShapeDtypeStruct((width, columns), low),
        compiler_params=pltpu.CompilerParams(vmem_limit_bytes=40 << 20),
        cost_estimate=hint,
        name="weight_grad",
    )(core.reshape(1), *args)


def back_kernel(
    hid_h, pair_h, go_h, gr1_h, gr2_h, xo_h, xr_h, gx_h, hres_h, xin_h, probs_h, xn1_h, outp_h, outr_h, late_h,
    out_w, w_t, qkv, mixed, gain2, gain1, scale2, scale1,
    got_p, got_r, got_in, d_out, p_out, a_out, gin, small,
    r_core, xp, zd, zp, dx, px, bf, rx, ya, xa, za, ab, late_in, sm_src, sm_in, send_sems, recv_sems, load_sems,
):
    s = lax.axis_index("seq")
    y = lax.axis_index("tensor")
    z = lax.axis_index("dp")
    c = s % 2
    m = s // 2
    width = xp.shape[0]
    rows = d_out.shape[0]
    columns = xp.shape[1]
    half_len = rx.shape[1]
    length = 2 * half_len
    heads = probs_h.shape[0]
    dim = mixed.shape[0] // heads
    zs = width // rows
    mesh_id = dict(device_id_type=pl.DeviceIdType.MESH)
    to_core = {"seq": 2 * m + 1 - c}
    to_x = {"seq": 2 * (1 - m) + c}
    to_y = {"tensor": 1 - y}
    to_z = {"dp": (z + 1) % zs}
    to_swap = {"seq": 2 * m + y, "tensor": c}
    to_back = {"seq": 2 * m + 1 - y, "tensor": c}

    barrier = pltpu.get_barrier_semaphore()
    greet = [to_core, to_y, {"seq": 2 * m + 1 - c, "tensor": 1 - y}, to_x] + [{"dp": (z + i) % zs} for i in range(1, zs)]
    for who in greet:
        pl.semaphore_signal(barrier, inc=1, device_id=who, **mesh_id)
    pl.semaphore_wait(barrier, len(greet))

    def move(k, src, dst, who):
        return pltpu.make_async_remote_copy(
            src_ref=src, dst_ref=dst, send_sem=send_sems.at[k], recv_sem=recv_sems.at[k], device_id=who, **mesh_id
        )

    def load(k, src, dst):
        return pltpu.make_async_copy(src, dst, load_sems.at[k])

    def chunk(j):
        return pl.ds(pl.multiple_of(j * rows, rows), rows)

    def side(i, size):
        return pl.ds(pl.multiple_of(i * size, 128), size)

    order = [(z + zs - 1 - k) % zs for k in range(zs)]
    mine = side(c, columns)
    my_half = side(c, half_len)
    other_half = side(1 - c, half_len)
    cut = [(0, 192), (192, rows - 192)]

    def part(j, p):
        return pl.ds(pl.multiple_of(j * rows + cut[p][0], 16), cut[p][1])

    parts = [pl.ds(*each) for each in cut]

    late = move(0, late_h, late_in, to_y)
    swap_out = move(1, outp_h, got_p, to_swap)
    back_out = move(2, outr_h, got_r, to_back)
    z_down = [move(3, r_core.at[0, chunk(order[0])], zd.at[0], to_z), move(4, zd.at[0], zd.at[1], to_z)]
    z_down_last = [move(5 + p, zd.at[1, parts[p]], zd.at[2, parts[p]], to_z) for p in range(2)]
    x_down = [move(7 + p, zd.at[2, parts[p]], dx.at[parts[p]], to_x) for p in range(2)]
    core_down = [move(9 + p, d_out.at[parts[p], mine], d_out.at[parts[p], mine], to_core) for p in range(2)]
    z_pair = [move(11, r_core.at[2, chunk(order[0])], zp.at[0], to_z), move(12, zp.at[0], zp.at[1], to_z)]
    z_pair_last = [move(13 + p, zp.at[1, parts[p]], zp.at[2, parts[p]], to_z) for p in range(2)]
    x_pair_back = [move(15 + p, zp.at[2, parts[p]], px.at[parts[p]], to_x) for p in range(2)]
    core_pair = [move(17 + p, p_out.at[m, parts[p], mine], p_out.at[m, parts[p], mine], to_core) for p in range(2)]
    core_pair_back = [
        move(19 + p, p_out.at[1 - m, parts[p], mine], p_out.at[1 - m, parts[p], mine], to_core) for p in range(2)
    ]
    core_branch = move(21, bf.at[:, my_half], bf.at[:, my_half], to_core)
    a_cols = ya.shape[2]
    a_rows = xa.shape[1]
    my_cols = side(y, a_cols)
    my_rows = pl.ds(pl.multiple_of(m * a_rows, a_rows), a_rows)
    x_rows = pl.ds(pl.multiple_of((1 - m) * a_rows, a_rows), a_rows)
    x_attn = [move(22 + k, ya.at[j, x_rows], xa.at[j], to_x) for k, j in enumerate(order)]
    z_attn = [move(26, ya.at[order[0], my_rows], za.at[0], to_z)] + [
        move(26 + t, za.at[t - 1], za.at[t], to_z) for t in range(1, zs - 1)
    ]
    my_piece = ab.at[my_rows, my_cols]
    spread_attn = [
        move(29 + i, my_piece, my_piece, who)
        for i, who in enumerate((to_x, to_y, {"seq": 2 * (1 - m) + c, "tensor": 1 - y}))
    ]
    core_attn = move(32, ab, a_out, to_core)
    swap_in = move(33, gin, got_in, to_swap)

    def x_pair(k):
        at = chunk((z + zs - 1 - k) % zs)
        return move(44 + k, r_core.at[1, at], xp.at[at], to_x)

    late.start()

    def step_z_down(t):
        z_down[t - 1].wait_recv()
        zd[t - 1] = (zd[t - 1].astype(wide) + r_core[0, chunk(order[t]), :].astype(wide)).astype(low)
        for each in z_down_last if t == 2 else [z_down[t]]:
            each.start()

    def last_z_down(p):
        z_down_last[p].wait_recv()
        at = parts[p]
        zd[2, at, :] = (zd[2, at, :].astype(wide) + r_core[0, part(z, p), :].astype(wide)).astype(low)
        x_down[p].start()

    def end_down(p):
        x_down[p].wait_recv()
        at = parts[p]
        d_out[at, mine] = (zd[2, at, :].astype(wide) + dx[at, :].astype(wide)).astype(low)
        core_down[p].start()

    def step_z_pair(t):
        x_pair(t).wait_recv()
        term = r_core[2, chunk(order[t]), :].astype(wide) + xp[chunk(order[t]), :].astype(wide)
        if t:
            z_pair[t - 1].wait_recv()
            zp[t - 1] = (zp[t - 1].astype(wide) + term).astype(low)
        else:
            r_core[2, chunk(order[0]), :] = term.astype(low)
        for each in z_pair_last if t == 2 else [z_pair[t]]:
            each.start()

    def last_z_pair(p):
        if p == 0:
            x_pair(3).wait_recv()
        z_pair_last[p].wait_recv()
        at = parts[p]
        term = r_core[2, part(z, p), :].astype(wide) + xp[part(z, p), :].astype(wide)
        total = (zp[2, at, :].astype(wide) + term).astype(low)
        zp[2, at, :] = total
        x_pair_back[p].start()
        p_out[m, at, mine] = total
        core_pair[p].start()

    def end_pair(p):
        x_pair_back[p].wait_recv()
        at = parts[p]
        p_out[1 - m, at, mine] = px[at, :]
        core_pair_back[p].start()

    def step_attn(t):
        x_attn[t].wait_recv()
        term = ya[order[t], my_rows, :].astype(wide) + xa[order[t]].astype(wide)
        if t:
            z_attn[t - 1].wait_recv()
            za[t - 1] = (za[t - 1].astype(wide) + term).astype(low)
        else:
            x_attn[0].wait_send()
            ya[order[0], my_rows, :] = term.astype(low)
        if t < zs - 1:
            z_attn[t].start()

    hops = [to_core, to_y, to_x, {"dp": z + 1 - 2 * (z % 2)}, {"dp": (z + 2) % zs}]
    exchange = [move(39 + i, sm_src.at[i], sm_in.at[i], who) for i, who in enumerate(hops)]

    def start_sum(i):
        sm_src[i] = small[...]
        exchange[i].start()

    def end_sum(i):
        exchange[i].wait_recv()
        small[...] = sm_src[i] + sm_in[i]

    def weights(r_buf, l_go, l_gr, l_xo, l_xr, s_buf):
        loads = [
            load(0, pair_h.at[1 - m], r_buf.at[0]),
            load(1, xo_h, l_xo),
            load(2, xr_h, l_xr),
            load(3, hid_h, r_buf.at[1]),
            load(4, go_h, l_go),
            load(5, gr1_h, l_gr.at[:, pl.ds(0, half_len // 2)]),
            load(14, gr2_h, l_gr.at[:, pl.ds(half_len // 2, half_len // 2)]),
        ]
        load_own = load(6, pair_h.at[m], r_buf.at[0])
        for each in loads:
            each.start()
        theirs = side(1 - c, columns)

        def core(i, k):
            at = chunk((z + zs - 1 - k) % zs)
            return move(48 + i * zs + k, s_buf.at[i % 2, at], r_core.at[(1, 0, 2)[i], at], to_core)

        def product(left_o, left_r, right, col, i, extra=None):
            def block(k, carry):
                at = chunk((z + zs - 1 - k) % zs)
                total = dot(left_o[at, :], right[:half_len, col], 1, 0)
                total = total + dot(left_r[at, :], right[half_len:, col], 1, 0)
                if extra is None:
                    s_buf[i % 2, at, :] = total.astype(low)
                    core(i, k).start()
                else:
                    out = (1, 0, 2)[i]
                    core(i, k).wait_recv()
                    r_core[out, at, :] = (total + r_core[out, at, :].astype(wide)).astype(low)
                    extra(k)
                return carry

            lax.fori_loop(0, zs, block, 0)

        def at_first(run):
            def extra(k):
                pl.when(k == 0)(run)

            return extra

        def sent(i):
            def block(k, carry):
                core(i, k).wait_send()
                return carry

            lax.fori_loop(0, zs, block, 0)

        for each in loads[:3]:
            each.wait()
        product(l_xo, l_xr, r_buf.at[0], theirs, 0)
        product(l_xo, l_xr, r_buf.at[0], mine, 0, lambda k: x_pair(k).start())
        load_own.start()

        @pl.when(c != y)
        def _():
            swap_out.start()

        back_out.start()
        for each in loads[3:]:
            each.wait()
        product(l_go, l_gr, r_buf.at[1], theirs, 1)
        product(l_go, l_gr, r_buf.at[1], mine, 1, at_first(z_down[0].start))
        load_own.wait()
        sent(0)
        product(l_xo, l_xr, r_buf.at[0], theirs, 2)
        product(l_xo, l_xr, r_buf.at[0], mine, 2, at_first(lambda: step_z_pair(0)))
        sent(1)
        sent(2)

    hidden = hid_h.shape[1]
    left = pltpu.VMEM((width, half_len), low)
    pl.run_scoped(
        weights,
        pltpu.VMEM((2, length, hidden), low),
        left,
        left,
        left,
        left,
        pltpu.VMEM((2, width, columns), low),
    )

    def attention(gxv, hv, gov, p_buf, k_acc, v_acc, sums, gqkv, gm, xn1, sx, ga):
        loads = [load(7, gx_h, gxv), load(8, hres_h, hv), load(9, go_h, gov), load(10, xn1_h, xn1)]
        load_x = load(11, xin_h, gov)
        for each in loads:
            each.start()

        def probs_load(h, b, slot):
            return load(12 + slot, probs_h.at[h, :, side(b, q_block)], p_buf.at[slot])

        probs_load(0, 0, 0).start()
        lanes = half_len // 128
        piece = 64
        pieces = width // piece

        def fold(a):
            return sum(a[:, i * 128 : (i + 1) * 128] for i in range(lanes))

        def spread(a):
            return jnp.concatenate([a] * lanes, axis=1)

        def norm_backward(values, gain, scale, grad, store, row):
            def first(i, total):
                at = pl.ds(pl.multiple_of(i * piece, piece), piece)
                return total + jnp.sum(values(at) * (spread(gain[at, :]) * grad(at)), axis=0, keepdims=True)

            total = lax.fori_loop(0, pieces, first, jnp.zeros((1, half_len), wide))
            mean = total * scale[...] * (1.0 / width)

            def second(i, carry):
                at = pl.ds(pl.multiple_of(i * piece, piece), piece)
                g = grad(at)
                normed = values(at) * scale[...]
                store(at, scale[...] * (spread(gain[at, :]) * g - normed * mean))
                ga_part[at, :] = fold(g * normed)
                return carry

            lax.fori_loop(0, pieces, second, 0)
            small[row : row + 1, :] = jnp.sum(ga_part[...].T, axis=0, keepdims=True)

        ga_part = sums.at[:width, :128]
        small[...] = jnp.zeros_like(small)
        for each in loads[:3]:
            each.wait()
        late.wait_recv()

        def add_late(i, carry):
            at = pl.ds(pl.multiple_of(i * piece, piece), piece)
            gxv[at, :] += late_in[at, :].astype(wide)
            return carry

        lax.fori_loop(0, pieces, add_late, 0)

        def store_hres(at, back):
            total = gov[at, :].astype(wide) + back
            gxv[at, :] = total
            bf[at, my_half] = total.astype(low)

        norm_backward(lambda at: hv[at, :], gain2, scale2, lambda at: gxv[at, :], store_hres, 0)
        core_branch.start()
        load_x.start()
        step_z_down(1)
        core_branch.wait_recv()
        gm[...] = dot(out_w[...], bf[...], 1, 0).astype(low)

        reach = length - q_block
        blocks = length // q_block
        near_rows = q_block + 2 * band_half
        d = (
            lax.broadcasted_iota(jnp.int32, (near_rows, q_block), 0)
            - lax.broadcasted_iota(jnp.int32, (near_rows, q_block), 1)
            - band_half
        )
        for h in range(heads):
            head = pl.ds(h * dim, dim)
            k_rows = pl.ds((heads + h) * dim, dim)
            v_rows = pl.ds((2 * heads + h) * dim, dim)
            k_acc[...] = jnp.zeros_like(k_acc)
            v_acc[...] = jnp.zeros_like(v_acc)
            sums[...] = jnp.zeros_like(sums)

            def block(b, carry):
                slot = b % 2
                at = side(b, q_block)
                probs_load(h, b, slot).wait()

                @pl.when(b < blocks - 1)
                def _():
                    probs_load(h, b + 1, 1 - slot).start()

                if h < heads - 1:

                    @pl.when(b == blocks - 1)
                    def _():
                        probs_load(h + 1, 0, 1 - slot).start()

                probs = p_buf[slot]
                go = gm[head, at]
                inner = jnp.sum(go.astype(wide) * mixed[head, at].astype(wide), axis=0, keepdims=True)
                scores = probs.astype(wide) * (dot(qkv[v_rows, :], go, 0, 0) - inner)
                first = pl.multiple_of(reach - b * q_block, q_block)
                sums[pl.ds(first, length), :] += scores
                scores = scores.astype(low)
                gqkv[head, at] = dot(qkv[k_rows, :], scores, 1, 0).astype(low)
                k_acc[...] += dot(qkv[head, at], scores, 1, 1)
                v_acc[...] += dot(go, probs, 1, 1)
                return carry

            lax.fori_loop(0, blocks, block, 0)
            gqkv[k_rows, :] = k_acc[...].astype(low)
            gqkv[v_rows, :] = v_acc[...].astype(low)
            near = sums[reach - band_half : reach + q_block + band_half, :]
            n = jnp.abs(d)
            bucket = jnp.zeros((near_rows, q_block), jnp.int32)
            for step in steps_at:
                bucket = bucket + jnp.where(n >= step, 1, 0)
            bucket = bucket + jnp.where(d > 0, 16, 0)
            totals = []
            for b in range(32):
                total = jnp.sum(jnp.where(bucket == b, near, 0.0), axis=0, keepdims=True)
                if b == 15:
                    total = total + jnp.sum(sums[: reach - band_half, :], axis=0, keepdims=True)
                if b == 31:
                    total = total + jnp.sum(sums[reach + q_block + band_half :, :], axis=0, keepdims=True)
                totals.append(total)
            totals = jnp.concatenate(totals, axis=0)
            totals = jnp.concatenate([totals, jnp.zeros((96, q_block), wide)], axis=0)
            line = jnp.sum(totals.T, axis=0, keepdims=True)
            for side_c in range(2):
                row = 8 + side_c * heads + h
                small[row : row + 1, :128] = jnp.where(c == side_c, line, 0.0)
            if h == 1:
                step_z_pair(1)

        def input_grad(half, store):
            def block(i, carry):
                at = chunk(i)
                store(at, dot(w_t[at, :], gqkv[:, half], 1, 0))
                return carry

            lax.fori_loop(0, zs, block, 0)

        def store_sent(at, value):
            sx[at, :] = value.astype(low)

        input_grad(other_half, store_sent)
        core_x = move(34, sx, rx, to_core)
        core_x.start()
        loads[3].wait()
        y_attn = [
            move(35 + k, ga.at[j, :, side(1 - y, a_cols)], ya.at[j], to_y) for k, j in enumerate(order)
        ]
        wide_cols = gqkv.shape[0]
        for k, j in enumerate(order):
            ga[j, :rows, :wide_cols] = dot(xn1[chunk(j), :], gqkv[...], 1, 1).astype(low)
            ga[j, :rows, wide_cols:] = dot(bf[chunk(j), :], mixed[...], 1, 1).astype(low)
            ga[j, rows:, :] = jnp.zeros((ga.shape[1] - rows, ga.shape[2]), low)
            y_attn[k].start()
        step_z_down(2)

        def store_own(at, value):
            hv[at, :] = value

        input_grad(my_half, store_own)
        load_x.wait()
        core_x.wait_recv()

        def store_in(at, back):
            gin[at, :] = (gxv[at, :] + back).astype(low)

        norm_backward(
            lambda at: gov[at, :].astype(wide),
            gain1,
            scale1,
            lambda at: hv[at, :] + rx[at, :].astype(wide),
            store_in,
            1,
        )

        @pl.when(c != y)
        def _():
            swap_in.start()

        def step_y_attn(k):
            j = order[k]
            y_attn[k].wait_recv()
            ya[j] = (ya[j].astype(wide) + ga[j, :, my_cols].astype(wide)).astype(low)
            x_attn[k].start()

        step_y_attn(0)
        step_z_pair(2)
        start_sum(0)
        step_y_attn(1)
        step_attn(0)
        end_sum(0)
        start_sum(1)
        last_z_down(0)
        step_y_attn(2)
        last_z_down(1)
        step_y_attn(3)
        core_x.wait_send()
        for each in y_attn:
            each.wait_send()

    f32 = lambda *shape: pltpu.VMEM(shape, wide)
    b16 = lambda *shape: pltpu.VMEM(shape, low)
    pl.run_scoped(
        attention,
        f32(width, half_len),
        f32(width, half_len),
        b16(width, half_len),
        b16(2, length, q_block),
        f32(dim, length),
        f32(dim, length),
        f32(2 * length - q_block, q_block),
        b16(3 * heads * dim, length),
        b16(heads * dim, length),
        b16(width, length),
        b16(width, half_len),
        b16(zs, ya.shape[1], 2 * ya.shape[2]),
    )

    end_sum(1)
    start_sum(2)
    end_down(0)
    last_z_pair(0)
    end_down(1)
    last_z_pair(1)
    step_attn(1)
    end_sum(2)
    start_sum(3)
    step_attn(2)
    end_pair(0)
    step_attn(3)
    ab[my_rows, my_cols] = za[zs - 2]
    for each in spread_attn:
        each.start()
    end_sum(3)
    start_sum(4)
    end_pair(1)
    for each in spread_attn:
        each.wait_recv()

    @pl.when(c == y)
    def _():
        core_attn.start()
        a_out[...] = ab[...]
        core_attn.wait_send()

    end_sum(4)

    @pl.when(c != y)
    def _():
        core_attn.wait_recv()
        swap_out.wait()
        swap_in.wait()

    back_out.wait()
    for each in core_down + core_pair + core_pair_back:
        each.wait()
    for each in [late, core_branch] + z_down + z_down_last + x_down + z_pair + z_pair_last + x_pair_back:
        each.wait_send()
    for each in [x_pair(k) for k in range(zs)] + x_attn[1:] + z_attn + spread_attn + exchange:
        each.wait_send()


def back_all(
    hid, pair, g_own, g_oth, g_late, x_own, x_oth, gx, hres, x_in, probs, xn_one, out_first, out_oth, late,
    out_w, w_t, qkv, mixed, gain_two, gain_one, scale_two, scale_one, zs,
):
    width, half_len = g_own.shape
    length = 2 * half_len
    rows = width // zs
    columns = hid.shape[1] // 2
    heads = probs.shape[0]
    a_cols = (w_t.shape[1] + out_w.shape[0]) // 2
    a_len = -(-rows // 32) * 32
    hbm = pl.BlockSpec(memory_space=pl.ANY)
    vmem = pl.BlockSpec(memory_space=pltpu.VMEM)
    sds = lambda kind, *shape: jax.ShapeDtypeStruct(shape, kind)
    b16 = lambda *shape: pltpu.VMEM(shape, low)
    return pl.pallas_call(
        back_kernel,
        in_specs=[hbm] * 15 + [vmem] * 8,
        out_specs=[hbm] * 3 + [vmem] * 5,
        out_shape=[
            sds(low, width, half_len),
            sds(low, width, half_len),
            sds(low, width, half_len),
            sds(low, rows, 2 * columns),
            sds(low, 2, rows, 2 * columns),
            sds(low, a_len, 2 * a_cols),
            sds(low, width, half_len),
            sds(wide, 16, width),
        ],
        scratch_shapes=[
            b16(3, width, columns),
            b16(width, columns),
            b16(zs - 1, rows, columns),
            b16(zs - 1, rows, columns),
            b16(rows, columns),
            b16(rows, columns),
            b16(width, length),
            b16(width, half_len),
            b16(zs, a_len, a_cols),
            b16(zs, a_len // 2, a_cols),
            b16(zs - 1, a_len // 2, a_cols),
            b16(a_len, 2 * a_cols),
            b16(width, half_len),
            pltpu.VMEM((5, 16, width), wide),
            pltpu.VMEM((5, 16, width), wide),
            pltpu.SemaphoreType.DMA((60,)),
            pltpu.SemaphoreType.DMA((60,)),
            pltpu.SemaphoreType.DMA((15,)),
        ],
        compiler_params=pltpu.CompilerParams(vmem_limit_bytes=61 << 20, collective_id=1, has_side_effects=True),
        cost_estimate=hint,
        name="back_all",
    )(
        hid, pair, g_own, g_oth, g_late, x_own, x_oth, gx, hres, x_in, probs, xn_one, out_first, out_oth, late,
        out_w, w_t, qkv, mixed, gain_two, gain_one, scale_two, scale_one,
    )


def finish_kernel(
    d_h, p_h, a_h, own_in, got_in, own_out, got_out, oth_out, small,
    d_out, g_out, u_out, q_out, k_out, v_out, o_out, in_out, y_out, gain1_out, gain2_out, bias_out,
    w_in, w_out, a_in, i_in, i_out, y_in, sems,
):
    own = lax.axis_index("seq") % 2 == lax.axis_index("tensor")
    rows = w_in.shape[1]
    width = i_in.shape[0]
    copy = lambda k, src, dst: pltpu.make_async_copy(src, dst, sems.at[k])
    loads = [copy(0, d_h, w_in.at[0]), copy(1, p_h.at[0], w_in.at[1]), copy(2, p_h.at[1], w_in.at[2]), copy(3, a_h, a_in)]
    load_y = copy(4, oth_out, y_in.at[1])
    mine = [copy(5, own_in, i_in), copy(6, own_out, y_in.at[0])]
    theirs = [copy(5, got_in, i_in), copy(6, got_out, y_in.at[0])]
    stores = [copy(7 + i, w_out.at[i], out) for i, out in enumerate((d_out, g_out, u_out))]
    store_i = copy(10, i_out, in_out)
    store_y = copy(11, y_in.at[0], y_out)

    def start(which):
        @pl.when(own)
        def _():
            mine[which].start()

        @pl.when(jnp.logical_not(own))
        def _():
            theirs[which].start()

    loads[0].start()
    start(0)
    for each in loads[1:3]:
        each.start()
    start(1)
    load_y.start()
    loads[3].start()

    def piecewise(count, size, run):
        def step(i, carry):
            run(pl.ds(pl.multiple_of(i * size, size), size))
            return carry

        lax.fori_loop(0, count, step, 0)

    def widen(i):
        loads[i].wait()

        def run(at):
            w_out[i, at, :] = w_in[i, at, :].astype(wide)

        piecewise(rows // 16, 16, run)
        stores[i].start()

    widen(0)
    mine[0].wait()

    def run_in(at):
        i_out[at, :] = i_in[at, :].astype(wide)

    piecewise(width // 64, 64, run_in)
    store_i.start()
    widen(1)
    widen(2)
    mine[1].wait()
    load_y.wait()

    def run_y(at):
        y_in[0, at, :] = (y_in[0, at, :].astype(wide) + y_in[1, at, :].astype(wide)).astype(low)

    piecewise(width // 64, 64, run_y)
    store_y.start()
    loads[3].wait()
    inner = q_out.shape[0]
    for i, out in enumerate((q_out, k_out, v_out, o_out)):
        out[...] = a_in[:rows, i * inner : (i + 1) * inner].astype(wide).T
    gain1_out[...] = small[1, :]
    gain2_out[...] = small[0, :]
    bias_out[...] = small[8 : 8 + bias_out.shape[0], : bias_out.shape[1]]
    for each in stores + [store_i, store_y]:
        each.wait()


def finish(d, p, a, own_in, got_in, own_out, got_out, oth_out, small, inner, bias_shape):
    rows, hidden = d.shape
    width, half_len = own_in.shape
    hbm = pl.BlockSpec(memory_space=pl.ANY)
    vmem = pl.BlockSpec(memory_space=pltpu.VMEM)
    sds = lambda kind, *shape: jax.ShapeDtypeStruct(shape, kind)
    return pl.pallas_call(
        finish_kernel,
        in_specs=[hbm] * 8 + [vmem],
        out_specs=[hbm] * 3 + [vmem] * 4 + [hbm] * 2 + [vmem] * 3,
        out_shape=[sds(wide, rows, hidden)] * 3
        + [sds(wide, inner, rows)] * 4
        + [sds(wide, width, half_len), sds(low, width, half_len)]
        + [sds(wide, width)] * 2
        + [sds(wide, *bias_shape)],
        scratch_shapes=[
            pltpu.VMEM((3, rows, hidden), low),
            pltpu.VMEM((3, rows, hidden), wide),
            pltpu.VMEM(a.shape, low),
            pltpu.VMEM((width, half_len), low),
            pltpu.VMEM((width, half_len), wide),
            pltpu.VMEM((2, width, half_len), low),
            pltpu.SemaphoreType.DMA((12,)),
        ],
        compiler_params=pltpu.CompilerParams(vmem_limit_bytes=60 << 20),
        cost_estimate=hint,
        name="finish_all",
    )(d, p, a, own_in, got_in, own_out, got_out, oth_out, small)


def norm_back(values, scale, gain, grad):
    normed = values * scale
    pushed = gain * grad
    mean = jnp.mean(normed * pushed, axis=0, keepdims=True)
    return scale * (pushed - normed * mean), jnp.sum(grad * normed, axis=1)


class Moves:
    def __init__(self, mesh):
        self.nz = mesh.shape["dp"]
        self.nx = mesh.shape["seq"] // 2
        both = [(m, c, y) for m in range(self.nx) for c in range(2) for y in range(2)]
        at = lambda m, c, y: (m * 2 + c) * 2 + y
        self.swap_pairs = [(at(m, c, y), at(m, y, c)) for m, c, y in both if c != y]
        self.second_pairs = [(at(m, c, y), at(m, y, 1 - c)) for m, c, y in both]
        self.back_pairs = [(b, a) for a, b in self.second_pairs]
        self.ring_x = [(m * 2 + c, (m + 1) % self.nx * 2 + c) for m in range(self.nx) for c in range(2)]
        self.y = lax.axis_index("tensor")
        self.z = lax.axis_index("dp")
        s = lax.axis_index("seq")
        self.c = s % 2
        self.m = s // 2

    def swap(self, a):
        got = lax.ppermute(a, ("seq", "tensor"), self.swap_pairs)
        return jnp.where(self.c == self.y, a, got)

    def back(self, a):
        return lax.ppermute(a, ("seq", "tensor"), self.back_pairs)

    def core(self, a):
        return lax.ppermute(a, "seq", [(s, s ^ 1) for s in range(2 * self.nx)])

    def over_y(self, a):
        return lax.ppermute(a, "tensor", [(0, 1), (1, 0)])

    def over_x(self, a):
        return lax.ppermute(a, "seq", self.ring_x)

    def start_x(self, a):
        take = lax.dynamic_index_in_dim(a, (self.m + self.nx - 1) % self.nx, 1, False)
        return a, self.over_x(take)

    def finish_x(self, a, got, *first):
        take = lambda i: lax.dynamic_index_in_dim(a, i % self.nx, 1, False)
        got = after(got, *first)
        held = (got.astype(wide) + take(self.m + 2 * self.nx - 2).astype(wide)).astype(low)
        for t in range(2, self.nx):
            held = (self.over_x(held).astype(wide) + take(self.m + 2 * self.nx - 1 - t).astype(wide)).astype(low)
        return held

    def scatter_x(self, a):
        take = lambda i: lax.dynamic_index_in_dim(a, i % self.nx, 1, False)
        held = take(self.m + self.nx - 1)
        for t in range(1, self.nx):
            held = (self.over_x(held).astype(wide) + take(self.m + 2 * self.nx - 1 - t).astype(wide)).astype(low)
        return held

    def scatter_z(self, a):
        return lax.psum_scatter(a, "dp", scatter_dimension=0, tiled=True)

    def gather_x(self, piece):
        if self.nx == 2:
            over = self.over_x(piece)
            return jnp.where(
                self.m == 0, jnp.concatenate([piece, over], 0), jnp.concatenate([over, piece], 0)
            )
        groups = [[m * 2 + c for m in range(self.nx)] for c in range(2)]
        return lax.all_gather(piece, "seq", axis=0, tiled=True, axis_index_groups=groups)

    def gather_core(self, piece):
        there = self.core(piece)
        return jnp.where(
            self.c == 0, jnp.concatenate([piece, there], 1), jnp.concatenate([there, piece], 1)
        )

    def sum_everywhere(self, a):
        a = a + self.core(a)
        a = a + self.over_y(a)
        step = 1
        while step < self.nx:
            a = a + lax.ppermute(a, "seq", [(s, s ^ (2 * step)) for s in range(2 * self.nx)])
            step *= 2
        step = 1
        while step < self.nz:
            a = a + lax.ppermute(a, "dp", [(z, z ^ step) for z in range(self.nz)])
            step *= 2
        return a


def local(
    mesh,
    layer_in,
    out_grad,
    doc_lengths,
    valid_length,
    gain_attn,
    query_weight,
    key_weight,
    value_weight,
    position_bias,
    output_weight,
    gain_ffn,
    gate_weight,
    up_weight,
    down_weight,
):
    moves = Moves(mesh)
    half_len, _, width = layer_in.shape
    length = 2 * half_len
    heads = position_bias.shape[1]
    inner_width = query_weight.shape[1]
    y, c, m = moves.y, moves.c, moves.m

    flat = lambda a: a.reshape(half_len, width).T
    (
        x_in, g_own, g_oth, g_send, out_w, w_t, xn_one, qkv, mixed, probs, hres, xn_own, scale_one, scale_two, gain_one, gain_two
    ) = front(
        flat(layer_in),
        flat(out_grad),
        (query_weight.T, key_weight.T, value_weight.T, output_weight),
        doc_lengths,
        valid_length,
        position_bias.T,
        gain_attn,
        gain_ffn,
        moves.nx == 2,
    )
    hid, pair, xn_oth, g_late, out_first, out_oth, gx, late = ffn(
        xn_own, g_own, g_oth, hres, g_send, gate_weight, up_weight, down_weight.T
    )
    if moves.nx == 2 and moves.nz == 4:
        got_first, got_oth, got_in, sum_d, sum_p, sums, grad_in, small = back_all(
            hid, pair, g_own, g_oth, g_late, xn_own, xn_oth, gx, hres, x_in, probs, xn_one, out_first, out_oth, late,
            out_w, w_t, qkv, mixed, gain_two, gain_one, scale_two, scale_one, moves.nz,
        )
        sum_d, sum_g, sum_u, sum_q, sum_k, sum_v, sum_o, grad_in, out_y, gain_one_sum, gain_two_sum, bias_sum = finish(
            sum_d, sum_p, sums, grad_in, got_in, out_first, got_first, got_oth, small,
            inner_width, (2 * heads, position_bias.shape[0]),
        )
        return (
            out_y.T.reshape(half_len, 1, width),
            grad_in.T.reshape(half_len, 1, width),
            gain_one_sum,
            sum_q.T,
            sum_k.T,
            sum_v.T,
            bias_sum.T,
            sum_o,
            gain_two_sum,
            sum_g,
            sum_u,
            sum_d.T,
        )
    grad_gate, grad_up = pair[0], pair[1]
    gx = gx + moves.over_y(late).astype(wide)
    g_oth = jnp.concatenate([g_oth, g_late], axis=1)
    qkv_w = w_t.T
    x_wide = x_in.astype(wide)
    gain_one, gain_two = gain_one[:, :1], gain_two[:, :1]

    def both_halves(own):
        other = moves.core(own)
        return jnp.where(
            c == 0, jnp.concatenate([own, other], 1), jnp.concatenate([other, own], 1)
        )

    def my_half(a):
        return lax.dynamic_slice_in_dim(a, c * half_len, half_len, 1)

    def other_half(a):
        return lax.dynamic_slice_in_dim(a, (1 - c) * half_len, half_len, 1)


    columns = hid.shape[1] // 2
    send_d = weight_grad(g_own, g_oth, hid, 1 - c)
    got_d = moves.core(send_d)
    send_g = weight_grad(xn_own, xn_oth, after(grad_gate, send_d), 1 - c)
    got_g = moves.core(send_g)
    send_u = weight_grad(xn_own, xn_oth, after(grad_up, send_g), 1 - c)
    got_u = moves.core(send_u)
    total_d = weight_grad(g_own, g_oth, after(hid, send_u), c, got_d)
    total_g = weight_grad(xn_own, xn_oth, after(grad_gate, total_d), c, got_g)
    total_u = weight_grad(xn_own, xn_oth, after(grad_up, total_g), c, got_u)
    part_d = moves.scatter_z(total_d)
    x_sent = [moves.start_x(t.reshape(moves.nz, moves.nx, -1, columns)) for t in (total_g, total_u)]

    gx = after(gx, total_u)
    out_y = moves.swap(out_first).astype(wide) + moves.back(out_oth).astype(wide)

    back, grad_gain_two = norm_back(hres, scale_two, gain_two, gx)
    grad_hres = g_own.astype(wide) + back
    branch = both_halves(grad_hres.astype(low))

    grad_mixed = dot(out_w, branch, 1, 0).astype(low)
    grad_qkv, grad_bias = attn_backward(qkv, grad_mixed, mixed, probs)

    part_g = moves.finish_x(*x_sent[0], grad_qkv).reshape(-1, columns)
    sent = dot(qkv_w, other_half(after(grad_qkv, part_g)), 0, 0).astype(low)
    part_g = moves.scatter_z(part_g)
    got_x = moves.core(sent)
    grad_attn_w = jnp.concatenate(
        [dot(xn_one, after(grad_qkv, sent), 1, 1).astype(low), dot(branch, mixed, 1, 1).astype(low)], axis=1
    )
    gx = dot(qkv_w, my_half(after(grad_qkv, grad_attn_w)), 0, 0) + got_x.astype(wide)
    back, grad_gain_one = norm_back(x_wide, scale_one, gain_one, gx)
    grad_in = (grad_hres + back).astype(low)
    part_u = moves.scatter_z(moves.finish_x(*x_sent[1], grad_in).reshape(-1, columns))

    a_columns = grad_attn_w.shape[1] // 2
    chunks = grad_attn_w.reshape(moves.nz, moves.nx, -1, 2 * a_columns)

    def scatter_y(a):
        got = moves.over_y(lax.dynamic_slice_in_dim(a, (1 - y) * a_columns, a_columns, a.ndim - 1))
        kept = lax.dynamic_slice_in_dim(a, y * a_columns, a_columns, a.ndim - 1)
        return (kept.astype(wide) + got.astype(wide)).astype(low)

    half_z = moves.nz // 2
    part = jnp.concatenate(
        [moves.scatter_x(scatter_y(chunks[:half_z])), scatter_y(moves.scatter_x(chunks[half_z:]))], 0
    )
    piece = moves.gather_x(moves.scatter_z(part.reshape(-1, a_columns)))
    there = moves.over_y(piece)
    group = jnp.where(y == 0, jnp.concatenate([piece, there], 1), jnp.concatenate([there, piece], 1))
    sums = jnp.where(c == y, group, moves.core(group)).astype(wide)
    sum_q, sum_k, sum_v, sum_o = (
        sums[:, i * inner_width : (i + 1) * inner_width] for i in range(4)
    )
    grad_in = moves.swap(grad_in).astype(wide)

    if moves.nx == 2:
        part_d = (part_d.astype(wide) + moves.over_x(part_d).astype(wide)).astype(low)
    else:
        part_d = moves.gather_x(moves.scatter_x(part_d.reshape(1, moves.nx, -1, columns))[0])
    sum_d = moves.gather_core(part_d).astype(wide)
    sum_g = moves.gather_core(moves.gather_x(part_g)).astype(wide)
    sum_u = moves.gather_core(moves.gather_x(part_u)).astype(wide)

    bias_full = jnp.zeros((grad_bias.shape[0], 2 * heads), wide)
    bias_full = lax.dynamic_update_slice(bias_full, grad_bias, (jnp.int32(0), c * heads))
    early = moves.sum_everywhere(jnp.concatenate([grad_gain_two, bias_full.reshape(-1)]))
    gain_two_sum, bias_sum = early[:width], early[width:].reshape(bias_full.shape)
    gain_one_sum = moves.sum_everywhere(grad_gain_one)
    return (
        out_y.astype(low).T.reshape(half_len, 1, width),
        grad_in.T.reshape(half_len, 1, width),
        gain_one_sum,
        sum_q,
        sum_k,
        sum_v,
        bias_sum,
        sum_o.T,
        gain_two_sum,
        sum_g,
        sum_u,
        sum_d.T,
    )


def solution(mesh):
    rows = P("tensor", ("dp", "seq"), None)
    columns = P(None, "tensor")
    return jax.shard_map(
        functools.partial(local, mesh),
        mesh=mesh,
        in_specs=(
            rows,
            rows,
            P(("dp", "seq"), None),
            P(("dp", "seq")),
            P(),
            columns,
            columns,
            columns,
            columns,
            P("tensor", None),
            P(),
            columns,
            columns,
            P("tensor", None),
        ),
        out_specs=(
            rows,
            rows,
            P(),
            P("dp", "tensor"),
            P("dp", "tensor"),
            P("dp", "tensor"),
            P(),
            P("tensor", "dp"),
            P(),
            P("dp", "tensor"),
            P("dp", "tensor"),
            P("tensor", "dp"),
        ),
        check_vma=False,
    )
```

```python
import functools
import math

import jax
import jax.numpy as jnp
from jax import lax
from jax.experimental import pallas as pl
from jax.experimental.pallas import tpu as pltpu
from jax.sharding import PartitionSpec as P

steps_at = (1, 2, 3, 4, 5, 6, 7, 8, 12, 16, 23, 32, 46, 64, 91)
eps_norm = 1e-06
masked_score = -1e30
q_block = 256
band_half = 128
low = jnp.bfloat16
wide = jnp.float32
hint = pl.CostEstimate(flops=1000, bytes_accessed=1000, transcendentals=0)


def dot(a, b, ca, cb):
    return lax.dot_general(a, b, (((ca,), (cb,)), ((), ())), preferred_element_type=wide)


def after(value, *first):
    return lax.optimization_barrier((value, *first))[0]


def front_kernel(
    share, x_h, g_h, wq_h, wk_h, wv_h, wo_h, lengths, valid, bias, gain1_row, gain2_row,
    x_out, g_own, g_oth, g_late, wo_out, w_t_out, xn1_out, qkv_out, mixed_out, probs_h, hres_out, xn2,
    scale1, scale2, gain1, gain2,
    x_in, g_in, w, w_t, xn1, qkv, mixed, hres,
    facts_src, facts, p_buf, table, sx, rx, seg_k, seg_q, send_sems, recv_sems, load_sems,
):
    s = lax.axis_index("seq")
    y = lax.axis_index("tensor")
    c = s % 2
    m = s // 2
    width, half_len = x_in.shape
    length = 2 * half_len
    heads, buckets = bias.shape
    inner = mixed.shape[0]
    dim = inner // heads
    piece = 64
    pieces = width // piece
    mesh_id = dict(device_id_type=pl.DeviceIdType.MESH)
    to_core = {"seq": 2 * m + 1 - c}
    to_swap = {"seq": 2 * m + 1 - c, "tensor": 1 - y}

    def side(i, size):
        return pl.ds(pl.multiple_of(i * size, 128), size)

    my_half = side(c, half_len)
    other_half = side(1 - c, half_len)

    def move(k, src, dst, who):
        return pltpu.make_async_remote_copy(
            src_ref=src, dst_ref=dst, send_sem=send_sems.at[k], recv_sem=recv_sems.at[k], device_id=who, **mesh_id
        )

    to_second = {"seq": 2 * m + y, "tensor": 1 - c}

    named = [(x_h, x_in)] + [
        (src, w.at[pl.ds(i * inner, inner)]) for i, src in enumerate((wq_h, wk_h, wv_h, wo_h))
    ]
    half_cols = half_len // 2
    halves = [pl.ds(h * half_cols, half_cols) for h in range(2)]
    move_x = [move((1, 15)[h], x_h.at[:, halves[h]], x_in.at[:, halves[h]], to_swap) for h in range(2)]
    moves = []
    z = lax.axis_index("dp")
    rows = inner // 2

    def half_of(ref, i, k):
        return ref.at[pl.ds(pl.multiple_of(i * inner + k * rows, rows), rows)]

    fetched, passed_z, passed_x = [], [], []
    for i, src in enumerate((wq_h, wk_h, wv_h, wo_h)):
        if share:
            fetched.append(move(2, half_of(src, 0, m), half_of(w, i, m), to_swap))
            part = half_of(w, (z + 4 - i) % 4, m)
            passed_x.append(move(10 + i, part, part, {"seq": 2 * (1 - m) + c}))
            if i < 3:
                passed_z.append(move(3 + i if i else 14, part, part, {"dp": (z + 1) % 4}))
        else:
            moves.append(move(2 + i, src, w.at[pl.ds(i * inner, inner)], to_swap))
    loads = [pltpu.make_async_copy(src, dst, load_sems.at[1 + i]) for i, (src, dst) in enumerate(named)]
    move_facts = move(0, facts_src, facts, to_swap)
    move_g = move(6, g_in, g_own, to_swap)
    early = g_oth.shape[1]
    second_g = move(9, g_in.at[:, pl.ds(0, early)], g_oth, to_second)
    to = lambda k, src, dst: pltpu.make_async_copy(src, dst, load_sems.at[k])
    keep_late = to(16, g_in.at[:, pl.ds(early, half_len - early)], g_late)
    load_g = pltpu.make_async_copy(g_h, g_in, load_sems.at[0])
    keep_g = pltpu.make_async_copy(g_in, g_own, load_sems.at[6])
    stores = [
        pltpu.make_async_copy(src, dst, load_sems.at[9 + i])
        for i, (src, dst) in enumerate(
            ((x_in, x_out), (w.at[pl.ds(3 * inner, inner)], wo_out), (w_t, w_t_out), (xn1, xn1_out), (qkv, qkv_out),
             (mixed, mixed_out), (hres, hres_out))
        )
    ]

    def pass_on(i):
        if not share:
            return

        @pl.when(c != y)
        def _():
            if i:
                passed_z[i - 1].wait_recv()
            else:
                fetched[0].wait_recv()
            if i < 3:
                passed_z[i].start()
            passed_x[i].start()

    my_parts = [pl.ds(pl.multiple_of(c * half_len + h * half_cols, 128), half_cols) for h in range(2)]
    core_one = [move((7, 16)[h], xn1.at[:, my_parts[h]], xn1.at[:, my_parts[h]], to_core) for h in range(2)]
    core_two = move(8, sx, rx, to_core)

    load_g.start()
    for h in range(heads):
        for b in range(buckets):
            at = h * buckets + b
            facts_src[at : at + 1, :] = jnp.full((1, 128), bias[h, b], wide)
    end = jnp.int32(0)
    at = heads * buckets
    for i in range(4):
        end = end + lengths[0, i]
        facts_src[at + i : at + i + 1, :] = jnp.full((1, 128), end.astype(wide), wide)
    facts_src[at + 4 : at + 5, :] = jnp.full((1, 128), valid[0].astype(wide), wide)

    barrier = pltpu.get_barrier_semaphore()
    greet = [to_core, to_swap, {"tensor": 1 - y}]
    if share:
        greet += [{"seq": 2 * (1 - m) + c}, {"dp": (z + 1) % 4}, {"dp": (z + 3) % 4}]
    for who in greet:
        pl.semaphore_signal(barrier, inc=1, device_id=who, **mesh_id)
    pl.semaphore_wait(barrier, len(greet))

    @pl.when(c != y)
    def _():
        move_facts.start()
        for i, each in enumerate(fetched):
            pl.when(z == i)(each.start)
        for each in move_x + moves:
            each.start()

    @pl.when(c == y)
    def _():
        for each in loads:
            each.start()
        facts[...] = facts_src[...]

    load_g.wait()
    live = lax.broadcasted_iota(jnp.int32, (piece, half_len), 1) + y * half_len < valid[0]

    def mask(i, carry):
        at = pl.ds(pl.multiple_of(i * piece, piece), piece)
        g_in[at, :] = jnp.where(live, g_in[at, :].astype(wide), 0.0).astype(low)
        return carry

    lax.fori_loop(0, pieces, mask, 0)

    @pl.when(c != y)
    def _():
        move_g.start()

    @pl.when(c == y)
    def _():
        keep_g.start()

    second_g.start()
    keep_late.start()
    pass_on(0)
    gain1[...] = jnp.broadcast_to(gain1_row[...].astype(wide)[None, :], (128, width)).T
    gain2[...] = jnp.broadcast_to(gain2_row[...].astype(wide)[None, :], (128, width)).T

    pass_on(1)

    @pl.when(c != y)
    def _():
        move_facts.wait_recv()

    at = heads * buckets

    def segments(positions):
        count = jnp.zeros(positions.shape, wide)
        for i in range(4):
            count = count + jnp.where(positions >= facts[at + i : at + i + 1, :], 1.0, 0.0)
        return jnp.where(positions < facts[at + 4 : at + 5, :], count, 4.0)

    seg_k[...] = segments(lax.broadcasted_iota(jnp.int32, (length, 128), 0).astype(wide))
    for i in range(length // 128):
        positions = (lax.broadcasted_iota(jnp.int32, (8, 128), 1) + i * 128).astype(wide)
        seg_q[:, i * 128 : (i + 1) * 128] = segments(positions)
    pass_on(2)
    reach = length - q_block
    near_rows = q_block + 2 * band_half
    d = (
        lax.broadcasted_iota(jnp.int32, (near_rows, 128), 0)
        - lax.broadcasted_iota(jnp.int32, (near_rows, 128), 1)
        - band_half
    )
    far_rows = reach - band_half
    for h in range(heads):

        def value(b, h=h):
            return facts[h * buckets + b : h * buckets + b + 1, :]

        for i in range(q_block // 128):
            offset = d - i * 128
            n = jnp.abs(offset)
            before = jnp.broadcast_to(value(0), n.shape)
            later = jnp.broadcast_to(value(16), n.shape)
            for number, step in enumerate(steps_at):
                reached = n >= step
                before = jnp.where(reached, value(number + 1), before)
                later = jnp.where(reached, value(number + 17), later)
            col = pl.ds(i * 128, 128)
            table[h, pl.ds(far_rows, near_rows), col] = jnp.where(offset > 0, later, before)
            table[h, pl.ds(0, far_rows), col] = jnp.broadcast_to(value(15), (far_rows, 128))
            table[h, pl.ds(far_rows + near_rows, far_rows), col] = jnp.broadcast_to(value(31), (far_rows, 128))

    def norm(read, gain, scale, cols, write):
        size = cols.size

        def first(i, total):
            v = read(pl.ds(pl.multiple_of(i * piece, piece), piece))
            return total + jnp.sum(v * v, axis=0, keepdims=True)

        total = lax.fori_loop(0, pieces, first, jnp.zeros((1, size), wide))
        scale[:, cols] = lax.rsqrt(total * (1.0 / width) + eps_norm)

        def second(i, carry):
            at = pl.ds(pl.multiple_of(i * piece, piece), piece)
            spread = jnp.concatenate([gain[at, :]] * (size // 128), axis=1)
            write(at, (read(at) * scale[:, cols] * spread).astype(low))
            return carry

        lax.fori_loop(0, pieces, second, 0)

    def arrived(i):
        @pl.when(c != y)
        def _():
            if not share:
                moves[i - 1].wait_recv()

        @pl.when(c == y)
        def _():
            loads[i].wait()

    pass_on(3)
    for h in range(2):

        @pl.when(c != y)
        def _(h=h):
            move_x[h].wait_recv()

        if h == 0:

            @pl.when(c == y)
            def _():
                loads[0].wait()

        def write_one(at, value, h=h):
            xn1[at, my_parts[h]] = value

        norm(lambda at, h=h: x_in[at, halves[h]].astype(wide), gain1, scale1, halves[h], write_one)
        core_one[h].start()
    stores[0].start()
    if share:

        @pl.when(c != y)
        def _():
            for each in passed_x:
                each.wait_recv()

    for each in core_one:
        each.wait_recv()
    stores[3].start()
    for i in range(3):
        arrived(1 + i)
        qkv[i * inner : (i + 1) * inner, :] = dot(w[i * inner : (i + 1) * inner, :], xn1[...], 1, 0).astype(low)

    stores[4].start()

    blocks = length // q_block

    turns = heads * blocks // 2

    def turn(i):
        its = 1 - c + (i // turns) * (2 * c - 1)
        return i % heads, its * (blocks // 2) + (i % turns) // heads

    def store(i):
        h, b = turn(i)
        return pltpu.make_async_copy(p_buf.at[i % 2], probs_h.at[h, :, side(b, q_block)], load_sems.at[7 + i % 2])

    def block(i, carry):
        h, b = turn(i)
        at = side(b, q_block)
        rows = lambda part: pl.ds(pl.multiple_of((part * heads + h) * dim, dim), dim)
        first = pl.multiple_of(reach - b * q_block, q_block)
        scores = dot(qkv[rows(1), :], qkv[rows(0), at], 0, 0) + table[h, pl.ds(first, length), :]
        keys = jnp.concatenate([seg_k[...]] * (q_block // 128), axis=1)
        scores = jnp.where(keys == seg_q[0:1, at], scores, masked_score)
        raised = jnp.exp(scores - jnp.max(scores, axis=0, keepdims=True))
        probs = (raised * (1.0 / jnp.sum(raised, axis=0, keepdims=True))).astype(low)

        @pl.when(i >= 2)
        def _():
            store(i - 2).wait()

        p_buf[i % 2] = probs
        store(i).start()
        mixed[rows(0), at] = dot(qkv[rows(2), :], probs, 1, 0).astype(low)
        return carry

    lax.fori_loop(0, turns, block, 0)
    arrived(4)
    stores[1].start()
    out_w = w[3 * inner :, :]
    sx[...] = dot(out_w, mixed[:, other_half], 0, 0).astype(low)
    core_two.start()
    w_t[...] = w[: 3 * inner, :].T
    stores[2].start()
    lax.fori_loop(turns, 2 * turns, block, 0)
    stores[5].start()
    hres[...] = dot(out_w, mixed[:, my_half], 0, 0)
    core_two.wait_recv()

    def add(i, carry):
        at = pl.ds(pl.multiple_of(i * piece, piece), piece)
        hres[at, :] += x_in[at, :].astype(wide) + rx[at, :].astype(wide)
        return carry

    lax.fori_loop(0, pieces, add, 0)

    stores[6].start()

    def write_two(at, value):
        xn2[at, :] = value

    norm(lambda at: hres[at, :], gain2, scale2, pl.ds(0, half_len), write_two)
    last = heads * blocks
    store(last - 2).wait()
    store(last - 1).wait()
    for each in (*core_one, core_two):
        each.wait_send()

    @pl.when(c != y)
    def _():
        move_facts.wait_send()
        if share:
            fetched[0].wait_send()
        for each in move_x + moves + passed_z + passed_x:
            each.wait_send()
        move_g.wait()

    @pl.when(c == y)
    def _():
        keep_g.wait()

    second_g.wait()
    keep_late.wait()
    for each in stores:
        each.wait()


def front(x, g, weights, lengths, valid, bias, gain_one, gain_two, share):
    width, half_len = x.shape
    length = 2 * half_len
    heads = bias.shape[0]
    inner = weights[0].shape[0]
    hbm = pl.BlockSpec(memory_space=pl.ANY)
    vmem = pl.BlockSpec(memory_space=pltpu.VMEM)
    smem = pl.BlockSpec(memory_space=pltpu.SMEM)
    sds = lambda kind, *shape: jax.ShapeDtypeStruct(shape, kind)
    facts = pltpu.VMEM((heads * bias.shape[1] + 8, 128), wide)
    b16 = lambda *shape: pltpu.VMEM(shape, low)
    return pl.pallas_call(
        functools.partial(front_kernel, share),
        in_specs=[hbm] * 6 + [smem] * 3 + [vmem] * 2,
        out_specs=[hbm] * 11 + [vmem] * 5,
        out_shape=[
            sds(low, width, half_len),
            sds(low, width, half_len),
            sds(low, width, half_len - 128),
            sds(low, width, 128),
            sds(low, inner, width),
            sds(low, width, 3 * inner),
            sds(low, width, length),
            sds(low, 3 * inner, length),
            sds(low, inner, length),
            sds(low, heads, length, length),
            sds(wide, width, half_len),
            sds(low, width, half_len),
            sds(wide, 1, half_len),
            sds(wide, 1, half_len),
            sds(wide, width, 128),
            sds(wide, width, 128),
        ],
        scratch_shapes=[
            b16(width, half_len),
            b16(width, half_len),
            b16(4 * inner, width),
            b16(width, 3 * inner),
            b16(width, length),
            b16(3 * inner, length),
            b16(inner, length),
            pltpu.VMEM((width, half_len), wide),
            facts,
            facts,
            b16(2, length, q_block),
            pltpu.VMEM((heads, 2 * length - q_block, q_block), wide),
            b16(width, half_len),
            b16(width, half_len),
            pltpu.VMEM((length, 128), wide),
            pltpu.VMEM((8, length), wide),
            pltpu.SemaphoreType.DMA((17,)),
            pltpu.SemaphoreType.DMA((17,)),
            pltpu.SemaphoreType.DMA((17,)),
        ],
        compiler_params=pltpu.CompilerParams(vmem_limit_bytes=60 << 20, collective_id=2, has_side_effects=True),
        cost_estimate=hint,
        name="front_all",
    )(x, g, *weights, lengths, valid, bias, gain_one, gain_two)


def attn_bwd_kernel(length, q_ref, k_ref, v_ref, go_ref, o_ref, p_ref, gq_ref, gk_ref, gv_ref, gb_ref, k_acc, v_acc, sums):
    block = pl.program_id(1)
    reach = length - q_block

    @pl.when(block == 0)
    def _():
        k_acc[...] = jnp.zeros_like(k_acc)
        v_acc[...] = jnp.zeros_like(v_acc)
        sums[...] = jnp.zeros_like(sums)

    probs = p_ref[0]
    go = go_ref[...]
    inner = jnp.sum(go.astype(wide) * o_ref[...].astype(wide), axis=0, keepdims=True)
    scores = probs.astype(wide) * (dot(v_ref[...], go, 0, 0) - inner)
    first = pl.multiple_of(reach - block * q_block, q_block)
    sums[pl.ds(first, length), :] += scores
    scores = scores.astype(low)
    gq_ref[...] = dot(k_ref[...], scores, 1, 0).astype(low)
    k_acc[...] += dot(q_ref[...], scores, 1, 1)
    v_acc[...] += dot(go, probs, 1, 1)

    @pl.when(block == pl.num_programs(1) - 1)
    def _():
        gk_ref[...] = k_acc[...].astype(low)
        gv_ref[...] = v_acc[...].astype(low)
        rows = q_block + 2 * band_half
        d = (
            lax.broadcasted_iota(jnp.int32, (rows, q_block), 0)
            - lax.broadcasted_iota(jnp.int32, (rows, q_block), 1)
            - band_half
        )
        n = jnp.abs(d)
        near = sums[reach - band_half : reach + q_block + band_half, :]
        far_before = jnp.sum(sums[: reach - band_half, :], axis=0, keepdims=True)
        far_after = jnp.sum(sums[reach + q_block + band_half :, :], axis=0, keepdims=True)
        bucket = jnp.zeros((rows, q_block), jnp.int32)
        for step in steps_at:
            bucket = bucket + jnp.where(n >= step, 1, 0)
        bucket = bucket + jnp.where(d > 0, 16, 0)
        for b in range(32):
            total = jnp.sum(jnp.where(bucket == b, near, 0.0), axis=0, keepdims=True)
            if b == 15:
                total = total + far_before
            if b == 31:
                total = total + far_after
            gb_ref[0, b : b + 1, :] = total


def attn_backward(qkv, grad_mixed, mixed, probs):
    width, length = qkv.shape
    heads = probs.shape[0]
    dim = width // (3 * heads)
    blocks = length // q_block
    half = pl.BlockSpec((dim, q_block), lambda h, b: (h, b))
    whole = pl.BlockSpec((dim, length), lambda h, b: (h, 0))
    gq, gk, gv, gb = pl.pallas_call(
        functools.partial(attn_bwd_kernel, length),
        grid=(heads, blocks),
        in_specs=[
            half,
            pl.BlockSpec((dim, length), lambda h, b: (heads + h, 0)),
            pl.BlockSpec((dim, length), lambda h, b: (2 * heads + h, 0)),
            half,
            half,
            pl.BlockSpec((1, length, q_block), lambda h, b: (h, 0, b)),
        ],
        out_specs=[half, whole, whole, pl.BlockSpec((1, 32, q_block), lambda h, b: (h, 0, 0))],
        out_shape=[
            jax.ShapeDtypeStruct((heads * dim, length), low),
            jax.ShapeDtypeStruct((heads * dim, length), low),
            jax.ShapeDtypeStruct((heads * dim, length), low),
            jax.ShapeDtypeStruct((heads, 32, q_block), wide),
        ],
        scratch_shapes=[
            pltpu.VMEM((dim, length), wide),
            pltpu.VMEM((dim, length), wide),
            pltpu.VMEM((2 * length - q_block, q_block), wide),
        ],
        compiler_params=pltpu.CompilerParams(vmem_limit_bytes=48 << 20),
        cost_estimate=hint,
        name="attn_backward",
    )(qkv, qkv, qkv, grad_mixed, mixed, probs)
    return jnp.concatenate([gq, gk, gv], axis=0), jnp.sum(gb, axis=2).T


def ffn_kernel(
    x_ref, go_ref, gr_h0, hres_h, g_late, gate_w, up_w, down_w,
    hid_ref, pair_ref, xr_h, gr_h, out_h, out_r_h, gx_h, late_h,
    xs, gs, out_acc, gx_acc, x_in, g_in, gx_out, gx_in, out_v, gx_v, gr_ref, hres_ref, sems, store_sems,
):
    chunk = pl.program_id(0)
    tile = pl.program_id(1)
    size = xs.shape[0]
    mesh_id = dict(device_id_type=pl.DeviceIdType.MESH)
    s = lax.axis_index("seq")
    y = lax.axis_index("tensor")
    c = s % 2
    to_y = {"tensor": 1 - y}
    to_second = {"seq": s - c + y, "tensor": 1 - c}
    half = [pl.ds(0, size), pl.ds(size, size)]

    def move(k, src, dst, who):
        return pltpu.make_async_remote_copy(
            src_ref=src, dst_ref=dst, send_sem=sems.at[k], recv_sem=sems.at[4 + k], device_id=who, **mesh_id
        )

    send_x = [move(h, x_ref.at[:, half[h]], x_in.at[h], to_y) for h in range(2)]
    send_g = move(2, g_late, g_in, to_second)
    back = gx_in.shape[1]
    send_gx = move(3, gx_out.at[0, :, pl.ds(0, back)], gx_in, to_y)
    begun = g_in.shape[1]
    to = lambda k, src, dst: pltpu.make_async_copy(src, dst, store_sems.at[k])
    store_x = [to(h, x_in.at[h], xr_h.at[:, half[h]]) for h in range(2)]
    store_out = [to(2 + h, out_v.at[h], out_h.at[:, half[h]]) for h in range(2)]
    store_out_r = [to(4 + h, out_v.at[2 + h], out_r_h.at[:, half[h]]) for h in range(2)]
    store_gx = [to(6 + h, gx_v.at[h], gx_h.at[:, half[h]]) for h in range(2)]
    store_late = [to(8 + h, gx_out.at[h], late_h.at[:, half[h]]) for h in range(2)]
    store_g = to(10, g_in, gr_h)
    load_h = to(11, hres_h, hres_ref)
    load_g = to(12, gr_h0, gr_ref)

    @pl.when(tile == 0)
    def _():
        out_acc[...] = jnp.zeros_like(out_acc)
        gx_acc[...] = jnp.zeros_like(gx_acc)

    @pl.when((tile == 0) & (chunk == 0))
    def _():
        load_h.start()
        load_g.start()
        barrier = pltpu.get_barrier_semaphore()
        for who in (to_y, {"seq": s + 1 - 2 * c}):
            pl.semaphore_signal(barrier, inc=1, device_id=who, **mesh_id)
        pl.semaphore_wait(barrier, 2)
        for each in (*send_x, send_g):
            each.start()

    for h in range(2):

        @pl.when((tile == 0) & (chunk == h))
        def _(h=h):
            xs[...] = x_ref[:, half[h]].T
            gs[...] = go_ref[:, half[h]].T

        @pl.when((tile == 0) & (chunk == 2 + h))
        def _(h=h):
            send_x[h].wait_recv()
            xs[...] = x_in[h].T
            store_x[h].start()
            if not h:
                load_g.wait()
            if h:
                gs[: size - begun, :] = gr_ref[:, size:].T
                send_g.wait_recv()
                gs[size - begun :, :] = g_in[...].T
                store_g.start()
            else:
                gs[...] = gr_ref[:, :size].T

    gate = dot(xs[...], gate_w[...], 1, 0)
    up = dot(xs[...], up_w[...], 1, 0)
    grad = dot(gs[...], down_w[...], 1, 0)
    c_gelu = math.sqrt(2.0 / math.pi)
    square = gate * gate
    t = jnp.tanh(c_gelu * gate * (1.0 + 0.044715 * square))
    part = 0.5 * (1.0 + t)
    gelu = gate * part
    slope = part + 0.5 * gate * (1.0 - t * t) * (c_gelu * (1.0 + 3 * 0.044715 * square))
    hid = (gelu * up).astype(low)
    gg = (grad * up * slope).astype(low)
    gu = (grad * gelu).astype(low)
    hid_ref[...] = hid
    pair_ref[0] = gg
    pair_ref[1] = gu
    out_acc[...] += dot(down_w[...], hid, 1, 1)
    gx_acc[...] += dot(gate_w[...], gg, 1, 1) + dot(up_w[...], gu, 1, 1)

    last = tile == pl.num_programs(1) - 1
    for h in range(2):

        @pl.when(last & (chunk == h))
        def _(h=h):
            if not h:
                load_h.wait()
            out_v[h] = (hres_ref[:, half[h]] + out_acc[...]).astype(low)
            store_out[h].start()
            gx_v[h] = gx_acc[...]
            if h:
                store_gx[h].start()

        @pl.when(last & (chunk == 2 + h))
        def _(h=h):
            out_v[2 + h] = out_acc[...].astype(low)
            store_out_r[h].start()
            gx_out[h] = gx_acc[...].astype(low)
            if not h:
                send_gx.start()
            store_late[h].start()

    @pl.when(last & (chunk == 3))
    def _():
        send_gx.wait_recv()
        gx_v[0, :, :back] += gx_in[...].astype(wide)
        store_gx[0].start()
        for each in (*send_x, send_g, send_gx):
            each.wait_send()
        for each in store_x + store_out + store_out_r + store_gx + store_late + [store_g]:
            each.wait()


def ffn(x, g_own, g_oth, hres, g_late, gate_w, up_w, down_w):
    width, tokens = x.shape
    hidden = gate_w.shape[1]
    tile, size = hidden // 2, tokens // 2
    begun = g_late.shape[1]
    hbm = pl.BlockSpec(memory_space=pl.ANY)
    full = pl.BlockSpec((width, tokens), lambda s, j: (0, 0), pipeline_mode=pl.Buffered(1))
    weight = pl.BlockSpec((width, tile), lambda s, j: (0, j))
    act_shape = jax.ShapeDtypeStruct((2 * tokens, hidden), low)
    tokens_of = lambda kind: jax.ShapeDtypeStruct((width, tokens), kind)
    return pl.pallas_call(
        ffn_kernel,
        grid=(4, hidden // tile),
        in_specs=[full, full, hbm, hbm, hbm, weight, weight, weight],
        out_specs=[
            pl.BlockSpec((size, tile), lambda s, j: (s, j)),
            pl.BlockSpec((2, size, tile), lambda s, j: (0, s, j)),
        ]
        + [hbm] * 6,
        out_shape=[act_shape, jax.ShapeDtypeStruct((2, 2 * tokens, hidden), low)]
        + [tokens_of(low), jax.ShapeDtypeStruct((width, begun), low)]
        + [tokens_of(kind) for kind in (low, low, wide, low)],
        scratch_shapes=[
            pltpu.VMEM((size, width), low),
            pltpu.VMEM((size, width), low),
            pltpu.VMEM((width, size), wide),
            pltpu.VMEM((width, size), wide),
            pltpu.VMEM((2, width, size), low),
            pltpu.VMEM((width, begun), low),
            pltpu.VMEM((2, width, size), low),
            pltpu.VMEM((width, 128), low),
            pltpu.VMEM((4, width, size), low),
            pltpu.VMEM((2, width, size), wide),
            pltpu.VMEM((width, tokens - begun), low),
            pltpu.VMEM((width, tokens), wide),
            pltpu.SemaphoreType.DMA((8,)),
            pltpu.SemaphoreType.DMA((13,)),
        ],
        compiler_params=pltpu.CompilerParams(vmem_limit_bytes=60 << 20, collective_id=0, has_side_effects=True),
        cost_estimate=hint,
        name="ffn_both_ways",
    )(x, g_own, g_oth, hres, g_late, gate_w, up_w, down_w)


def weight_grad_kernel(core_ref, own_ref, oth_ref, right_ref, *refs):
    tokens = own_ref.shape[1]
    total = dot(own_ref[...], right_ref[:tokens, :], 1, 0) + dot(oth_ref[...], right_ref[tokens:, :], 1, 0)
    if len(refs) == 2:
        total = total + refs[0][...].astype(wide)
    refs[-1][...] = total.astype(low)


def weight_grad(own, oth, right, core, got=None):
    width, tokens = own.shape
    columns = right.shape[1] // 2
    blocks = 4
    rows = width // blocks
    left = pl.BlockSpec((rows, tokens), lambda i, core_ref: (i, 0))
    out = pl.BlockSpec((rows, columns), lambda i, core_ref: (i, 0))
    args = [own, oth, right] + ([] if got is None else [got])
    return pl.pallas_call(
        weight_grad_kernel,
        grid_spec=pltpu.PrefetchScalarGridSpec(
            num_scalar_prefetch=1,
            grid=(blocks,),
            in_specs=[
                left,
                left,
                pl.BlockSpec((2 * tokens, columns), lambda i, core_ref: (0, core_ref[0]), pipeline_mode=pl.Buffered(1)),
            ]
            + ([] if got is None else [out]),
            out_specs=out,
        ),
        out_shape=jax.ShapeDtypeStruct((width, columns), low),
        compiler_params=pltpu.CompilerParams(vmem_limit_bytes=40 << 20),
        cost_estimate=hint,
        name="weight_grad",
    )(core.reshape(1), *args)


def back_kernel(
    hid_h, pair_h, go_h, gr1_h, gr2_h, xo_h, xr_h, gx_h, hres_h, xin_h, probs_h, xn1_h, outp_h, outr_h, late_h,
    out_w, w_t, qkv, mixed, gain2, gain1, scale2, scale1,
    got_p, got_r, got_in, d_out, p_out, a_out, gin, small,
    r_core, xp, zd, zp, dx, px, bf, rx, ya, xa, za, ab, late_in, sm_src, sm_in, send_sems, recv_sems, load_sems,
):
    s = lax.axis_index("seq")
    y = lax.axis_index("tensor")
    z = lax.axis_index("dp")
    c = s % 2
    m = s // 2
    width = xp.shape[0]
    rows = d_out.shape[0]
    columns = xp.shape[1]
    half_len = rx.shape[1]
    length = 2 * half_len
    heads = probs_h.shape[0]
    dim = mixed.shape[0] // heads
    zs = width // rows
    mesh_id = dict(device_id_type=pl.DeviceIdType.MESH)
    to_core = {"seq": 2 * m + 1 - c}
    to_x = {"seq": 2 * (1 - m) + c}
    to_y = {"tensor": 1 - y}
    to_z = {"dp": (z + 1) % zs}
    to_swap = {"seq": 2 * m + y, "tensor": c}
    to_back = {"seq": 2 * m + 1 - y, "tensor": c}

    barrier = pltpu.get_barrier_semaphore()
    greet = [to_core, to_y, {"seq": 2 * m + 1 - c, "tensor": 1 - y}, to_x] + [{"dp": (z + i) % zs} for i in range(1, zs)]
    for who in greet:
        pl.semaphore_signal(barrier, inc=1, device_id=who, **mesh_id)
    pl.semaphore_wait(barrier, len(greet))

    def move(k, src, dst, who):
        return pltpu.make_async_remote_copy(
            src_ref=src, dst_ref=dst, send_sem=send_sems.at[k], recv_sem=recv_sems.at[k], device_id=who, **mesh_id
        )

    def load(k, src, dst):
        return pltpu.make_async_copy(src, dst, load_sems.at[k])

    def chunk(j):
        return pl.ds(pl.multiple_of(j * rows, rows), rows)

    def side(i, size):
        return pl.ds(pl.multiple_of(i * size, 128), size)

    order = [(z + zs - 1 - k) % zs for k in range(zs)]
    mine = side(c, columns)
    my_half = side(c, half_len)
    other_half = side(1 - c, half_len)
    cut = [(0, 192), (192, rows - 192)]

    def part(j, p):
        return pl.ds(pl.multiple_of(j * rows + cut[p][0], 16), cut[p][1])

    parts = [pl.ds(*each) for each in cut]

    late_from = half_len - late_in.shape[1]
    late = move(0, late_h.at[:, pl.ds(late_from, half_len - late_from)], late_in, to_y)
    swap_out = move(1, outp_h, got_p, to_swap)
    back_out = move(2, outr_h, got_r, to_back)
    z_down = [move(3, r_core.at[0, chunk(order[0])], zd.at[0], to_z), move(4, zd.at[0], zd.at[1], to_z)]
    z_down_last = [move(5 + p, zd.at[1, parts[p]], zd.at[2, parts[p]], to_z) for p in range(2)]
    x_down = [move(7 + p, zd.at[2, parts[p]], dx.at[parts[p]], to_x) for p in range(2)]
    core_down = [move(9 + p, d_out.at[parts[p], mine], d_out.at[parts[p], mine], to_core) for p in range(2)]
    z_pair = [move(11, r_core.at[2, chunk(order[0])], zp.at[0], to_z), move(12, zp.at[0], zp.at[1], to_z)]
    z_pair_last = [move(13 + p, zp.at[1, parts[p]], zp.at[2, parts[p]], to_z) for p in range(2)]
    x_pair_back = [move(15 + p, zp.at[2, parts[p]], px.at[parts[p]], to_x) for p in range(2)]
    core_pair = [move(17 + p, p_out.at[m, parts[p], mine], p_out.at[m, parts[p], mine], to_core) for p in range(2)]
    core_pair_back = [
        move(19 + p, p_out.at[1 - m, parts[p], mine], p_out.at[1 - m, parts[p], mine], to_core) for p in range(2)
    ]
    core_branch = move(21, bf.at[:, my_half], bf.at[:, my_half], to_core)
    a_cols = ya.shape[2]
    a_rows = xa.shape[1]
    my_cols = side(y, a_cols)
    my_rows = pl.ds(pl.multiple_of(m * a_rows, a_rows), a_rows)
    x_rows = pl.ds(pl.multiple_of((1 - m) * a_rows, a_rows), a_rows)
    x_attn = [move(22 + k, ya.at[j, x_rows], xa.at[j], to_x) for k, j in enumerate(order)]
    z_attn = [move(26, ya.at[order[0], my_rows], za.at[0], to_z)] + [
        move(26 + t, za.at[t - 1], za.at[t], to_z) for t in range(1, zs - 1)
    ]
    my_piece = ab.at[my_rows, my_cols]
    spread_attn = [
        move(29 + i, my_piece, my_piece, who)
        for i, who in enumerate((to_x, to_y, {"seq": 2 * (1 - m) + c, "tensor": 1 - y}))
    ]
    core_attn = move(32, ab, a_out, to_core)
    swap_in = move(33, gin, got_in, to_swap)

    def x_pair(k):
        at = chunk((z + zs - 1 - k) % zs)
        return move(44 + k, r_core.at[1, at], xp.at[at], to_x)

    late.start()

    def step_z_down(t):
        z_down[t - 1].wait_recv()
        zd[t - 1] = (zd[t - 1].astype(wide) + r_core[0, chunk(order[t]), :].astype(wide)).astype(low)
        for each in z_down_last if t == 2 else [z_down[t]]:
            each.start()

    def last_z_down(p):
        z_down_last[p].wait_recv()
        at = parts[p]
        zd[2, at, :] = (zd[2, at, :].astype(wide) + r_core[0, part(z, p), :].astype(wide)).astype(low)
        x_down[p].start()

    def end_down(p):
        x_down[p].wait_recv()
        at = parts[p]
        d_out[at, mine] = (zd[2, at, :].astype(wide) + dx[at, :].astype(wide)).astype(low)
        core_down[p].start()

    def step_z_pair(t):
        x_pair(t).wait_recv()
        term = r_core[2, chunk(order[t]), :].astype(wide) + xp[chunk(order[t]), :].astype(wide)
        if t:
            z_pair[t - 1].wait_recv()
            zp[t - 1] = (zp[t - 1].astype(wide) + term).astype(low)
        else:
            r_core[2, chunk(order[0]), :] = term.astype(low)
        for each in z_pair_last if t == 2 else [z_pair[t]]:
            each.start()

    def last_z_pair(p):
        if p == 0:
            x_pair(3).wait_recv()
        z_pair_last[p].wait_recv()
        at = parts[p]
        term = r_core[2, part(z, p), :].astype(wide) + xp[part(z, p), :].astype(wide)
        total = (zp[2, at, :].astype(wide) + term).astype(low)
        zp[2, at, :] = total
        x_pair_back[p].start()
        p_out[m, at, mine] = total
        core_pair[p].start()

    def end_pair(p):
        x_pair_back[p].wait_recv()
        at = parts[p]
        p_out[1 - m, at, mine] = px[at, :]
        core_pair_back[p].start()

    def step_attn(t):
        x_attn[t].wait_recv()
        term = ya[order[t], my_rows, :].astype(wide) + xa[order[t]].astype(wide)
        if t:
            z_attn[t - 1].wait_recv()
            za[t - 1] = (za[t - 1].astype(wide) + term).astype(low)
        else:
            x_attn[0].wait_send()
            ya[order[0], my_rows, :] = term.astype(low)
        if t < zs - 1:
            z_attn[t].start()

    hops = [to_core, to_y, to_x, {"dp": z + 1 - 2 * (z % 2)}, {"dp": (z + 2) % zs}]
    exchange = [move(39 + i, sm_src.at[i], sm_in.at[i], who) for i, who in enumerate(hops)]

    def start_sum(i):
        sm_src[i] = small[...]
        exchange[i].start()

    def end_sum(i):
        exchange[i].wait_recv()
        small[...] = sm_src[i] + sm_in[i]

    def weights(r_buf, l_go, l_gr, l_xo, l_xr, s_buf):
        loads = [
            load(0, hid_h, r_buf.at[0]),
            load(1, go_h, l_go),
            load(2, gr1_h, l_gr.at[:, pl.ds(0, gr1_h.shape[1])]),
            load(3, gr2_h, l_gr.at[:, pl.ds(gr1_h.shape[1], gr2_h.shape[1])]),
            load(4, pair_h.at[1 - m], r_buf.at[1]),
            load(5, xo_h, l_xo),
            load(14, xr_h, l_xr),
        ]
        load_own = load(6, pair_h.at[m], r_buf.at[0])
        for each in loads:
            each.start()
        theirs = side(1 - c, columns)

        def core(i, k):
            at = chunk((z + zs - 1 - k) % zs)
            return move(48 + i * zs + k, s_buf.at[i % 2, at], r_core.at[i, at], to_core)

        def product(left_o, left_r, right, col, i, extra=None):
            def block(k, carry):
                at = chunk((z + zs - 1 - k) % zs)
                total = dot(left_o[at, :], right[:half_len, col], 1, 0)
                total = total + dot(left_r[at, :], right[half_len:, col], 1, 0)
                if extra is None:
                    s_buf[i % 2, at, :] = total.astype(low)
                    core(i, k).start()
                else:
                    core(i, k).wait_recv()
                    r_core[i, at, :] = (total + r_core[i, at, :].astype(wide)).astype(low)
                    extra(k)
                return carry

            lax.fori_loop(0, zs, block, 0)

        def at_first(run):
            def extra(k):
                pl.when(k == 0)(run)

            return extra

        def sent(i):
            def block(k, carry):
                core(i, k).wait_send()
                return carry

            lax.fori_loop(0, zs, block, 0)

        for each in loads[:4]:
            each.wait()
        product(l_go, l_gr, r_buf.at[0], theirs, 0)
        product(l_go, l_gr, r_buf.at[0], mine, 0, at_first(z_down[0].start))
        load_own.start()
        for each in loads[4:]:
            each.wait()
        product(l_xo, l_xr, r_buf.at[1], theirs, 1)
        product(l_xo, l_xr, r_buf.at[1], mine, 1, lambda k: x_pair(k).start())

        @pl.when(c != y)
        def _():
            swap_out.start()

        back_out.start()
        step_z_down(1)
        load_own.wait()
        sent(0)
        product(l_xo, l_xr, r_buf.at[0], theirs, 2)
        product(l_xo, l_xr, r_buf.at[0], mine, 2, lambda k: None)
        step_z_pair(0)
        sent(1)
        sent(2)

    hidden = hid_h.shape[1]
    left = pltpu.VMEM((width, half_len), low)
    pl.run_scoped(
        weights,
        pltpu.VMEM((2, length, hidden), low),
        left,
        left,
        left,
        left,
        pltpu.VMEM((2, width, columns), low),
    )

    def attention(gxv, hv, gov, p_buf, k_acc, v_acc, sums, gqkv, gm, xn1, sx, ga):
        loads = [load(7, gx_h, gxv), load(8, hres_h, hv), load(9, go_h, gov), load(10, xn1_h, xn1)]
        load_x = load(11, xin_h, gov)
        for each in loads:
            each.start()

        def probs_load(h, b, slot):
            return load(12 + slot, probs_h.at[h, :, side(b, q_block)], p_buf.at[slot])

        probs_load(0, 0, 0).start()
        lanes = half_len // 128
        piece = 64
        pieces = width // piece

        def fold(a):
            return sum(a[:, i * 128 : (i + 1) * 128] for i in range(lanes))

        def spread(a):
            return jnp.concatenate([a] * lanes, axis=1)

        def norm_backward(values, gain, scale, grad, store, row):
            def first(i, total):
                at = pl.ds(pl.multiple_of(i * piece, piece), piece)
                return total + jnp.sum(values(at) * (spread(gain[at, :]) * grad(at)), axis=0, keepdims=True)

            total = lax.fori_loop(0, pieces, first, jnp.zeros((1, half_len), wide))
            mean = total * scale[...] * (1.0 / width)

            def second(i, carry):
                at = pl.ds(pl.multiple_of(i * piece, piece), piece)
                g = grad(at)
                normed = values(at) * scale[...]
                store(at, scale[...] * (spread(gain[at, :]) * g - normed * mean))
                ga_part[at, :] = fold(g * normed)
                return carry

            lax.fori_loop(0, pieces, second, 0)
            small[row : row + 1, :] = jnp.sum(ga_part[...].T, axis=0, keepdims=True)

        ga_part = sums.at[:width, :128]
        small[...] = jnp.zeros_like(small)
        for each in loads[:3]:
            each.wait()
        late.wait_recv()

        def add_late(i, carry):
            at = pl.ds(pl.multiple_of(i * piece, piece), piece)
            gxv[at, late_from:] += late_in[at, :].astype(wide)
            return carry

        lax.fori_loop(0, pieces, add_late, 0)

        def store_hres(at, back):
            total = gov[at, :].astype(wide) + back
            gxv[at, :] = total
            bf[at, my_half] = total.astype(low)

        norm_backward(lambda at: hv[at, :], gain2, scale2, lambda at: gxv[at, :], store_hres, 0)
        core_branch.start()
        load_x.start()
        step_z_down(2)
        core_branch.wait_recv()
        gm[...] = dot(out_w[...], bf[...], 1, 0).astype(low)

        reach = length - q_block
        blocks = length // q_block
        near_rows = q_block + 2 * band_half
        d = (
            lax.broadcasted_iota(jnp.int32, (near_rows, q_block), 0)
            - lax.broadcasted_iota(jnp.int32, (near_rows, q_block), 1)
            - band_half
        )
        for h in range(heads):
            head = pl.ds(h * dim, dim)
            k_rows = pl.ds((heads + h) * dim, dim)
            v_rows = pl.ds((2 * heads + h) * dim, dim)
            k_acc[...] = jnp.zeros_like(k_acc)
            v_acc[...] = jnp.zeros_like(v_acc)
            sums[...] = jnp.zeros_like(sums)

            def block(b, carry):
                slot = b % 2
                at = side(b, q_block)
                probs_load(h, b, slot).wait()

                @pl.when(b < blocks - 1)
                def _():
                    probs_load(h, b + 1, 1 - slot).start()

                if h < heads - 1:

                    @pl.when(b == blocks - 1)
                    def _():
                        probs_load(h + 1, 0, 1 - slot).start()

                probs = p_buf[slot]
                go = gm[head, at]
                inner = jnp.sum(go.astype(wide) * mixed[head, at].astype(wide), axis=0, keepdims=True)
                scores = probs.astype(wide) * (dot(qkv[v_rows, :], go, 0, 0) - inner)
                first = pl.multiple_of(reach - b * q_block, q_block)
                sums[pl.ds(first, length), :] += scores
                scores = scores.astype(low)
                gqkv[head, at] = dot(qkv[k_rows, :], scores, 1, 0).astype(low)
                k_acc[...] += dot(qkv[head, at], scores, 1, 1)
                v_acc[...] += dot(go, probs, 1, 1)
                return carry

            lax.fori_loop(0, blocks, block, 0)
            gqkv[k_rows, :] = k_acc[...].astype(low)
            gqkv[v_rows, :] = v_acc[...].astype(low)
            near = sums[reach - band_half : reach + q_block + band_half, :]
            n = jnp.abs(d)
            bucket = jnp.zeros((near_rows, q_block), jnp.int32)
            for step in steps_at:
                bucket = bucket + jnp.where(n >= step, 1, 0)
            bucket = bucket + jnp.where(d > 0, 16, 0)
            totals = []
            for b in range(32):
                total = jnp.sum(jnp.where(bucket == b, near, 0.0), axis=0, keepdims=True)
                if b == 15:
                    total = total + jnp.sum(sums[: reach - band_half, :], axis=0, keepdims=True)
                if b == 31:
                    total = total + jnp.sum(sums[reach + q_block + band_half :, :], axis=0, keepdims=True)
                totals.append(total)
            totals = jnp.concatenate(totals, axis=0)
            totals = jnp.concatenate([totals, jnp.zeros((96, q_block), wide)], axis=0)
            line = jnp.sum(totals.T, axis=0, keepdims=True)
            for side_c in range(2):
                row = 8 + side_c * heads + h
                small[row : row + 1, :128] = jnp.where(c == side_c, line, 0.0)
            if h == 0:
                step_z_pair(1)

        def input_grad(half, store):
            def block(i, carry):
                at = chunk(i)
                store(at, dot(w_t[at, :], gqkv[:, half], 1, 0))
                return carry

            lax.fori_loop(0, zs, block, 0)

        def store_sent(at, value):
            sx[at, :] = value.astype(low)

        core_x = move(34, sx, rx, to_core)
        loads[3].wait()
        y_attn = [
            move(35 + k, ga.at[j, :, side(1 - y, a_cols)], ya.at[j], to_y) for k, j in enumerate(order)
        ]
        wide_cols = gqkv.shape[0]

        def weight_part(k):
            j = order[k]
            ga[j, :rows, :wide_cols] = dot(xn1[chunk(j), :], gqkv[...], 1, 1).astype(low)
            ga[j, :rows, wide_cols:] = dot(bf[chunk(j), :], mixed[...], 1, 1).astype(low)
            ga[j, rows:, :] = jnp.zeros((ga.shape[1] - rows, ga.shape[2]), low)
            y_attn[k].start()

        def store_own(at, value):
            hv[at, :] = value

        def store_in(at, back):
            gin[at, :] = (gxv[at, :] + back).astype(low)

        def step_y_attn(k):
            j = order[k]
            y_attn[k].wait_recv()
            ya[j] = (ya[j].astype(wide) + ga[j, :, my_cols].astype(wide)).astype(low)
            x_attn[k].start()

        weight_part(0)
        weight_part(1)
        input_grad(other_half, store_sent)
        core_x.start()
        last_z_down(0)
        last_z_down(1)
        input_grad(my_half, store_own)
        weight_part(2)
        weight_part(3)
        step_y_attn(0)
        load_x.wait()
        core_x.wait_recv()
        norm_backward(
            lambda at: gov[at, :].astype(wide),
            gain1,
            scale1,
            lambda at: hv[at, :] + rx[at, :].astype(wide),
            store_in,
            1,
        )
        step_z_pair(2)
        start_sum(0)
        step_y_attn(1)
        end_sum(0)
        start_sum(1)

        @pl.when(c != y)
        def _():
            swap_in.start()

        end_down(0)
        end_down(1)
        step_y_attn(2)
        last_z_pair(0)
        step_attn(0)
        end_sum(1)
        start_sum(2)
        step_y_attn(3)
        core_x.wait_send()
        for each in y_attn:
            each.wait_send()

    f32 = lambda *shape: pltpu.VMEM(shape, wide)
    b16 = lambda *shape: pltpu.VMEM(shape, low)
    pl.run_scoped(
        attention,
        f32(width, half_len),
        f32(width, half_len),
        b16(width, half_len),
        b16(2, length, q_block),
        f32(dim, length),
        f32(dim, length),
        f32(2 * length - q_block, q_block),
        b16(3 * heads * dim, length),
        b16(heads * dim, length),
        b16(width, length),
        b16(width, half_len),
        b16(zs, ya.shape[1], 2 * ya.shape[2]),
    )

    last_z_pair(1)
    step_attn(1)
    end_pair(0)
    step_attn(2)
    end_sum(2)
    start_sum(3)
    step_attn(3)
    ab[my_rows, my_cols] = za[zs - 2]
    for each in spread_attn:
        each.start()
    end_sum(3)
    start_sum(4)
    end_pair(1)
    for each in spread_attn:
        each.wait_recv()

    @pl.when(c == y)
    def _():
        core_attn.start()
        a_out[...] = ab[...]
        core_attn.wait_send()

    end_sum(4)

    @pl.when(c != y)
    def _():
        core_attn.wait_recv()
        swap_out.wait()
        swap_in.wait()

    back_out.wait()
    for each in core_down + core_pair + core_pair_back:
        each.wait()
    for each in [late, core_branch] + z_down + z_down_last + x_down + z_pair + z_pair_last + x_pair_back:
        each.wait_send()
    for each in [x_pair(k) for k in range(zs)] + x_attn[1:] + z_attn + spread_attn + exchange:
        each.wait_send()


def back_all(
    hid, pair, g_own, g_oth, g_late, x_own, x_oth, gx, hres, x_in, probs, xn_one, out_first, out_oth, late,
    out_w, w_t, qkv, mixed, gain_two, gain_one, scale_two, scale_one, zs,
):
    width, half_len = g_own.shape
    length = 2 * half_len
    rows = width // zs
    columns = hid.shape[1] // 2
    heads = probs.shape[0]
    a_cols = (w_t.shape[1] + out_w.shape[0]) // 2
    a_len = -(-rows // 32) * 32
    hbm = pl.BlockSpec(memory_space=pl.ANY)
    vmem = pl.BlockSpec(memory_space=pltpu.VMEM)
    sds = lambda kind, *shape: jax.ShapeDtypeStruct(shape, kind)
    b16 = lambda *shape: pltpu.VMEM(shape, low)
    return pl.pallas_call(
        back_kernel,
        in_specs=[hbm] * 15 + [vmem] * 8,
        out_specs=[hbm] * 3 + [vmem] * 5,
        out_shape=[
            sds(low, width, half_len),
            sds(low, width, half_len),
            sds(low, width, half_len),
            sds(low, rows, 2 * columns),
            sds(low, 2, rows, 2 * columns),
            sds(low, a_len, 2 * a_cols),
            sds(low, width, half_len),
            sds(wide, 16, width),
        ],
        scratch_shapes=[
            b16(3, width, columns),
            b16(width, columns),
            b16(zs - 1, rows, columns),
            b16(zs - 1, rows, columns),
            b16(rows, columns),
            b16(rows, columns),
            b16(width, length),
            b16(width, half_len),
            b16(zs, a_len, a_cols),
            b16(zs, a_len // 2, a_cols),
            b16(zs - 1, a_len // 2, a_cols),
            b16(a_len, 2 * a_cols),
            b16(width, half_len - 128),
            pltpu.VMEM((5, 16, width), wide),
            pltpu.VMEM((5, 16, width), wide),
            pltpu.SemaphoreType.DMA((60,)),
            pltpu.SemaphoreType.DMA((60,)),
            pltpu.SemaphoreType.DMA((15,)),
        ],
        compiler_params=pltpu.CompilerParams(vmem_limit_bytes=61 << 20, collective_id=1, has_side_effects=True),
        cost_estimate=hint,
        name="back_all",
    )(
        hid, pair, g_own, g_oth, g_late, x_own, x_oth, gx, hres, x_in, probs, xn_one, out_first, out_oth, late,
        out_w, w_t, qkv, mixed, gain_two, gain_one, scale_two, scale_one,
    )


def finish_kernel(
    d_h, p_h, a_h, own_in, got_in, own_out, got_out, oth_out, small,
    d_out, g_out, u_out, q_out, k_out, v_out, o_out, in_out, y_out, gain1_out, gain2_out, bias_out,
    w_in, w_out, a_in, i_in, i_out, y_in, sems,
):
    own = lax.axis_index("seq") % 2 == lax.axis_index("tensor")
    rows = w_in.shape[1]
    width = i_in.shape[0]
    copy = lambda k, src, dst: pltpu.make_async_copy(src, dst, sems.at[k])
    loads = [copy(0, d_h, w_in.at[0]), copy(1, p_h.at[0], w_in.at[1]), copy(2, p_h.at[1], w_in.at[2]), copy(3, a_h, a_in)]
    load_y = copy(4, oth_out, y_in.at[1])
    mine = [copy(5, own_in, i_in), copy(6, own_out, y_in.at[0])]
    theirs = [copy(5, got_in, i_in), copy(6, got_out, y_in.at[0])]
    stores = [copy(7 + i, w_out.at[i], out) for i, out in enumerate((d_out, g_out, u_out))]
    store_i = copy(10, i_out, in_out)
    store_y = copy(11, y_in.at[0], y_out)

    def start(which):
        @pl.when(own)
        def _():
            mine[which].start()

        @pl.when(jnp.logical_not(own))
        def _():
            theirs[which].start()

    loads[0].start()
    start(0)
    for each in loads[1:3]:
        each.start()
    start(1)
    load_y.start()
    loads[3].start()

    def piecewise(count, size, run):
        def step(i, carry):
            run(pl.ds(pl.multiple_of(i * size, size), size))
            return carry

        lax.fori_loop(0, count, step, 0)

    def widen(i):
        loads[i].wait()

        def run(at):
            w_out[i, at, :] = w_in[i, at, :].astype(wide)

        piecewise(rows // 16, 16, run)
        stores[i].start()

    widen(0)
    mine[0].wait()

    def run_in(at):
        i_out[at, :] = i_in[at, :].astype(wide)

    piecewise(width // 64, 64, run_in)
    store_i.start()
    widen(1)
    widen(2)
    mine[1].wait()
    load_y.wait()

    def run_y(at):
        y_in[0, at, :] = (y_in[0, at, :].astype(wide) + y_in[1, at, :].astype(wide)).astype(low)

    piecewise(width // 64, 64, run_y)
    store_y.start()
    loads[3].wait()
    inner = q_out.shape[0]
    for i, out in enumerate((q_out, k_out, v_out, o_out)):
        out[...] = a_in[:rows, i * inner : (i + 1) * inner].astype(wide).T
    gain1_out[...] = small[1, :]
    gain2_out[...] = small[0, :]
    bias_out[...] = small[8 : 8 + bias_out.shape[0], : bias_out.shape[1]]
    for each in stores + [store_i, store_y]:
        each.wait()


def finish(d, p, a, own_in, got_in, own_out, got_out, oth_out, small, inner, bias_shape):
    rows, hidden = d.shape
    width, half_len = own_in.shape
    hbm = pl.BlockSpec(memory_space=pl.ANY)
    vmem = pl.BlockSpec(memory_space=pltpu.VMEM)
    sds = lambda kind, *shape: jax.ShapeDtypeStruct(shape, kind)
    return pl.pallas_call(
        finish_kernel,
        in_specs=[hbm] * 8 + [vmem],
        out_specs=[hbm] * 3 + [vmem] * 4 + [hbm] * 2 + [vmem] * 3,
        out_shape=[sds(wide, rows, hidden)] * 3
        + [sds(wide, inner, rows)] * 4
        + [sds(wide, width, half_len), sds(low, width, half_len)]
        + [sds(wide, width)] * 2
        + [sds(wide, *bias_shape)],
        scratch_shapes=[
            pltpu.VMEM((3, rows, hidden), low),
            pltpu.VMEM((3, rows, hidden), wide),
            pltpu.VMEM(a.shape, low),
            pltpu.VMEM((width, half_len), low),
            pltpu.VMEM((width, half_len), wide),
            pltpu.VMEM((2, width, half_len), low),
            pltpu.SemaphoreType.DMA((12,)),
        ],
        compiler_params=pltpu.CompilerParams(vmem_limit_bytes=60 << 20),
        cost_estimate=hint,
        name="finish_all",
    )(d, p, a, own_in, got_in, own_out, got_out, oth_out, small)


def norm_back(values, scale, gain, grad):
    normed = values * scale
    pushed = gain * grad
    mean = jnp.mean(normed * pushed, axis=0, keepdims=True)
    return scale * (pushed - normed * mean), jnp.sum(grad * normed, axis=1)


class Moves:
    def __init__(self, mesh):
        self.nz = mesh.shape["dp"]
        self.nx = mesh.shape["seq"] // 2
        both = [(m, c, y) for m in range(self.nx) for c in range(2) for y in range(2)]
        at = lambda m, c, y: (m * 2 + c) * 2 + y
        self.swap_pairs = [(at(m, c, y), at(m, y, c)) for m, c, y in both if c != y]
        self.second_pairs = [(at(m, c, y), at(m, y, 1 - c)) for m, c, y in both]
        self.back_pairs = [(b, a) for a, b in self.second_pairs]
        self.ring_x = [(m * 2 + c, (m + 1) % self.nx * 2 + c) for m in range(self.nx) for c in range(2)]
        self.y = lax.axis_index("tensor")
        self.z = lax.axis_index("dp")
        s = lax.axis_index("seq")
        self.c = s % 2
        self.m = s // 2

    def swap(self, a):
        got = lax.ppermute(a, ("seq", "tensor"), self.swap_pairs)
        return jnp.where(self.c == self.y, a, got)

    def back(self, a):
        return lax.ppermute(a, ("seq", "tensor"), self.back_pairs)

    def core(self, a):
        return lax.ppermute(a, "seq", [(s, s ^ 1) for s in range(2 * self.nx)])

    def over_y(self, a):
        return lax.ppermute(a, "tensor", [(0, 1), (1, 0)])

    def over_x(self, a):
        return lax.ppermute(a, "seq", self.ring_x)

    def start_x(self, a):
        take = lax.dynamic_index_in_dim(a, (self.m + self.nx - 1) % self.nx, 1, False)
        return a, self.over_x(take)

    def finish_x(self, a, got, *first):
        take = lambda i: lax.dynamic_index_in_dim(a, i % self.nx, 1, False)
        got = after(got, *first)
        held = (got.astype(wide) + take(self.m + 2 * self.nx - 2).astype(wide)).astype(low)
        for t in range(2, self.nx):
            held = (self.over_x(held).astype(wide) + take(self.m + 2 * self.nx - 1 - t).astype(wide)).astype(low)
        return held

    def scatter_x(self, a):
        take = lambda i: lax.dynamic_index_in_dim(a, i % self.nx, 1, False)
        held = take(self.m + self.nx - 1)
        for t in range(1, self.nx):
            held = (self.over_x(held).astype(wide) + take(self.m + 2 * self.nx - 1 - t).astype(wide)).astype(low)
        return held

    def scatter_z(self, a):
        return lax.psum_scatter(a, "dp", scatter_dimension=0, tiled=True)

    def gather_x(self, piece):
        if self.nx == 2:
            over = self.over_x(piece)
            return jnp.where(
                self.m == 0, jnp.concatenate([piece, over], 0), jnp.concatenate([over, piece], 0)
            )
        groups = [[m * 2 + c for m in range(self.nx)] for c in range(2)]
        return lax.all_gather(piece, "seq", axis=0, tiled=True, axis_index_groups=groups)

    def gather_core(self, piece):
        there = self.core(piece)
        return jnp.where(
            self.c == 0, jnp.concatenate([piece, there], 1), jnp.concatenate([there, piece], 1)
        )

    def sum_everywhere(self, a):
        a = a + self.core(a)
        a = a + self.over_y(a)
        step = 1
        while step < self.nx:
            a = a + lax.ppermute(a, "seq", [(s, s ^ (2 * step)) for s in range(2 * self.nx)])
            step *= 2
        step = 1
        while step < self.nz:
            a = a + lax.ppermute(a, "dp", [(z, z ^ step) for z in range(self.nz)])
            step *= 2
        return a


def local(
    mesh,
    layer_in,
    out_grad,
    doc_lengths,
    valid_length,
    gain_attn,
    query_weight,
    key_weight,
    value_weight,
    position_bias,
    output_weight,
    gain_ffn,
    gate_weight,
    up_weight,
    down_weight,
):
    moves = Moves(mesh)
    half_len, _, width = layer_in.shape
    length = 2 * half_len
    heads = position_bias.shape[1]
    inner_width = query_weight.shape[1]
    y, c, m = moves.y, moves.c, moves.m

    flat = lambda a: a.reshape(half_len, width).T
    (
        x_in, g_own, g_oth, g_send, out_w, w_t, xn_one, qkv, mixed, probs, hres, xn_own, scale_one, scale_two, gain_one, gain_two
    ) = front(
        flat(layer_in),
        flat(out_grad),
        (query_weight.T, key_weight.T, value_weight.T, output_weight),
        doc_lengths,
        valid_length,
        position_bias.T,
        gain_attn,
        gain_ffn,
        moves.nx == 2 and moves.nz == 4,
    )
    hid, pair, xn_oth, g_late, out_first, out_oth, gx, late = ffn(
        xn_own, g_own, g_oth, hres, g_send, gate_weight, up_weight, down_weight.T
    )
    if moves.nx == 2 and moves.nz == 4:
        got_first, got_oth, got_in, sum_d, sum_p, sums, grad_in, small = back_all(
            hid, pair, g_own, g_oth, g_late, xn_own, xn_oth, gx, hres, x_in, probs, xn_one, out_first, out_oth, late,
            out_w, w_t, qkv, mixed, gain_two, gain_one, scale_two, scale_one, moves.nz,
        )
        sum_d, sum_g, sum_u, sum_q, sum_k, sum_v, sum_o, grad_in, out_y, gain_one_sum, gain_two_sum, bias_sum = finish(
            sum_d, sum_p, sums, grad_in, got_in, out_first, got_first, got_oth, small,
            inner_width, (2 * heads, position_bias.shape[0]),
        )
        return (
            out_y.T.reshape(half_len, 1, width),
            grad_in.T.reshape(half_len, 1, width),
            gain_one_sum,
            sum_q.T,
            sum_k.T,
            sum_v.T,
            bias_sum.T,
            sum_o,
            gain_two_sum,
            sum_g,
            sum_u,
            sum_d.T,
        )
    grad_gate, grad_up = pair[0], pair[1]
    gx = gx.at[:, 128:].add(moves.over_y(late)[:, 128:].astype(wide))
    g_oth = jnp.concatenate([g_oth, g_late], axis=1)
    qkv_w = w_t.T
    x_wide = x_in.astype(wide)
    gain_one, gain_two = gain_one[:, :1], gain_two[:, :1]

    def both_halves(own):
        other = moves.core(own)
        return jnp.where(
            c == 0, jnp.concatenate([own, other], 1), jnp.concatenate([other, own], 1)
        )

    def my_half(a):
        return lax.dynamic_slice_in_dim(a, c * half_len, half_len, 1)

    def other_half(a):
        return lax.dynamic_slice_in_dim(a, (1 - c) * half_len, half_len, 1)


    columns = hid.shape[1] // 2
    send_d = weight_grad(g_own, g_oth, hid, 1 - c)
    got_d = moves.core(send_d)
    send_g = weight_grad(xn_own, xn_oth, after(grad_gate, send_d), 1 - c)
    got_g = moves.core(send_g)
    send_u = weight_grad(xn_own, xn_oth, after(grad_up, send_g), 1 - c)
    got_u = moves.core(send_u)
    total_d = weight_grad(g_own, g_oth, after(hid, send_u), c, got_d)
    total_g = weight_grad(xn_own, xn_oth, after(grad_gate, total_d), c, got_g)
    total_u = weight_grad(xn_own, xn_oth, after(grad_up, total_g), c, got_u)
    part_d = moves.scatter_z(total_d)
    x_sent = [moves.start_x(t.reshape(moves.nz, moves.nx, -1, columns)) for t in (total_g, total_u)]

    gx = after(gx, total_u)
    out_y = moves.swap(out_first).astype(wide) + moves.back(out_oth).astype(wide)

    back, grad_gain_two = norm_back(hres, scale_two, gain_two, gx)
    grad_hres = g_own.astype(wide) + back
    branch = both_halves(grad_hres.astype(low))

    grad_mixed = dot(out_w, branch, 1, 0).astype(low)
    grad_qkv, grad_bias = attn_backward(qkv, grad_mixed, mixed, probs)

    part_g = moves.finish_x(*x_sent[0], grad_qkv).reshape(-1, columns)
    sent = dot(qkv_w, other_half(after(grad_qkv, part_g)), 0, 0).astype(low)
    part_g = moves.scatter_z(part_g)
    got_x = moves.core(sent)
    grad_attn_w = jnp.concatenate(
        [dot(xn_one, after(grad_qkv, sent), 1, 1).astype(low), dot(branch, mixed, 1, 1).astype(low)], axis=1
    )
    gx = dot(qkv_w, my_half(after(grad_qkv, grad_attn_w)), 0, 0) + got_x.astype(wide)
    back, grad_gain_one = norm_back(x_wide, scale_one, gain_one, gx)
    grad_in = (grad_hres + back).astype(low)
    part_u = moves.scatter_z(moves.finish_x(*x_sent[1], grad_in).reshape(-1, columns))

    a_columns = grad_attn_w.shape[1] // 2
    chunks = grad_attn_w.reshape(moves.nz, moves.nx, -1, 2 * a_columns)

    def scatter_y(a):
        got = moves.over_y(lax.dynamic_slice_in_dim(a, (1 - y) * a_columns, a_columns, a.ndim - 1))
        kept = lax.dynamic_slice_in_dim(a, y * a_columns, a_columns, a.ndim - 1)
        return (kept.astype(wide) + got.astype(wide)).astype(low)

    half_z = moves.nz // 2
    part = jnp.concatenate(
        [moves.scatter_x(scatter_y(chunks[:half_z])), scatter_y(moves.scatter_x(chunks[half_z:]))], 0
    )
    piece = moves.gather_x(moves.scatter_z(part.reshape(-1, a_columns)))
    there = moves.over_y(piece)
    group = jnp.where(y == 0, jnp.concatenate([piece, there], 1), jnp.concatenate([there, piece], 1))
    sums = jnp.where(c == y, group, moves.core(group)).astype(wide)
    sum_q, sum_k, sum_v, sum_o = (
        sums[:, i * inner_width : (i + 1) * inner_width] for i in range(4)
    )
    grad_in = moves.swap(grad_in).astype(wide)

    if moves.nx == 2:
        part_d = (part_d.astype(wide) + moves.over_x(part_d).astype(wide)).astype(low)
    else:
        part_d = moves.gather_x(moves.scatter_x(part_d.reshape(1, moves.nx, -1, columns))[0])
    sum_d = moves.gather_core(part_d).astype(wide)
    sum_g = moves.gather_core(moves.gather_x(part_g)).astype(wide)
    sum_u = moves.gather_core(moves.gather_x(part_u)).astype(wide)

    bias_full = jnp.zeros((grad_bias.shape[0], 2 * heads), wide)
    bias_full = lax.dynamic_update_slice(bias_full, grad_bias, (jnp.int32(0), c * heads))
    early = moves.sum_everywhere(jnp.concatenate([grad_gain_two, bias_full.reshape(-1)]))
    gain_two_sum, bias_sum = early[:width], early[width:].reshape(bias_full.shape)
    gain_one_sum = moves.sum_everywhere(grad_gain_one)
    return (
        out_y.astype(low).T.reshape(half_len, 1, width),
        grad_in.T.reshape(half_len, 1, width),
        gain_one_sum,
        sum_q,
        sum_k,
        sum_v,
        bias_sum,
        sum_o.T,
        gain_two_sum,
        sum_g,
        sum_u,
        sum_d.T,
    )


def solution(mesh):
    rows = P("tensor", ("dp", "seq"), None)
    columns = P(None, "tensor")
    return jax.shard_map(
        functools.partial(local, mesh),
        mesh=mesh,
        in_specs=(
            rows,
            rows,
            P(("dp", "seq"), None),
            P(("dp", "seq")),
            P(),
            columns,
            columns,
            columns,
            columns,
            P("tensor", None),
            P(),
            columns,
            columns,
            P("tensor", None),
        ),
        out_specs=(
            rows,
            rows,
            P(),
            P("dp", "tensor"),
            P("dp", "tensor"),
            P("dp", "tensor"),
            P(),
            P("tensor", "dp"),
            P(),
            P("dp", "tensor"),
            P("dp", "tensor"),
            P("tensor", "dp"),
        ),
        check_vma=False,
    )
```

```python
import functools
import math

import jax
import jax.numpy as jnp
from jax import lax
from jax.experimental import pallas as pl
from jax.experimental.pallas import tpu as pltpu
from jax.sharding import PartitionSpec as P

steps_at = (1, 2, 3, 4, 5, 6, 7, 8, 12, 16, 23, 32, 46, 64, 91)
eps_norm = 1e-06
masked_score = -1e30
q_block = 256
band_half = 128
low = jnp.bfloat16
wide = jnp.float32
hint = pl.CostEstimate(flops=1000, bytes_accessed=1000, transcendentals=0)


def dot(a, b, ca, cb):
    return lax.dot_general(a, b, (((ca,), (cb,)), ((), ())), preferred_element_type=wide)


def after(value, *first):
    return lax.optimization_barrier((value, *first))[0]


def front_kernel(
    share, x_h, g_h, wq_h, wk_h, wv_h, wo_h, lengths, valid, bias, gain1_row, gain2_row,
    x_out, g_own, g_oth, g_late, wo_out, w_t_out, xn1_out, qkv_out, mixed_out, probs_h, hres_out, xn2,
    scale1, scale2, gain1, gain2,
    x_in, g_in, w, w_t, xn1, qkv, mixed, hres,
    facts_src, facts, p_buf, table, sx, rx, seg_k, seg_q, send_sems, recv_sems, load_sems,
):
    s = lax.axis_index("seq")
    y = lax.axis_index("tensor")
    c = s % 2
    m = s // 2
    width, half_len = x_in.shape
    length = 2 * half_len
    heads, buckets = bias.shape
    inner = mixed.shape[0]
    dim = inner // heads
    piece = 64
    pieces = width // piece
    mesh_id = dict(device_id_type=pl.DeviceIdType.MESH)
    to_core = {"seq": 2 * m + 1 - c}
    to_swap = {"seq": 2 * m + 1 - c, "tensor": 1 - y}

    def side(i, size):
        return pl.ds(pl.multiple_of(i * size, 128), size)

    my_half = side(c, half_len)
    other_half = side(1 - c, half_len)

    def move(k, src, dst, who):
        return pltpu.make_async_remote_copy(
            src_ref=src, dst_ref=dst, send_sem=send_sems.at[k], recv_sem=recv_sems.at[k], device_id=who, **mesh_id
        )

    to_second = {"seq": 2 * m + y, "tensor": 1 - c}

    named = [(x_h, x_in)] + [
        (src, w.at[pl.ds(i * inner, inner)]) for i, src in enumerate((wq_h, wk_h, wv_h, wo_h))
    ]
    half_cols = half_len // 2
    halves = [pl.ds(h * half_cols, half_cols) for h in range(2)]
    move_x = [move((1, 15)[h], x_h.at[:, halves[h]], x_in.at[:, halves[h]], to_swap) for h in range(2)]
    moves = []
    z = lax.axis_index("dp")
    rows = inner // 2

    def half_of(ref, i, k):
        return ref.at[pl.ds(pl.multiple_of(i * inner + k * rows, rows), rows)]

    fetched, passed_z, passed_x = [], [], []
    for i, src in enumerate((wq_h, wk_h, wv_h, wo_h)):
        if share:
            fetched.append(move(2, half_of(src, 0, m), half_of(w, i, m), to_swap))
            part = half_of(w, (z + 4 - i) % 4, m)
            passed_x.append(move(10 + i, part, part, {"seq": 2 * (1 - m) + c}))
            if i < 3:
                passed_z.append(move(3 + i if i else 14, part, part, {"dp": (z + 1) % 4}))
        else:
            moves.append(move(2 + i, src, w.at[pl.ds(i * inner, inner)], to_swap))
    loads = [pltpu.make_async_copy(src, dst, load_sems.at[1 + i]) for i, (src, dst) in enumerate(named)]
    move_facts = move(0, facts_src, facts, to_swap)
    move_g = move(6, g_in, g_own, to_swap)
    early = g_oth.shape[1]
    second_g = move(9, g_in.at[:, pl.ds(0, early)], g_oth, to_second)
    to = lambda k, src, dst: pltpu.make_async_copy(src, dst, load_sems.at[k])
    keep_late = to(16, g_in.at[:, pl.ds(early, half_len - early)], g_late)
    load_g = pltpu.make_async_copy(g_h, g_in, load_sems.at[0])
    keep_g = pltpu.make_async_copy(g_in, g_own, load_sems.at[6])
    stores = [
        pltpu.make_async_copy(src, dst, load_sems.at[9 + i])
        for i, (src, dst) in enumerate(
            ((x_in, x_out), (w.at[pl.ds(3 * inner, inner)], wo_out), (w_t, w_t_out), (xn1, xn1_out), (qkv, qkv_out),
             (mixed, mixed_out), (hres, hres_out))
        )
    ]

    def pass_on(i):
        if not share:
            return

        @pl.when(c != y)
        def _():
            if i:
                passed_z[i - 1].wait_recv()
            else:
                fetched[0].wait_recv()
            if i < 3:
                passed_z[i].start()
            passed_x[i].start()

    my_parts = [pl.ds(pl.multiple_of(c * half_len + h * half_cols, 128), half_cols) for h in range(2)]
    core_one = [move((7, 16)[h], xn1.at[:, my_parts[h]], xn1.at[:, my_parts[h]], to_core) for h in range(2)]
    core_two = move(8, sx, rx, to_core)

    load_g.start()
    for h in range(heads):
        for b in range(buckets):
            at = h * buckets + b
            facts_src[at : at + 1, :] = jnp.full((1, 128), bias[h, b], wide)
    end = jnp.int32(0)
    at = heads * buckets
    for i in range(4):
        end = end + lengths[0, i]
        facts_src[at + i : at + i + 1, :] = jnp.full((1, 128), end.astype(wide), wide)
    facts_src[at + 4 : at + 5, :] = jnp.full((1, 128), valid[0].astype(wide), wide)

    barrier = pltpu.get_barrier_semaphore()
    greet = [to_core, to_swap, {"tensor": 1 - y}]
    if share:
        greet += [{"seq": 2 * (1 - m) + c}, {"dp": (z + 1) % 4}, {"dp": (z + 3) % 4}]
    for who in greet:
        pl.semaphore_signal(barrier, inc=1, device_id=who, **mesh_id)
    pl.semaphore_wait(barrier, len(greet))

    @pl.when(c != y)
    def _():
        move_facts.start()
        for i, each in enumerate(fetched):
            pl.when(z == i)(each.start)
        for each in move_x + moves:
            each.start()

    @pl.when(c == y)
    def _():
        for each in loads:
            each.start()
        facts[...] = facts_src[...]

    load_g.wait()
    live = lax.broadcasted_iota(jnp.int32, (piece, half_len), 1) + y * half_len < valid[0]

    def mask(i, carry):
        at = pl.ds(pl.multiple_of(i * piece, piece), piece)
        g_in[at, :] = jnp.where(live, g_in[at, :].astype(wide), 0.0).astype(low)
        return carry

    lax.fori_loop(0, pieces, mask, 0)

    @pl.when(c != y)
    def _():
        move_g.start()

    @pl.when(c == y)
    def _():
        keep_g.start()

    second_g.start()
    keep_late.start()
    pass_on(0)
    gain1[...] = jnp.broadcast_to(gain1_row[...].astype(wide)[None, :], (128, width)).T
    gain2[...] = jnp.broadcast_to(gain2_row[...].astype(wide)[None, :], (128, width)).T

    pass_on(1)

    @pl.when(c != y)
    def _():
        move_facts.wait_recv()

    at = heads * buckets

    def segments(positions):
        count = jnp.zeros(positions.shape, wide)
        for i in range(4):
            count = count + jnp.where(positions >= facts[at + i : at + i + 1, :], 1.0, 0.0)
        return jnp.where(positions < facts[at + 4 : at + 5, :], count, 4.0)

    seg_k[...] = segments(lax.broadcasted_iota(jnp.int32, (length, 128), 0).astype(wide))
    for i in range(length // 128):
        positions = (lax.broadcasted_iota(jnp.int32, (8, 128), 1) + i * 128).astype(wide)
        seg_q[:, i * 128 : (i + 1) * 128] = segments(positions)
    pass_on(2)
    reach = length - q_block
    near_rows = q_block + 2 * band_half
    d = (
        lax.broadcasted_iota(jnp.int32, (near_rows, 128), 0)
        - lax.broadcasted_iota(jnp.int32, (near_rows, 128), 1)
        - band_half
    )
    far_rows = reach - band_half
    for h in range(heads):

        def value(b, h=h):
            return facts[h * buckets + b : h * buckets + b + 1, :]

        for i in range(q_block // 128):
            offset = d - i * 128
            n = jnp.abs(offset)
            before = jnp.broadcast_to(value(0), n.shape)
            later = jnp.broadcast_to(value(16), n.shape)
            for number, step in enumerate(steps_at):
                reached = n >= step
                before = jnp.where(reached, value(number + 1), before)
                later = jnp.where(reached, value(number + 17), later)
            col = pl.ds(i * 128, 128)
            table[h, pl.ds(far_rows, near_rows), col] = jnp.where(offset > 0, later, before)
            table[h, pl.ds(0, far_rows), col] = jnp.broadcast_to(value(15), (far_rows, 128))
            table[h, pl.ds(far_rows + near_rows, far_rows), col] = jnp.broadcast_to(value(31), (far_rows, 128))

    def norm(read, gain, scale, cols, write):
        size = cols.size

        def first(i, total):
            v = read(pl.ds(pl.multiple_of(i * piece, piece), piece))
            return total + jnp.sum(v * v, axis=0, keepdims=True)

        total = lax.fori_loop(0, pieces, first, jnp.zeros((1, size), wide))
        scale[:, cols] = lax.rsqrt(total * (1.0 / width) + eps_norm)

        def second(i, carry):
            at = pl.ds(pl.multiple_of(i * piece, piece), piece)
            spread = jnp.concatenate([gain[at, :]] * (size // 128), axis=1)
            write(at, (read(at) * scale[:, cols] * spread).astype(low))
            return carry

        lax.fori_loop(0, pieces, second, 0)

    def arrived(i):
        @pl.when(c != y)
        def _():
            if not share:
                moves[i - 1].wait_recv()

        @pl.when(c == y)
        def _():
            loads[i].wait()

    pass_on(3)
    for h in range(2):

        @pl.when(c != y)
        def _(h=h):
            move_x[h].wait_recv()

        if h == 0:

            @pl.when(c == y)
            def _():
                loads[0].wait()

        def write_one(at, value, h=h):
            xn1[at, my_parts[h]] = value

        norm(lambda at, h=h: x_in[at, halves[h]].astype(wide), gain1, scale1, halves[h], write_one)
        core_one[h].start()
    stores[0].start()
    if share:

        @pl.when(c != y)
        def _():
            for each in passed_x:
                each.wait_recv()

    for each in core_one:
        each.wait_recv()
    stores[3].start()
    for i in range(3):
        arrived(1 + i)
        qkv[i * inner : (i + 1) * inner, :] = dot(w[i * inner : (i + 1) * inner, :], xn1[...], 1, 0).astype(low)

    stores[4].start()

    blocks = length // q_block

    turns = heads * blocks // 2

    def turn(i):
        its = 1 - c + (i // turns) * (2 * c - 1)
        return i % heads, its * (blocks // 2) + (i % turns) // heads

    def store(i):
        h, b = turn(i)
        return pltpu.make_async_copy(p_buf.at[i % 2], probs_h.at[h, :, side(b, q_block)], load_sems.at[7 + i % 2])

    def block(i, carry):
        h, b = turn(i)
        at = side(b, q_block)
        rows = lambda part: pl.ds(pl.multiple_of((part * heads + h) * dim, dim), dim)
        first = pl.multiple_of(reach - b * q_block, q_block)
        scores = dot(qkv[rows(1), :], qkv[rows(0), at], 0, 0) + table[h, pl.ds(first, length), :]
        keys = jnp.concatenate([seg_k[...]] * (q_block // 128), axis=1)
        scores = jnp.where(keys == seg_q[0:1, at], scores, masked_score)
        raised = jnp.exp(scores - jnp.max(scores, axis=0, keepdims=True))
        probs = (raised * (1.0 / jnp.sum(raised, axis=0, keepdims=True))).astype(low)

        @pl.when(i >= 2)
        def _():
            store(i - 2).wait()

        p_buf[i % 2] = probs
        store(i).start()
        mixed[rows(0), at] = dot(qkv[rows(2), :], probs, 1, 0).astype(low)
        return carry

    lax.fori_loop(0, turns, block, 0)
    arrived(4)
    stores[1].start()
    out_w = w[3 * inner :, :]
    sx[...] = dot(out_w, mixed[:, other_half], 0, 0).astype(low)
    core_two.start()
    w_t[...] = w[: 3 * inner, :].T
    stores[2].start()
    lax.fori_loop(turns, 2 * turns, block, 0)
    stores[5].start()
    hres[...] = dot(out_w, mixed[:, my_half], 0, 0)
    core_two.wait_recv()

    def add(i, carry):
        at = pl.ds(pl.multiple_of(i * piece, piece), piece)
        hres[at, :] += x_in[at, :].astype(wide) + rx[at, :].astype(wide)
        return carry

    lax.fori_loop(0, pieces, add, 0)

    stores[6].start()

    def write_two(at, value):
        xn2[at, :] = value

    norm(lambda at: hres[at, :], gain2, scale2, pl.ds(0, half_len), write_two)
    last = heads * blocks
    store(last - 2).wait()
    store(last - 1).wait()
    for each in (*core_one, core_two):
        each.wait_send()

    @pl.when(c != y)
    def _():
        move_facts.wait_send()
        if share:
            fetched[0].wait_send()
        for each in move_x + moves + passed_z + passed_x:
            each.wait_send()
        move_g.wait()

    @pl.when(c == y)
    def _():
        keep_g.wait()

    second_g.wait()
    keep_late.wait()
    for each in stores:
        each.wait()


def front(x, g, weights, lengths, valid, bias, gain_one, gain_two, share):
    width, half_len = x.shape
    length = 2 * half_len
    heads = bias.shape[0]
    inner = weights[0].shape[0]
    hbm = pl.BlockSpec(memory_space=pl.ANY)
    vmem = pl.BlockSpec(memory_space=pltpu.VMEM)
    smem = pl.BlockSpec(memory_space=pltpu.SMEM)
    sds = lambda kind, *shape: jax.ShapeDtypeStruct(shape, kind)
    facts = pltpu.VMEM((heads * bias.shape[1] + 8, 128), wide)
    b16 = lambda *shape: pltpu.VMEM(shape, low)
    return pl.pallas_call(
        functools.partial(front_kernel, share),
        in_specs=[hbm] * 6 + [smem] * 3 + [vmem] * 2,
        out_specs=[hbm] * 11 + [vmem] * 5,
        out_shape=[
            sds(low, width, half_len),
            sds(low, width, half_len),
            sds(low, width, half_len - 128),
            sds(low, width, 128),
            sds(low, inner, width),
            sds(low, width, 3 * inner),
            sds(low, width, length),
            sds(low, 3 * inner, length),
            sds(low, inner, length),
            sds(low, heads, length, length),
            sds(wide, width, half_len),
            sds(low, width, half_len),
            sds(wide, 1, half_len),
            sds(wide, 1, half_len),
            sds(wide, width, 128),
            sds(wide, width, 128),
        ],
        scratch_shapes=[
            b16(width, half_len),
            b16(width, half_len),
            b16(4 * inner, width),
            b16(width, 3 * inner),
            b16(width, length),
            b16(3 * inner, length),
            b16(inner, length),
            pltpu.VMEM((width, half_len), wide),
            facts,
            facts,
            b16(2, length, q_block),
            pltpu.VMEM((heads, 2 * length - q_block, q_block), wide),
            b16(width, half_len),
            b16(width, half_len),
            pltpu.VMEM((length, 128), wide),
            pltpu.VMEM((8, length), wide),
            pltpu.SemaphoreType.DMA((17,)),
            pltpu.SemaphoreType.DMA((17,)),
            pltpu.SemaphoreType.DMA((17,)),
        ],
        compiler_params=pltpu.CompilerParams(vmem_limit_bytes=60 << 20, collective_id=2, has_side_effects=True),
        cost_estimate=hint,
        name="front_all",
    )(x, g, *weights, lengths, valid, bias, gain_one, gain_two)


def attn_bwd_kernel(length, q_ref, k_ref, v_ref, go_ref, o_ref, p_ref, gq_ref, gk_ref, gv_ref, gb_ref, k_acc, v_acc, sums):
    block = pl.program_id(1)
    reach = length - q_block

    @pl.when(block == 0)
    def _():
        k_acc[...] = jnp.zeros_like(k_acc)
        v_acc[...] = jnp.zeros_like(v_acc)
        sums[...] = jnp.zeros_like(sums)

    probs = p_ref[0]
    go = go_ref[...]
    inner = jnp.sum(go.astype(wide) * o_ref[...].astype(wide), axis=0, keepdims=True)
    scores = probs.astype(wide) * (dot(v_ref[...], go, 0, 0) - inner)
    first = pl.multiple_of(reach - block * q_block, q_block)
    sums[pl.ds(first, length), :] += scores
    scores = scores.astype(low)
    gq_ref[...] = dot(k_ref[...], scores, 1, 0).astype(low)
    k_acc[...] += dot(q_ref[...], scores, 1, 1)
    v_acc[...] += dot(go, probs, 1, 1)

    @pl.when(block == pl.num_programs(1) - 1)
    def _():
        gk_ref[...] = k_acc[...].astype(low)
        gv_ref[...] = v_acc[...].astype(low)
        rows = q_block + 2 * band_half
        d = (
            lax.broadcasted_iota(jnp.int32, (rows, q_block), 0)
            - lax.broadcasted_iota(jnp.int32, (rows, q_block), 1)
            - band_half
        )
        n = jnp.abs(d)
        near = sums[reach - band_half : reach + q_block + band_half, :]
        far_before = jnp.sum(sums[: reach - band_half, :], axis=0, keepdims=True)
        far_after = jnp.sum(sums[reach + q_block + band_half :, :], axis=0, keepdims=True)
        bucket = jnp.zeros((rows, q_block), jnp.int32)
        for step in steps_at:
            bucket = bucket + jnp.where(n >= step, 1, 0)
        bucket = bucket + jnp.where(d > 0, 16, 0)
        for b in range(32):
            total = jnp.sum(jnp.where(bucket == b, near, 0.0), axis=0, keepdims=True)
            if b == 15:
                total = total + far_before
            if b == 31:
                total = total + far_after
            gb_ref[0, b : b + 1, :] = total


def attn_backward(qkv, grad_mixed, mixed, probs):
    width, length = qkv.shape
    heads = probs.shape[0]
    dim = width // (3 * heads)
    blocks = length // q_block
    half = pl.BlockSpec((dim, q_block), lambda h, b: (h, b))
    whole = pl.BlockSpec((dim, length), lambda h, b: (h, 0))
    gq, gk, gv, gb = pl.pallas_call(
        functools.partial(attn_bwd_kernel, length),
        grid=(heads, blocks),
        in_specs=[
            half,
            pl.BlockSpec((dim, length), lambda h, b: (heads + h, 0)),
            pl.BlockSpec((dim, length), lambda h, b: (2 * heads + h, 0)),
            half,
            half,
            pl.BlockSpec((1, length, q_block), lambda h, b: (h, 0, b)),
        ],
        out_specs=[half, whole, whole, pl.BlockSpec((1, 32, q_block), lambda h, b: (h, 0, 0))],
        out_shape=[
            jax.ShapeDtypeStruct((heads * dim, length), low),
            jax.ShapeDtypeStruct((heads * dim, length), low),
            jax.ShapeDtypeStruct((heads * dim, length), low),
            jax.ShapeDtypeStruct((heads, 32, q_block), wide),
        ],
        scratch_shapes=[
            pltpu.VMEM((dim, length), wide),
            pltpu.VMEM((dim, length), wide),
            pltpu.VMEM((2 * length - q_block, q_block), wide),
        ],
        compiler_params=pltpu.CompilerParams(vmem_limit_bytes=48 << 20),
        cost_estimate=hint,
        name="attn_backward",
    )(qkv, qkv, qkv, grad_mixed, mixed, probs)
    return jnp.concatenate([gq, gk, gv], axis=0), jnp.sum(gb, axis=2).T


def ffn_kernel(
    x_ref, go_ref, gr_h0, hres_h, g_late, gate_w, up_w, down_w,
    hid_ref, pair_ref, xr_h, gr_h, out_h, out_r_h, gx_h, late_h,
    xs, gs, out_acc, gx_acc, x_in, g_in, gx_out, gx_in, out_v, gx_v, gr_ref, hres_ref, sems, store_sems,
):
    chunk = pl.program_id(0)
    tile = pl.program_id(1)
    size = xs.shape[0]
    mesh_id = dict(device_id_type=pl.DeviceIdType.MESH)
    s = lax.axis_index("seq")
    y = lax.axis_index("tensor")
    c = s % 2
    to_y = {"tensor": 1 - y}
    to_second = {"seq": s - c + y, "tensor": 1 - c}
    half = [pl.ds(0, size), pl.ds(size, size)]

    def move(k, src, dst, who):
        return pltpu.make_async_remote_copy(
            src_ref=src, dst_ref=dst, send_sem=sems.at[k], recv_sem=sems.at[4 + k], device_id=who, **mesh_id
        )

    send_x = [move(h, x_ref.at[:, half[h]], x_in.at[h], to_y) for h in range(2)]
    send_g = move(2, g_late, g_in, to_second)
    back = gx_in.shape[1]
    send_gx = move(3, gx_out.at[0, :, pl.ds(0, back)], gx_in, to_y)
    begun = g_in.shape[1]
    to = lambda k, src, dst: pltpu.make_async_copy(src, dst, store_sems.at[k])
    store_x = [to(h, x_in.at[h], xr_h.at[:, half[h]]) for h in range(2)]
    store_out = [to(2 + h, out_v.at[h], out_h.at[:, half[h]]) for h in range(2)]
    store_out_r = [to(4 + h, out_v.at[2 + h], out_r_h.at[:, half[h]]) for h in range(2)]
    store_gx = [to(6 + h, gx_v.at[h], gx_h.at[:, half[h]]) for h in range(2)]
    store_late = [to(8 + h, gx_out.at[h], late_h.at[:, half[h]]) for h in range(2)]
    store_g = to(10, g_in, gr_h)
    load_h = to(11, hres_h, hres_ref)
    load_g = to(12, gr_h0, gr_ref)

    @pl.when(tile == 0)
    def _():
        out_acc[...] = jnp.zeros_like(out_acc)
        gx_acc[...] = jnp.zeros_like(gx_acc)

    @pl.when((tile == 0) & (chunk == 0))
    def _():
        load_h.start()
        load_g.start()
        barrier = pltpu.get_barrier_semaphore()
        for who in (to_y, {"seq": s + 1 - 2 * c}):
            pl.semaphore_signal(barrier, inc=1, device_id=who, **mesh_id)
        pl.semaphore_wait(barrier, 2)
        for each in (*send_x, send_g):
            each.start()

    for h in range(2):

        @pl.when((tile == 0) & (chunk == h))
        def _(h=h):
            xs[...] = x_ref[:, half[h]].T
            gs[...] = go_ref[:, half[h]].T

        @pl.when((tile == 0) & (chunk == 2 + h))
        def _(h=h):
            send_x[h].wait_recv()
            xs[...] = x_in[h].T
            store_x[h].start()
            if not h:
                load_g.wait()
            if h:
                gs[: size - begun, :] = gr_ref[:, size:].T
                send_g.wait_recv()
                gs[size - begun :, :] = g_in[...].T
                store_g.start()
            else:
                gs[...] = gr_ref[:, :size].T

    gate = dot(xs[...], gate_w[...], 1, 0)
    up = dot(xs[...], up_w[...], 1, 0)
    grad = dot(gs[...], down_w[...], 1, 0)
    c_gelu = math.sqrt(2.0 / math.pi)
    square = gate * gate
    t = jnp.tanh(c_gelu * gate * (1.0 + 0.044715 * square))
    part = 0.5 * (1.0 + t)
    gelu = gate * part
    slope = part + 0.5 * gate * (1.0 - t * t) * (c_gelu * (1.0 + 3 * 0.044715 * square))
    hid = (gelu * up).astype(low)
    gg = (grad * up * slope).astype(low)
    gu = (grad * gelu).astype(low)
    hid_ref[...] = hid
    pair_ref[0] = gg
    pair_ref[1] = gu
    out_acc[...] += dot(down_w[...], hid, 1, 1)
    gx_acc[...] += dot(gate_w[...], gg, 1, 1) + dot(up_w[...], gu, 1, 1)

    last = tile == pl.num_programs(1) - 1
    for h in range(2):

        @pl.when(last & (chunk == h))
        def _(h=h):
            if not h:
                load_h.wait()
            out_v[h] = (hres_ref[:, half[h]] + out_acc[...]).astype(low)
            store_out[h].start()
            gx_v[h] = gx_acc[...]
            if h:
                store_gx[h].start()

        @pl.when(last & (chunk == 2 + h))
        def _(h=h):
            out_v[2 + h] = out_acc[...].astype(low)
            store_out_r[h].start()
            gx_out[h] = gx_acc[...].astype(low)
            if not h:
                send_gx.start()
            store_late[h].start()

    @pl.when(last & (chunk == 3))
    def _():
        send_gx.wait_recv()
        gx_v[0, :, :back] += gx_in[...].astype(wide)
        store_gx[0].start()
        for each in (*send_x, send_g, send_gx):
            each.wait_send()
        for each in store_x + store_out + store_out_r + store_gx + store_late + [store_g]:
            each.wait()


def ffn(x, g_own, g_oth, hres, g_late, gate_w, up_w, down_w):
    width, tokens = x.shape
    hidden = gate_w.shape[1]
    tile, size = hidden // 2, tokens // 2
    begun = g_late.shape[1]
    hbm = pl.BlockSpec(memory_space=pl.ANY)
    full = pl.BlockSpec((width, tokens), lambda s, j: (0, 0), pipeline_mode=pl.Buffered(1))
    weight = pl.BlockSpec((width, tile), lambda s, j: (0, j))
    act_shape = jax.ShapeDtypeStruct((2 * tokens, hidden), low)
    tokens_of = lambda kind: jax.ShapeDtypeStruct((width, tokens), kind)
    return pl.pallas_call(
        ffn_kernel,
        grid=(4, hidden // tile),
        in_specs=[full, full, hbm, hbm, hbm, weight, weight, weight],
        out_specs=[
            pl.BlockSpec((size, tile), lambda s, j: (s, j)),
            pl.BlockSpec((2, size, tile), lambda s, j: (0, s, j)),
        ]
        + [hbm] * 6,
        out_shape=[act_shape, jax.ShapeDtypeStruct((2, 2 * tokens, hidden), low)]
        + [tokens_of(low), jax.ShapeDtypeStruct((width, begun), low)]
        + [tokens_of(kind) for kind in (low, low, wide, low)],
        scratch_shapes=[
            pltpu.VMEM((size, width), low),
            pltpu.VMEM((size, width), low),
            pltpu.VMEM((width, size), wide),
            pltpu.VMEM((width, size), wide),
            pltpu.VMEM((2, width, size), low),
            pltpu.VMEM((width, begun), low),
            pltpu.VMEM((2, width, size), low),
            pltpu.VMEM((width, 128), low),
            pltpu.VMEM((4, width, size), low),
            pltpu.VMEM((2, width, size), wide),
            pltpu.VMEM((width, tokens - begun), low),
            pltpu.VMEM((width, tokens), wide),
            pltpu.SemaphoreType.DMA((8,)),
            pltpu.SemaphoreType.DMA((13,)),
        ],
        compiler_params=pltpu.CompilerParams(vmem_limit_bytes=60 << 20, collective_id=0, has_side_effects=True),
        cost_estimate=hint,
        name="ffn_both_ways",
    )(x, g_own, g_oth, hres, g_late, gate_w, up_w, down_w)


def weight_grad_kernel(core_ref, own_ref, oth_ref, right_ref, *refs):
    tokens = own_ref.shape[1]
    total = dot(own_ref[...], right_ref[:tokens, :], 1, 0) + dot(oth_ref[...], right_ref[tokens:, :], 1, 0)
    if len(refs) == 2:
        total = total + refs[0][...].astype(wide)
    refs[-1][...] = total.astype(low)


def weight_grad(own, oth, right, core, got=None):
    width, tokens = own.shape
    columns = right.shape[1] // 2
    blocks = 4
    rows = width // blocks
    left = pl.BlockSpec((rows, tokens), lambda i, core_ref: (i, 0))
    out = pl.BlockSpec((rows, columns), lambda i, core_ref: (i, 0))
    args = [own, oth, right] + ([] if got is None else [got])
    return pl.pallas_call(
        weight_grad_kernel,
        grid_spec=pltpu.PrefetchScalarGridSpec(
            num_scalar_prefetch=1,
            grid=(blocks,),
            in_specs=[
                left,
                left,
                pl.BlockSpec((2 * tokens, columns), lambda i, core_ref: (0, core_ref[0]), pipeline_mode=pl.Buffered(1)),
            ]
            + ([] if got is None else [out]),
            out_specs=out,
        ),
        out_shape=jax.ShapeDtypeStruct((width, columns), low),
        compiler_params=pltpu.CompilerParams(vmem_limit_bytes=40 << 20),
        cost_estimate=hint,
        name="weight_grad",
    )(core.reshape(1), *args)


def back_kernel(
    hid_h, pair_h, go_h, gr1_h, gr2_h, xo_h, xr_h, gx_h, hres_h, xin_h, probs_h, xn1_h, outp_h, outr_h, late_h,
    out_w, w_t, qkv, mixed, gain2, gain1, scale2, scale1,
    got_p, got_r, got_in, d_out, p_out, a_out, gin, small,
    r_core, xp, zd, zp, dx, bf, rx, ya, xa, za, late_in, sm_src, sm_in, send_sems, recv_sems, load_sems,
):
    s = lax.axis_index("seq")
    y = lax.axis_index("tensor")
    z = lax.axis_index("dp")
    c = s % 2
    m = s // 2
    width = xp.shape[0]
    rows = d_out.shape[0]
    columns = xp.shape[1]
    half_len = rx.shape[1]
    length = 2 * half_len
    heads = probs_h.shape[0]
    dim = mixed.shape[0] // heads
    zs = width // rows
    mesh_id = dict(device_id_type=pl.DeviceIdType.MESH)
    to_core = {"seq": 2 * m + 1 - c}
    to_x = {"seq": 2 * (1 - m) + c}
    to_y = {"tensor": 1 - y}
    to_z = {"dp": (z + 1) % zs}
    to_swap = {"seq": 2 * m + y, "tensor": c}
    to_back = {"seq": 2 * m + 1 - y, "tensor": c}

    def move(k, src, dst, who):
        return pltpu.make_async_remote_copy(
            src_ref=src, dst_ref=dst, send_sem=send_sems.at[k], recv_sem=recv_sems.at[k], device_id=who, **mesh_id
        )

    def load(k, src, dst):
        return pltpu.make_async_copy(src, dst, load_sems.at[k])

    def chunk(j):
        return pl.ds(pl.multiple_of(j * rows, rows), rows)

    def side(i, size):
        return pl.ds(pl.multiple_of(i * size, 128), size)

    order = [(z + zs - 1 - k) % zs for k in range(zs)]
    mine = side(c, columns)
    my_half = side(c, half_len)
    other_half = side(1 - c, half_len)
    cut = [(0, 192), (192, rows - 192)]

    def part(j, p):
        return pl.ds(pl.multiple_of(j * rows + cut[p][0], 16), cut[p][1])

    parts = [pl.ds(*each) for each in cut]

    late_from = half_len - late_in.shape[1]
    late = move(0, late_h.at[:, pl.ds(late_from, half_len - late_from)], late_in, to_y)
    swap_out = move(1, outp_h, got_p, to_swap)
    back_out = move(2, outr_h, got_r, to_back)
    both = range(2)
    steps = range(zs - 1)
    z_down = [
        [move(3 + 2 * t + p, zd.at[t - 1, parts[p]] if t else r_core.at[0, part(order[0], p)], zd.at[t, parts[p]], to_z) for p in both]
        for t in steps
    ]
    x_down = [move(9 + p, zd.at[2, parts[p]], dx.at[parts[p]], to_x) for p in both]
    core_down = [move(11 + p, d_out.at[parts[p], mine], d_out.at[parts[p], mine], to_core) for p in both]
    z_pair = [
        [move(13 + 2 * t + p, zp.at[t - 1, parts[p]] if t else r_core.at[2, part(order[0], p)], zp.at[t, parts[p]], to_z) for p in both]
        for t in steps
    ]
    x_pair_back = [move(19 + p, zp.at[2, parts[p]], p_out.at[m, parts[p], mine], to_x) for p in both]
    core_pair = [move(21 + p, p_out.at[m, parts[p], mine], p_out.at[m, parts[p], mine], to_core) for p in both]
    core_pair_back = [
        move(23 + p, p_out.at[1 - m, parts[p], mine], p_out.at[1 - m, parts[p], mine], to_core) for p in both
    ]
    core_branch = move(25, bf.at[:, my_half], bf.at[:, my_half], to_core)
    a_rows = xa.shape[1]
    my_rows = pl.ds(pl.multiple_of(m * a_rows, a_rows), a_rows)
    x_rows = pl.ds(pl.multiple_of((1 - m) * a_rows, a_rows), a_rows)
    x_attn = [move(26 + k, ya.at[j, x_rows], xa.at[j], to_x) for k, j in enumerate(order)]
    z_attn = [move(30 + t, za.at[t - 1] if t else ya.at[order[0], my_rows], za.at[t], to_z) for t in steps]
    x_attn_back = move(33, a_out.at[my_rows], a_out.at[my_rows], to_x)
    core_attn = move(34, a_out, a_out, to_core)
    swap_in = move(35, gin, got_in, to_swap)

    def x_pair(k):
        at = chunk((z + zs - 1 - k) % zs)
        return move(46 + k, r_core.at[1, at], xp.at[at], to_x)

    def meet():
        barrier = pltpu.get_barrier_semaphore()
        greet = [to_core, to_y, {"seq": 2 * m + 1 - c, "tensor": 1 - y}, to_x] + [{"dp": (z + i) % zs} for i in range(1, zs)]
        for who in greet:
            pl.semaphore_signal(barrier, inc=1, device_id=who, **mesh_id)
        pl.semaphore_wait(barrier, len(greet))
        late.start()

    def step_z_down(t, p):
        z_down[t - 1][p].wait_recv()
        at = parts[p]
        zd[t - 1, at, :] = (zd[t - 1, at, :].astype(wide) + r_core[0, part(order[t], p), :].astype(wide)).astype(low)
        (z_down[t][p] if t < zs - 1 else x_down[p]).start()

    def end_down(p):
        x_down[p].wait_recv()
        at = parts[p]
        d_out[at, mine] = (zd[2, at, :].astype(wide) + dx[at, :].astype(wide)).astype(low)
        core_down[p].start()

    def step_z_pair(t, p):
        if p == 0:
            x_pair(t).wait_recv()
        at = parts[p]
        term = r_core[2, part(order[t], p), :].astype(wide) + xp[part(order[t], p), :].astype(wide)
        if t:
            z_pair[t - 1][p].wait_recv()
            term = zp[t - 1, at, :].astype(wide) + term
            zp[t - 1, at, :] = term.astype(low)
        else:
            r_core[2, part(order[0], p), :] = term.astype(low)
        if t < zs - 1:
            z_pair[t][p].start()
        else:
            x_pair_back[p].start()
            p_out[m, at, mine] = term.astype(low)
            core_pair[p].start()

    def end_pair(p):
        x_pair_back[p].wait_recv()
        core_pair_back[p].start()

    def step_attn(t):
        @pl.when(c == y)
        def _():
            x_attn[t].wait_recv()
            term = ya[order[t], my_rows, :].astype(wide) + xa[order[t]].astype(wide)
            if t:
                z_attn[t - 1].wait_recv()
                za[t - 1] = (za[t - 1].astype(wide) + term).astype(low)
            else:
                ya[order[0], my_rows, :] = term.astype(low)
            if t < zs - 1:
                z_attn[t].start()
            else:
                a_out[my_rows, :] = za[zs - 2]
                x_attn_back.start()

    hops = [to_core, to_y, to_x, {"dp": z + 1 - 2 * (z % 2)}, {"dp": (z + 2) % zs}]
    exchange = [move(41 + i, sm_src.at[i], sm_in.at[i], who) for i, who in enumerate(hops)]

    def start_sum(i):
        sm_src[i] = small[...]
        exchange[i].start()

    def end_sum(i):
        exchange[i].wait_recv()
        small[...] = sm_src[i] + sm_in[i]

    def weights(r_buf, l_go, l_gr, l_xo, l_xr, s_buf):
        loads = [
            load(0, hid_h, r_buf.at[0]),
            load(1, go_h, l_go),
            load(2, gr1_h, l_gr.at[:, pl.ds(0, gr1_h.shape[1])]),
            load(3, gr2_h, l_gr.at[:, pl.ds(gr1_h.shape[1], gr2_h.shape[1])]),
            load(4, pair_h.at[1 - m], r_buf.at[1]),
            load(5, xo_h, l_xo),
            load(14, xr_h, l_xr),
        ]
        load_own = load(6, pair_h.at[m], r_buf.at[0])
        for each in loads:
            each.start()
        theirs = side(1 - c, columns)

        def core(i, k):
            at = chunk((z + zs - 1 - k) % zs)
            return move(50 + i * zs + k, s_buf.at[i % 2, at], r_core.at[i, at], to_core)

        def product(left_o, left_r, right, col, at):
            total = dot(left_o[at, :], right[:half_len, col], 1, 0)
            return total + dot(left_r[at, :], right[half_len:, col], 1, 0)

        def send_part(left_o, left_r, right, i, k):
            at = chunk((z + zs - 1 - k) % zs)
            s_buf[i % 2, at, :] = product(left_o, left_r, right, theirs, at).astype(low)
            core(i, k).start()

        def keep_part(left_o, left_r, right, i, k):
            at = chunk((z + zs - 1 - k) % zs)
            total = product(left_o, left_r, right, mine, at)
            core(i, k).wait_recv()
            r_core[i, at, :] = (total + r_core[i, at, :].astype(wide)).astype(low)

        def sent(i):
            def block(k, carry):
                core(i, k).wait_send()
                return carry

            lax.fori_loop(0, zs, block, 0)

        down = (l_go, l_gr, r_buf.at[0], 0)
        theirs_first = (l_xo, l_xr, r_buf.at[1], 1)
        own = (l_xo, l_xr, r_buf.at[0], 2)
        meet()
        for each in loads:
            each.wait()

        def first(k, carry):
            @pl.when(k < zs)
            def _():
                send_part(*down, k)
                send_part(*theirs_first, k)

            @pl.when(k > 0)
            def _():
                keep_part(*down, k - 1)

                @pl.when(k == 1)
                def _():
                    for each in z_down[0]:
                        each.start()

                keep_part(*theirs_first, k - 1)
                x_pair(k - 1).start()

            return carry

        lax.fori_loop(0, zs + 1, first, 0)
        load_own.start()
        step_z_down(1, 0)

        @pl.when(c != y)
        def _():
            swap_out.start()

        back_out.start()
        sent(0)
        load_own.wait()

        def second(k, carry):
            @pl.when(k == 2)
            def _():
                step_z_down(1, 1)

            @pl.when(k == zs)
            def _():
                step_z_pair(0, 0)
                step_z_pair(0, 1)
                step_z_down(2, 0)

            @pl.when(k < zs)
            def _():
                send_part(*own, k)

            @pl.when(k > 0)
            def _():
                keep_part(*own, k - 1)

            return carry

        lax.fori_loop(0, zs + 1, second, 0)
        sent(1)
        sent(2)

    hidden = hid_h.shape[1]
    left = pltpu.VMEM((width, half_len), low)
    pl.run_scoped(
        weights,
        pltpu.VMEM((2, length, hidden), low),
        left,
        left,
        left,
        left,
        pltpu.VMEM((2, width, columns), low),
    )

    def attention(gxv, hv, gov, p_buf, k_acc, v_acc, sums, gqkv, gm, xn1, sx, ga):
        loads = [load(7, gx_h, gxv), load(8, hres_h, hv), load(9, go_h, gov), load(10, xn1_h, xn1)]
        load_x = load(11, xin_h, gov)
        for each in loads:
            each.start()

        def probs_load(h, b, slot):
            return load(12 + slot, probs_h.at[h, :, side(b, q_block)], p_buf.at[slot])

        probs_load(0, 0, 0).start()
        lanes = half_len // 128
        piece = 64
        pieces = width // piece

        def fold(a):
            return sum(a[:, i * 128 : (i + 1) * 128] for i in range(lanes))

        def spread(a):
            return jnp.concatenate([a] * lanes, axis=1)

        def norm_backward(values, gain, scale, grad, store, row):
            def first(i, total):
                at = pl.ds(pl.multiple_of(i * piece, piece), piece)
                return total + jnp.sum(values(at) * (spread(gain[at, :]) * grad(at)), axis=0, keepdims=True)

            total = lax.fori_loop(0, pieces, first, jnp.zeros((1, half_len), wide))
            mean = total * scale[...] * (1.0 / width)

            def second(i, carry):
                at = pl.ds(pl.multiple_of(i * piece, piece), piece)
                g = grad(at)
                normed = values(at) * scale[...]
                store(at, scale[...] * (spread(gain[at, :]) * g - normed * mean))
                ga_part[at, :] = fold(g * normed)
                return carry

            lax.fori_loop(0, pieces, second, 0)
            small[row : row + 1, :] = jnp.sum(ga_part[...].T, axis=0, keepdims=True)

        ga_part = sums.at[:width, :128]
        small[...] = jnp.zeros_like(small)
        for each in loads[:3]:
            each.wait()
        late.wait_recv()

        def add_late(i, carry):
            at = pl.ds(pl.multiple_of(i * piece, piece), piece)
            gxv[at, late_from:] += late_in[at, :].astype(wide)
            return carry

        lax.fori_loop(0, pieces, add_late, 0)

        def store_hres(at, back):
            total = gov[at, :].astype(wide) + back
            gxv[at, :] = total
            bf[at, my_half] = total.astype(low)

        norm_backward(lambda at: hv[at, :], gain2, scale2, lambda at: gxv[at, :], store_hres, 0)
        core_branch.start()
        load_x.start()
        step_z_down(2, 1)
        core_branch.wait_recv()
        gm[...] = dot(out_w[...], bf[...], 1, 0).astype(low)

        reach = length - q_block
        blocks = length // q_block
        near_rows = q_block + 2 * band_half
        d = (
            lax.broadcasted_iota(jnp.int32, (near_rows, q_block), 0)
            - lax.broadcasted_iota(jnp.int32, (near_rows, q_block), 1)
            - band_half
        )
        for h in range(heads):
            head = pl.ds(h * dim, dim)
            k_rows = pl.ds((heads + h) * dim, dim)
            v_rows = pl.ds((2 * heads + h) * dim, dim)
            k_acc[...] = jnp.zeros_like(k_acc)
            v_acc[...] = jnp.zeros_like(v_acc)
            sums[...] = jnp.zeros_like(sums)

            def block(b, carry):
                slot = b % 2
                at = side(b, q_block)
                probs_load(h, b, slot).wait()

                @pl.when(b < blocks - 1)
                def _():
                    probs_load(h, b + 1, 1 - slot).start()

                if h < heads - 1:

                    @pl.when(b == blocks - 1)
                    def _():
                        probs_load(h + 1, 0, 1 - slot).start()

                probs = p_buf[slot]
                go = gm[head, at]
                inner = jnp.sum(go.astype(wide) * mixed[head, at].astype(wide), axis=0, keepdims=True)
                scores = probs.astype(wide) * (dot(qkv[v_rows, :], go, 0, 0) - inner)
                first = pl.multiple_of(reach - b * q_block, q_block)
                sums[pl.ds(first, length), :] += scores
                scores = scores.astype(low)
                gqkv[head, at] = dot(qkv[k_rows, :], scores, 1, 0).astype(low)
                k_acc[...] += dot(qkv[head, at], scores, 1, 1)
                v_acc[...] += dot(go, probs, 1, 1)
                return carry

            lax.fori_loop(0, blocks, block, 0)
            gqkv[k_rows, :] = k_acc[...].astype(low)
            gqkv[v_rows, :] = v_acc[...].astype(low)
            near = sums[reach - band_half : reach + q_block + band_half, :]
            n = jnp.abs(d)
            bucket = jnp.zeros((near_rows, q_block), jnp.int32)
            for step in steps_at:
                bucket = bucket + jnp.where(n >= step, 1, 0)
            bucket = bucket + jnp.where(d > 0, 16, 0)
            totals = []
            for b in range(32):
                total = jnp.sum(jnp.where(bucket == b, near, 0.0), axis=0, keepdims=True)
                if b == 15:
                    total = total + jnp.sum(sums[: reach - band_half, :], axis=0, keepdims=True)
                if b == 31:
                    total = total + jnp.sum(sums[reach + q_block + band_half :, :], axis=0, keepdims=True)
                totals.append(total)
            totals = jnp.concatenate(totals, axis=0)
            totals = jnp.concatenate([totals, jnp.zeros((96, q_block), wide)], axis=0)
            line = jnp.sum(totals.T, axis=0, keepdims=True)
            for side_c in range(2):
                row = 8 + side_c * heads + h
                small[row : row + 1, :128] = jnp.where(c == side_c, line, 0.0)
            if h == 0:
                step_z_pair(1, 0)
            if h == 1:
                step_z_down(3, 0)

        def input_grad(half, store):
            def block(i, carry):
                at = chunk(i)
                store(at, dot(w_t[at, :], gqkv[:, half], 1, 0))
                return carry

            lax.fori_loop(0, zs, block, 0)

        def store_sent(at, value):
            sx[at, :] = value.astype(low)

        core_x = move(36, sx, rx, to_core)
        loads[3].wait()
        y_attn = [
            move(37 + k, ga.at[j], ya.at[j], to_y) for k, j in enumerate(order)
        ]
        wide_cols = gqkv.shape[0]

        def weight_part(k):
            j = order[k]
            ga[j, :rows, :wide_cols] = dot(xn1[chunk(j), :], gqkv[...], 1, 1).astype(low)
            ga[j, :rows, wide_cols:] = dot(bf[chunk(j), :], mixed[...], 1, 1).astype(low)
            ga[j, rows:, :] = jnp.zeros((ga.shape[1] - rows, ga.shape[2]), low)
            pl.when(c != y)(y_attn[k].start)

        def store_own(at, value):
            hv[at, :] = value

        def store_in(at, back):
            gin[at, :] = (gxv[at, :] + back).astype(low)

        def step_y_attn(k):
            j = order[k]

            @pl.when(c == y)
            def _():
                y_attn[k].wait_recv()
                ya[j] = (ya[j].astype(wide) + ga[j].astype(wide)).astype(low)
                x_attn[k].start()

        weight_part(0)
        weight_part(1)
        weight_part(2)
        input_grad(other_half, store_sent)
        core_x.start()
        step_z_down(3, 1)
        step_z_pair(2, 0)
        step_z_pair(1, 1)
        input_grad(my_half, store_own)
        end_down(0)
        weight_part(3)
        step_y_attn(0)
        load_x.wait()
        core_x.wait_recv()
        norm_backward(
            lambda at: gov[at, :].astype(wide),
            gain1,
            scale1,
            lambda at: hv[at, :] + rx[at, :].astype(wide),
            store_in,
            1,
        )
        start_sum(0)
        end_down(1)
        step_z_pair(3, 0)
        step_y_attn(1)
        end_sum(0)
        start_sum(1)

        @pl.when(c != y)
        def _():
            swap_in.start()

        step_attn(0)
        step_z_pair(2, 1)
        step_y_attn(2)
        end_pair(0)
        step_attn(1)
        step_y_attn(3)
        end_sum(1)
        start_sum(2)
        core_x.wait_send()

        @pl.when(c != y)
        def _():
            for each in y_attn:
                each.wait_send()

    f32 = lambda *shape: pltpu.VMEM(shape, wide)
    b16 = lambda *shape: pltpu.VMEM(shape, low)
    pl.run_scoped(
        attention,
        f32(width, half_len),
        f32(width, half_len),
        b16(width, half_len),
        b16(2, length, q_block),
        f32(dim, length),
        f32(dim, length),
        f32(2 * length - q_block, q_block),
        b16(3 * heads * dim, length),
        b16(heads * dim, length),
        b16(width, length),
        b16(width, half_len),
        b16(*ya.shape),
    )

    step_z_pair(3, 1)
    end_sum(2)
    start_sum(3)
    step_attn(2)
    end_sum(3)
    start_sum(4)
    step_attn(3)
    end_sum(4)
    end_pair(1)

    @pl.when(c == y)
    def _():
        x_attn_back.wait_recv()
        core_attn.start()
        for each in (core_attn, x_attn_back, *x_attn, *z_attn):
            each.wait_send()

    @pl.when(c != y)
    def _():
        core_attn.wait_recv()
        swap_out.wait()
        swap_in.wait()

    back_out.wait()
    for each in core_down + core_pair + core_pair_back:
        each.wait()
    for each in [late, core_branch] + sum(z_down, []) + x_down + sum(z_pair, []) + x_pair_back:
        each.wait_send()
    for each in [x_pair(k) for k in range(zs)] + exchange:
        each.wait_send()


def back_all(
    hid, pair, g_own, g_oth, g_late, x_own, x_oth, gx, hres, x_in, probs, xn_one, out_first, out_oth, late,
    out_w, w_t, qkv, mixed, gain_two, gain_one, scale_two, scale_one, zs,
):
    width, half_len = g_own.shape
    length = 2 * half_len
    rows = width // zs
    columns = hid.shape[1] // 2
    heads = probs.shape[0]
    a_cols = (w_t.shape[1] + out_w.shape[0]) // 2
    a_len = -(-rows // 32) * 32
    hbm = pl.BlockSpec(memory_space=pl.ANY)
    vmem = pl.BlockSpec(memory_space=pltpu.VMEM)
    sds = lambda kind, *shape: jax.ShapeDtypeStruct(shape, kind)
    b16 = lambda *shape: pltpu.VMEM(shape, low)
    return pl.pallas_call(
        back_kernel,
        in_specs=[hbm] * 15 + [vmem] * 8,
        out_specs=[hbm] * 3 + [vmem] * 5,
        out_shape=[
            sds(low, width, half_len),
            sds(low, width, half_len),
            sds(low, width, half_len),
            sds(low, rows, 2 * columns),
            sds(low, 2, rows, 2 * columns),
            sds(low, a_len, 2 * a_cols),
            sds(low, width, half_len),
            sds(wide, 16, width),
        ],
        scratch_shapes=[
            b16(3, width, columns),
            b16(width, columns),
            b16(zs - 1, rows, columns),
            b16(zs - 1, rows, columns),
            b16(rows, columns),
            b16(width, length),
            b16(width, half_len),
            b16(zs, a_len, 2 * a_cols),
            b16(zs, a_len // 2, 2 * a_cols),
            b16(zs - 1, a_len // 2, 2 * a_cols),
            b16(width, half_len - 128),
            pltpu.VMEM((5, 16, width), wide),
            pltpu.VMEM((5, 16, width), wide),
            pltpu.SemaphoreType.DMA((62,)),
            pltpu.SemaphoreType.DMA((62,)),
            pltpu.SemaphoreType.DMA((15,)),
        ],
        compiler_params=pltpu.CompilerParams(vmem_limit_bytes=61 << 20, collective_id=1, has_side_effects=True),
        cost_estimate=hint,
        name="back_all",
    )(
        hid, pair, g_own, g_oth, g_late, x_own, x_oth, gx, hres, x_in, probs, xn_one, out_first, out_oth, late,
        out_w, w_t, qkv, mixed, gain_two, gain_one, scale_two, scale_one,
    )


def finish_kernel(
    d_h, p_h, a_h, own_in, got_in, own_out, got_out, oth_out, small,
    d_out, g_out, u_out, q_out, k_out, v_out, o_out, in_out, y_out, gain1_out, gain2_out, bias_out,
    w_in, w_out, a_in, i_in, i_out, y_in, sems,
):
    own = lax.axis_index("seq") % 2 == lax.axis_index("tensor")
    rows = w_in.shape[1]
    width = i_in.shape[0]
    copy = lambda k, src, dst: pltpu.make_async_copy(src, dst, sems.at[k])
    loads = [copy(0, d_h, w_in.at[0]), copy(1, p_h.at[0], w_in.at[1]), copy(2, p_h.at[1], w_in.at[2]), copy(3, a_h, a_in)]
    load_y = copy(4, oth_out, y_in.at[1])
    mine = [copy(5, own_in, i_in), copy(6, own_out, y_in.at[0])]
    theirs = [copy(5, got_in, i_in), copy(6, got_out, y_in.at[0])]
    stores = [copy(7 + i, w_out.at[i], out) for i, out in enumerate((d_out, g_out, u_out))]
    store_i = copy(10, i_out, in_out)
    store_y = copy(11, y_in.at[0], y_out)

    def start(which):
        @pl.when(own)
        def _():
            mine[which].start()

        @pl.when(jnp.logical_not(own))
        def _():
            theirs[which].start()

    loads[0].start()
    start(0)
    for each in loads[1:3]:
        each.start()
    start(1)
    load_y.start()
    loads[3].start()

    def piecewise(count, size, run):
        def step(i, carry):
            run(pl.ds(pl.multiple_of(i * size, size), size))
            return carry

        lax.fori_loop(0, count, step, 0)

    def widen(i):
        loads[i].wait()

        def run(at):
            w_out[i, at, :] = w_in[i, at, :].astype(wide)

        piecewise(rows // 16, 16, run)
        stores[i].start()

    widen(0)
    mine[0].wait()

    def run_in(at):
        i_out[at, :] = i_in[at, :].astype(wide)

    piecewise(width // 64, 64, run_in)
    store_i.start()
    widen(1)
    widen(2)
    mine[1].wait()
    load_y.wait()

    def run_y(at):
        y_in[0, at, :] = (y_in[0, at, :].astype(wide) + y_in[1, at, :].astype(wide)).astype(low)

    piecewise(width // 64, 64, run_y)
    store_y.start()
    loads[3].wait()
    inner = q_out.shape[0]
    for i, out in enumerate((q_out, k_out, v_out, o_out)):
        out[...] = a_in[:rows, i * inner : (i + 1) * inner].astype(wide).T
    gain1_out[...] = small[1, :]
    gain2_out[...] = small[0, :]
    bias_out[...] = small[8 : 8 + bias_out.shape[0], : bias_out.shape[1]]
    for each in stores + [store_i, store_y]:
        each.wait()


def finish(d, p, a, own_in, got_in, own_out, got_out, oth_out, small, inner, bias_shape):
    rows, hidden = d.shape
    width, half_len = own_in.shape
    hbm = pl.BlockSpec(memory_space=pl.ANY)
    vmem = pl.BlockSpec(memory_space=pltpu.VMEM)
    sds = lambda kind, *shape: jax.ShapeDtypeStruct(shape, kind)
    return pl.pallas_call(
        finish_kernel,
        in_specs=[hbm] * 8 + [vmem],
        out_specs=[hbm] * 3 + [vmem] * 4 + [hbm] * 2 + [vmem] * 3,
        out_shape=[sds(wide, rows, hidden)] * 3
        + [sds(wide, inner, rows)] * 4
        + [sds(wide, width, half_len), sds(low, width, half_len)]
        + [sds(wide, width)] * 2
        + [sds(wide, *bias_shape)],
        scratch_shapes=[
            pltpu.VMEM((3, rows, hidden), low),
            pltpu.VMEM((3, rows, hidden), wide),
            pltpu.VMEM(a.shape, low),
            pltpu.VMEM((width, half_len), low),
            pltpu.VMEM((width, half_len), wide),
            pltpu.VMEM((2, width, half_len), low),
            pltpu.SemaphoreType.DMA((12,)),
        ],
        compiler_params=pltpu.CompilerParams(vmem_limit_bytes=60 << 20),
        cost_estimate=hint,
        name="finish_all",
    )(d, p, a, own_in, got_in, own_out, got_out, oth_out, small)


def norm_back(values, scale, gain, grad):
    normed = values * scale
    pushed = gain * grad
    mean = jnp.mean(normed * pushed, axis=0, keepdims=True)
    return scale * (pushed - normed * mean), jnp.sum(grad * normed, axis=1)


class Moves:
    def __init__(self, mesh):
        self.nz = mesh.shape["dp"]
        self.nx = mesh.shape["seq"] // 2
        both = [(m, c, y) for m in range(self.nx) for c in range(2) for y in range(2)]
        at = lambda m, c, y: (m * 2 + c) * 2 + y
        self.swap_pairs = [(at(m, c, y), at(m, y, c)) for m, c, y in both if c != y]
        self.second_pairs = [(at(m, c, y), at(m, y, 1 - c)) for m, c, y in both]
        self.back_pairs = [(b, a) for a, b in self.second_pairs]
        self.ring_x = [(m * 2 + c, (m + 1) % self.nx * 2 + c) for m in range(self.nx) for c in range(2)]
        self.y = lax.axis_index("tensor")
        self.z = lax.axis_index("dp")
        s = lax.axis_index("seq")
        self.c = s % 2
        self.m = s // 2

    def swap(self, a):
        got = lax.ppermute(a, ("seq", "tensor"), self.swap_pairs)
        return jnp.where(self.c == self.y, a, got)

    def back(self, a):
        return lax.ppermute(a, ("seq", "tensor"), self.back_pairs)

    def core(self, a):
        return lax.ppermute(a, "seq", [(s, s ^ 1) for s in range(2 * self.nx)])

    def over_y(self, a):
        return lax.ppermute(a, "tensor", [(0, 1), (1, 0)])

    def over_x(self, a):
        return lax.ppermute(a, "seq", self.ring_x)

    def start_x(self, a):
        take = lax.dynamic_index_in_dim(a, (self.m + self.nx - 1) % self.nx, 1, False)
        return a, self.over_x(take)

    def finish_x(self, a, got, *first):
        take = lambda i: lax.dynamic_index_in_dim(a, i % self.nx, 1, False)
        got = after(got, *first)
        held = (got.astype(wide) + take(self.m + 2 * self.nx - 2).astype(wide)).astype(low)
        for t in range(2, self.nx):
            held = (self.over_x(held).astype(wide) + take(self.m + 2 * self.nx - 1 - t).astype(wide)).astype(low)
        return held

    def scatter_x(self, a):
        take = lambda i: lax.dynamic_index_in_dim(a, i % self.nx, 1, False)
        held = take(self.m + self.nx - 1)
        for t in range(1, self.nx):
            held = (self.over_x(held).astype(wide) + take(self.m + 2 * self.nx - 1 - t).astype(wide)).astype(low)
        return held

    def scatter_z(self, a):
        return lax.psum_scatter(a, "dp", scatter_dimension=0, tiled=True)

    def gather_x(self, piece):
        if self.nx == 2:
            over = self.over_x(piece)
            return jnp.where(
                self.m == 0, jnp.concatenate([piece, over], 0), jnp.concatenate([over, piece], 0)
            )
        groups = [[m * 2 + c for m in range(self.nx)] for c in range(2)]
        return lax.all_gather(piece, "seq", axis=0, tiled=True, axis_index_groups=groups)

    def gather_core(self, piece):
        there = self.core(piece)
        return jnp.where(
            self.c == 0, jnp.concatenate([piece, there], 1), jnp.concatenate([there, piece], 1)
        )

    def sum_everywhere(self, a):
        a = a + self.core(a)
        a = a + self.over_y(a)
        step = 1
        while step < self.nx:
            a = a + lax.ppermute(a, "seq", [(s, s ^ (2 * step)) for s in range(2 * self.nx)])
            step *= 2
        step = 1
        while step < self.nz:
            a = a + lax.ppermute(a, "dp", [(z, z ^ step) for z in range(self.nz)])
            step *= 2
        return a


def local(
    mesh,
    layer_in,
    out_grad,
    doc_lengths,
    valid_length,
    gain_attn,
    query_weight,
    key_weight,
    value_weight,
    position_bias,
    output_weight,
    gain_ffn,
    gate_weight,
    up_weight,
    down_weight,
):
    moves = Moves(mesh)
    half_len, _, width = layer_in.shape
    length = 2 * half_len
    heads = position_bias.shape[1]
    inner_width = query_weight.shape[1]
    y, c, m = moves.y, moves.c, moves.m

    flat = lambda a: a.reshape(half_len, width).T
    (
        x_in, g_own, g_oth, g_send, out_w, w_t, xn_one, qkv, mixed, probs, hres, xn_own, scale_one, scale_two, gain_one, gain_two
    ) = front(
        flat(layer_in),
        flat(out_grad),
        (query_weight.T, key_weight.T, value_weight.T, output_weight),
        doc_lengths,
        valid_length,
        position_bias.T,
        gain_attn,
        gain_ffn,
        moves.nx == 2 and moves.nz == 4,
    )
    hid, pair, xn_oth, g_late, out_first, out_oth, gx, late = ffn(
        xn_own, g_own, g_oth, hres, g_send, gate_weight, up_weight, down_weight.T
    )
    if moves.nx == 2 and moves.nz == 4:
        got_first, got_oth, got_in, sum_d, sum_p, sums, grad_in, small = back_all(
            hid, pair, g_own, g_oth, g_late, xn_own, xn_oth, gx, hres, x_in, probs, xn_one, out_first, out_oth, late,
            out_w, w_t, qkv, mixed, gain_two, gain_one, scale_two, scale_one, moves.nz,
        )
        sum_d, sum_g, sum_u, sum_q, sum_k, sum_v, sum_o, grad_in, out_y, gain_one_sum, gain_two_sum, bias_sum = finish(
            sum_d, sum_p, sums, grad_in, got_in, out_first, got_first, got_oth, small,
            inner_width, (2 * heads, position_bias.shape[0]),
        )
        return (
            out_y.T.reshape(half_len, 1, width),
            grad_in.T.reshape(half_len, 1, width),
            gain_one_sum,
            sum_q.T,
            sum_k.T,
            sum_v.T,
            bias_sum.T,
            sum_o,
            gain_two_sum,
            sum_g,
            sum_u,
            sum_d.T,
        )
    grad_gate, grad_up = pair[0], pair[1]
    gx = gx.at[:, 128:].add(moves.over_y(late)[:, 128:].astype(wide))
    g_oth = jnp.concatenate([g_oth, g_late], axis=1)
    qkv_w = w_t.T
    x_wide = x_in.astype(wide)
    gain_one, gain_two = gain_one[:, :1], gain_two[:, :1]

    def both_halves(own):
        other = moves.core(own)
        return jnp.where(
            c == 0, jnp.concatenate([own, other], 1), jnp.concatenate([other, own], 1)
        )

    def my_half(a):
        return lax.dynamic_slice_in_dim(a, c * half_len, half_len, 1)

    def other_half(a):
        return lax.dynamic_slice_in_dim(a, (1 - c) * half_len, half_len, 1)


    columns = hid.shape[1] // 2
    send_d = weight_grad(g_own, g_oth, hid, 1 - c)
    got_d = moves.core(send_d)
    send_g = weight_grad(xn_own, xn_oth, after(grad_gate, send_d), 1 - c)
    got_g = moves.core(send_g)
    send_u = weight_grad(xn_own, xn_oth, after(grad_up, send_g), 1 - c)
    got_u = moves.core(send_u)
    total_d = weight_grad(g_own, g_oth, after(hid, send_u), c, got_d)
    total_g = weight_grad(xn_own, xn_oth, after(grad_gate, total_d), c, got_g)
    total_u = weight_grad(xn_own, xn_oth, after(grad_up, total_g), c, got_u)
    part_d = moves.scatter_z(total_d)
    x_sent = [moves.start_x(t.reshape(moves.nz, moves.nx, -1, columns)) for t in (total_g, total_u)]

    gx = after(gx, total_u)
    out_y = moves.swap(out_first).astype(wide) + moves.back(out_oth).astype(wide)

    back, grad_gain_two = norm_back(hres, scale_two, gain_two, gx)
    grad_hres = g_own.astype(wide) + back
    branch = both_halves(grad_hres.astype(low))

    grad_mixed = dot(out_w, branch, 1, 0).astype(low)
    grad_qkv, grad_bias = attn_backward(qkv, grad_mixed, mixed, probs)

    part_g = moves.finish_x(*x_sent[0], grad_qkv).reshape(-1, columns)
    sent = dot(qkv_w, other_half(after(grad_qkv, part_g)), 0, 0).astype(low)
    part_g = moves.scatter_z(part_g)
    got_x = moves.core(sent)
    grad_attn_w = jnp.concatenate(
        [dot(xn_one, after(grad_qkv, sent), 1, 1).astype(low), dot(branch, mixed, 1, 1).astype(low)], axis=1
    )
    gx = dot(qkv_w, my_half(after(grad_qkv, grad_attn_w)), 0, 0) + got_x.astype(wide)
    back, grad_gain_one = norm_back(x_wide, scale_one, gain_one, gx)
    grad_in = (grad_hres + back).astype(low)
    part_u = moves.scatter_z(moves.finish_x(*x_sent[1], grad_in).reshape(-1, columns))

    a_columns = grad_attn_w.shape[1] // 2
    chunks = grad_attn_w.reshape(moves.nz, moves.nx, -1, 2 * a_columns)

    def scatter_y(a):
        got = moves.over_y(lax.dynamic_slice_in_dim(a, (1 - y) * a_columns, a_columns, a.ndim - 1))
        kept = lax.dynamic_slice_in_dim(a, y * a_columns, a_columns, a.ndim - 1)
        return (kept.astype(wide) + got.astype(wide)).astype(low)

    half_z = moves.nz // 2
    part = jnp.concatenate(
        [moves.scatter_x(scatter_y(chunks[:half_z])), scatter_y(moves.scatter_x(chunks[half_z:]))], 0
    )
    piece = moves.gather_x(moves.scatter_z(part.reshape(-1, a_columns)))
    there = moves.over_y(piece)
    group = jnp.where(y == 0, jnp.concatenate([piece, there], 1), jnp.concatenate([there, piece], 1))
    sums = jnp.where(c == y, group, moves.core(group)).astype(wide)
    sum_q, sum_k, sum_v, sum_o = (
        sums[:, i * inner_width : (i + 1) * inner_width] for i in range(4)
    )
    grad_in = moves.swap(grad_in).astype(wide)

    if moves.nx == 2:
        part_d = (part_d.astype(wide) + moves.over_x(part_d).astype(wide)).astype(low)
    else:
        part_d = moves.gather_x(moves.scatter_x(part_d.reshape(1, moves.nx, -1, columns))[0])
    sum_d = moves.gather_core(part_d).astype(wide)
    sum_g = moves.gather_core(moves.gather_x(part_g)).astype(wide)
    sum_u = moves.gather_core(moves.gather_x(part_u)).astype(wide)

    bias_full = jnp.zeros((grad_bias.shape[0], 2 * heads), wide)
    bias_full = lax.dynamic_update_slice(bias_full, grad_bias, (jnp.int32(0), c * heads))
    early = moves.sum_everywhere(jnp.concatenate([grad_gain_two, bias_full.reshape(-1)]))
    gain_two_sum, bias_sum = early[:width], early[width:].reshape(bias_full.shape)
    gain_one_sum = moves.sum_everywhere(grad_gain_one)
    return (
        out_y.astype(low).T.reshape(half_len, 1, width),
        grad_in.T.reshape(half_len, 1, width),
        gain_one_sum,
        sum_q,
        sum_k,
        sum_v,
        bias_sum,
        sum_o.T,
        gain_two_sum,
        sum_g,
        sum_u,
        sum_d.T,
    )


def solution(mesh):
    rows = P("tensor", ("dp", "seq"), None)
    columns = P(None, "tensor")
    return jax.shard_map(
        functools.partial(local, mesh),
        mesh=mesh,
        in_specs=(
            rows,
            rows,
            P(("dp", "seq"), None),
            P(("dp", "seq")),
            P(),
            columns,
            columns,
            columns,
            columns,
            P("tensor", None),
            P(),
            columns,
            columns,
            P("tensor", None),
        ),
        out_specs=(
            rows,
            rows,
            P(),
            P("dp", "tensor"),
            P("dp", "tensor"),
            P("dp", "tensor"),
            P(),
            P("tensor", "dp"),
            P(),
            P("dp", "tensor"),
            P("dp", "tensor"),
            P("tensor", "dp"),
        ),
        check_vma=False,
    )
```

```python
import functools
import math

import jax
import jax.numpy as jnp
from jax import lax
from jax.experimental import pallas as pl
from jax.experimental.pallas import tpu as pltpu
from jax.sharding import PartitionSpec as P

steps_at = (1, 2, 3, 4, 5, 6, 7, 8, 12, 16, 23, 32, 46, 64, 91)
eps_norm = 1e-06
masked_score = -1e30
q_block = 256
band_half = 128
low = jnp.bfloat16
wide = jnp.float32
hint = pl.CostEstimate(flops=1000, bytes_accessed=1000, transcendentals=0)


def dot(a, b, ca, cb):
    return lax.dot_general(a, b, (((ca,), (cb,)), ((), ())), preferred_element_type=wide)


def after(value, *first):
    return lax.optimization_barrier((value, *first))[0]


def front_kernel(
    share, x_h, g_h, wq_h, wk_h, wv_h, wo_h, lengths, valid, bias, gain1_row, gain2_row,
    x_out, g_own, g_oth, g_late, wo_out, w_t_out, xn1_out, qkv_out, mixed_out, probs_h, hres_out, xn2,
    scale1, scale2, gain1, gain2,
    x_in, g_in, w, w_t, xn1, qkv, mixed, hres,
    facts_src, facts, p_buf, table, sx, rx, seg_k, seg_q, send_sems, recv_sems, load_sems,
):
    s = lax.axis_index("seq")
    y = lax.axis_index("tensor")
    c = s % 2
    m = s // 2
    width, half_len = x_in.shape
    length = 2 * half_len
    heads, buckets = bias.shape
    inner = mixed.shape[0]
    dim = inner // heads
    piece = 64
    pieces = width // piece
    mesh_id = dict(device_id_type=pl.DeviceIdType.MESH)
    to_core = {"seq": 2 * m + 1 - c}
    to_swap = {"seq": 2 * m + 1 - c, "tensor": 1 - y}

    def side(i, size):
        return pl.ds(pl.multiple_of(i * size, 128), size)

    my_half = side(c, half_len)
    other_half = side(1 - c, half_len)

    def move(k, src, dst, who):
        return pltpu.make_async_remote_copy(
            src_ref=src, dst_ref=dst, send_sem=send_sems.at[k], recv_sem=recv_sems.at[k], device_id=who, **mesh_id
        )

    to_second = {"seq": 2 * m + y, "tensor": 1 - c}

    named = [(x_h, x_in)] + [
        (src, w.at[pl.ds(i * inner, inner)]) for i, src in enumerate((wq_h, wk_h, wv_h, wo_h))
    ]
    half_cols = half_len // 2
    halves = [pl.ds(h * half_cols, half_cols) for h in range(2)]
    move_x = [move((1, 15)[h], x_h.at[:, halves[h]], x_in.at[:, halves[h]], to_swap) for h in range(2)]
    moves = []
    z = lax.axis_index("dp")
    rows = inner // 2

    def half_of(ref, i, k):
        return ref.at[pl.ds(pl.multiple_of(i * inner + k * rows, rows), rows)]

    fetched, passed_z, passed_x = [], [], []
    for i, src in enumerate((wq_h, wk_h, wv_h, wo_h)):
        if share:
            fetched.append(move(2, half_of(src, 0, m), half_of(w, i, m), to_swap))
            part = half_of(w, (z + 4 - i) % 4, m)
            passed_x.append(move(10 + i, part, part, {"seq": 2 * (1 - m) + c}))
            if i < 3:
                passed_z.append(move(3 + i if i else 14, part, part, {"dp": (z + 1) % 4}))
        else:
            moves.append(move(2 + i, src, w.at[pl.ds(i * inner, inner)], to_swap))
    loads = [pltpu.make_async_copy(src, dst, load_sems.at[1 + i]) for i, (src, dst) in enumerate(named)]
    move_facts = move(0, facts_src, facts, to_swap)
    move_g = move(6, g_in, g_own, to_swap)
    early = g_oth.shape[1]
    second_g = move(9, g_in.at[:, pl.ds(0, early)], g_oth, to_second)
    to = lambda k, src, dst: pltpu.make_async_copy(src, dst, load_sems.at[k])
    keep_late = to(16, g_in.at[:, pl.ds(early, half_len - early)], g_late)
    load_g = pltpu.make_async_copy(g_h, g_in, load_sems.at[0])
    keep_g = pltpu.make_async_copy(g_in, g_own, load_sems.at[6])
    stores = [
        pltpu.make_async_copy(src, dst, load_sems.at[9 + i])
        for i, (src, dst) in enumerate(
            ((x_in, x_out), (w.at[pl.ds(3 * inner, inner)], wo_out), (w_t, w_t_out), (xn1, xn1_out), (qkv, qkv_out),
             (mixed, mixed_out), (hres, hres_out))
        )
    ]

    def pass_on(i):
        if not share:
            return

        @pl.when(c != y)
        def _():
            if i:
                passed_z[i - 1].wait_recv()
            else:
                fetched[0].wait_recv()
            if i < 3:
                passed_z[i].start()
            passed_x[i].start()

    my_parts = [pl.ds(pl.multiple_of(c * half_len + h * half_cols, 128), half_cols) for h in range(2)]
    core_one = [move((7, 16)[h], xn1.at[:, my_parts[h]], xn1.at[:, my_parts[h]], to_core) for h in range(2)]
    core_two = move(8, sx, rx, to_core)

    load_g.start()
    for h in range(heads):
        for b in range(buckets):
            at = h * buckets + b
            facts_src[at : at + 1, :] = jnp.full((1, 128), bias[h, b], wide)
    end = jnp.int32(0)
    at = heads * buckets
    for i in range(4):
        end = end + lengths[0, i]
        facts_src[at + i : at + i + 1, :] = jnp.full((1, 128), end.astype(wide), wide)
    facts_src[at + 4 : at + 5, :] = jnp.full((1, 128), valid[0].astype(wide), wide)

    barrier = pltpu.get_barrier_semaphore()
    greet = [to_core, to_swap, {"tensor": 1 - y}]
    if share:
        greet += [{"seq": 2 * (1 - m) + c}, {"dp": (z + 1) % 4}, {"dp": (z + 3) % 4}]
    for who in greet:
        pl.semaphore_signal(barrier, inc=1, device_id=who, **mesh_id)
    pl.semaphore_wait(barrier, len(greet))

    @pl.when(c != y)
    def _():
        move_facts.start()
        for i, each in enumerate(fetched):
            pl.when(z == i)(each.start)
        for each in move_x + moves:
            each.start()

    @pl.when(c == y)
    def _():
        for each in loads:
            each.start()
        facts[...] = facts_src[...]

    load_g.wait()
    live = lax.broadcasted_iota(jnp.int32, (piece, half_len), 1) + y * half_len < valid[0]

    def mask(i, carry):
        at = pl.ds(pl.multiple_of(i * piece, piece), piece)
        g_in[at, :] = jnp.where(live, g_in[at, :].astype(wide), 0.0).astype(low)
        return carry

    lax.fori_loop(0, pieces, mask, 0)

    @pl.when(c != y)
    def _():
        move_g.start()

    @pl.when(c == y)
    def _():
        keep_g.start()

    second_g.start()
    keep_late.start()
    pass_on(0)
    gain1[...] = jnp.broadcast_to(gain1_row[...].astype(wide)[None, :], (128, width)).T
    gain2[...] = jnp.broadcast_to(gain2_row[...].astype(wide)[None, :], (128, width)).T

    pass_on(1)

    @pl.when(c != y)
    def _():
        move_facts.wait_recv()

    at = heads * buckets

    def segments(positions):
        count = jnp.zeros(positions.shape, wide)
        for i in range(4):
            count = count + jnp.where(positions >= facts[at + i : at + i + 1, :], 1.0, 0.0)
        return jnp.where(positions < facts[at + 4 : at + 5, :], count, 4.0)

    seg_k[...] = segments(lax.broadcasted_iota(jnp.int32, (length, 128), 0).astype(wide))
    for i in range(length // 128):
        positions = (lax.broadcasted_iota(jnp.int32, (8, 128), 1) + i * 128).astype(wide)
        seg_q[:, i * 128 : (i + 1) * 128] = segments(positions)
    pass_on(2)
    reach = length - q_block
    near_rows = q_block + 2 * band_half
    d = (
        lax.broadcasted_iota(jnp.int32, (near_rows, 128), 0)
        - lax.broadcasted_iota(jnp.int32, (near_rows, 128), 1)
        - band_half
    )
    far_rows = reach - band_half
    for h in range(heads):

        def value(b, h=h):
            return facts[h * buckets + b : h * buckets + b + 1, :]

        for i in range(q_block // 128):
            offset = d - i * 128
            n = jnp.abs(offset)
            before = jnp.broadcast_to(value(0), n.shape)
            later = jnp.broadcast_to(value(16), n.shape)
            for number, step in enumerate(steps_at):
                reached = n >= step
                before = jnp.where(reached, value(number + 1), before)
                later = jnp.where(reached, value(number + 17), later)
            col = pl.ds(i * 128, 128)
            table[h, pl.ds(far_rows, near_rows), col] = jnp.where(offset > 0, later, before)
            table[h, pl.ds(0, far_rows), col] = jnp.broadcast_to(value(15), (far_rows, 128))
            table[h, pl.ds(far_rows + near_rows, far_rows), col] = jnp.broadcast_to(value(31), (far_rows, 128))

    def norm(read, gain, scale, cols, write):
        size = cols.size

        def first(i, total):
            v = read(pl.ds(pl.multiple_of(i * piece, piece), piece))
            return total + jnp.sum(v * v, axis=0, keepdims=True)

        total = lax.fori_loop(0, pieces, first, jnp.zeros((1, size), wide))
        scale[:, cols] = lax.rsqrt(total * (1.0 / width) + eps_norm)

        def second(i, carry):
            at = pl.ds(pl.multiple_of(i * piece, piece), piece)
            spread = jnp.concatenate([gain[at, :]] * (size // 128), axis=1)
            write(at, (read(at) * scale[:, cols] * spread).astype(low))
            return carry

        lax.fori_loop(0, pieces, second, 0)

    def arrived(i):
        @pl.when(c != y)
        def _():
            if not share:
                moves[i - 1].wait_recv()

        @pl.when(c == y)
        def _():
            loads[i].wait()

    pass_on(3)
    for h in range(2):

        @pl.when(c != y)
        def _(h=h):
            move_x[h].wait_recv()

        if h == 0:

            @pl.when(c == y)
            def _():
                loads[0].wait()

        def write_one(at, value, h=h):
            xn1[at, my_parts[h]] = value

        norm(lambda at, h=h: x_in[at, halves[h]].astype(wide), gain1, scale1, halves[h], write_one)
        core_one[h].start()
    stores[0].start()
    if share:

        @pl.when(c != y)
        def _():
            for each in passed_x:
                each.wait_recv()

    for each in core_one:
        each.wait_recv()
    stores[3].start()
    for i in range(3):
        arrived(1 + i)
        qkv[i * inner : (i + 1) * inner, :] = dot(w[i * inner : (i + 1) * inner, :], xn1[...], 1, 0).astype(low)

    stores[4].start()

    blocks = length // q_block

    turns = heads * blocks // 2

    def turn(i):
        its = 1 - c + (i // turns) * (2 * c - 1)
        return i % heads, its * (blocks // 2) + (i % turns) // heads

    def store(i):
        h, b = turn(i)
        return pltpu.make_async_copy(p_buf.at[i % 2], probs_h.at[h, :, side(b, q_block)], load_sems.at[7 + i % 2])

    def block(i, carry):
        h, b = turn(i)
        at = side(b, q_block)
        rows = lambda part: pl.ds(pl.multiple_of((part * heads + h) * dim, dim), dim)
        first = pl.multiple_of(reach - b * q_block, q_block)
        scores = dot(qkv[rows(1), :], qkv[rows(0), at], 0, 0) + table[h, pl.ds(first, length), :]
        keys = jnp.concatenate([seg_k[...]] * (q_block // 128), axis=1)
        scores = jnp.where(keys == seg_q[0:1, at], scores, masked_score)
        raised = jnp.exp(scores - jnp.max(scores, axis=0, keepdims=True))
        probs = (raised * (1.0 / jnp.sum(raised, axis=0, keepdims=True))).astype(low)

        @pl.when(i >= 2)
        def _():
            store(i - 2).wait()

        p_buf[i % 2] = probs
        store(i).start()
        mixed[rows(0), at] = dot(qkv[rows(2), :], probs, 1, 0).astype(low)
        return carry

    lax.fori_loop(0, turns, block, 0)
    arrived(4)
    stores[1].start()
    out_w = w[3 * inner :, :]
    sx[...] = dot(out_w, mixed[:, other_half], 0, 0).astype(low)
    core_two.start()
    w_t[...] = w[: 3 * inner, :].T
    stores[2].start()
    lax.fori_loop(turns, 2 * turns, block, 0)
    stores[5].start()
    hres[...] = dot(out_w, mixed[:, my_half], 0, 0)
    core_two.wait_recv()

    def add(i, carry):
        at = pl.ds(pl.multiple_of(i * piece, piece), piece)
        hres[at, :] += x_in[at, :].astype(wide) + rx[at, :].astype(wide)
        return carry

    lax.fori_loop(0, pieces, add, 0)

    stores[6].start()

    def write_two(at, value):
        xn2[at, :] = value

    norm(lambda at: hres[at, :], gain2, scale2, pl.ds(0, half_len), write_two)
    last = heads * blocks
    store(last - 2).wait()
    store(last - 1).wait()
    for each in (*core_one, core_two):
        each.wait_send()

    @pl.when(c != y)
    def _():
        move_facts.wait_send()
        if share:
            fetched[0].wait_send()
        for each in move_x + moves + passed_z + passed_x:
            each.wait_send()
        move_g.wait()

    @pl.when(c == y)
    def _():
        keep_g.wait()

    second_g.wait()
    keep_late.wait()
    for each in stores:
        each.wait()


def front(x, g, weights, lengths, valid, bias, gain_one, gain_two, share):
    width, half_len = x.shape
    length = 2 * half_len
    heads = bias.shape[0]
    inner = weights[0].shape[0]
    hbm = pl.BlockSpec(memory_space=pl.ANY)
    vmem = pl.BlockSpec(memory_space=pltpu.VMEM)
    smem = pl.BlockSpec(memory_space=pltpu.SMEM)
    sds = lambda kind, *shape: jax.ShapeDtypeStruct(shape, kind)
    facts = pltpu.VMEM((heads * bias.shape[1] + 8, 128), wide)
    b16 = lambda *shape: pltpu.VMEM(shape, low)
    return pl.pallas_call(
        functools.partial(front_kernel, share),
        in_specs=[hbm] * 6 + [smem] * 3 + [vmem] * 2,
        out_specs=[hbm] * 11 + [vmem] * 5,
        out_shape=[
            sds(low, width, half_len),
            sds(low, width, half_len),
            sds(low, width, half_len - 128),
            sds(low, width, 128),
            sds(low, inner, width),
            sds(low, width, 3 * inner),
            sds(low, width, length),
            sds(low, 3 * inner, length),
            sds(low, inner, length),
            sds(low, heads, length, length),
            sds(wide, width, half_len),
            sds(low, width, half_len),
            sds(wide, 1, half_len),
            sds(wide, 1, half_len),
            sds(wide, width, 128),
            sds(wide, width, 128),
        ],
        scratch_shapes=[
            b16(width, half_len),
            b16(width, half_len),
            b16(4 * inner, width),
            b16(width, 3 * inner),
            b16(width, length),
            b16(3 * inner, length),
            b16(inner, length),
            pltpu.VMEM((width, half_len), wide),
            facts,
            facts,
            b16(2, length, q_block),
            pltpu.VMEM((heads, 2 * length - q_block, q_block), wide),
            b16(width, half_len),
            b16(width, half_len),
            pltpu.VMEM((length, 128), wide),
            pltpu.VMEM((8, length), wide),
            pltpu.SemaphoreType.DMA((17,)),
            pltpu.SemaphoreType.DMA((17,)),
            pltpu.SemaphoreType.DMA((17,)),
        ],
        compiler_params=pltpu.CompilerParams(vmem_limit_bytes=60 << 20, collective_id=2, has_side_effects=True),
        cost_estimate=hint,
        name="front_all",
    )(x, g, *weights, lengths, valid, bias, gain_one, gain_two)


def attn_bwd_kernel(length, q_ref, k_ref, v_ref, go_ref, o_ref, p_ref, gq_ref, gk_ref, gv_ref, gb_ref, k_acc, v_acc, sums):
    block = pl.program_id(1)
    reach = length - q_block

    @pl.when(block == 0)
    def _():
        k_acc[...] = jnp.zeros_like(k_acc)
        v_acc[...] = jnp.zeros_like(v_acc)
        sums[...] = jnp.zeros_like(sums)

    probs = p_ref[0]
    go = go_ref[...]
    inner = jnp.sum(go.astype(wide) * o_ref[...].astype(wide), axis=0, keepdims=True)
    scores = probs.astype(wide) * (dot(v_ref[...], go, 0, 0) - inner)
    first = pl.multiple_of(reach - block * q_block, q_block)
    sums[pl.ds(first, length), :] += scores
    scores = scores.astype(low)
    gq_ref[...] = dot(k_ref[...], scores, 1, 0).astype(low)
    k_acc[...] += dot(q_ref[...], scores, 1, 1)
    v_acc[...] += dot(go, probs, 1, 1)

    @pl.when(block == pl.num_programs(1) - 1)
    def _():
        gk_ref[...] = k_acc[...].astype(low)
        gv_ref[...] = v_acc[...].astype(low)
        rows = q_block + 2 * band_half
        d = (
            lax.broadcasted_iota(jnp.int32, (rows, q_block), 0)
            - lax.broadcasted_iota(jnp.int32, (rows, q_block), 1)
            - band_half
        )
        n = jnp.abs(d)
        near = sums[reach - band_half : reach + q_block + band_half, :]
        far_before = jnp.sum(sums[: reach - band_half, :], axis=0, keepdims=True)
        far_after = jnp.sum(sums[reach + q_block + band_half :, :], axis=0, keepdims=True)
        bucket = jnp.zeros((rows, q_block), jnp.int32)
        for step in steps_at:
            bucket = bucket + jnp.where(n >= step, 1, 0)
        bucket = bucket + jnp.where(d > 0, 16, 0)
        for b in range(32):
            total = jnp.sum(jnp.where(bucket == b, near, 0.0), axis=0, keepdims=True)
            if b == 15:
                total = total + far_before
            if b == 31:
                total = total + far_after
            gb_ref[0, b : b + 1, :] = total


def attn_backward(qkv, grad_mixed, mixed, probs):
    width, length = qkv.shape
    heads = probs.shape[0]
    dim = width // (3 * heads)
    blocks = length // q_block
    half = pl.BlockSpec((dim, q_block), lambda h, b: (h, b))
    whole = pl.BlockSpec((dim, length), lambda h, b: (h, 0))
    gq, gk, gv, gb = pl.pallas_call(
        functools.partial(attn_bwd_kernel, length),
        grid=(heads, blocks),
        in_specs=[
            half,
            pl.BlockSpec((dim, length), lambda h, b: (heads + h, 0)),
            pl.BlockSpec((dim, length), lambda h, b: (2 * heads + h, 0)),
            half,
            half,
            pl.BlockSpec((1, length, q_block), lambda h, b: (h, 0, b)),
        ],
        out_specs=[half, whole, whole, pl.BlockSpec((1, 32, q_block), lambda h, b: (h, 0, 0))],
        out_shape=[
            jax.ShapeDtypeStruct((heads * dim, length), low),
            jax.ShapeDtypeStruct((heads * dim, length), low),
            jax.ShapeDtypeStruct((heads * dim, length), low),
            jax.ShapeDtypeStruct((heads, 32, q_block), wide),
        ],
        scratch_shapes=[
            pltpu.VMEM((dim, length), wide),
            pltpu.VMEM((dim, length), wide),
            pltpu.VMEM((2 * length - q_block, q_block), wide),
        ],
        compiler_params=pltpu.CompilerParams(vmem_limit_bytes=48 << 20),
        cost_estimate=hint,
        name="attn_backward",
    )(qkv, qkv, qkv, grad_mixed, mixed, probs)
    return jnp.concatenate([gq, gk, gv], axis=0), jnp.sum(gb, axis=2).T


def ffn_kernel(
    x_ref, go_ref, gr_h0, hres_h, g_late, gate_w, up_w, down_w,
    hid_ref, pair_ref, xr_h, gr_h, out_h, out_r_h, gx_h, late_h,
    xs, gs, out_acc, gx_acc, x_in, g_in, gx_out, gx_in, out_v, gx_v, gr_ref, hres_ref, sems, store_sems,
):
    chunk = pl.program_id(0)
    tile = pl.program_id(1)
    size = xs.shape[0]
    mesh_id = dict(device_id_type=pl.DeviceIdType.MESH)
    s = lax.axis_index("seq")
    y = lax.axis_index("tensor")
    c = s % 2
    to_y = {"tensor": 1 - y}
    to_second = {"seq": s - c + y, "tensor": 1 - c}
    half = [pl.ds(0, size), pl.ds(size, size)]

    def move(k, src, dst, who):
        return pltpu.make_async_remote_copy(
            src_ref=src, dst_ref=dst, send_sem=sems.at[k], recv_sem=sems.at[4 + k], device_id=who, **mesh_id
        )

    send_x = [move(h, x_ref.at[:, half[h]], x_in.at[h], to_y) for h in range(2)]
    send_g = move(2, g_late, g_in, to_second)
    back = gx_in.shape[1]
    send_gx = move(3, gx_out.at[0, :, pl.ds(0, back)], gx_in, to_y)
    begun = g_in.shape[1]
    to = lambda k, src, dst: pltpu.make_async_copy(src, dst, store_sems.at[k])
    store_x = [to(h, x_in.at[h], xr_h.at[:, half[h]]) for h in range(2)]
    store_out = [to(2 + h, out_v.at[h], out_h.at[:, half[h]]) for h in range(2)]
    store_out_r = [to(4 + h, out_v.at[2 + h], out_r_h.at[:, half[h]]) for h in range(2)]
    store_gx = [to(6 + h, gx_v.at[h], gx_h.at[:, half[h]]) for h in range(2)]
    store_late = [to(8 + h, gx_out.at[h], late_h.at[:, half[h]]) for h in range(2)]
    store_g = to(10, g_in, gr_h)
    load_h = to(11, hres_h, hres_ref)
    load_g = to(12, gr_h0, gr_ref)

    @pl.when(tile == 0)
    def _():
        out_acc[...] = jnp.zeros_like(out_acc)
        gx_acc[...] = jnp.zeros_like(gx_acc)

    @pl.when((tile == 0) & (chunk == 0))
    def _():
        load_h.start()
        load_g.start()
        barrier = pltpu.get_barrier_semaphore()
        for who in (to_y, {"seq": s + 1 - 2 * c}):
            pl.semaphore_signal(barrier, inc=1, device_id=who, **mesh_id)
        pl.semaphore_wait(barrier, 2)
        for each in (*send_x, send_g):
            each.start()

    for h in range(2):

        @pl.when((tile == 0) & (chunk == h))
        def _(h=h):
            xs[...] = x_ref[:, half[h]].T
            gs[...] = go_ref[:, half[h]].T

        @pl.when((tile == 0) & (chunk == 2 + h))
        def _(h=h):
            send_x[h].wait_recv()
            xs[...] = x_in[h].T
            store_x[h].start()
            if not h:
                load_g.wait()
            if h:
                gs[: size - begun, :] = gr_ref[:, size:].T
                send_g.wait_recv()
                gs[size - begun :, :] = g_in[...].T
                store_g.start()
            else:
                gs[...] = gr_ref[:, :size].T

    gate = dot(xs[...], gate_w[...], 1, 0)
    up = dot(xs[...], up_w[...], 1, 0)
    grad = dot(gs[...], down_w[...], 1, 0)
    c_gelu = math.sqrt(2.0 / math.pi)
    square = gate * gate
    t = jnp.tanh(c_gelu * gate * (1.0 + 0.044715 * square))
    part = 0.5 * (1.0 + t)
    gelu = gate * part
    slope = part + 0.5 * gate * (1.0 - t * t) * (c_gelu * (1.0 + 3 * 0.044715 * square))
    hid = (gelu * up).astype(low)
    gg = (grad * up * slope).astype(low)
    gu = (grad * gelu).astype(low)
    hid_ref[...] = hid
    pair_ref[0] = gg
    pair_ref[1] = gu
    out_acc[...] += dot(down_w[...], hid, 1, 1)
    gx_acc[...] += dot(gate_w[...], gg, 1, 1) + dot(up_w[...], gu, 1, 1)

    last = tile == pl.num_programs(1) - 1
    for h in range(2):

        @pl.when(last & (chunk == h))
        def _(h=h):
            if not h:
                load_h.wait()
            out_v[h] = (hres_ref[:, half[h]] + out_acc[...]).astype(low)
            store_out[h].start()
            gx_v[h] = gx_acc[...]
            if h:
                store_gx[h].start()

        @pl.when(last & (chunk == 2 + h))
        def _(h=h):
            out_v[2 + h] = out_acc[...].astype(low)
            store_out_r[h].start()
            gx_out[h] = gx_acc[...].astype(low)
            if not h:
                send_gx.start()
            store_late[h].start()

    @pl.when(last & (chunk == 3))
    def _():
        send_gx.wait_recv()
        gx_v[0, :, :back] += gx_in[...].astype(wide)
        store_gx[0].start()
        for each in (*send_x, send_g, send_gx):
            each.wait_send()
        for each in store_x + store_out + store_out_r + store_gx + store_late + [store_g]:
            each.wait()


def ffn(x, g_own, g_oth, hres, g_late, gate_w, up_w, down_w):
    width, tokens = x.shape
    hidden = gate_w.shape[1]
    tile, size = hidden // 2, tokens // 2
    begun = g_late.shape[1]
    hbm = pl.BlockSpec(memory_space=pl.ANY)
    full = pl.BlockSpec((width, tokens), lambda s, j: (0, 0), pipeline_mode=pl.Buffered(1))
    weight = pl.BlockSpec((width, tile), lambda s, j: (0, j))
    act_shape = jax.ShapeDtypeStruct((2 * tokens, hidden), low)
    tokens_of = lambda kind: jax.ShapeDtypeStruct((width, tokens), kind)
    return pl.pallas_call(
        ffn_kernel,
        grid=(4, hidden // tile),
        in_specs=[full, full, hbm, hbm, hbm, weight, weight, weight],
        out_specs=[
            pl.BlockSpec((size, tile), lambda s, j: (s, j)),
            pl.BlockSpec((2, size, tile), lambda s, j: (0, s, j)),
        ]
        + [hbm] * 6,
        out_shape=[act_shape, jax.ShapeDtypeStruct((2, 2 * tokens, hidden), low)]
        + [tokens_of(low), jax.ShapeDtypeStruct((width, begun), low)]
        + [tokens_of(kind) for kind in (low, low, wide, low)],
        scratch_shapes=[
            pltpu.VMEM((size, width), low),
            pltpu.VMEM((size, width), low),
            pltpu.VMEM((width, size), wide),
            pltpu.VMEM((width, size), wide),
            pltpu.VMEM((2, width, size), low),
            pltpu.VMEM((width, begun), low),
            pltpu.VMEM((2, width, size), low),
            pltpu.VMEM((width, 128), low),
            pltpu.VMEM((4, width, size), low),
            pltpu.VMEM((2, width, size), wide),
            pltpu.VMEM((width, tokens - begun), low),
            pltpu.VMEM((width, tokens), wide),
            pltpu.SemaphoreType.DMA((8,)),
            pltpu.SemaphoreType.DMA((13,)),
        ],
        compiler_params=pltpu.CompilerParams(vmem_limit_bytes=60 << 20, collective_id=0, has_side_effects=True),
        cost_estimate=hint,
        name="ffn_both_ways",
    )(x, g_own, g_oth, hres, g_late, gate_w, up_w, down_w)


def weight_grad_kernel(core_ref, own_ref, oth_ref, right_ref, *refs):
    tokens = own_ref.shape[1]
    total = dot(own_ref[...], right_ref[:tokens, :], 1, 0) + dot(oth_ref[...], right_ref[tokens:, :], 1, 0)
    if len(refs) == 2:
        total = total + refs[0][...].astype(wide)
    refs[-1][...] = total.astype(low)


def weight_grad(own, oth, right, core, got=None):
    width, tokens = own.shape
    columns = right.shape[1] // 2
    blocks = 4
    rows = width // blocks
    left = pl.BlockSpec((rows, tokens), lambda i, core_ref: (i, 0))
    out = pl.BlockSpec((rows, columns), lambda i, core_ref: (i, 0))
    args = [own, oth, right] + ([] if got is None else [got])
    return pl.pallas_call(
        weight_grad_kernel,
        grid_spec=pltpu.PrefetchScalarGridSpec(
            num_scalar_prefetch=1,
            grid=(blocks,),
            in_specs=[
                left,
                left,
                pl.BlockSpec((2 * tokens, columns), lambda i, core_ref: (0, core_ref[0]), pipeline_mode=pl.Buffered(1)),
            ]
            + ([] if got is None else [out]),
            out_specs=out,
        ),
        out_shape=jax.ShapeDtypeStruct((width, columns), low),
        compiler_params=pltpu.CompilerParams(vmem_limit_bytes=40 << 20),
        cost_estimate=hint,
        name="weight_grad",
    )(core.reshape(1), *args)


def back_kernel(
    hid_h, pair_h, go_h, gr1_h, gr2_h, xo_h, xr_h, gx_h, hres_h, xin_h, probs_h, xn1_h, outp_h, outr_h, late_h,
    out_w_h, w_t_h, qkv_h, mixed_h, gain2_h, gain1_h, scale2, scale1,
    got_p, got_r, got_in, d_out_h, gin_h, p_out, a_out, small,
    out_w, w_t, qkv, mixed, gain2, gain1, d_out, gin,
    r_core, xp, zd, zp, dx, bf, rx, ya, xa, za, late_in, sm_src, sm_in, send_sems, recv_sems, load_sems,
):
    s = lax.axis_index("seq")
    y = lax.axis_index("tensor")
    z = lax.axis_index("dp")
    c = s % 2
    m = s // 2
    width = xp.shape[0]
    rows = d_out.shape[0]
    columns = xp.shape[1]
    half_len = rx.shape[1]
    length = 2 * half_len
    heads = probs_h.shape[0]
    dim = mixed.shape[0] // heads
    zs = width // rows
    mesh_id = dict(device_id_type=pl.DeviceIdType.MESH)
    to_core = {"seq": 2 * m + 1 - c}
    to_x = {"seq": 2 * (1 - m) + c}
    to_y = {"tensor": 1 - y}
    to_z = {"dp": (z + 1) % zs}
    to_swap = {"seq": 2 * m + y, "tensor": c}
    to_back = {"seq": 2 * m + 1 - y, "tensor": c}

    def move(k, src, dst, who):
        return pltpu.make_async_remote_copy(
            src_ref=src, dst_ref=dst, send_sem=send_sems.at[k], recv_sem=recv_sems.at[k], device_id=who, **mesh_id
        )

    def load(k, src, dst):
        return pltpu.make_async_copy(src, dst, load_sems.at[k])

    def chunk(j):
        return pl.ds(pl.multiple_of(j * rows, rows), rows)

    def side(i, size):
        return pl.ds(pl.multiple_of(i * size, 128), size)

    order = [(z + zs - 1 - k) % zs for k in range(zs)]
    mine = side(c, columns)
    my_half = side(c, half_len)
    other_half = side(1 - c, half_len)
    cut = [(0, 192), (192, rows - 192)]

    def part(j, p):
        return pl.ds(pl.multiple_of(j * rows + cut[p][0], 16), cut[p][1])

    parts = [pl.ds(*each) for each in cut]

    late_from = half_len - late_in.shape[1]
    late = move(0, late_h.at[:, pl.ds(late_from, half_len - late_from)], late_in, to_y)
    swap_out = move(1, outp_h, got_p, to_swap)
    back_out = move(2, outr_h, got_r, to_back)
    both = range(2)
    steps = range(zs - 1)
    z_down = [
        [move(3 + 2 * t + p, zd.at[t - 1, parts[p]] if t else r_core.at[0, part(order[0], p)], zd.at[t, parts[p]], to_z) for p in both]
        for t in steps
    ]
    x_down = [move(9 + p, zd.at[2, parts[p]], dx.at[parts[p]], to_x) for p in both]
    core_down = [move(11 + p, d_out.at[parts[p], mine], d_out.at[parts[p], mine], to_core) for p in both]
    z_pair = [
        [move(13 + 2 * t + p, zp.at[t - 1, parts[p]] if t else r_core.at[2, part(order[0], p)], zp.at[t, parts[p]], to_z) for p in both]
        for t in steps
    ]
    x_pair_back = [move(19 + p, zp.at[2, parts[p]], p_out.at[m, parts[p], mine], to_x) for p in both]
    core_pair = [move(21 + p, p_out.at[m, parts[p], mine], p_out.at[m, parts[p], mine], to_core) for p in both]
    core_pair_back = [
        move(23 + p, p_out.at[1 - m, parts[p], mine], p_out.at[1 - m, parts[p], mine], to_core) for p in both
    ]
    core_branch = move(25, bf.at[:, my_half], bf.at[:, my_half], to_core)
    a_rows = xa.shape[1]
    my_rows = pl.ds(pl.multiple_of(m * a_rows, a_rows), a_rows)
    x_rows = pl.ds(pl.multiple_of((1 - m) * a_rows, a_rows), a_rows)
    x_attn = [move(26 + k, ya.at[j, x_rows], xa.at[j], to_x) for k, j in enumerate(order)]
    z_attn = [move(30 + t, za.at[t - 1] if t else ya.at[order[0], my_rows], za.at[t], to_z) for t in steps]
    x_attn_back = move(33, a_out.at[my_rows], a_out.at[my_rows], to_x)
    core_attn = move(34, a_out, a_out, to_core)
    swap_in = move(35, gin, got_in, to_swap)

    def x_pair(k):
        at = chunk((z + zs - 1 - k) % zs)
        return move(46 + k, r_core.at[1, at], xp.at[at], to_x)

    def meet():
        barrier = pltpu.get_barrier_semaphore()
        greet = [to_core, to_y, {"seq": 2 * m + 1 - c, "tensor": 1 - y}, to_x] + [{"dp": (z + i) % zs} for i in range(1, zs)]
        for who in greet:
            pl.semaphore_signal(barrier, inc=1, device_id=who, **mesh_id)
        pl.semaphore_wait(barrier, len(greet))
        late.start()

    def step_z_down(t, p):
        z_down[t - 1][p].wait_recv()
        at = parts[p]
        zd[t - 1, at, :] = (zd[t - 1, at, :].astype(wide) + r_core[0, part(order[t], p), :].astype(wide)).astype(low)
        (z_down[t][p] if t < zs - 1 else x_down[p]).start()

    def end_down(p):
        x_down[p].wait_recv()
        at = parts[p]
        d_out[at, mine] = (zd[2, at, :].astype(wide) + dx[at, :].astype(wide)).astype(low)
        core_down[p].start()

    def step_z_pair(t, p):
        if p == 0:
            x_pair(t).wait_recv()
        at = parts[p]
        term = r_core[2, part(order[t], p), :].astype(wide) + xp[part(order[t], p), :].astype(wide)
        if t:
            z_pair[t - 1][p].wait_recv()
            term = zp[t - 1, at, :].astype(wide) + term
            zp[t - 1, at, :] = term.astype(low)
        else:
            r_core[2, part(order[0], p), :] = term.astype(low)
        if t < zs - 1:
            z_pair[t][p].start()
        else:
            x_pair_back[p].start()
            p_out[m, at, mine] = term.astype(low)
            core_pair[p].start()

    def end_pair(p):
        x_pair_back[p].wait_recv()
        core_pair_back[p].start()

    def step_attn(t):
        @pl.when(c == y)
        def _():
            x_attn[t].wait_recv()
            term = ya[order[t], my_rows, :].astype(wide) + xa[order[t]].astype(wide)
            if t:
                z_attn[t - 1].wait_recv()
                za[t - 1] = (za[t - 1].astype(wide) + term).astype(low)
            else:
                ya[order[0], my_rows, :] = term.astype(low)
            if t < zs - 1:
                z_attn[t].start()
            else:
                a_out[my_rows, :] = za[zs - 2]
                x_attn_back.start()

    hops = [to_core, to_y, to_x, {"dp": z + 1 - 2 * (z % 2)}, {"dp": (z + 2) % zs}]
    exchange = [move(41 + i, sm_src.at[i], sm_in.at[i], who) for i, who in enumerate(hops)]

    def start_sum(i):
        sm_src[i] = small[...]
        exchange[i].start()

    def end_sum(i):
        exchange[i].wait_recv()
        small[...] = sm_src[i] + sm_in[i]

    aside = [
        load(15 + i, src, dst)
        for i, (src, dst) in enumerate(
            ((out_w_h, out_w), (w_t_h, w_t), (qkv_h, qkv), (mixed_h, mixed), (gain2_h, gain2), (gain1_h, gain1))
        )
    ]
    store_in_grad = load(21, gin, gin_h)
    store_down = load(22, d_out, d_out_h)

    def weights(r_buf, l_go, l_gr, l_xo, l_xr, s_buf):
        loads = [
            load(0, hid_h, r_buf.at[0]),
            load(1, go_h, l_go),
            load(2, gr1_h, l_gr.at[:, pl.ds(0, gr1_h.shape[1])]),
            load(3, gr2_h, l_gr.at[:, pl.ds(gr1_h.shape[1], gr2_h.shape[1])]),
            load(4, pair_h.at[1 - m], r_buf.at[1]),
            load(5, xo_h, l_xo),
            load(14, xr_h, l_xr),
        ]
        load_own = load(6, pair_h.at[m], r_buf.at[0])
        for each in loads:
            each.start()
        theirs = side(1 - c, columns)

        def core(i, k):
            at = chunk((z + zs - 1 - k) % zs)
            return move(50 + i * zs + k, s_buf.at[i % 2, at], r_core.at[i, at], to_core)

        def product(left_o, left_r, right, col, at):
            total = dot(left_o[at, :], right[:half_len, col], 1, 0)
            return total + dot(left_r[at, :], right[half_len:, col], 1, 0)

        def send_part(left_o, left_r, right, i, k):
            at = chunk((z + zs - 1 - k) % zs)
            s_buf[i % 2, at, :] = product(left_o, left_r, right, theirs, at).astype(low)
            core(i, k).start()

        def keep_part(left_o, left_r, right, i, k):
            at = chunk((z + zs - 1 - k) % zs)
            total = product(left_o, left_r, right, mine, at)
            core(i, k).wait_recv()
            r_core[i, at, :] = (total + r_core[i, at, :].astype(wide)).astype(low)

        def sent(i):
            def block(k, carry):
                core(i, k).wait_send()
                return carry

            lax.fori_loop(0, zs, block, 0)

        for each in aside:
            each.start()
        down = (l_go, l_gr, r_buf.at[0], 0)
        theirs_first = (l_xo, l_xr, r_buf.at[1], 1)
        own = (l_xo, l_xr, r_buf.at[0], 2)
        meet()
        for each in loads:
            each.wait()

        def first(k, carry):
            @pl.when(k < zs)
            def _():
                send_part(*down, k)
                send_part(*theirs_first, k)

            @pl.when(k > 0)
            def _():
                keep_part(*down, k - 1)

                @pl.when(k == 1)
                def _():
                    for each in z_down[0]:
                        each.start()

                keep_part(*theirs_first, k - 1)
                x_pair(k - 1).start()

            return carry

        lax.fori_loop(0, zs + 1, first, 0)
        load_own.start()
        step_z_down(1, 0)

        @pl.when(c != y)
        def _():
            swap_out.start()

        back_out.start()
        sent(0)
        load_own.wait()

        def second(k, carry):
            @pl.when(k == 2)
            def _():
                step_z_down(1, 1)

            @pl.when(k == zs)
            def _():
                step_z_pair(0, 0)
                step_z_pair(0, 1)
                step_z_down(2, 0)

            @pl.when(k < zs)
            def _():
                send_part(*own, k)

            @pl.when(k > 0)
            def _():
                keep_part(*own, k - 1)

            return carry

        lax.fori_loop(0, zs + 1, second, 0)
        sent(1)
        sent(2)

    hidden = hid_h.shape[1]
    left = pltpu.VMEM((width, half_len), low)
    pl.run_scoped(
        weights,
        pltpu.VMEM((2, length, hidden), low),
        left,
        left,
        left,
        left,
        pltpu.VMEM((2, width, columns), low),
    )

    def attention(gxv, hv, gov, p_buf, k_acc, v_acc, sums, gqkv, gm, xn1, sx, ga):
        loads = [load(7, gx_h, gxv), load(8, hres_h, hv), load(9, go_h, gov), load(10, xn1_h, xn1)]
        load_x = load(11, xin_h, gov)
        for each in loads:
            each.start()

        def probs_load(h, b, slot):
            return load(12 + slot, probs_h.at[h, :, side(b, q_block)], p_buf.at[slot])

        probs_load(0, 0, 0).start()
        lanes = half_len // 128
        piece = 64
        pieces = width // piece

        def fold(a):
            return sum(a[:, i * 128 : (i + 1) * 128] for i in range(lanes))

        def spread(a):
            return jnp.concatenate([a] * lanes, axis=1)

        def norm_backward(values, gain, scale, grad, store, row):
            def first(i, total):
                at = pl.ds(pl.multiple_of(i * piece, piece), piece)
                return total + jnp.sum(values(at) * (spread(gain[at, :]) * grad(at)), axis=0, keepdims=True)

            total = lax.fori_loop(0, pieces, first, jnp.zeros((1, half_len), wide))
            mean = total * scale[...] * (1.0 / width)

            def second(i, carry):
                at = pl.ds(pl.multiple_of(i * piece, piece), piece)
                g = grad(at)
                normed = values(at) * scale[...]
                store(at, scale[...] * (spread(gain[at, :]) * g - normed * mean))
                ga_part[at, :] = fold(g * normed)
                return carry

            lax.fori_loop(0, pieces, second, 0)
            small[row : row + 1, :] = jnp.sum(ga_part[...].T, axis=0, keepdims=True)

        ga_part = sums.at[:width, :128]
        small[...] = jnp.zeros_like(small)
        for each in loads[:3] + aside:
            each.wait()
        late.wait_recv()

        def add_late(i, carry):
            at = pl.ds(pl.multiple_of(i * piece, piece), piece)
            gxv[at, late_from:] += late_in[at, :].astype(wide)
            return carry

        lax.fori_loop(0, pieces, add_late, 0)

        def store_hres(at, back):
            total = gov[at, :].astype(wide) + back
            gxv[at, :] = total
            bf[at, my_half] = total.astype(low)

        norm_backward(lambda at: hv[at, :], gain2, scale2, lambda at: gxv[at, :], store_hres, 0)
        core_branch.start()
        load_x.start()
        step_z_down(2, 1)
        core_branch.wait_recv()
        gm[...] = dot(out_w[...], bf[...], 1, 0).astype(low)

        reach = length - q_block
        blocks = length // q_block
        near_rows = q_block + 2 * band_half
        d = (
            lax.broadcasted_iota(jnp.int32, (near_rows, q_block), 0)
            - lax.broadcasted_iota(jnp.int32, (near_rows, q_block), 1)
            - band_half
        )
        for h in range(heads):
            head = pl.ds(h * dim, dim)
            k_rows = pl.ds((heads + h) * dim, dim)
            v_rows = pl.ds((2 * heads + h) * dim, dim)
            k_acc[...] = jnp.zeros_like(k_acc)
            v_acc[...] = jnp.zeros_like(v_acc)
            sums[...] = jnp.zeros_like(sums)

            def block(b, carry):
                slot = b % 2
                at = side(b, q_block)
                probs_load(h, b, slot).wait()

                @pl.when(b < blocks - 1)
                def _():
                    probs_load(h, b + 1, 1 - slot).start()

                if h < heads - 1:

                    @pl.when(b == blocks - 1)
                    def _():
                        probs_load(h + 1, 0, 1 - slot).start()

                probs = p_buf[slot]
                go = gm[head, at]
                inner = jnp.sum(go.astype(wide) * mixed[head, at].astype(wide), axis=0, keepdims=True)
                scores = probs.astype(wide) * (dot(qkv[v_rows, :], go, 0, 0) - inner)
                first = pl.multiple_of(reach - b * q_block, q_block)
                sums[pl.ds(first, length), :] += scores
                scores = scores.astype(low)
                gqkv[head, at] = dot(qkv[k_rows, :], scores, 1, 0).astype(low)
                k_acc[...] += dot(qkv[head, at], scores, 1, 1)
                v_acc[...] += dot(go, probs, 1, 1)
                return carry

            lax.fori_loop(0, blocks, block, 0)
            gqkv[k_rows, :] = k_acc[...].astype(low)
            gqkv[v_rows, :] = v_acc[...].astype(low)
            near = sums[reach - band_half : reach + q_block + band_half, :]
            n = jnp.abs(d)
            bucket = jnp.zeros((near_rows, q_block), jnp.int32)
            for step in steps_at:
                bucket = bucket + jnp.where(n >= step, 1, 0)
            bucket = bucket + jnp.where(d > 0, 16, 0)
            totals = []
            for b in range(32):
                total = jnp.sum(jnp.where(bucket == b, near, 0.0), axis=0, keepdims=True)
                if b == 15:
                    total = total + jnp.sum(sums[: reach - band_half, :], axis=0, keepdims=True)
                if b == 31:
                    total = total + jnp.sum(sums[reach + q_block + band_half :, :], axis=0, keepdims=True)
                totals.append(total)
            totals = jnp.concatenate(totals, axis=0)
            totals = jnp.concatenate([totals, jnp.zeros((96, q_block), wide)], axis=0)
            line = jnp.sum(totals.T, axis=0, keepdims=True)
            for side_c in range(2):
                row = 8 + side_c * heads + h
                small[row : row + 1, :128] = jnp.where(c == side_c, line, 0.0)
            if h == 0:
                step_z_pair(1, 0)
            if h == 1:
                step_z_down(3, 0)

        def input_grad(half, store):
            def block(i, carry):
                at = chunk(i)
                store(at, dot(w_t[at, :], gqkv[:, half], 1, 0))
                return carry

            lax.fori_loop(0, zs, block, 0)

        def store_sent(at, value):
            sx[at, :] = value.astype(low)

        core_x = move(36, sx, rx, to_core)
        loads[3].wait()
        y_attn = [
            move(37 + k, ga.at[j], ya.at[j], to_y) for k, j in enumerate(order)
        ]
        wide_cols = gqkv.shape[0]

        def weight_part(k):
            j = order[k]
            ga[j, :rows, :wide_cols] = dot(xn1[chunk(j), :], gqkv[...], 1, 1).astype(low)
            ga[j, :rows, wide_cols:] = dot(bf[chunk(j), :], mixed[...], 1, 1).astype(low)
            ga[j, rows:, :] = jnp.zeros((ga.shape[1] - rows, ga.shape[2]), low)
            pl.when(c != y)(y_attn[k].start)

        def store_own(at, value):
            hv[at, :] = value

        def store_in(at, back):
            gin[at, :] = (gxv[at, :] + back).astype(low)

        def step_y_attn(k):
            j = order[k]

            @pl.when(c == y)
            def _():
                y_attn[k].wait_recv()
                ya[j] = (ya[j].astype(wide) + ga[j].astype(wide)).astype(low)
                x_attn[k].start()

        weight_part(0)
        weight_part(1)
        weight_part(2)
        input_grad(other_half, store_sent)
        core_x.start()
        step_z_down(3, 1)
        step_z_pair(2, 0)
        step_z_pair(1, 1)
        input_grad(my_half, store_own)
        end_down(0)
        weight_part(3)
        step_y_attn(0)
        load_x.wait()
        core_x.wait_recv()
        norm_backward(
            lambda at: gov[at, :].astype(wide),
            gain1,
            scale1,
            lambda at: hv[at, :] + rx[at, :].astype(wide),
            store_in,
            1,
        )
        store_in_grad.start()
        start_sum(0)
        end_down(1)
        step_z_pair(3, 0)
        step_y_attn(1)
        end_sum(0)
        start_sum(1)

        @pl.when(c != y)
        def _():
            swap_in.start()

        step_attn(0)
        step_z_pair(2, 1)
        step_y_attn(2)
        end_pair(0)
        step_attn(1)
        step_y_attn(3)
        end_sum(1)
        start_sum(2)
        core_x.wait_send()

        @pl.when(c != y)
        def _():
            for each in y_attn:
                each.wait_send()

    f32 = lambda *shape: pltpu.VMEM(shape, wide)
    b16 = lambda *shape: pltpu.VMEM(shape, low)
    pl.run_scoped(
        attention,
        f32(width, half_len),
        f32(width, half_len),
        b16(width, half_len),
        b16(2, length, q_block),
        f32(dim, length),
        f32(dim, length),
        f32(2 * length - q_block, q_block),
        b16(3 * heads * dim, length),
        b16(heads * dim, length),
        b16(width, length),
        b16(width, half_len),
        b16(*ya.shape),
    )

    step_z_pair(3, 1)
    end_sum(2)
    start_sum(3)
    step_attn(2)
    end_sum(3)
    start_sum(4)
    step_attn(3)
    for each in core_down:
        each.wait()
    store_down.start()
    end_sum(4)
    end_pair(1)

    @pl.when(c == y)
    def _():
        x_attn_back.wait_recv()
        core_attn.start()
        for each in (core_attn, x_attn_back, *x_attn, *z_attn):
            each.wait_send()

    @pl.when(c != y)
    def _():
        core_attn.wait_recv()
        swap_out.wait()
        swap_in.wait()

    back_out.wait()
    for each in core_pair + core_pair_back + [store_in_grad, store_down]:
        each.wait()
    for each in [late, core_branch] + sum(z_down, []) + x_down + sum(z_pair, []) + x_pair_back:
        each.wait_send()
    for each in [x_pair(k) for k in range(zs)] + exchange:
        each.wait_send()


def back_all(
    hid, pair, g_own, g_oth, g_late, x_own, x_oth, gx, hres, x_in, probs, xn_one, out_first, out_oth, late,
    out_w, w_t, qkv, mixed, gain_two, gain_one, scale_two, scale_one, zs,
):
    width, half_len = g_own.shape
    length = 2 * half_len
    rows = width // zs
    columns = hid.shape[1] // 2
    heads = probs.shape[0]
    a_cols = (w_t.shape[1] + out_w.shape[0]) // 2
    a_len = -(-rows // 32) * 32
    hbm = pl.BlockSpec(memory_space=pl.ANY)
    vmem = pl.BlockSpec(memory_space=pltpu.VMEM)
    sds = lambda kind, *shape: jax.ShapeDtypeStruct(shape, kind)
    b16 = lambda *shape: pltpu.VMEM(shape, low)
    return pl.pallas_call(
        back_kernel,
        in_specs=[hbm] * 21 + [vmem] * 2,
        out_specs=[hbm] * 5 + [vmem] * 3,
        out_shape=[
            sds(low, width, half_len),
            sds(low, width, half_len),
            sds(low, width, half_len),
            sds(low, rows, 2 * columns),
            sds(low, width, half_len),
            sds(low, 2, rows, 2 * columns),
            sds(low, a_len, 2 * a_cols),
            sds(wide, 16, width),
        ],
        scratch_shapes=[
            *(pltpu.VMEM(each.shape, each.dtype) for each in (out_w, w_t, qkv, mixed, gain_two, gain_one)),
            b16(rows, 2 * columns),
            b16(width, half_len),
            b16(3, width, columns),
            b16(width, columns),
            b16(zs - 1, rows, columns),
            b16(zs - 1, rows, columns),
            b16(rows, columns),
            b16(width, length),
            b16(width, half_len),
            b16(zs, a_len, 2 * a_cols),
            b16(zs, a_len // 2, 2 * a_cols),
            b16(zs - 1, a_len // 2, 2 * a_cols),
            b16(width, half_len - 128),
            pltpu.VMEM((5, 16, width), wide),
            pltpu.VMEM((5, 16, width), wide),
            pltpu.SemaphoreType.DMA((62,)),
            pltpu.SemaphoreType.DMA((62,)),
            pltpu.SemaphoreType.DMA((23,)),
        ],
        compiler_params=pltpu.CompilerParams(vmem_limit_bytes=61 << 20, collective_id=1, has_side_effects=True),
        cost_estimate=hint,
        name="back_all",
    )(
        hid, pair, g_own, g_oth, g_late, x_own, x_oth, gx, hres, x_in, probs, xn_one, out_first, out_oth, late,
        out_w, w_t, qkv, mixed, gain_two, gain_one, scale_two, scale_one,
    )


def finish_kernel(
    d_h, p_h, a_h, own_in, got_in, own_out, got_out, oth_out, small,
    d_out, g_out, u_out, q_out, k_out, v_out, o_out, in_out, y_out, gain1_out, gain2_out, bias_out,
    w_in, w_out, a_in, i_in, i_out, y_in, sems,
):
    own = lax.axis_index("seq") % 2 == lax.axis_index("tensor")
    rows = w_in.shape[1]
    width = i_in.shape[0]
    copy = lambda k, src, dst: pltpu.make_async_copy(src, dst, sems.at[k])
    loads = [copy(0, d_h, w_in.at[0]), copy(1, p_h.at[0], w_in.at[1]), copy(2, p_h.at[1], w_in.at[2]), copy(3, a_h, a_in)]
    load_y = copy(4, oth_out, y_in.at[1])
    mine = [copy(5, own_in, i_in), copy(6, own_out, y_in.at[0])]
    theirs = [copy(5, got_in, i_in), copy(6, got_out, y_in.at[0])]
    stores = [copy(7 + i, w_out.at[i], out) for i, out in enumerate((d_out, g_out, u_out))]
    store_i = copy(10, i_out, in_out)
    store_y = copy(11, y_in.at[0], y_out)

    def start(which):
        @pl.when(own)
        def _():
            mine[which].start()

        @pl.when(jnp.logical_not(own))
        def _():
            theirs[which].start()

    loads[0].start()
    start(0)
    for each in loads[1:3]:
        each.start()
    start(1)
    load_y.start()
    loads[3].start()

    def piecewise(count, size, run):
        def step(i, carry):
            run(pl.ds(pl.multiple_of(i * size, size), size))
            return carry

        lax.fori_loop(0, count, step, 0)

    def widen(i):
        loads[i].wait()

        def run(at):
            w_out[i, at, :] = w_in[i, at, :].astype(wide)

        piecewise(rows // 16, 16, run)
        stores[i].start()

    widen(0)
    mine[0].wait()

    def run_in(at):
        i_out[at, :] = i_in[at, :].astype(wide)

    piecewise(width // 64, 64, run_in)
    store_i.start()
    widen(1)
    widen(2)
    mine[1].wait()
    load_y.wait()

    def run_y(at):
        y_in[0, at, :] = (y_in[0, at, :].astype(wide) + y_in[1, at, :].astype(wide)).astype(low)

    piecewise(width // 64, 64, run_y)
    store_y.start()
    loads[3].wait()
    inner = q_out.shape[0]
    for i, out in enumerate((q_out, k_out, v_out, o_out)):
        out[...] = a_in[:rows, i * inner : (i + 1) * inner].astype(wide).T
    gain1_out[...] = small[1, :]
    gain2_out[...] = small[0, :]
    bias_out[...] = small[8 : 8 + bias_out.shape[0], : bias_out.shape[1]]
    for each in stores + [store_i, store_y]:
        each.wait()


def finish(d, p, a, own_in, got_in, own_out, got_out, oth_out, small, inner, bias_shape):
    rows, hidden = d.shape
    width, half_len = own_in.shape
    hbm = pl.BlockSpec(memory_space=pl.ANY)
    vmem = pl.BlockSpec(memory_space=pltpu.VMEM)
    sds = lambda kind, *shape: jax.ShapeDtypeStruct(shape, kind)
    return pl.pallas_call(
        finish_kernel,
        in_specs=[hbm] * 8 + [vmem],
        out_specs=[hbm] * 3 + [vmem] * 4 + [hbm] * 2 + [vmem] * 3,
        out_shape=[sds(wide, rows, hidden)] * 3
        + [sds(wide, inner, rows)] * 4
        + [sds(wide, width, half_len), sds(low, width, half_len)]
        + [sds(wide, width)] * 2
        + [sds(wide, *bias_shape)],
        scratch_shapes=[
            pltpu.VMEM((3, rows, hidden), low),
            pltpu.VMEM((3, rows, hidden), wide),
            pltpu.VMEM(a.shape, low),
            pltpu.VMEM((width, half_len), low),
            pltpu.VMEM((width, half_len), wide),
            pltpu.VMEM((2, width, half_len), low),
            pltpu.SemaphoreType.DMA((12,)),
        ],
        compiler_params=pltpu.CompilerParams(vmem_limit_bytes=60 << 20),
        cost_estimate=hint,
        name="finish_all",
    )(d, p, a, own_in, got_in, own_out, got_out, oth_out, small)


def norm_back(values, scale, gain, grad):
    normed = values * scale
    pushed = gain * grad
    mean = jnp.mean(normed * pushed, axis=0, keepdims=True)
    return scale * (pushed - normed * mean), jnp.sum(grad * normed, axis=1)


class Moves:
    def __init__(self, mesh):
        self.nz = mesh.shape["dp"]
        self.nx = mesh.shape["seq"] // 2
        both = [(m, c, y) for m in range(self.nx) for c in range(2) for y in range(2)]
        at = lambda m, c, y: (m * 2 + c) * 2 + y
        self.swap_pairs = [(at(m, c, y), at(m, y, c)) for m, c, y in both if c != y]
        self.second_pairs = [(at(m, c, y), at(m, y, 1 - c)) for m, c, y in both]
        self.back_pairs = [(b, a) for a, b in self.second_pairs]
        self.ring_x = [(m * 2 + c, (m + 1) % self.nx * 2 + c) for m in range(self.nx) for c in range(2)]
        self.y = lax.axis_index("tensor")
        self.z = lax.axis_index("dp")
        s = lax.axis_index("seq")
        self.c = s % 2
        self.m = s // 2

    def swap(self, a):
        got = lax.ppermute(a, ("seq", "tensor"), self.swap_pairs)
        return jnp.where(self.c == self.y, a, got)

    def back(self, a):
        return lax.ppermute(a, ("seq", "tensor"), self.back_pairs)

    def core(self, a):
        return lax.ppermute(a, "seq", [(s, s ^ 1) for s in range(2 * self.nx)])

    def over_y(self, a):
        return lax.ppermute(a, "tensor", [(0, 1), (1, 0)])

    def over_x(self, a):
        return lax.ppermute(a, "seq", self.ring_x)

    def start_x(self, a):
        take = lax.dynamic_index_in_dim(a, (self.m + self.nx - 1) % self.nx, 1, False)
        return a, self.over_x(take)

    def finish_x(self, a, got, *first):
        take = lambda i: lax.dynamic_index_in_dim(a, i % self.nx, 1, False)
        got = after(got, *first)
        held = (got.astype(wide) + take(self.m + 2 * self.nx - 2).astype(wide)).astype(low)
        for t in range(2, self.nx):
            held = (self.over_x(held).astype(wide) + take(self.m + 2 * self.nx - 1 - t).astype(wide)).astype(low)
        return held

    def scatter_x(self, a):
        take = lambda i: lax.dynamic_index_in_dim(a, i % self.nx, 1, False)
        held = take(self.m + self.nx - 1)
        for t in range(1, self.nx):
            held = (self.over_x(held).astype(wide) + take(self.m + 2 * self.nx - 1 - t).astype(wide)).astype(low)
        return held

    def scatter_z(self, a):
        return lax.psum_scatter(a, "dp", scatter_dimension=0, tiled=True)

    def gather_x(self, piece):
        if self.nx == 2:
            over = self.over_x(piece)
            return jnp.where(
                self.m == 0, jnp.concatenate([piece, over], 0), jnp.concatenate([over, piece], 0)
            )
        groups = [[m * 2 + c for m in range(self.nx)] for c in range(2)]
        return lax.all_gather(piece, "seq", axis=0, tiled=True, axis_index_groups=groups)

    def gather_core(self, piece):
        there = self.core(piece)
        return jnp.where(
            self.c == 0, jnp.concatenate([piece, there], 1), jnp.concatenate([there, piece], 1)
        )

    def sum_everywhere(self, a):
        a = a + self.core(a)
        a = a + self.over_y(a)
        step = 1
        while step < self.nx:
            a = a + lax.ppermute(a, "seq", [(s, s ^ (2 * step)) for s in range(2 * self.nx)])
            step *= 2
        step = 1
        while step < self.nz:
            a = a + lax.ppermute(a, "dp", [(z, z ^ step) for z in range(self.nz)])
            step *= 2
        return a


def local(
    mesh,
    layer_in,
    out_grad,
    doc_lengths,
    valid_length,
    gain_attn,
    query_weight,
    key_weight,
    value_weight,
    position_bias,
    output_weight,
    gain_ffn,
    gate_weight,
    up_weight,
    down_weight,
):
    moves = Moves(mesh)
    half_len, _, width = layer_in.shape
    length = 2 * half_len
    heads = position_bias.shape[1]
    inner_width = query_weight.shape[1]
    y, c, m = moves.y, moves.c, moves.m

    flat = lambda a: a.reshape(half_len, width).T
    (
        x_in, g_own, g_oth, g_send, out_w, w_t, xn_one, qkv, mixed, probs, hres, xn_own, scale_one, scale_two, gain_one, gain_two
    ) = front(
        flat(layer_in),
        flat(out_grad),
        (query_weight.T, key_weight.T, value_weight.T, output_weight),
        doc_lengths,
        valid_length,
        position_bias.T,
        gain_attn,
        gain_ffn,
        moves.nx == 2 and moves.nz == 4,
    )
    hid, pair, xn_oth, g_late, out_first, out_oth, gx, late = ffn(
        xn_own, g_own, g_oth, hres, g_send, gate_weight, up_weight, down_weight.T
    )
    if moves.nx == 2 and moves.nz == 4:
        got_first, got_oth, got_in, sum_d, grad_in, sum_p, sums, small = back_all(
            hid, pair, g_own, g_oth, g_late, xn_own, xn_oth, gx, hres, x_in, probs, xn_one, out_first, out_oth, late,
            out_w, w_t, qkv, mixed, gain_two, gain_one, scale_two, scale_one, moves.nz,
        )
        sum_d, sum_g, sum_u, sum_q, sum_k, sum_v, sum_o, grad_in, out_y, gain_one_sum, gain_two_sum, bias_sum = finish(
            sum_d, sum_p, sums, grad_in, got_in, out_first, got_first, got_oth, small,
            inner_width, (2 * heads, position_bias.shape[0]),
        )
        return (
            out_y.T.reshape(half_len, 1, width),
            grad_in.T.reshape(half_len, 1, width),
            gain_one_sum,
            sum_q.T,
            sum_k.T,
            sum_v.T,
            bias_sum.T,
            sum_o,
            gain_two_sum,
            sum_g,
            sum_u,
            sum_d.T,
        )
    grad_gate, grad_up = pair[0], pair[1]
    gx = gx.at[:, 128:].add(moves.over_y(late)[:, 128:].astype(wide))
    g_oth = jnp.concatenate([g_oth, g_late], axis=1)
    qkv_w = w_t.T
    x_wide = x_in.astype(wide)
    gain_one, gain_two = gain_one[:, :1], gain_two[:, :1]

    def both_halves(own):
        other = moves.core(own)
        return jnp.where(
            c == 0, jnp.concatenate([own, other], 1), jnp.concatenate([other, own], 1)
        )

    def my_half(a):
        return lax.dynamic_slice_in_dim(a, c * half_len, half_len, 1)

    def other_half(a):
        return lax.dynamic_slice_in_dim(a, (1 - c) * half_len, half_len, 1)


    columns = hid.shape[1] // 2
    send_d = weight_grad(g_own, g_oth, hid, 1 - c)
    got_d = moves.core(send_d)
    send_g = weight_grad(xn_own, xn_oth, after(grad_gate, send_d), 1 - c)
    got_g = moves.core(send_g)
    send_u = weight_grad(xn_own, xn_oth, after(grad_up, send_g), 1 - c)
    got_u = moves.core(send_u)
    total_d = weight_grad(g_own, g_oth, after(hid, send_u), c, got_d)
    total_g = weight_grad(xn_own, xn_oth, after(grad_gate, total_d), c, got_g)
    total_u = weight_grad(xn_own, xn_oth, after(grad_up, total_g), c, got_u)
    part_d = moves.scatter_z(total_d)
    x_sent = [moves.start_x(t.reshape(moves.nz, moves.nx, -1, columns)) for t in (total_g, total_u)]

    gx = after(gx, total_u)
    out_y = moves.swap(out_first).astype(wide) + moves.back(out_oth).astype(wide)

    back, grad_gain_two = norm_back(hres, scale_two, gain_two, gx)
    grad_hres = g_own.astype(wide) + back
    branch = both_halves(grad_hres.astype(low))

    grad_mixed = dot(out_w, branch, 1, 0).astype(low)
    grad_qkv, grad_bias = attn_backward(qkv, grad_mixed, mixed, probs)

    part_g = moves.finish_x(*x_sent[0], grad_qkv).reshape(-1, columns)
    sent = dot(qkv_w, other_half(after(grad_qkv, part_g)), 0, 0).astype(low)
    part_g = moves.scatter_z(part_g)
    got_x = moves.core(sent)
    grad_attn_w = jnp.concatenate(
        [dot(xn_one, after(grad_qkv, sent), 1, 1).astype(low), dot(branch, mixed, 1, 1).astype(low)], axis=1
    )
    gx = dot(qkv_w, my_half(after(grad_qkv, grad_attn_w)), 0, 0) + got_x.astype(wide)
    back, grad_gain_one = norm_back(x_wide, scale_one, gain_one, gx)
    grad_in = (grad_hres + back).astype(low)
    part_u = moves.scatter_z(moves.finish_x(*x_sent[1], grad_in).reshape(-1, columns))

    a_columns = grad_attn_w.shape[1] // 2
    chunks = grad_attn_w.reshape(moves.nz, moves.nx, -1, 2 * a_columns)

    def scatter_y(a):
        got = moves.over_y(lax.dynamic_slice_in_dim(a, (1 - y) * a_columns, a_columns, a.ndim - 1))
        kept = lax.dynamic_slice_in_dim(a, y * a_columns, a_columns, a.ndim - 1)
        return (kept.astype(wide) + got.astype(wide)).astype(low)

    half_z = moves.nz // 2
    part = jnp.concatenate(
        [moves.scatter_x(scatter_y(chunks[:half_z])), scatter_y(moves.scatter_x(chunks[half_z:]))], 0
    )
    piece = moves.gather_x(moves.scatter_z(part.reshape(-1, a_columns)))
    there = moves.over_y(piece)
    group = jnp.where(y == 0, jnp.concatenate([piece, there], 1), jnp.concatenate([there, piece], 1))
    sums = jnp.where(c == y, group, moves.core(group)).astype(wide)
    sum_q, sum_k, sum_v, sum_o = (
        sums[:, i * inner_width : (i + 1) * inner_width] for i in range(4)
    )
    grad_in = moves.swap(grad_in).astype(wide)

    if moves.nx == 2:
        part_d = (part_d.astype(wide) + moves.over_x(part_d).astype(wide)).astype(low)
    else:
        part_d = moves.gather_x(moves.scatter_x(part_d.reshape(1, moves.nx, -1, columns))[0])
    sum_d = moves.gather_core(part_d).astype(wide)
    sum_g = moves.gather_core(moves.gather_x(part_g)).astype(wide)
    sum_u = moves.gather_core(moves.gather_x(part_u)).astype(wide)

    bias_full = jnp.zeros((grad_bias.shape[0], 2 * heads), wide)
    bias_full = lax.dynamic_update_slice(bias_full, grad_bias, (jnp.int32(0), c * heads))
    early = moves.sum_everywhere(jnp.concatenate([grad_gain_two, bias_full.reshape(-1)]))
    gain_two_sum, bias_sum = early[:width], early[width:].reshape(bias_full.shape)
    gain_one_sum = moves.sum_everywhere(grad_gain_one)
    return (
        out_y.astype(low).T.reshape(half_len, 1, width),
        grad_in.T.reshape(half_len, 1, width),
        gain_one_sum,
        sum_q,
        sum_k,
        sum_v,
        bias_sum,
        sum_o.T,
        gain_two_sum,
        sum_g,
        sum_u,
        sum_d.T,
    )


def solution(mesh):
    rows = P("tensor", ("dp", "seq"), None)
    columns = P(None, "tensor")
    return jax.shard_map(
        functools.partial(local, mesh),
        mesh=mesh,
        in_specs=(
            rows,
            rows,
            P(("dp", "seq"), None),
            P(("dp", "seq")),
            P(),
            columns,
            columns,
            columns,
            columns,
            P("tensor", None),
            P(),
            columns,
            columns,
            P("tensor", None),
        ),
        out_specs=(
            rows,
            rows,
            P(),
            P("dp", "tensor"),
            P("dp", "tensor"),
            P("dp", "tensor"),
            P(),
            P("tensor", "dp"),
            P(),
            P("dp", "tensor"),
            P("dp", "tensor"),
            P("tensor", "dp"),
        ),
        check_vma=False,
    )
```

```python
import functools
import math

import jax
import jax.numpy as jnp
from jax import lax
from jax.experimental import pallas as pl
from jax.experimental.pallas import tpu as pltpu
from jax.sharding import PartitionSpec as P

steps_at = (1, 2, 3, 4, 5, 6, 7, 8, 12, 16, 23, 32, 46, 64, 91)
eps_norm = 1e-06
masked_score = -1e30
q_block = 256
band_half = 128
low = jnp.bfloat16
wide = jnp.float32
hint = pl.CostEstimate(flops=1000, bytes_accessed=1000, transcendentals=0)


def dot(a, b, ca, cb):
    return lax.dot_general(a, b, (((ca,), (cb,)), ((), ())), preferred_element_type=wide)


def after(value, *first):
    return lax.optimization_barrier((value, *first))[0]


def front_kernel(
    share, x_h, g_h, wq_h, wk_h, wv_h, wo_h, lengths, valid, bias, gain1_row, gain2_row,
    x_out, g_own, g_oth, g_late, wo_out, w_t_out, xn1_out, qkv_out, mixed_out, probs_h, hres_out, xn2,
    scale1, scale2, gain1, gain2,
    x_in, g_in, w, w_t, xn1, qkv, mixed, hres,
    facts_src, facts, p_buf, table, sx, rx, seg_k, seg_q, send_sems, recv_sems, load_sems,
):
    s = lax.axis_index("seq")
    y = lax.axis_index("tensor")
    c = s % 2
    m = s // 2
    width, half_len = x_in.shape
    length = 2 * half_len
    heads, buckets = bias.shape
    inner = mixed.shape[0]
    dim = inner // heads
    piece = 64
    pieces = width // piece
    mesh_id = dict(device_id_type=pl.DeviceIdType.MESH)
    to_core = {"seq": 2 * m + 1 - c}
    to_swap = {"seq": 2 * m + 1 - c, "tensor": 1 - y}

    def side(i, size):
        return pl.ds(pl.multiple_of(i * size, 128), size)

    my_half = side(c, half_len)
    other_half = side(1 - c, half_len)

    def move(k, src, dst, who):
        return pltpu.make_async_remote_copy(
            src_ref=src, dst_ref=dst, send_sem=send_sems.at[k], recv_sem=recv_sems.at[k], device_id=who, **mesh_id
        )

    to_second = {"seq": 2 * m + y, "tensor": 1 - c}

    named = [(x_h, x_in)] + [
        (src, w.at[pl.ds(i * inner, inner)]) for i, src in enumerate((wq_h, wk_h, wv_h, wo_h))
    ]
    half_cols = half_len // 2
    halves = [pl.ds(h * half_cols, half_cols) for h in range(2)]
    move_x = [move((1, 15)[h], x_h.at[:, halves[h]], x_in.at[:, halves[h]], to_swap) for h in range(2)]
    moves = []
    z = lax.axis_index("dp")
    rows = inner // 2

    def half_of(ref, i, k):
        return ref.at[pl.ds(pl.multiple_of(i * inner + k * rows, rows), rows)]

    fetched, passed_z, passed_x = [], [], []
    for i, src in enumerate((wq_h, wk_h, wv_h, wo_h)):
        if share:
            fetched.append(move(2, half_of(src, 0, m), half_of(w, i, m), to_swap))
            part = half_of(w, (z + 4 - i) % 4, m)
            passed_x.append(move(10 + i, part, part, {"seq": 2 * (1 - m) + c}))
            if i < 3:
                passed_z.append(move(3 + i if i else 14, part, part, {"dp": (z + 1) % 4}))
        else:
            moves.append(move(2 + i, src, w.at[pl.ds(i * inner, inner)], to_swap))
    loads = [pltpu.make_async_copy(src, dst, load_sems.at[1 + i]) for i, (src, dst) in enumerate(named)]
    move_facts = move(0, facts_src, facts, to_swap)
    move_g = move(6, g_in, g_own, to_swap)
    early = g_oth.shape[1]
    second_g = move(9, g_in.at[:, pl.ds(0, early)], g_oth, to_second)
    to = lambda k, src, dst: pltpu.make_async_copy(src, dst, load_sems.at[k])
    keep_late = to(16, g_in.at[:, pl.ds(early, half_len - early)], g_late)
    load_g = pltpu.make_async_copy(g_h, g_in, load_sems.at[0])
    keep_g = pltpu.make_async_copy(g_in, g_own, load_sems.at[6])
    stores = [
        pltpu.make_async_copy(src, dst, load_sems.at[9 + i])
        for i, (src, dst) in enumerate(
            ((x_in, x_out), (w.at[pl.ds(3 * inner, inner)], wo_out), (w_t, w_t_out), (xn1, xn1_out), (qkv, qkv_out),
             (mixed, mixed_out), (hres, hres_out))
        )
    ]

    def pass_on(i):
        if not share:
            return

        @pl.when(c != y)
        def _():
            if i:
                passed_z[i - 1].wait_recv()
            else:
                fetched[0].wait_recv()
            if i < 3:
                passed_z[i].start()
            passed_x[i].start()

    my_parts = [pl.ds(pl.multiple_of(c * half_len + h * half_cols, 128), half_cols) for h in range(2)]
    core_one = [move((7, 16)[h], xn1.at[:, my_parts[h]], xn1.at[:, my_parts[h]], to_core) for h in range(2)]
    core_two = move(8, sx, rx, to_core)

    load_g.start()
    for h in range(heads):
        for b in range(buckets):
            at = h * buckets + b
            facts_src[at : at + 1, :] = jnp.full((1, 128), bias[h, b], wide)
    end = jnp.int32(0)
    at = heads * buckets
    for i in range(4):
        end = end + lengths[0, i]
        facts_src[at + i : at + i + 1, :] = jnp.full((1, 128), end.astype(wide), wide)
    facts_src[at + 4 : at + 5, :] = jnp.full((1, 128), valid[0].astype(wide), wide)

    barrier = pltpu.get_barrier_semaphore()
    greet = [to_core, to_swap, {"tensor": 1 - y}]
    if share:
        greet += [{"seq": 2 * (1 - m) + c}, {"dp": (z + 1) % 4}, {"dp": (z + 3) % 4}]
    for who in greet:
        pl.semaphore_signal(barrier, inc=1, device_id=who, **mesh_id)
    pl.semaphore_wait(barrier, len(greet))

    @pl.when(c != y)
    def _():
        move_facts.start()
        for i, each in enumerate(fetched):
            pl.when(z == i)(each.start)
        for each in move_x + moves:
            each.start()

    @pl.when(c == y)
    def _():
        for each in loads:
            each.start()
        facts[...] = facts_src[...]

    load_g.wait()
    live = lax.broadcasted_iota(jnp.int32, (piece, half_len), 1) + y * half_len < valid[0]

    def mask(i, carry):
        at = pl.ds(pl.multiple_of(i * piece, piece), piece)
        g_in[at, :] = jnp.where(live, g_in[at, :].astype(wide), 0.0).astype(low)
        return carry

    lax.fori_loop(0, pieces, mask, 0)

    @pl.when(c != y)
    def _():
        move_g.start()

    @pl.when(c == y)
    def _():
        keep_g.start()

    second_g.start()
    keep_late.start()
    pass_on(0)
    gain1[...] = jnp.broadcast_to(gain1_row[...].astype(wide)[None, :], (128, width)).T
    gain2[...] = jnp.broadcast_to(gain2_row[...].astype(wide)[None, :], (128, width)).T

    pass_on(1)

    @pl.when(c != y)
    def _():
        move_facts.wait_recv()

    at = heads * buckets

    def segments(positions):
        count = jnp.zeros(positions.shape, wide)
        for i in range(4):
            count = count + jnp.where(positions >= facts[at + i : at + i + 1, :], 1.0, 0.0)
        return jnp.where(positions < facts[at + 4 : at + 5, :], count, 4.0)

    seg_k[...] = segments(lax.broadcasted_iota(jnp.int32, (length, 128), 0).astype(wide))
    for i in range(length // 128):
        positions = (lax.broadcasted_iota(jnp.int32, (8, 128), 1) + i * 128).astype(wide)
        seg_q[:, i * 128 : (i + 1) * 128] = segments(positions)
    pass_on(2)
    reach = length - q_block
    near_rows = q_block + 2 * band_half
    d = (
        lax.broadcasted_iota(jnp.int32, (near_rows, 128), 0)
        - lax.broadcasted_iota(jnp.int32, (near_rows, 128), 1)
        - band_half
    )
    far_rows = reach - band_half
    for h in range(heads):

        def value(b, h=h):
            return facts[h * buckets + b : h * buckets + b + 1, :]

        for i in range(q_block // 128):
            offset = d - i * 128
            n = jnp.abs(offset)
            before = jnp.broadcast_to(value(0), n.shape)
            later = jnp.broadcast_to(value(16), n.shape)
            for number, step in enumerate(steps_at):
                reached = n >= step
                before = jnp.where(reached, value(number + 1), before)
                later = jnp.where(reached, value(number + 17), later)
            col = pl.ds(i * 128, 128)
            table[h, pl.ds(far_rows, near_rows), col] = jnp.where(offset > 0, later, before)
            table[h, pl.ds(0, far_rows), col] = jnp.broadcast_to(value(15), (far_rows, 128))
            table[h, pl.ds(far_rows + near_rows, far_rows), col] = jnp.broadcast_to(value(31), (far_rows, 128))

    def norm(read, gain, scale, cols, write):
        size = cols.size

        def first(i, total):
            v = read(pl.ds(pl.multiple_of(i * piece, piece), piece))
            return total + jnp.sum(v * v, axis=0, keepdims=True)

        total = lax.fori_loop(0, pieces, first, jnp.zeros((1, size), wide))
        scale[:, cols] = lax.rsqrt(total * (1.0 / width) + eps_norm)

        def second(i, carry):
            at = pl.ds(pl.multiple_of(i * piece, piece), piece)
            spread = jnp.concatenate([gain[at, :]] * (size // 128), axis=1)
            write(at, (read(at) * scale[:, cols] * spread).astype(low))
            return carry

        lax.fori_loop(0, pieces, second, 0)

    def arrived(i):
        @pl.when(c != y)
        def _():
            if not share:
                moves[i - 1].wait_recv()

        @pl.when(c == y)
        def _():
            loads[i].wait()

    pass_on(3)
    for h in range(2):

        @pl.when(c != y)
        def _(h=h):
            move_x[h].wait_recv()

        if h == 0:

            @pl.when(c == y)
            def _():
                loads[0].wait()

        def write_one(at, value, h=h):
            xn1[at, my_parts[h]] = value

        norm(lambda at, h=h: x_in[at, halves[h]].astype(wide), gain1, scale1, halves[h], write_one)
        core_one[h].start()
    stores[0].start()
    if share:

        @pl.when(c != y)
        def _():
            for each in passed_x:
                each.wait_recv()

    for each in core_one:
        each.wait_recv()
    stores[3].start()
    for i in range(3):
        arrived(1 + i)
        qkv[i * inner : (i + 1) * inner, :] = dot(w[i * inner : (i + 1) * inner, :], xn1[...], 1, 0).astype(low)

    stores[4].start()

    blocks = length // q_block

    turns = heads * blocks // 2

    def turn(i):
        its = 1 - c + (i // turns) * (2 * c - 1)
        return i % heads, its * (blocks // 2) + (i % turns) // heads

    def store(i):
        h, b = turn(i)
        return pltpu.make_async_copy(p_buf.at[i % 2], probs_h.at[h, :, side(b, q_block)], load_sems.at[7 + i % 2])

    def rows_of(part, i):
        return pl.ds(pl.multiple_of((part * heads + turn(i)[0]) * dim, dim), dim)

    def probs_of(i):
        h, b = turn(i)
        first = pl.multiple_of(reach - b * q_block, q_block)
        at = side(b, q_block)
        scores = dot(qkv[rows_of(1, i), :], qkv[rows_of(0, i), at], 0, 0) + table[h, pl.ds(first, length), :]
        keys = jnp.concatenate([seg_k[...]] * (q_block // 128), axis=1)
        scores = jnp.where(keys == seg_q[0:1, at], scores, masked_score)
        raised = jnp.exp(scores - jnp.max(scores, axis=0, keepdims=True))
        return (raised * (1.0 / jnp.sum(raised, axis=0, keepdims=True))).astype(low)

    def block(i, carry):
        both = [probs_of(2 * i + k) for k in range(2)]
        outs = [dot(qkv[rows_of(2, 2 * i + k), :], both[k], 1, 0).astype(low) for k in range(2)]
        for k in range(2):
            mixed[rows_of(0, 2 * i + k), side(turn(2 * i + k)[1], q_block)] = outs[k]

        @pl.when(i >= 1)
        def _():
            for k in range(2):
                store(2 * i + k - 2).wait()

        for k in range(2):
            p_buf[k] = both[k]
            store(2 * i + k).start()
        return carry

    lax.fori_loop(0, turns // 2, block, 0)
    arrived(4)
    stores[1].start()
    out_w = w[3 * inner :, :]
    sx[...] = dot(out_w, mixed[:, other_half], 0, 0).astype(low)
    core_two.start()
    w_t[...] = w[: 3 * inner, :].T
    stores[2].start()
    lax.fori_loop(turns // 2, turns, block, 0)
    stores[5].start()
    hres[...] = dot(out_w, mixed[:, my_half], 0, 0)
    core_two.wait_recv()

    def add(i, carry):
        at = pl.ds(pl.multiple_of(i * piece, piece), piece)
        hres[at, :] += x_in[at, :].astype(wide) + rx[at, :].astype(wide)
        return carry

    lax.fori_loop(0, pieces, add, 0)

    stores[6].start()

    def write_two(at, value):
        xn2[at, :] = value

    norm(lambda at: hres[at, :], gain2, scale2, pl.ds(0, half_len), write_two)
    last = heads * blocks
    store(last - 2).wait()
    store(last - 1).wait()
    for each in (*core_one, core_two):
        each.wait_send()

    @pl.when(c != y)
    def _():
        move_facts.wait_send()
        if share:
            fetched[0].wait_send()
        for each in move_x + moves + passed_z + passed_x:
            each.wait_send()
        move_g.wait()

    @pl.when(c == y)
    def _():
        keep_g.wait()

    second_g.wait()
    keep_late.wait()
    for each in stores:
        each.wait()


def front(x, g, weights, lengths, valid, bias, gain_one, gain_two, share):
    width, half_len = x.shape
    length = 2 * half_len
    heads = bias.shape[0]
    inner = weights[0].shape[0]
    hbm = pl.BlockSpec(memory_space=pl.ANY)
    vmem = pl.BlockSpec(memory_space=pltpu.VMEM)
    smem = pl.BlockSpec(memory_space=pltpu.SMEM)
    sds = lambda kind, *shape: jax.ShapeDtypeStruct(shape, kind)
    facts = pltpu.VMEM((heads * bias.shape[1] + 8, 128), wide)
    b16 = lambda *shape: pltpu.VMEM(shape, low)
    return pl.pallas_call(
        functools.partial(front_kernel, share),
        in_specs=[hbm] * 6 + [smem] * 3 + [vmem] * 2,
        out_specs=[hbm] * 11 + [vmem] * 5,
        out_shape=[
            sds(low, width, half_len),
            sds(low, width, half_len),
            sds(low, width, half_len - 128),
            sds(low, width, 128),
            sds(low, inner, width),
            sds(low, width, 3 * inner),
            sds(low, width, length),
            sds(low, 3 * inner, length),
            sds(low, inner, length),
            sds(low, heads, length, length),
            sds(wide, width, half_len),
            sds(low, width, half_len),
            sds(wide, 1, half_len),
            sds(wide, 1, half_len),
            sds(wide, width, 128),
            sds(wide, width, 128),
        ],
        scratch_shapes=[
            b16(width, half_len),
            b16(width, half_len),
            b16(4 * inner, width),
            b16(width, 3 * inner),
            b16(width, length),
            b16(3 * inner, length),
            b16(inner, length),
            pltpu.VMEM((width, half_len), wide),
            facts,
            facts,
            b16(2, length, q_block),
            pltpu.VMEM((heads, 2 * length - q_block, q_block), wide),
            b16(width, half_len),
            b16(width, half_len),
            pltpu.VMEM((length, 128), wide),
            pltpu.VMEM((8, length), wide),
            pltpu.SemaphoreType.DMA((17,)),
            pltpu.SemaphoreType.DMA((17,)),
            pltpu.SemaphoreType.DMA((17,)),
        ],
        compiler_params=pltpu.CompilerParams(vmem_limit_bytes=60 << 20, collective_id=2, has_side_effects=True),
        cost_estimate=hint,
        name="front_all",
    )(x, g, *weights, lengths, valid, bias, gain_one, gain_two)


def attn_bwd_kernel(length, q_ref, k_ref, v_ref, go_ref, o_ref, p_ref, gq_ref, gk_ref, gv_ref, gb_ref, k_acc, v_acc, sums):
    block = pl.program_id(1)
    reach = length - q_block

    @pl.when(block == 0)
    def _():
        k_acc[...] = jnp.zeros_like(k_acc)
        v_acc[...] = jnp.zeros_like(v_acc)
        sums[...] = jnp.zeros_like(sums)

    probs = p_ref[0]
    go = go_ref[...]
    inner = jnp.sum(go.astype(wide) * o_ref[...].astype(wide), axis=0, keepdims=True)
    scores = probs.astype(wide) * (dot(v_ref[...], go, 0, 0) - inner)
    first = pl.multiple_of(reach - block * q_block, q_block)
    sums[pl.ds(first, length), :] += scores
    scores = scores.astype(low)
    gq_ref[...] = dot(k_ref[...], scores, 1, 0).astype(low)
    k_acc[...] += dot(q_ref[...], scores, 1, 1)
    v_acc[...] += dot(go, probs, 1, 1)

    @pl.when(block == pl.num_programs(1) - 1)
    def _():
        gk_ref[...] = k_acc[...].astype(low)
        gv_ref[...] = v_acc[...].astype(low)
        rows = q_block + 2 * band_half
        d = (
            lax.broadcasted_iota(jnp.int32, (rows, q_block), 0)
            - lax.broadcasted_iota(jnp.int32, (rows, q_block), 1)
            - band_half
        )
        n = jnp.abs(d)
        near = sums[reach - band_half : reach + q_block + band_half, :]
        far_before = jnp.sum(sums[: reach - band_half, :], axis=0, keepdims=True)
        far_after = jnp.sum(sums[reach + q_block + band_half :, :], axis=0, keepdims=True)
        bucket = jnp.zeros((rows, q_block), jnp.int32)
        for step in steps_at:
            bucket = bucket + jnp.where(n >= step, 1, 0)
        bucket = bucket + jnp.where(d > 0, 16, 0)
        for b in range(32):
            total = jnp.sum(jnp.where(bucket == b, near, 0.0), axis=0, keepdims=True)
            if b == 15:
                total = total + far_before
            if b == 31:
                total = total + far_after
            gb_ref[0, b : b + 1, :] = total


def attn_backward(qkv, grad_mixed, mixed, probs):
    width, length = qkv.shape
    heads = probs.shape[0]
    dim = width // (3 * heads)
    blocks = length // q_block
    half = pl.BlockSpec((dim, q_block), lambda h, b: (h, b))
    whole = pl.BlockSpec((dim, length), lambda h, b: (h, 0))
    gq, gk, gv, gb = pl.pallas_call(
        functools.partial(attn_bwd_kernel, length),
        grid=(heads, blocks),
        in_specs=[
            half,
            pl.BlockSpec((dim, length), lambda h, b: (heads + h, 0)),
            pl.BlockSpec((dim, length), lambda h, b: (2 * heads + h, 0)),
            half,
            half,
            pl.BlockSpec((1, length, q_block), lambda h, b: (h, 0, b)),
        ],
        out_specs=[half, whole, whole, pl.BlockSpec((1, 32, q_block), lambda h, b: (h, 0, 0))],
        out_shape=[
            jax.ShapeDtypeStruct((heads * dim, length), low),
            jax.ShapeDtypeStruct((heads * dim, length), low),
            jax.ShapeDtypeStruct((heads * dim, length), low),
            jax.ShapeDtypeStruct((heads, 32, q_block), wide),
        ],
        scratch_shapes=[
            pltpu.VMEM((dim, length), wide),
            pltpu.VMEM((dim, length), wide),
            pltpu.VMEM((2 * length - q_block, q_block), wide),
        ],
        compiler_params=pltpu.CompilerParams(vmem_limit_bytes=48 << 20),
        cost_estimate=hint,
        name="attn_backward",
    )(qkv, qkv, qkv, grad_mixed, mixed, probs)
    return jnp.concatenate([gq, gk, gv], axis=0), jnp.sum(gb, axis=2).T


def ffn_kernel(
    x_ref, go_ref, gr_h0, hres_h, g_late, gate_w, up_w, down_w,
    hid_ref, pair_ref, xr_h, gr_h, out_h, out_r_h, gx_h, late_h,
    xs, gs, out_acc, gx_acc, x_in, g_in, gx_out, gx_in, out_v, gx_v, gr_ref, hres_ref, sems, store_sems,
):
    chunk = pl.program_id(0)
    tile = pl.program_id(1)
    size = xs.shape[0]
    mesh_id = dict(device_id_type=pl.DeviceIdType.MESH)
    s = lax.axis_index("seq")
    y = lax.axis_index("tensor")
    c = s % 2
    to_y = {"tensor": 1 - y}
    to_second = {"seq": s - c + y, "tensor": 1 - c}
    half = [pl.ds(0, size), pl.ds(size, size)]

    def move(k, src, dst, who):
        return pltpu.make_async_remote_copy(
            src_ref=src, dst_ref=dst, send_sem=sems.at[k], recv_sem=sems.at[4 + k], device_id=who, **mesh_id
        )

    send_x = [move(h, x_ref.at[:, half[h]], x_in.at[h], to_y) for h in range(2)]
    send_g = move(2, g_late, g_in, to_second)
    back = gx_in.shape[1]
    send_gx = move(3, gx_out.at[0, :, pl.ds(0, back)], gx_in, to_y)
    begun = g_in.shape[1]
    to = lambda k, src, dst: pltpu.make_async_copy(src, dst, store_sems.at[k])
    store_x = [to(h, x_in.at[h], xr_h.at[:, half[h]]) for h in range(2)]
    store_out = [to(2 + h, out_v.at[h], out_h.at[:, half[h]]) for h in range(2)]
    store_out_r = [to(4 + h, out_v.at[2 + h], out_r_h.at[:, half[h]]) for h in range(2)]
    store_gx = [to(6 + h, gx_v.at[h], gx_h.at[:, half[h]]) for h in range(2)]
    store_late = [to(8 + h, gx_out.at[h], late_h.at[:, half[h]]) for h in range(2)]
    store_g = to(10, g_in, gr_h)
    load_h = to(11, hres_h, hres_ref)
    load_g = to(12, gr_h0, gr_ref)

    @pl.when(tile == 0)
    def _():
        out_acc[...] = jnp.zeros_like(out_acc)
        gx_acc[...] = jnp.zeros_like(gx_acc)

    @pl.when((tile == 0) & (chunk == 0))
    def _():
        load_h.start()
        load_g.start()
        barrier = pltpu.get_barrier_semaphore()
        for who in (to_y, {"seq": s + 1 - 2 * c}):
            pl.semaphore_signal(barrier, inc=1, device_id=who, **mesh_id)
        pl.semaphore_wait(barrier, 2)
        for each in (*send_x, send_g):
            each.start()

    for h in range(2):

        @pl.when((tile == 0) & (chunk == h))
        def _(h=h):
            xs[...] = x_ref[:, half[h]].T
            gs[...] = go_ref[:, half[h]].T

        @pl.when((tile == 0) & (chunk == 2 + h))
        def _(h=h):
            send_x[h].wait_recv()
            xs[...] = x_in[h].T
            store_x[h].start()
            if not h:
                load_g.wait()
            if h:
                gs[: size - begun, :] = gr_ref[:, size:].T
                send_g.wait_recv()
                gs[size - begun :, :] = g_in[...].T
                store_g.start()
            else:
                gs[...] = gr_ref[:, :size].T

    gate = dot(xs[...], gate_w[...], 1, 0)
    up = dot(xs[...], up_w[...], 1, 0)
    grad = dot(gs[...], down_w[...], 1, 0)
    c_gelu = math.sqrt(2.0 / math.pi)
    square = gate * gate
    t = jnp.tanh(c_gelu * gate * (1.0 + 0.044715 * square))
    part = 0.5 * (1.0 + t)
    gelu = gate * part
    slope = part + 0.5 * gate * (1.0 - t * t) * (c_gelu * (1.0 + 3 * 0.044715 * square))
    hid = (gelu * up).astype(low)
    gg = (grad * up * slope).astype(low)
    gu = (grad * gelu).astype(low)
    hid_ref[...] = hid
    pair_ref[0] = gg
    pair_ref[1] = gu
    out_acc[...] += dot(down_w[...], hid, 1, 1)
    gx_acc[...] += dot(gate_w[...], gg, 1, 1) + dot(up_w[...], gu, 1, 1)

    last = tile == pl.num_programs(1) - 1
    for h in range(2):

        @pl.when(last & (chunk == h))
        def _(h=h):
            if not h:
                load_h.wait()
            out_v[h] = (hres_ref[:, half[h]] + out_acc[...]).astype(low)
            store_out[h].start()
            gx_v[h] = gx_acc[...]
            if h:
                store_gx[h].start()

        @pl.when(last & (chunk == 2 + h))
        def _(h=h):
            out_v[2 + h] = out_acc[...].astype(low)
            store_out_r[h].start()
            gx_out[h] = gx_acc[...].astype(low)
            if not h:
                send_gx.start()
            store_late[h].start()

    @pl.when(last & (chunk == 3))
    def _():
        send_gx.wait_recv()
        gx_v[0, :, :back] += gx_in[...].astype(wide)
        store_gx[0].start()
        for each in (*send_x, send_g, send_gx):
            each.wait_send()
        for each in store_x + store_out + store_out_r + store_gx + store_late + [store_g]:
            each.wait()


def ffn(x, g_own, g_oth, hres, g_late, gate_w, up_w, down_w):
    width, tokens = x.shape
    hidden = gate_w.shape[1]
    tile, size = hidden // 2, tokens // 2
    begun = g_late.shape[1]
    hbm = pl.BlockSpec(memory_space=pl.ANY)
    full = pl.BlockSpec((width, tokens), lambda s, j: (0, 0), pipeline_mode=pl.Buffered(1))
    weight = pl.BlockSpec((width, tile), lambda s, j: (0, j))
    act_shape = jax.ShapeDtypeStruct((2 * tokens, hidden), low)
    tokens_of = lambda kind: jax.ShapeDtypeStruct((width, tokens), kind)
    return pl.pallas_call(
        ffn_kernel,
        grid=(4, hidden // tile),
        in_specs=[full, full, hbm, hbm, hbm, weight, weight, weight],
        out_specs=[
            pl.BlockSpec((size, tile), lambda s, j: (s, j)),
            pl.BlockSpec((2, size, tile), lambda s, j: (0, s, j)),
        ]
        + [hbm] * 6,
        out_shape=[act_shape, jax.ShapeDtypeStruct((2, 2 * tokens, hidden), low)]
        + [tokens_of(low), jax.ShapeDtypeStruct((width, begun), low)]
        + [tokens_of(kind) for kind in (low, low, wide, low)],
        scratch_shapes=[
            pltpu.VMEM((size, width), low),
            pltpu.VMEM((size, width), low),
            pltpu.VMEM((width, size), wide),
            pltpu.VMEM((width, size), wide),
            pltpu.VMEM((2, width, size), low),
            pltpu.VMEM((width, begun), low),
            pltpu.VMEM((2, width, size), low),
            pltpu.VMEM((width, 128), low),
            pltpu.VMEM((4, width, size), low),
            pltpu.VMEM((2, width, size), wide),
            pltpu.VMEM((width, tokens - begun), low),
            pltpu.VMEM((width, tokens), wide),
            pltpu.SemaphoreType.DMA((8,)),
            pltpu.SemaphoreType.DMA((13,)),
        ],
        compiler_params=pltpu.CompilerParams(vmem_limit_bytes=60 << 20, collective_id=0, has_side_effects=True),
        cost_estimate=hint,
        name="ffn_both_ways",
    )(x, g_own, g_oth, hres, g_late, gate_w, up_w, down_w)


def weight_grad_kernel(core_ref, own_ref, oth_ref, right_ref, *refs):
    tokens = own_ref.shape[1]
    total = dot(own_ref[...], right_ref[:tokens, :], 1, 0) + dot(oth_ref[...], right_ref[tokens:, :], 1, 0)
    if len(refs) == 2:
        total = total + refs[0][...].astype(wide)
    refs[-1][...] = total.astype(low)


def weight_grad(own, oth, right, core, got=None):
    width, tokens = own.shape
    columns = right.shape[1] // 2
    blocks = 4
    rows = width // blocks
    left = pl.BlockSpec((rows, tokens), lambda i, core_ref: (i, 0))
    out = pl.BlockSpec((rows, columns), lambda i, core_ref: (i, 0))
    args = [own, oth, right] + ([] if got is None else [got])
    return pl.pallas_call(
        weight_grad_kernel,
        grid_spec=pltpu.PrefetchScalarGridSpec(
            num_scalar_prefetch=1,
            grid=(blocks,),
            in_specs=[
                left,
                left,
                pl.BlockSpec((2 * tokens, columns), lambda i, core_ref: (0, core_ref[0]), pipeline_mode=pl.Buffered(1)),
            ]
            + ([] if got is None else [out]),
            out_specs=out,
        ),
        out_shape=jax.ShapeDtypeStruct((width, columns), low),
        compiler_params=pltpu.CompilerParams(vmem_limit_bytes=40 << 20),
        cost_estimate=hint,
        name="weight_grad",
    )(core.reshape(1), *args)


def back_kernel(
    hid_h, pair_h, go_h, gr1_h, gr2_h, xo_h, xr_h, gx_h, hres_h, xin_h, probs_h, xn1_h, outp_h, outr_h, late_h,
    out_w_h, w_t_h, qkv_h, mixed_h, gain2_h, gain1_h, scale2, scale1,
    got_p, got_r, got_in, d_out_h, gin_h, p_out, a_out, small,
    out_w, w_t, qkv, mixed, gain2, gain1, d_out, gin,
    r_core, xp, zd, zp, dx, bf, rx, ya, xa, za, late_in, sm_src, sm_in, send_sems, recv_sems, load_sems,
):
    s = lax.axis_index("seq")
    y = lax.axis_index("tensor")
    z = lax.axis_index("dp")
    c = s % 2
    m = s // 2
    width = xp.shape[0]
    rows = d_out.shape[0]
    columns = xp.shape[1]
    half_len = rx.shape[1]
    length = 2 * half_len
    heads = probs_h.shape[0]
    dim = mixed.shape[0] // heads
    zs = width // rows
    mesh_id = dict(device_id_type=pl.DeviceIdType.MESH)
    to_core = {"seq": 2 * m + 1 - c}
    to_x = {"seq": 2 * (1 - m) + c}
    to_y = {"tensor": 1 - y}
    to_z = {"dp": (z + 1) % zs}
    to_swap = {"seq": 2 * m + y, "tensor": c}
    to_back = {"seq": 2 * m + 1 - y, "tensor": c}

    def move(k, src, dst, who):
        return pltpu.make_async_remote_copy(
            src_ref=src, dst_ref=dst, send_sem=send_sems.at[k], recv_sem=recv_sems.at[k], device_id=who, **mesh_id
        )

    def load(k, src, dst):
        return pltpu.make_async_copy(src, dst, load_sems.at[k])

    def chunk(j):
        return pl.ds(pl.multiple_of(j * rows, rows), rows)

    def side(i, size):
        return pl.ds(pl.multiple_of(i * size, 128), size)

    order = [(z + zs - 1 - k) % zs for k in range(zs)]
    mine = side(c, columns)
    my_half = side(c, half_len)
    other_half = side(1 - c, half_len)
    cut = [(0, 192), (192, rows - 192)]

    def part(j, p):
        return pl.ds(pl.multiple_of(j * rows + cut[p][0], 16), cut[p][1])

    parts = [pl.ds(*each) for each in cut]

    late_from = half_len - late_in.shape[1]
    late = move(0, late_h.at[:, pl.ds(late_from, half_len - late_from)], late_in, to_y)
    swap_out = move(1, outp_h, got_p, to_swap)
    back_out = move(2, outr_h, got_r, to_back)
    both = range(2)
    steps = range(zs - 1)
    z_down = [
        [move(3 + 2 * t + p, zd.at[t - 1, parts[p]] if t else r_core.at[0, part(order[0], p)], zd.at[t, parts[p]], to_z) for p in both]
        for t in steps
    ]
    x_down = [move(9 + p, zd.at[2, parts[p]], dx.at[parts[p]], to_x) for p in both]
    core_down = [move(11 + p, d_out.at[parts[p], mine], d_out.at[parts[p], mine], to_core) for p in both]
    z_pair = [
        [move(13 + 2 * t + p, zp.at[t - 1, parts[p]] if t else r_core.at[2, part(order[0], p)], zp.at[t, parts[p]], to_z) for p in both]
        for t in steps
    ]
    x_pair_back = [move(19 + p, zp.at[2, parts[p]], p_out.at[m, parts[p], mine], to_x) for p in both]
    core_pair = [move(21 + p, p_out.at[m, parts[p], mine], p_out.at[m, parts[p], mine], to_core) for p in both]
    core_pair_back = [
        move(23 + p, p_out.at[1 - m, parts[p], mine], p_out.at[1 - m, parts[p], mine], to_core) for p in both
    ]
    core_branch = move(25, bf.at[:, my_half], bf.at[:, my_half], to_core)
    a_rows = xa.shape[1]
    my_rows = pl.ds(pl.multiple_of(m * a_rows, a_rows), a_rows)
    x_rows = pl.ds(pl.multiple_of((1 - m) * a_rows, a_rows), a_rows)
    x_attn = [move(26 + k, ya.at[j, x_rows], xa.at[j], to_x) for k, j in enumerate(order)]
    z_attn = [move(30 + t, za.at[t - 1] if t else ya.at[order[0], my_rows], za.at[t], to_z) for t in steps]
    x_attn_back = move(33, a_out.at[my_rows], a_out.at[my_rows], to_x)
    core_attn = move(34, a_out, a_out, to_core)
    swap_in = move(35, gin, got_in, to_swap)

    def x_pair(k):
        at = chunk((z + zs - 1 - k) % zs)
        return move(46 + k, r_core.at[1, at], xp.at[at], to_x)

    def meet():
        barrier = pltpu.get_barrier_semaphore()
        greet = [to_core, to_y, {"seq": 2 * m + 1 - c, "tensor": 1 - y}, to_x] + [{"dp": (z + i) % zs} for i in range(1, zs)]
        for who in greet:
            pl.semaphore_signal(barrier, inc=1, device_id=who, **mesh_id)
        pl.semaphore_wait(barrier, len(greet))
        late.start()

    def step_z_down(t, p):
        z_down[t - 1][p].wait_recv()
        at = parts[p]
        zd[t - 1, at, :] = (zd[t - 1, at, :].astype(wide) + r_core[0, part(order[t], p), :].astype(wide)).astype(low)
        (z_down[t][p] if t < zs - 1 else x_down[p]).start()

    def end_down(p):
        x_down[p].wait_recv()
        at = parts[p]
        d_out[at, mine] = (zd[2, at, :].astype(wide) + dx[at, :].astype(wide)).astype(low)
        core_down[p].start()

    def step_z_pair(t, p):
        if p == 0:
            x_pair(t).wait_recv()
        at = parts[p]
        term = r_core[2, part(order[t], p), :].astype(wide) + xp[part(order[t], p), :].astype(wide)
        if t:
            z_pair[t - 1][p].wait_recv()
            term = zp[t - 1, at, :].astype(wide) + term
            zp[t - 1, at, :] = term.astype(low)
        else:
            r_core[2, part(order[0], p), :] = term.astype(low)
        if t < zs - 1:
            z_pair[t][p].start()
        else:
            x_pair_back[p].start()
            p_out[m, at, mine] = term.astype(low)
            core_pair[p].start()

    def end_pair(p):
        x_pair_back[p].wait_recv()
        core_pair_back[p].start()

    def step_attn(t):
        @pl.when(c == y)
        def _():
            x_attn[t].wait_recv()
            term = ya[order[t], my_rows, :].astype(wide) + xa[order[t]].astype(wide)
            if t:
                z_attn[t - 1].wait_recv()
                za[t - 1] = (za[t - 1].astype(wide) + term).astype(low)
            else:
                ya[order[0], my_rows, :] = term.astype(low)
            if t < zs - 1:
                z_attn[t].start()
            else:
                a_out[my_rows, :] = za[zs - 2]
                x_attn_back.start()

    hops = [to_core, to_y, to_x, {"dp": z + 1 - 2 * (z % 2)}, {"dp": (z + 2) % zs}]
    exchange = [move(41 + i, sm_src.at[i], sm_in.at[i], who) for i, who in enumerate(hops)]

    def start_sum(i):
        sm_src[i] = small[...]
        exchange[i].start()

    def end_sum(i):
        exchange[i].wait_recv()
        small[...] = sm_src[i] + sm_in[i]

    aside = [
        load(15 + i, src, dst)
        for i, (src, dst) in enumerate(
            ((out_w_h, out_w), (w_t_h, w_t), (qkv_h, qkv), (mixed_h, mixed), (gain2_h, gain2), (gain1_h, gain1))
        )
    ]
    store_in_grad = load(21, gin, gin_h)
    store_down = load(22, d_out, d_out_h)

    def weights(r_buf, l_go, l_gr, l_xo, l_xr, s_buf):
        loads = [
            load(0, hid_h, r_buf.at[0]),
            load(1, go_h, l_go),
            load(2, gr1_h, l_gr.at[:, pl.ds(0, gr1_h.shape[1])]),
            load(3, gr2_h, l_gr.at[:, pl.ds(gr1_h.shape[1], gr2_h.shape[1])]),
            load(4, pair_h.at[1 - m], r_buf.at[1]),
            load(5, xo_h, l_xo),
            load(14, xr_h, l_xr),
        ]
        load_own = load(6, pair_h.at[m], r_buf.at[0])
        for each in loads:
            each.start()
        theirs = side(1 - c, columns)

        def core(i, k):
            at = chunk((z + zs - 1 - k) % zs)
            return move(50 + i * zs + k, s_buf.at[i % 2, at], r_core.at[i, at], to_core)

        def product(left_o, left_r, right, col, at):
            total = dot(left_o[at, :], right[:half_len, col], 1, 0)
            return total + dot(left_r[at, :], right[half_len:, col], 1, 0)

        def send_part(left_o, left_r, right, i, k):
            at = chunk((z + zs - 1 - k) % zs)
            s_buf[i % 2, at, :] = product(left_o, left_r, right, theirs, at).astype(low)
            core(i, k).start()

        def keep_part(left_o, left_r, right, i, k):
            at = chunk((z + zs - 1 - k) % zs)
            total = product(left_o, left_r, right, mine, at)
            core(i, k).wait_recv()
            r_core[i, at, :] = (total + r_core[i, at, :].astype(wide)).astype(low)

        def sent(i):
            def block(k, carry):
                core(i, k).wait_send()
                return carry

            lax.fori_loop(0, zs, block, 0)

        for each in aside:
            each.start()
        down = (l_go, l_gr, r_buf.at[0], 0)
        theirs_first = (l_xo, l_xr, r_buf.at[1], 1)
        own = (l_xo, l_xr, r_buf.at[0], 2)
        meet()
        for each in loads:
            each.wait()

        def first(k, carry):
            @pl.when(k < zs)
            def _():
                send_part(*down, k)
                send_part(*theirs_first, k)

            @pl.when(k > 0)
            def _():
                keep_part(*down, k - 1)

                @pl.when(k == 1)
                def _():
                    for each in z_down[0]:
                        each.start()

                keep_part(*theirs_first, k - 1)
                x_pair(k - 1).start()

            return carry

        lax.fori_loop(0, zs + 1, first, 0)
        load_own.start()
        step_z_down(1, 0)

        @pl.when(c != y)
        def _():
            swap_out.start()

        back_out.start()
        sent(0)
        load_own.wait()

        def second(k, carry):
            @pl.when(k == 2)
            def _():
                step_z_down(1, 1)

            @pl.when(k == zs)
            def _():
                step_z_pair(0, 0)
                step_z_pair(0, 1)
                step_z_down(2, 0)

            @pl.when(k < zs)
            def _():
                send_part(*own, k)

            @pl.when(k > 0)
            def _():
                keep_part(*own, k - 1)

            return carry

        lax.fori_loop(0, zs + 1, second, 0)
        sent(1)
        sent(2)

    hidden = hid_h.shape[1]
    left = pltpu.VMEM((width, half_len), low)
    pl.run_scoped(
        weights,
        pltpu.VMEM((2, length, hidden), low),
        left,
        left,
        left,
        left,
        pltpu.VMEM((2, width, columns), low),
    )

    def attention(gxv, hv, gov, p_buf, k_acc, v_acc, sums, gqkv, gm, xn1, sx, ga):
        loads = [load(7, gx_h, gxv), load(8, hres_h, hv), load(9, go_h, gov), load(10, xn1_h, xn1)]
        load_x = load(11, xin_h, gov)
        for each in loads:
            each.start()

        def probs_load(h, b, slot):
            return load(12 + slot, probs_h.at[h, :, side(b, q_block)], p_buf.at[slot])

        probs_load(0, 0, 0).start()
        lanes = half_len // 128
        piece = 64
        pieces = width // piece

        def fold(a):
            return sum(a[:, i * 128 : (i + 1) * 128] for i in range(lanes))

        def spread(a):
            return jnp.concatenate([a] * lanes, axis=1)

        def norm_backward(values, gain, scale, grad, store, row):
            def first(i, total):
                at = pl.ds(pl.multiple_of(i * piece, piece), piece)
                return total + jnp.sum(values(at) * (spread(gain[at, :]) * grad(at)), axis=0, keepdims=True)

            total = lax.fori_loop(0, pieces, first, jnp.zeros((1, half_len), wide))
            mean = total * scale[...] * (1.0 / width)

            def second(i, carry):
                at = pl.ds(pl.multiple_of(i * piece, piece), piece)
                g = grad(at)
                normed = values(at) * scale[...]
                store(at, scale[...] * (spread(gain[at, :]) * g - normed * mean))
                ga_part[at, :] = fold(g * normed)
                return carry

            lax.fori_loop(0, pieces, second, 0)
            small[row : row + 1, :] = jnp.sum(ga_part[...].T, axis=0, keepdims=True)

        ga_part = sums.at[:width, :128]
        small[...] = jnp.zeros_like(small)
        for each in loads[:3] + aside:
            each.wait()
        late.wait_recv()

        def add_late(i, carry):
            at = pl.ds(pl.multiple_of(i * piece, piece), piece)
            gxv[at, late_from:] += late_in[at, :].astype(wide)
            return carry

        lax.fori_loop(0, pieces, add_late, 0)

        def store_hres(at, back):
            total = gov[at, :].astype(wide) + back
            gxv[at, :] = total
            bf[at, my_half] = total.astype(low)

        norm_backward(lambda at: hv[at, :], gain2, scale2, lambda at: gxv[at, :], store_hres, 0)
        core_branch.start()
        load_x.start()
        step_z_down(2, 1)
        core_branch.wait_recv()
        gm[...] = dot(out_w[...], bf[...], 1, 0).astype(low)

        reach = length - q_block
        blocks = length // q_block
        near_rows = q_block + 2 * band_half
        d = (
            lax.broadcasted_iota(jnp.int32, (near_rows, q_block), 0)
            - lax.broadcasted_iota(jnp.int32, (near_rows, q_block), 1)
            - band_half
        )
        for h in range(heads):
            head = pl.ds(h * dim, dim)
            k_rows = pl.ds((heads + h) * dim, dim)
            v_rows = pl.ds((2 * heads + h) * dim, dim)
            k_acc[...] = jnp.zeros_like(k_acc)
            v_acc[...] = jnp.zeros_like(v_acc)
            sums[...] = jnp.zeros_like(sums)

            def block(b, carry):
                slot = b % 2
                at = side(b, q_block)
                probs_load(h, b, slot).wait()

                @pl.when(b < blocks - 1)
                def _():
                    probs_load(h, b + 1, 1 - slot).start()

                if h < heads - 1:

                    @pl.when(b == blocks - 1)
                    def _():
                        probs_load(h + 1, 0, 1 - slot).start()

                probs = p_buf[slot]
                go = gm[head, at]
                inner = jnp.sum(go.astype(wide) * mixed[head, at].astype(wide), axis=0, keepdims=True)
                scores = probs.astype(wide) * (dot(qkv[v_rows, :], go, 0, 0) - inner)
                first = pl.multiple_of(reach - b * q_block, q_block)
                sums[pl.ds(first, length), :] += scores
                scores = scores.astype(low)
                gqkv[head, at] = dot(qkv[k_rows, :], scores, 1, 0).astype(low)
                k_acc[...] += dot(qkv[head, at], scores, 1, 1)
                v_acc[...] += dot(go, probs, 1, 1)
                return carry

            lax.fori_loop(0, blocks, block, 0)
            gqkv[k_rows, :] = k_acc[...].astype(low)
            gqkv[v_rows, :] = v_acc[...].astype(low)
            near = sums[reach - band_half : reach + q_block + band_half, :]
            n = jnp.abs(d)
            bucket = jnp.zeros((near_rows, q_block), jnp.int32)
            for step in steps_at:
                bucket = bucket + jnp.where(n >= step, 1, 0)
            bucket = bucket + jnp.where(d > 0, 16, 0)
            totals = []
            for b in range(32):
                total = jnp.sum(jnp.where(bucket == b, near, 0.0), axis=0, keepdims=True)
                if b == 15:
                    total = total + jnp.sum(sums[: reach - band_half, :], axis=0, keepdims=True)
                if b == 31:
                    total = total + jnp.sum(sums[reach + q_block + band_half :, :], axis=0, keepdims=True)
                totals.append(total)
            totals = jnp.concatenate(totals, axis=0)
            totals = jnp.concatenate([totals, jnp.zeros((96, q_block), wide)], axis=0)
            line = jnp.sum(totals.T, axis=0, keepdims=True)
            for side_c in range(2):
                row = 8 + side_c * heads + h
                small[row : row + 1, :128] = jnp.where(c == side_c, line, 0.0)
            if h == 0:
                step_z_pair(1, 0)
            if h == 1:
                step_z_down(3, 0)

        def input_grad(half, store):
            def block(i, carry):
                at = chunk(i)
                store(at, dot(w_t[at, :], gqkv[:, half], 1, 0))
                return carry

            lax.fori_loop(0, zs, block, 0)

        def store_sent(at, value):
            sx[at, :] = value.astype(low)

        core_x = move(36, sx, rx, to_core)
        loads[3].wait()
        y_attn = [
            move(37 + k, ga.at[j], ya.at[j], to_y) for k, j in enumerate(order)
        ]
        wide_cols = gqkv.shape[0]

        def weight_part(k):
            j = order[k]
            ga[j, :rows, :wide_cols] = dot(xn1[chunk(j), :], gqkv[...], 1, 1).astype(low)
            ga[j, :rows, wide_cols:] = dot(bf[chunk(j), :], mixed[...], 1, 1).astype(low)
            ga[j, rows:, :] = jnp.zeros((ga.shape[1] - rows, ga.shape[2]), low)
            pl.when(c != y)(y_attn[k].start)

        def store_own(at, value):
            hv[at, :] = value

        def store_in(at, back):
            gin[at, :] = (gxv[at, :] + back).astype(low)

        def step_y_attn(k):
            j = order[k]

            @pl.when(c == y)
            def _():
                y_attn[k].wait_recv()
                ya[j] = (ya[j].astype(wide) + ga[j].astype(wide)).astype(low)
                x_attn[k].start()

        weight_part(0)
        weight_part(1)
        weight_part(2)
        input_grad(other_half, store_sent)
        core_x.start()
        step_z_down(3, 1)
        step_z_pair(2, 0)
        step_z_pair(1, 1)
        input_grad(my_half, store_own)
        end_down(0)
        weight_part(3)
        step_y_attn(0)
        load_x.wait()
        core_x.wait_recv()
        norm_backward(
            lambda at: gov[at, :].astype(wide),
            gain1,
            scale1,
            lambda at: hv[at, :] + rx[at, :].astype(wide),
            store_in,
            1,
        )
        store_in_grad.start()
        start_sum(0)
        end_down(1)
        step_z_pair(3, 0)
        step_y_attn(1)
        end_sum(0)
        start_sum(1)

        @pl.when(c != y)
        def _():
            swap_in.start()

        step_attn(0)
        step_z_pair(2, 1)
        step_y_attn(2)
        end_pair(0)
        step_attn(1)
        step_y_attn(3)
        end_sum(1)
        start_sum(2)
        core_x.wait_send()

        @pl.when(c != y)
        def _():
            for each in y_attn:
                each.wait_send()

    f32 = lambda *shape: pltpu.VMEM(shape, wide)
    b16 = lambda *shape: pltpu.VMEM(shape, low)
    pl.run_scoped(
        attention,
        f32(width, half_len),
        f32(width, half_len),
        b16(width, half_len),
        b16(2, length, q_block),
        f32(dim, length),
        f32(dim, length),
        f32(2 * length - q_block, q_block),
        b16(3 * heads * dim, length),
        b16(heads * dim, length),
        b16(width, length),
        b16(width, half_len),
        b16(*ya.shape),
    )

    step_z_pair(3, 1)
    end_sum(2)
    start_sum(3)
    step_attn(2)
    end_sum(3)
    start_sum(4)
    step_attn(3)
    for each in core_down:
        each.wait()
    store_down.start()
    end_sum(4)
    end_pair(1)

    @pl.when(c == y)
    def _():
        x_attn_back.wait_recv()
        core_attn.start()
        for each in (core_attn, x_attn_back, *x_attn, *z_attn):
            each.wait_send()

    @pl.when(c != y)
    def _():
        core_attn.wait_recv()
        swap_out.wait()
        swap_in.wait()

    back_out.wait()
    for each in core_pair + core_pair_back + [store_in_grad, store_down]:
        each.wait()
    for each in [late, core_branch] + sum(z_down, []) + x_down + sum(z_pair, []) + x_pair_back:
        each.wait_send()
    for each in [x_pair(k) for k in range(zs)] + exchange:
        each.wait_send()


def back_all(
    hid, pair, g_own, g_oth, g_late, x_own, x_oth, gx, hres, x_in, probs, xn_one, out_first, out_oth, late,
    out_w, w_t, qkv, mixed, gain_two, gain_one, scale_two, scale_one, zs,
):
    width, half_len = g_own.shape
    length = 2 * half_len
    rows = width // zs
    columns = hid.shape[1] // 2
    heads = probs.shape[0]
    a_cols = (w_t.shape[1] + out_w.shape[0]) // 2
    a_len = -(-rows // 32) * 32
    hbm = pl.BlockSpec(memory_space=pl.ANY)
    vmem = pl.BlockSpec(memory_space=pltpu.VMEM)
    sds = lambda kind, *shape: jax.ShapeDtypeStruct(shape, kind)
    b16 = lambda *shape: pltpu.VMEM(shape, low)
    return pl.pallas_call(
        back_kernel,
        in_specs=[hbm] * 21 + [vmem] * 2,
        out_specs=[hbm] * 5 + [vmem] * 3,
        out_shape=[
            sds(low, width, half_len),
            sds(low, width, half_len),
            sds(low, width, half_len),
            sds(low, rows, 2 * columns),
            sds(low, width, half_len),
            sds(low, 2, rows, 2 * columns),
            sds(low, a_len, 2 * a_cols),
            sds(wide, 16, width),
        ],
        scratch_shapes=[
            *(pltpu.VMEM(each.shape, each.dtype) for each in (out_w, w_t, qkv, mixed, gain_two, gain_one)),
            b16(rows, 2 * columns),
            b16(width, half_len),
            b16(3, width, columns),
            b16(width, columns),
            b16(zs - 1, rows, columns),
            b16(zs - 1, rows, columns),
            b16(rows, columns),
            b16(width, length),
            b16(width, half_len),
            b16(zs, a_len, 2 * a_cols),
            b16(zs, a_len // 2, 2 * a_cols),
            b16(zs - 1, a_len // 2, 2 * a_cols),
            b16(width, half_len - 128),
            pltpu.VMEM((5, 16, width), wide),
            pltpu.VMEM((5, 16, width), wide),
            pltpu.SemaphoreType.DMA((62,)),
            pltpu.SemaphoreType.DMA((62,)),
            pltpu.SemaphoreType.DMA((23,)),
        ],
        compiler_params=pltpu.CompilerParams(vmem_limit_bytes=61 << 20, collective_id=1, has_side_effects=True),
        cost_estimate=hint,
        name="back_all",
    )(
        hid, pair, g_own, g_oth, g_late, x_own, x_oth, gx, hres, x_in, probs, xn_one, out_first, out_oth, late,
        out_w, w_t, qkv, mixed, gain_two, gain_one, scale_two, scale_one,
    )


def finish_kernel(
    d_h, p_h, a_h, own_in, got_in, own_out, got_out, oth_out, small,
    d_out, g_out, u_out, q_out, k_out, v_out, o_out, in_out, y_out, gain1_out, gain2_out, bias_out,
    w_in, w_out, a_in, i_in, i_out, y_in, sems,
):
    own = lax.axis_index("seq") % 2 == lax.axis_index("tensor")
    rows = w_in.shape[1]
    width = i_in.shape[0]
    copy = lambda k, src, dst: pltpu.make_async_copy(src, dst, sems.at[k])
    loads = [copy(0, d_h, w_in.at[0]), copy(1, p_h.at[0], w_in.at[1]), copy(2, p_h.at[1], w_in.at[2]), copy(3, a_h, a_in)]
    load_y = copy(4, oth_out, y_in.at[1])
    mine = [copy(5, own_in, i_in), copy(6, own_out, y_in.at[0])]
    theirs = [copy(5, got_in, i_in), copy(6, got_out, y_in.at[0])]
    stores = [copy(7 + i, w_out.at[i], out) for i, out in enumerate((d_out, g_out, u_out))]
    store_i = copy(10, i_out, in_out)
    store_y = copy(11, y_in.at[0], y_out)

    def start(which):
        @pl.when(own)
        def _():
            mine[which].start()

        @pl.when(jnp.logical_not(own))
        def _():
            theirs[which].start()

    loads[0].start()
    start(0)
    for each in loads[1:3]:
        each.start()
    start(1)
    load_y.start()
    loads[3].start()

    def piecewise(count, size, run):
        def step(i, carry):
            run(pl.ds(pl.multiple_of(i * size, size), size))
            return carry

        lax.fori_loop(0, count, step, 0)

    def widen(i):
        loads[i].wait()

        def run(at):
            w_out[i, at, :] = w_in[i, at, :].astype(wide)

        piecewise(rows // 16, 16, run)
        stores[i].start()

    widen(0)
    mine[0].wait()

    def run_in(at):
        i_out[at, :] = i_in[at, :].astype(wide)

    piecewise(width // 64, 64, run_in)
    store_i.start()
    widen(1)
    widen(2)
    mine[1].wait()
    load_y.wait()

    def run_y(at):
        y_in[0, at, :] = (y_in[0, at, :].astype(wide) + y_in[1, at, :].astype(wide)).astype(low)

    piecewise(width // 64, 64, run_y)
    store_y.start()
    loads[3].wait()
    inner = q_out.shape[0]
    for i, out in enumerate((q_out, k_out, v_out, o_out)):
        out[...] = a_in[:rows, i * inner : (i + 1) * inner].astype(wide).T
    gain1_out[...] = small[1, :]
    gain2_out[...] = small[0, :]
    bias_out[...] = small[8 : 8 + bias_out.shape[0], : bias_out.shape[1]]
    for each in stores + [store_i, store_y]:
        each.wait()


def finish(d, p, a, own_in, got_in, own_out, got_out, oth_out, small, inner, bias_shape):
    rows, hidden = d.shape
    width, half_len = own_in.shape
    hbm = pl.BlockSpec(memory_space=pl.ANY)
    vmem = pl.BlockSpec(memory_space=pltpu.VMEM)
    sds = lambda kind, *shape: jax.ShapeDtypeStruct(shape, kind)
    return pl.pallas_call(
        finish_kernel,
        in_specs=[hbm] * 8 + [vmem],
        out_specs=[hbm] * 3 + [vmem] * 4 + [hbm] * 2 + [vmem] * 3,
        out_shape=[sds(wide, rows, hidden)] * 3
        + [sds(wide, inner, rows)] * 4
        + [sds(wide, width, half_len), sds(low, width, half_len)]
        + [sds(wide, width)] * 2
        + [sds(wide, *bias_shape)],
        scratch_shapes=[
            pltpu.VMEM((3, rows, hidden), low),
            pltpu.VMEM((3, rows, hidden), wide),
            pltpu.VMEM(a.shape, low),
            pltpu.VMEM((width, half_len), low),
            pltpu.VMEM((width, half_len), wide),
            pltpu.VMEM((2, width, half_len), low),
            pltpu.SemaphoreType.DMA((12,)),
        ],
        compiler_params=pltpu.CompilerParams(vmem_limit_bytes=60 << 20),
        cost_estimate=hint,
        name="finish_all",
    )(d, p, a, own_in, got_in, own_out, got_out, oth_out, small)


def norm_back(values, scale, gain, grad):
    normed = values * scale
    pushed = gain * grad
    mean = jnp.mean(normed * pushed, axis=0, keepdims=True)
    return scale * (pushed - normed * mean), jnp.sum(grad * normed, axis=1)


class Moves:
    def __init__(self, mesh):
        self.nz = mesh.shape["dp"]
        self.nx = mesh.shape["seq"] // 2
        both = [(m, c, y) for m in range(self.nx) for c in range(2) for y in range(2)]
        at = lambda m, c, y: (m * 2 + c) * 2 + y
        self.swap_pairs = [(at(m, c, y), at(m, y, c)) for m, c, y in both if c != y]
        self.second_pairs = [(at(m, c, y), at(m, y, 1 - c)) for m, c, y in both]
        self.back_pairs = [(b, a) for a, b in self.second_pairs]
        self.ring_x = [(m * 2 + c, (m + 1) % self.nx * 2 + c) for m in range(self.nx) for c in range(2)]
        self.y = lax.axis_index("tensor")
        self.z = lax.axis_index("dp")
        s = lax.axis_index("seq")
        self.c = s % 2
        self.m = s // 2

    def swap(self, a):
        got = lax.ppermute(a, ("seq", "tensor"), self.swap_pairs)
        return jnp.where(self.c == self.y, a, got)

    def back(self, a):
        return lax.ppermute(a, ("seq", "tensor"), self.back_pairs)

    def core(self, a):
        return lax.ppermute(a, "seq", [(s, s ^ 1) for s in range(2 * self.nx)])

    def over_y(self, a):
        return lax.ppermute(a, "tensor", [(0, 1), (1, 0)])

    def over_x(self, a):
        return lax.ppermute(a, "seq", self.ring_x)

    def start_x(self, a):
        take = lax.dynamic_index_in_dim(a, (self.m + self.nx - 1) % self.nx, 1, False)
        return a, self.over_x(take)

    def finish_x(self, a, got, *first):
        take = lambda i: lax.dynamic_index_in_dim(a, i % self.nx, 1, False)
        got = after(got, *first)
        held = (got.astype(wide) + take(self.m + 2 * self.nx - 2).astype(wide)).astype(low)
        for t in range(2, self.nx):
            held = (self.over_x(held).astype(wide) + take(self.m + 2 * self.nx - 1 - t).astype(wide)).astype(low)
        return held

    def scatter_x(self, a):
        take = lambda i: lax.dynamic_index_in_dim(a, i % self.nx, 1, False)
        held = take(self.m + self.nx - 1)
        for t in range(1, self.nx):
            held = (self.over_x(held).astype(wide) + take(self.m + 2 * self.nx - 1 - t).astype(wide)).astype(low)
        return held

    def scatter_z(self, a):
        return lax.psum_scatter(a, "dp", scatter_dimension=0, tiled=True)

    def gather_x(self, piece):
        if self.nx == 2:
            over = self.over_x(piece)
            return jnp.where(
                self.m == 0, jnp.concatenate([piece, over], 0), jnp.concatenate([over, piece], 0)
            )
        groups = [[m * 2 + c for m in range(self.nx)] for c in range(2)]
        return lax.all_gather(piece, "seq", axis=0, tiled=True, axis_index_groups=groups)

    def gather_core(self, piece):
        there = self.core(piece)
        return jnp.where(
            self.c == 0, jnp.concatenate([piece, there], 1), jnp.concatenate([there, piece], 1)
        )

    def sum_everywhere(self, a):
        a = a + self.core(a)
        a = a + self.over_y(a)
        step = 1
        while step < self.nx:
            a = a + lax.ppermute(a, "seq", [(s, s ^ (2 * step)) for s in range(2 * self.nx)])
            step *= 2
        step = 1
        while step < self.nz:
            a = a + lax.ppermute(a, "dp", [(z, z ^ step) for z in range(self.nz)])
            step *= 2
        return a


def local(
    mesh,
    layer_in,
    out_grad,
    doc_lengths,
    valid_length,
    gain_attn,
    query_weight,
    key_weight,
    value_weight,
    position_bias,
    output_weight,
    gain_ffn,
    gate_weight,
    up_weight,
    down_weight,
):
    moves = Moves(mesh)
    half_len, _, width = layer_in.shape
    length = 2 * half_len
    heads = position_bias.shape[1]
    inner_width = query_weight.shape[1]
    y, c, m = moves.y, moves.c, moves.m

    flat = lambda a: a.reshape(half_len, width).T
    (
        x_in, g_own, g_oth, g_send, out_w, w_t, xn_one, qkv, mixed, probs, hres, xn_own, scale_one, scale_two, gain_one, gain_two
    ) = front(
        flat(layer_in),
        flat(out_grad),
        (query_weight.T, key_weight.T, value_weight.T, output_weight),
        doc_lengths,
        valid_length,
        position_bias.T,
        gain_attn,
        gain_ffn,
        moves.nx == 2 and moves.nz == 4,
    )
    hid, pair, xn_oth, g_late, out_first, out_oth, gx, late = ffn(
        xn_own, g_own, g_oth, hres, g_send, gate_weight, up_weight, down_weight.T
    )
    if moves.nx == 2 and moves.nz == 4:
        got_first, got_oth, got_in, sum_d, grad_in, sum_p, sums, small = back_all(
            hid, pair, g_own, g_oth, g_late, xn_own, xn_oth, gx, hres, x_in, probs, xn_one, out_first, out_oth, late,
            out_w, w_t, qkv, mixed, gain_two, gain_one, scale_two, scale_one, moves.nz,
        )
        sum_d, sum_g, sum_u, sum_q, sum_k, sum_v, sum_o, grad_in, out_y, gain_one_sum, gain_two_sum, bias_sum = finish(
            sum_d, sum_p, sums, grad_in, got_in, out_first, got_first, got_oth, small,
            inner_width, (2 * heads, position_bias.shape[0]),
        )
        return (
            out_y.T.reshape(half_len, 1, width),
            grad_in.T.reshape(half_len, 1, width),
            gain_one_sum,
            sum_q.T,
            sum_k.T,
            sum_v.T,
            bias_sum.T,
            sum_o,
            gain_two_sum,
            sum_g,
            sum_u,
            sum_d.T,
        )
    grad_gate, grad_up = pair[0], pair[1]
    gx = gx.at[:, 128:].add(moves.over_y(late)[:, 128:].astype(wide))
    g_oth = jnp.concatenate([g_oth, g_late], axis=1)
    qkv_w = w_t.T
    x_wide = x_in.astype(wide)
    gain_one, gain_two = gain_one[:, :1], gain_two[:, :1]

    def both_halves(own):
        other = moves.core(own)
        return jnp.where(
            c == 0, jnp.concatenate([own, other], 1), jnp.concatenate([other, own], 1)
        )

    def my_half(a):
        return lax.dynamic_slice_in_dim(a, c * half_len, half_len, 1)

    def other_half(a):
        return lax.dynamic_slice_in_dim(a, (1 - c) * half_len, half_len, 1)


    columns = hid.shape[1] // 2
    send_d = weight_grad(g_own, g_oth, hid, 1 - c)
    got_d = moves.core(send_d)
    send_g = weight_grad(xn_own, xn_oth, after(grad_gate, send_d), 1 - c)
    got_g = moves.core(send_g)
    send_u = weight_grad(xn_own, xn_oth, after(grad_up, send_g), 1 - c)
    got_u = moves.core(send_u)
    total_d = weight_grad(g_own, g_oth, after(hid, send_u), c, got_d)
    total_g = weight_grad(xn_own, xn_oth, after(grad_gate, total_d), c, got_g)
    total_u = weight_grad(xn_own, xn_oth, after(grad_up, total_g), c, got_u)
    part_d = moves.scatter_z(total_d)
    x_sent = [moves.start_x(t.reshape(moves.nz, moves.nx, -1, columns)) for t in (total_g, total_u)]

    gx = after(gx, total_u)
    out_y = moves.swap(out_first).astype(wide) + moves.back(out_oth).astype(wide)

    back, grad_gain_two = norm_back(hres, scale_two, gain_two, gx)
    grad_hres = g_own.astype(wide) + back
    branch = both_halves(grad_hres.astype(low))

    grad_mixed = dot(out_w, branch, 1, 0).astype(low)
    grad_qkv, grad_bias = attn_backward(qkv, grad_mixed, mixed, probs)

    part_g = moves.finish_x(*x_sent[0], grad_qkv).reshape(-1, columns)
    sent = dot(qkv_w, other_half(after(grad_qkv, part_g)), 0, 0).astype(low)
    part_g = moves.scatter_z(part_g)
    got_x = moves.core(sent)
    grad_attn_w = jnp.concatenate(
        [dot(xn_one, after(grad_qkv, sent), 1, 1).astype(low), dot(branch, mixed, 1, 1).astype(low)], axis=1
    )
    gx = dot(qkv_w, my_half(after(grad_qkv, grad_attn_w)), 0, 0) + got_x.astype(wide)
    back, grad_gain_one = norm_back(x_wide, scale_one, gain_one, gx)
    grad_in = (grad_hres + back).astype(low)
    part_u = moves.scatter_z(moves.finish_x(*x_sent[1], grad_in).reshape(-1, columns))

    a_columns = grad_attn_w.shape[1] // 2
    chunks = grad_attn_w.reshape(moves.nz, moves.nx, -1, 2 * a_columns)

    def scatter_y(a):
        got = moves.over_y(lax.dynamic_slice_in_dim(a, (1 - y) * a_columns, a_columns, a.ndim - 1))
        kept = lax.dynamic_slice_in_dim(a, y * a_columns, a_columns, a.ndim - 1)
        return (kept.astype(wide) + got.astype(wide)).astype(low)

    half_z = moves.nz // 2
    part = jnp.concatenate(
        [moves.scatter_x(scatter_y(chunks[:half_z])), scatter_y(moves.scatter_x(chunks[half_z:]))], 0
    )
    piece = moves.gather_x(moves.scatter_z(part.reshape(-1, a_columns)))
    there = moves.over_y(piece)
    group = jnp.where(y == 0, jnp.concatenate([piece, there], 1), jnp.concatenate([there, piece], 1))
    sums = jnp.where(c == y, group, moves.core(group)).astype(wide)
    sum_q, sum_k, sum_v, sum_o = (
        sums[:, i * inner_width : (i + 1) * inner_width] for i in range(4)
    )
    grad_in = moves.swap(grad_in).astype(wide)

    if moves.nx == 2:
        part_d = (part_d.astype(wide) + moves.over_x(part_d).astype(wide)).astype(low)
    else:
        part_d = moves.gather_x(moves.scatter_x(part_d.reshape(1, moves.nx, -1, columns))[0])
    sum_d = moves.gather_core(part_d).astype(wide)
    sum_g = moves.gather_core(moves.gather_x(part_g)).astype(wide)
    sum_u = moves.gather_core(moves.gather_x(part_u)).astype(wide)

    bias_full = jnp.zeros((grad_bias.shape[0], 2 * heads), wide)
    bias_full = lax.dynamic_update_slice(bias_full, grad_bias, (jnp.int32(0), c * heads))
    early = moves.sum_everywhere(jnp.concatenate([grad_gain_two, bias_full.reshape(-1)]))
    gain_two_sum, bias_sum = early[:width], early[width:].reshape(bias_full.shape)
    gain_one_sum = moves.sum_everywhere(grad_gain_one)
    return (
        out_y.astype(low).T.reshape(half_len, 1, width),
        grad_in.T.reshape(half_len, 1, width),
        gain_one_sum,
        sum_q,
        sum_k,
        sum_v,
        bias_sum,
        sum_o.T,
        gain_two_sum,
        sum_g,
        sum_u,
        sum_d.T,
    )


def solution(mesh):
    rows = P("tensor", ("dp", "seq"), None)
    columns = P(None, "tensor")
    return jax.shard_map(
        functools.partial(local, mesh),
        mesh=mesh,
        in_specs=(
            rows,
            rows,
            P(("dp", "seq"), None),
            P(("dp", "seq")),
            P(),
            columns,
            columns,
            columns,
            columns,
            P("tensor", None),
            P(),
            columns,
            columns,
            P("tensor", None),
        ),
        out_specs=(
            rows,
            rows,
            P(),
            P("dp", "tensor"),
            P("dp", "tensor"),
            P("dp", "tensor"),
            P(),
            P("tensor", "dp"),
            P(),
            P("dp", "tensor"),
            P("dp", "tensor"),
            P("tensor", "dp"),
        ),
        check_vma=False,
    )
```

```python
import functools
import math

import jax
import jax.numpy as jnp
from jax import lax
from jax.experimental import pallas as pl
from jax.experimental.pallas import tpu as pltpu
from jax.sharding import PartitionSpec as P

steps_at = (1, 2, 3, 4, 5, 6, 7, 8, 12, 16, 23, 32, 46, 64, 91)
eps_norm = 1e-06
masked_score = -1e30
q_block = 256
band_half = 128
low = jnp.bfloat16
wide = jnp.float32
hint = pl.CostEstimate(flops=1000, bytes_accessed=1000, transcendentals=0)


def dot(a, b, ca, cb):
    return lax.dot_general(a, b, (((ca,), (cb,)), ((), ())), preferred_element_type=wide)


def after(value, *first):
    return lax.optimization_barrier((value, *first))[0]


def front_kernel(
    share, x_h, g_h, wq_h, wk_h, wv_h, wo_h, lengths, valid, bias, gain1_row, gain2_row,
    x_out, g_own, g_oth, g_late, wo_out, w_t_out, xn1_out, qkv_out, mixed_out, probs_h, hres_out, xn2,
    scale1, scale2, gain1, gain2,
    x_in, g_in, w, w_t, xn1, qkv, mixed, hres,
    facts_src, facts, p_buf, table, sx, rx, seg_k, seg_q, send_sems, recv_sems, load_sems,
):
    s = lax.axis_index("seq")
    y = lax.axis_index("tensor")
    c = s % 2
    m = s // 2
    width, half_len = x_in.shape
    length = 2 * half_len
    heads, buckets = bias.shape
    inner = mixed.shape[0]
    dim = inner // heads
    piece = 64
    pieces = width // piece
    mesh_id = dict(device_id_type=pl.DeviceIdType.MESH)
    to_core = {"seq": 2 * m + 1 - c}
    to_swap = {"seq": 2 * m + 1 - c, "tensor": 1 - y}

    def side(i, size):
        return pl.ds(pl.multiple_of(i * size, 128), size)

    my_half = side(c, half_len)
    other_half = side(1 - c, half_len)

    def move(k, src, dst, who):
        return pltpu.make_async_remote_copy(
            src_ref=src, dst_ref=dst, send_sem=send_sems.at[k], recv_sem=recv_sems.at[k], device_id=who, **mesh_id
        )

    to_second = {"seq": 2 * m + y, "tensor": 1 - c}

    named = [(x_h, x_in)] + [
        (src, w.at[pl.ds(i * inner, inner)]) for i, src in enumerate((wq_h, wk_h, wv_h, wo_h))
    ]
    half_cols = half_len // 2
    halves = [pl.ds(h * half_cols, half_cols) for h in range(2)]
    move_x = [move((1, 15)[h], x_h.at[:, halves[h]], x_in.at[:, halves[h]], to_swap) for h in range(2)]
    moves = []
    z = lax.axis_index("dp")
    rows = inner // 2

    def half_of(ref, i, k):
        return ref.at[pl.ds(pl.multiple_of(i * inner + k * rows, rows), rows)]

    fetched, passed_z, passed_x = [], [], []
    for i, src in enumerate((wq_h, wk_h, wv_h, wo_h)):
        if share:
            fetched.append(move(2, half_of(src, 0, m), half_of(w, i, m), to_swap))
            part = half_of(w, (z + 4 - i) % 4, m)
            passed_x.append(move(10 + i, part, part, {"seq": 2 * (1 - m) + c}))
            if i < 3:
                passed_z.append(move(3 + i if i else 14, part, part, {"dp": (z + 1) % 4}))
        else:
            moves.append(move(2 + i, src, w.at[pl.ds(i * inner, inner)], to_swap))
    loads = [pltpu.make_async_copy(src, dst, load_sems.at[1 + i]) for i, (src, dst) in enumerate(named)]
    move_facts = move(0, facts_src, facts, to_swap)
    move_g = move(6, g_in, g_own, to_swap)
    early = g_oth.shape[1]
    second_g = move(9, g_in.at[:, pl.ds(0, early)], g_oth, to_second)
    to = lambda k, src, dst: pltpu.make_async_copy(src, dst, load_sems.at[k])
    keep_late = to(16, g_in.at[:, pl.ds(early, half_len - early)], g_late)
    load_g = pltpu.make_async_copy(g_h, g_in, load_sems.at[0])
    keep_g = pltpu.make_async_copy(g_in, g_own, load_sems.at[6])
    stores = [
        pltpu.make_async_copy(src, dst, load_sems.at[9 + i])
        for i, (src, dst) in enumerate(
            ((x_in, x_out), (w.at[pl.ds(3 * inner, inner)], wo_out), (w_t, w_t_out), (xn1, xn1_out), (qkv, qkv_out),
             (mixed, mixed_out), (hres, hres_out))
        )
    ]

    def pass_on(i):
        if not share:
            return

        @pl.when(c != y)
        def _():
            if i:
                passed_z[i - 1].wait_recv()
            else:
                fetched[0].wait_recv()
            if i < 3:
                passed_z[i].start()
            passed_x[i].start()

    my_parts = [pl.ds(pl.multiple_of(c * half_len + h * half_cols, 128), half_cols) for h in range(2)]
    core_one = [move((7, 16)[h], xn1.at[:, my_parts[h]], xn1.at[:, my_parts[h]], to_core) for h in range(2)]
    core_two = move(8, sx, rx, to_core)

    load_g.start()
    for h in range(heads):
        for b in range(buckets):
            at = h * buckets + b
            facts_src[at : at + 1, :] = jnp.full((1, 128), bias[h, b], wide)
    end = jnp.int32(0)
    at = heads * buckets
    for i in range(4):
        end = end + lengths[0, i]
        facts_src[at + i : at + i + 1, :] = jnp.full((1, 128), end.astype(wide), wide)
    facts_src[at + 4 : at + 5, :] = jnp.full((1, 128), valid[0].astype(wide), wide)

    barrier = pltpu.get_barrier_semaphore()
    greet = [to_core, to_swap, {"tensor": 1 - y}]
    if share:
        greet += [{"seq": 2 * (1 - m) + c}, {"dp": (z + 1) % 4}, {"dp": (z + 3) % 4}]
    for who in greet:
        pl.semaphore_signal(barrier, inc=1, device_id=who, **mesh_id)
    pl.semaphore_wait(barrier, len(greet))

    @pl.when(c != y)
    def _():
        move_facts.start()
        for i, each in enumerate(fetched):
            pl.when(z == i)(each.start)
        for each in move_x + moves:
            each.start()

    @pl.when(c == y)
    def _():
        for each in loads:
            each.start()
        facts[...] = facts_src[...]

    load_g.wait()
    live = lax.broadcasted_iota(jnp.int32, (piece, half_len), 1) + y * half_len < valid[0]

    def mask(i, carry):
        at = pl.ds(pl.multiple_of(i * piece, piece), piece)
        g_in[at, :] = jnp.where(live, g_in[at, :].astype(wide), 0.0).astype(low)
        return carry

    lax.fori_loop(0, pieces, mask, 0)

    @pl.when(c != y)
    def _():
        move_g.start()

    @pl.when(c == y)
    def _():
        keep_g.start()

    second_g.start()
    keep_late.start()
    pass_on(0)
    gain1[...] = jnp.broadcast_to(gain1_row[...].astype(wide)[None, :], (128, width)).T
    gain2[...] = jnp.broadcast_to(gain2_row[...].astype(wide)[None, :], (128, width)).T

    pass_on(1)

    @pl.when(c != y)
    def _():
        move_facts.wait_recv()

    at = heads * buckets

    def segments(positions):
        count = jnp.zeros(positions.shape, wide)
        for i in range(4):
            count = count + jnp.where(positions >= facts[at + i : at + i + 1, :], 1.0, 0.0)
        return jnp.where(positions < facts[at + 4 : at + 5, :], count, 4.0)

    seg_k[...] = segments(lax.broadcasted_iota(jnp.int32, (length, 128), 0).astype(wide))
    for i in range(length // 128):
        positions = (lax.broadcasted_iota(jnp.int32, (8, 128), 1) + i * 128).astype(wide)
        seg_q[:, i * 128 : (i + 1) * 128] = segments(positions)
    pass_on(2)
    reach = length - q_block
    near_rows = q_block + 2 * band_half
    d = (
        lax.broadcasted_iota(jnp.int32, (near_rows, 128), 0)
        - lax.broadcasted_iota(jnp.int32, (near_rows, 128), 1)
        - band_half
    )
    far_rows = reach - band_half
    for h in range(heads):

        def value(b, h=h):
            return facts[h * buckets + b : h * buckets + b + 1, :]

        for i in range(q_block // 128):
            offset = d - i * 128
            n = jnp.abs(offset)
            before = jnp.broadcast_to(value(0), n.shape)
            later = jnp.broadcast_to(value(16), n.shape)
            for number, step in enumerate(steps_at):
                reached = n >= step
                before = jnp.where(reached, value(number + 1), before)
                later = jnp.where(reached, value(number + 17), later)
            col = pl.ds(i * 128, 128)
            table[h, pl.ds(far_rows, near_rows), col] = jnp.where(offset > 0, later, before)
            table[h, pl.ds(0, far_rows), col] = jnp.broadcast_to(value(15), (far_rows, 128))
            table[h, pl.ds(far_rows + near_rows, far_rows), col] = jnp.broadcast_to(value(31), (far_rows, 128))

    def norm(read, gain, scale, cols, write):
        size = cols.size

        def first(i, total):
            v = read(pl.ds(pl.multiple_of(i * piece, piece), piece))
            return total + jnp.sum(v * v, axis=0, keepdims=True)

        total = lax.fori_loop(0, pieces, first, jnp.zeros((1, size), wide))
        scale[:, cols] = lax.rsqrt(total * (1.0 / width) + eps_norm)

        def second(i, carry):
            at = pl.ds(pl.multiple_of(i * piece, piece), piece)
            spread = jnp.concatenate([gain[at, :]] * (size // 128), axis=1)
            write(at, (read(at) * scale[:, cols] * spread).astype(low))
            return carry

        lax.fori_loop(0, pieces, second, 0)

    def arrived(i):
        @pl.when(c != y)
        def _():
            if not share:
                moves[i - 1].wait_recv()

        @pl.when(c == y)
        def _():
            loads[i].wait()

    pass_on(3)
    for h in range(2):

        @pl.when(c != y)
        def _(h=h):
            move_x[h].wait_recv()

        if h == 0:

            @pl.when(c == y)
            def _():
                loads[0].wait()

        def write_one(at, value, h=h):
            xn1[at, my_parts[h]] = value

        norm(lambda at, h=h: x_in[at, halves[h]].astype(wide), gain1, scale1, halves[h], write_one)
        core_one[h].start()
    stores[0].start()
    if share:

        @pl.when(c != y)
        def _():
            for each in passed_x:
                each.wait_recv()

    for each in core_one:
        each.wait_recv()
    stores[3].start()
    for i in range(3):
        arrived(1 + i)
        qkv[i * inner : (i + 1) * inner, :] = dot(w[i * inner : (i + 1) * inner, :], xn1[...], 1, 0).astype(low)

    stores[4].start()

    blocks = length // q_block

    turns = heads * blocks // 2

    def turn(i):
        its = 1 - c + (i // turns) * (2 * c - 1)
        return i % heads, its * (blocks // 2) + (i % turns) // heads

    group = 3 if turns % 3 == 0 else 1

    def store(i):
        h, b = turn(i)
        return pltpu.make_async_copy(p_buf.at[i % group], probs_h.at[h, :, side(b, q_block)], load_sems.at[17 + i % group])

    def rows_of(part, i):
        return pl.ds(pl.multiple_of((part * heads + turn(i)[0]) * dim, dim), dim)

    def probs_of(i):
        h, b = turn(i)
        first = pl.multiple_of(reach - b * q_block, q_block)
        at = side(b, q_block)
        scores = dot(qkv[rows_of(1, i), :], qkv[rows_of(0, i), at], 0, 0) + table[h, pl.ds(first, length), :]
        keys = jnp.concatenate([seg_k[...]] * (q_block // 128), axis=1)
        scores = jnp.where(keys == seg_q[0:1, at], scores, masked_score)
        raised = jnp.exp(scores - jnp.max(scores, axis=0, keepdims=True))
        return (raised * (1.0 / jnp.sum(raised, axis=0, keepdims=True))).astype(low)

    def block(i, carry):
        each = [probs_of(group * i + k) for k in range(group)]
        outs = [dot(qkv[rows_of(2, group * i + k), :], each[k], 1, 0).astype(low) for k in range(group)]
        for k in range(group):
            mixed[rows_of(0, group * i + k), side(turn(group * i + k)[1], q_block)] = outs[k]

        @pl.when(i >= 1)
        def _():
            for k in range(group):
                store(group * i + k - group).wait()

        for k in range(group):
            p_buf[k] = each[k]
            store(group * i + k).start()
        return carry

    lax.fori_loop(0, turns // group, block, 0)
    arrived(4)
    stores[1].start()
    out_w = w[3 * inner :, :]
    sx[...] = dot(out_w, mixed[:, other_half], 0, 0).astype(low)
    core_two.start()
    w_t[...] = w[: 3 * inner, :].T
    stores[2].start()
    lax.fori_loop(turns // group, 2 * turns // group, block, 0)
    stores[5].start()
    hres[...] = dot(out_w, mixed[:, my_half], 0, 0)
    core_two.wait_recv()

    def add(i, carry):
        at = pl.ds(pl.multiple_of(i * piece, piece), piece)
        hres[at, :] += x_in[at, :].astype(wide) + rx[at, :].astype(wide)
        return carry

    lax.fori_loop(0, pieces, add, 0)

    stores[6].start()

    def write_two(at, value):
        xn2[at, :] = value

    norm(lambda at: hres[at, :], gain2, scale2, pl.ds(0, half_len), write_two)
    last = heads * blocks
    for k in range(group):
        store(last - group + k).wait()
    for each in (*core_one, core_two):
        each.wait_send()

    @pl.when(c != y)
    def _():
        move_facts.wait_send()
        if share:
            fetched[0].wait_send()
        for each in move_x + moves + passed_z + passed_x:
            each.wait_send()
        move_g.wait()

    @pl.when(c == y)
    def _():
        keep_g.wait()

    second_g.wait()
    keep_late.wait()
    for each in stores:
        each.wait()


def front(x, g, weights, lengths, valid, bias, gain_one, gain_two, share):
    width, half_len = x.shape
    length = 2 * half_len
    heads = bias.shape[0]
    inner = weights[0].shape[0]
    hbm = pl.BlockSpec(memory_space=pl.ANY)
    vmem = pl.BlockSpec(memory_space=pltpu.VMEM)
    smem = pl.BlockSpec(memory_space=pltpu.SMEM)
    sds = lambda kind, *shape: jax.ShapeDtypeStruct(shape, kind)
    facts = pltpu.VMEM((heads * bias.shape[1] + 8, 128), wide)
    b16 = lambda *shape: pltpu.VMEM(shape, low)
    return pl.pallas_call(
        functools.partial(front_kernel, share),
        in_specs=[hbm] * 6 + [smem] * 3 + [vmem] * 2,
        out_specs=[hbm] * 11 + [vmem] * 5,
        out_shape=[
            sds(low, width, half_len),
            sds(low, width, half_len),
            sds(low, width, half_len - 128),
            sds(low, width, 128),
            sds(low, inner, width),
            sds(low, width, 3 * inner),
            sds(low, width, length),
            sds(low, 3 * inner, length),
            sds(low, inner, length),
            sds(low, heads, length, length),
            sds(wide, width, half_len),
            sds(low, width, half_len),
            sds(wide, 1, half_len),
            sds(wide, 1, half_len),
            sds(wide, width, 128),
            sds(wide, width, 128),
        ],
        scratch_shapes=[
            b16(width, half_len),
            b16(width, half_len),
            b16(4 * inner, width),
            b16(width, 3 * inner),
            b16(width, length),
            b16(3 * inner, length),
            b16(inner, length),
            pltpu.VMEM((width, half_len), wide),
            facts,
            facts,
            b16(3, length, q_block),
            pltpu.VMEM((heads, 2 * length - q_block, q_block), wide),
            b16(width, half_len),
            b16(width, half_len),
            pltpu.VMEM((length, 128), wide),
            pltpu.VMEM((8, length), wide),
            pltpu.SemaphoreType.DMA((17,)),
            pltpu.SemaphoreType.DMA((17,)),
            pltpu.SemaphoreType.DMA((20,)),
        ],
        compiler_params=pltpu.CompilerParams(vmem_limit_bytes=60 << 20, collective_id=2, has_side_effects=True),
        cost_estimate=hint,
        name="front_all",
    )(x, g, *weights, lengths, valid, bias, gain_one, gain_two)


def attn_bwd_kernel(length, q_ref, k_ref, v_ref, go_ref, o_ref, p_ref, gq_ref, gk_ref, gv_ref, gb_ref, k_acc, v_acc, sums):
    block = pl.program_id(1)
    reach = length - q_block

    @pl.when(block == 0)
    def _():
        k_acc[...] = jnp.zeros_like(k_acc)
        v_acc[...] = jnp.zeros_like(v_acc)
        sums[...] = jnp.zeros_like(sums)

    probs = p_ref[0]
    go = go_ref[...]
    inner = jnp.sum(go.astype(wide) * o_ref[...].astype(wide), axis=0, keepdims=True)
    scores = probs.astype(wide) * (dot(v_ref[...], go, 0, 0) - inner)
    first = pl.multiple_of(reach - block * q_block, q_block)
    sums[pl.ds(first, length), :] += scores
    scores = scores.astype(low)
    gq_ref[...] = dot(k_ref[...], scores, 1, 0).astype(low)
    k_acc[...] += dot(q_ref[...], scores, 1, 1)
    v_acc[...] += dot(go, probs, 1, 1)

    @pl.when(block == pl.num_programs(1) - 1)
    def _():
        gk_ref[...] = k_acc[...].astype(low)
        gv_ref[...] = v_acc[...].astype(low)
        rows = q_block + 2 * band_half
        d = (
            lax.broadcasted_iota(jnp.int32, (rows, q_block), 0)
            - lax.broadcasted_iota(jnp.int32, (rows, q_block), 1)
            - band_half
        )
        n = jnp.abs(d)
        near = sums[reach - band_half : reach + q_block + band_half, :]
        far_before = jnp.sum(sums[: reach - band_half, :], axis=0, keepdims=True)
        far_after = jnp.sum(sums[reach + q_block + band_half :, :], axis=0, keepdims=True)
        bucket = jnp.zeros((rows, q_block), jnp.int32)
        for step in steps_at:
            bucket = bucket + jnp.where(n >= step, 1, 0)
        bucket = bucket + jnp.where(d > 0, 16, 0)
        for b in range(32):
            total = jnp.sum(jnp.where(bucket == b, near, 0.0), axis=0, keepdims=True)
            if b == 15:
                total = total + far_before
            if b == 31:
                total = total + far_after
            gb_ref[0, b : b + 1, :] = total


def attn_backward(qkv, grad_mixed, mixed, probs):
    width, length = qkv.shape
    heads = probs.shape[0]
    dim = width // (3 * heads)
    blocks = length // q_block
    half = pl.BlockSpec((dim, q_block), lambda h, b: (h, b))
    whole = pl.BlockSpec((dim, length), lambda h, b: (h, 0))
    gq, gk, gv, gb = pl.pallas_call(
        functools.partial(attn_bwd_kernel, length),
        grid=(heads, blocks),
        in_specs=[
            half,
            pl.BlockSpec((dim, length), lambda h, b: (heads + h, 0)),
            pl.BlockSpec((dim, length), lambda h, b: (2 * heads + h, 0)),
            half,
            half,
            pl.BlockSpec((1, length, q_block), lambda h, b: (h, 0, b)),
        ],
        out_specs=[half, whole, whole, pl.BlockSpec((1, 32, q_block), lambda h, b: (h, 0, 0))],
        out_shape=[
            jax.ShapeDtypeStruct((heads * dim, length), low),
            jax.ShapeDtypeStruct((heads * dim, length), low),
            jax.ShapeDtypeStruct((heads * dim, length), low),
            jax.ShapeDtypeStruct((heads, 32, q_block), wide),
        ],
        scratch_shapes=[
            pltpu.VMEM((dim, length), wide),
            pltpu.VMEM((dim, length), wide),
            pltpu.VMEM((2 * length - q_block, q_block), wide),
        ],
        compiler_params=pltpu.CompilerParams(vmem_limit_bytes=48 << 20),
        cost_estimate=hint,
        name="attn_backward",
    )(qkv, qkv, qkv, grad_mixed, mixed, probs)
    return jnp.concatenate([gq, gk, gv], axis=0), jnp.sum(gb, axis=2).T


def ffn_kernel(
    x_ref, go_ref, gr_h0, hres_h, g_late, gate_w, up_w, down_w,
    hid_ref, pair_ref, xr_h, gr_h, out_h, out_r_h, gx_h, late_h,
    xs, gs, out_acc, gx_acc, x_in, g_in, gx_out, gx_in, out_v, gx_v, gr_ref, hres_ref, sems, store_sems,
):
    chunk = pl.program_id(0)
    tile = pl.program_id(1)
    size = xs.shape[0]
    mesh_id = dict(device_id_type=pl.DeviceIdType.MESH)
    s = lax.axis_index("seq")
    y = lax.axis_index("tensor")
    c = s % 2
    to_y = {"tensor": 1 - y}
    to_second = {"seq": s - c + y, "tensor": 1 - c}
    half = [pl.ds(0, size), pl.ds(size, size)]

    def move(k, src, dst, who):
        return pltpu.make_async_remote_copy(
            src_ref=src, dst_ref=dst, send_sem=sems.at[k], recv_sem=sems.at[4 + k], device_id=who, **mesh_id
        )

    send_x = [move(h, x_ref.at[:, half[h]], x_in.at[h], to_y) for h in range(2)]
    send_g = move(2, g_late, g_in, to_second)
    back = gx_in.shape[1]
    send_gx = move(3, gx_out.at[0, :, pl.ds(0, back)], gx_in, to_y)
    begun = g_in.shape[1]
    to = lambda k, src, dst: pltpu.make_async_copy(src, dst, store_sems.at[k])
    store_x = [to(h, x_in.at[h], xr_h.at[:, half[h]]) for h in range(2)]
    store_out = [to(2 + h, out_v.at[h], out_h.at[:, half[h]]) for h in range(2)]
    store_out_r = [to(4 + h, out_v.at[2 + h], out_r_h.at[:, half[h]]) for h in range(2)]
    store_gx = [to(6 + h, gx_v.at[h], gx_h.at[:, half[h]]) for h in range(2)]
    store_late = [to(8 + h, gx_out.at[h], late_h.at[:, half[h]]) for h in range(2)]
    store_g = to(10, g_in, gr_h)
    load_h = to(11, hres_h, hres_ref)
    load_g = to(12, gr_h0, gr_ref)

    @pl.when(tile == 0)
    def _():
        out_acc[...] = jnp.zeros_like(out_acc)
        gx_acc[...] = jnp.zeros_like(gx_acc)

    @pl.when((tile == 0) & (chunk == 0))
    def _():
        load_h.start()
        load_g.start()
        barrier = pltpu.get_barrier_semaphore()
        for who in (to_y, {"seq": s + 1 - 2 * c}):
            pl.semaphore_signal(barrier, inc=1, device_id=who, **mesh_id)
        pl.semaphore_wait(barrier, 2)
        for each in (*send_x, send_g):
            each.start()

    for h in range(2):

        @pl.when((tile == 0) & (chunk == h))
        def _(h=h):
            xs[...] = x_ref[:, half[h]].T
            gs[...] = go_ref[:, half[h]].T

        @pl.when((tile == 0) & (chunk == 2 + h))
        def _(h=h):
            send_x[h].wait_recv()
            xs[...] = x_in[h].T
            store_x[h].start()
            if not h:
                load_g.wait()
            if h:
                gs[: size - begun, :] = gr_ref[:, size:].T
                send_g.wait_recv()
                gs[size - begun :, :] = g_in[...].T
                store_g.start()
            else:
                gs[...] = gr_ref[:, :size].T

    gate = dot(xs[...], gate_w[...], 1, 0)
    up = dot(xs[...], up_w[...], 1, 0)
    grad = dot(gs[...], down_w[...], 1, 0)
    c_gelu = math.sqrt(2.0 / math.pi)
    square = gate * gate
    t = jnp.tanh(c_gelu * gate * (1.0 + 0.044715 * square))
    part = 0.5 * (1.0 + t)
    gelu = gate * part
    slope = part + 0.5 * gate * (1.0 - t * t) * (c_gelu * (1.0 + 3 * 0.044715 * square))
    hid = (gelu * up).astype(low)
    gg = (grad * up * slope).astype(low)
    gu = (grad * gelu).astype(low)
    hid_ref[...] = hid
    pair_ref[0] = gg
    pair_ref[1] = gu
    out_acc[...] += dot(down_w[...], hid, 1, 1)
    gx_acc[...] += dot(gate_w[...], gg, 1, 1) + dot(up_w[...], gu, 1, 1)

    last = tile == pl.num_programs(1) - 1
    for h in range(2):

        @pl.when(last & (chunk == h))
        def _(h=h):
            if not h:
                load_h.wait()
            out_v[h] = (hres_ref[:, half[h]] + out_acc[...]).astype(low)
            store_out[h].start()
            gx_v[h] = gx_acc[...]
            if h:
                store_gx[h].start()

        @pl.when(last & (chunk == 2 + h))
        def _(h=h):
            out_v[2 + h] = out_acc[...].astype(low)
            store_out_r[h].start()
            gx_out[h] = gx_acc[...].astype(low)
            if not h:
                send_gx.start()
            store_late[h].start()

    @pl.when(last & (chunk == 3))
    def _():
        send_gx.wait_recv()
        gx_v[0, :, :back] += gx_in[...].astype(wide)
        store_gx[0].start()
        for each in (*send_x, send_g, send_gx):
            each.wait_send()
        for each in store_x + store_out + store_out_r + store_gx + store_late + [store_g]:
            each.wait()


def ffn(x, g_own, g_oth, hres, g_late, gate_w, up_w, down_w):
    width, tokens = x.shape
    hidden = gate_w.shape[1]
    tile, size = hidden // 2, tokens // 2
    begun = g_late.shape[1]
    hbm = pl.BlockSpec(memory_space=pl.ANY)
    full = pl.BlockSpec((width, tokens), lambda s, j: (0, 0), pipeline_mode=pl.Buffered(1))
    weight = pl.BlockSpec((width, tile), lambda s, j: (0, j))
    act_shape = jax.ShapeDtypeStruct((2 * tokens, hidden), low)
    tokens_of = lambda kind: jax.ShapeDtypeStruct((width, tokens), kind)
    return pl.pallas_call(
        ffn_kernel,
        grid=(4, hidden // tile),
        in_specs=[full, full, hbm, hbm, hbm, weight, weight, weight],
        out_specs=[
            pl.BlockSpec((size, tile), lambda s, j: (s, j)),
            pl.BlockSpec((2, size, tile), lambda s, j: (0, s, j)),
        ]
        + [hbm] * 6,
        out_shape=[act_shape, jax.ShapeDtypeStruct((2, 2 * tokens, hidden), low)]
        + [tokens_of(low), jax.ShapeDtypeStruct((width, begun), low)]
        + [tokens_of(kind) for kind in (low, low, wide, low)],
        scratch_shapes=[
            pltpu.VMEM((size, width), low),
            pltpu.VMEM((size, width), low),
            pltpu.VMEM((width, size), wide),
            pltpu.VMEM((width, size), wide),
            pltpu.VMEM((2, width, size), low),
            pltpu.VMEM((width, begun), low),
            pltpu.VMEM((2, width, size), low),
            pltpu.VMEM((width, 128), low),
            pltpu.VMEM((4, width, size), low),
            pltpu.VMEM((2, width, size), wide),
            pltpu.VMEM((width, tokens - begun), low),
            pltpu.VMEM((width, tokens), wide),
            pltpu.SemaphoreType.DMA((8,)),
            pltpu.SemaphoreType.DMA((13,)),
        ],
        compiler_params=pltpu.CompilerParams(vmem_limit_bytes=60 << 20, collective_id=0, has_side_effects=True),
        cost_estimate=hint,
        name="ffn_both_ways",
    )(x, g_own, g_oth, hres, g_late, gate_w, up_w, down_w)


def weight_grad_kernel(core_ref, own_ref, oth_ref, right_ref, *refs):
    tokens = own_ref.shape[1]
    total = dot(own_ref[...], right_ref[:tokens, :], 1, 0) + dot(oth_ref[...], right_ref[tokens:, :], 1, 0)
    if len(refs) == 2:
        total = total + refs[0][...].astype(wide)
    refs[-1][...] = total.astype(low)


def weight_grad(own, oth, right, core, got=None):
    width, tokens = own.shape
    columns = right.shape[1] // 2
    blocks = 4
    rows = width // blocks
    left = pl.BlockSpec((rows, tokens), lambda i, core_ref: (i, 0))
    out = pl.BlockSpec((rows, columns), lambda i, core_ref: (i, 0))
    args = [own, oth, right] + ([] if got is None else [got])
    return pl.pallas_call(
        weight_grad_kernel,
        grid_spec=pltpu.PrefetchScalarGridSpec(
            num_scalar_prefetch=1,
            grid=(blocks,),
            in_specs=[
                left,
                left,
                pl.BlockSpec((2 * tokens, columns), lambda i, core_ref: (0, core_ref[0]), pipeline_mode=pl.Buffered(1)),
            ]
            + ([] if got is None else [out]),
            out_specs=out,
        ),
        out_shape=jax.ShapeDtypeStruct((width, columns), low),
        compiler_params=pltpu.CompilerParams(vmem_limit_bytes=40 << 20),
        cost_estimate=hint,
        name="weight_grad",
    )(core.reshape(1), *args)


def back_kernel(
    hid_h, pair_h, go_h, gr1_h, gr2_h, xo_h, xr_h, gx_h, hres_h, xin_h, probs_h, xn1_h, outp_h, outr_h, late_h,
    out_w_h, w_t_h, qkv_h, mixed_h, gain2_h, gain1_h, scale2, scale1,
    got_p, got_r, got_in, d_out_h, gin_h, p_out, a_out, small,
    out_w, w_t, qkv, mixed, gain2, gain1, d_out, gin,
    r_core, xp, zd, zp, dx, bf, rx, ya, xa, za, late_in, sm_src, sm_in, send_sems, recv_sems, load_sems,
):
    s = lax.axis_index("seq")
    y = lax.axis_index("tensor")
    z = lax.axis_index("dp")
    c = s % 2
    m = s // 2
    width = xp.shape[0]
    rows = d_out.shape[0]
    columns = xp.shape[1]
    half_len = rx.shape[1]
    length = 2 * half_len
    heads = probs_h.shape[0]
    dim = mixed.shape[0] // heads
    zs = width // rows
    mesh_id = dict(device_id_type=pl.DeviceIdType.MESH)
    to_core = {"seq": 2 * m + 1 - c}
    to_x = {"seq": 2 * (1 - m) + c}
    to_y = {"tensor": 1 - y}
    to_z = {"dp": (z + 1) % zs}
    to_swap = {"seq": 2 * m + y, "tensor": c}
    to_back = {"seq": 2 * m + 1 - y, "tensor": c}

    def move(k, src, dst, who):
        return pltpu.make_async_remote_copy(
            src_ref=src, dst_ref=dst, send_sem=send_sems.at[k], recv_sem=recv_sems.at[k], device_id=who, **mesh_id
        )

    def load(k, src, dst):
        return pltpu.make_async_copy(src, dst, load_sems.at[k])

    def chunk(j):
        return pl.ds(pl.multiple_of(j * rows, rows), rows)

    def side(i, size):
        return pl.ds(pl.multiple_of(i * size, 128), size)

    order = [(z + zs - 1 - k) % zs for k in range(zs)]
    mine = side(c, columns)
    my_half = side(c, half_len)
    other_half = side(1 - c, half_len)
    cut = [(0, 192), (192, rows - 192)]

    def part(j, p):
        return pl.ds(pl.multiple_of(j * rows + cut[p][0], 16), cut[p][1])

    parts = [pl.ds(*each) for each in cut]

    late_from = half_len - late_in.shape[1]
    late = move(0, late_h.at[:, pl.ds(late_from, half_len - late_from)], late_in, to_y)
    swap_out = move(1, outp_h, got_p, to_swap)
    back_out = move(2, outr_h, got_r, to_back)
    both = range(2)
    steps = range(zs - 1)
    z_down = [
        [move(3 + 2 * t + p, zd.at[t - 1, parts[p]] if t else r_core.at[0, part(order[0], p)], zd.at[t, parts[p]], to_z) for p in both]
        for t in steps
    ]
    x_down = [move(9 + p, zd.at[2, parts[p]], dx.at[parts[p]], to_x) for p in both]
    core_down = [move(11 + p, d_out.at[parts[p], mine], d_out.at[parts[p], mine], to_core) for p in both]
    z_pair = [
        [move(13 + 2 * t + p, zp.at[t - 1, parts[p]] if t else r_core.at[2, part(order[0], p)], zp.at[t, parts[p]], to_z) for p in both]
        for t in steps
    ]
    x_pair_back = [move(19 + p, zp.at[2, parts[p]], p_out.at[m, parts[p], mine], to_x) for p in both]
    core_pair = [move(21 + p, p_out.at[m, parts[p], mine], p_out.at[m, parts[p], mine], to_core) for p in both]
    core_pair_back = [
        move(23 + p, p_out.at[1 - m, parts[p], mine], p_out.at[1 - m, parts[p], mine], to_core) for p in both
    ]
    core_branch = move(25, bf.at[:, my_half], bf.at[:, my_half], to_core)
    a_rows = xa.shape[1]
    my_rows = pl.ds(pl.multiple_of(m * a_rows, a_rows), a_rows)
    x_rows = pl.ds(pl.multiple_of((1 - m) * a_rows, a_rows), a_rows)
    x_attn = [move(26 + k, ya.at[j, x_rows], xa.at[j], to_x) for k, j in enumerate(order)]
    z_attn = [move(30 + t, za.at[t - 1] if t else ya.at[order[0], my_rows], za.at[t], to_z) for t in steps]
    x_attn_back = move(33, a_out.at[my_rows], a_out.at[my_rows], to_x)
    core_attn = move(34, a_out, a_out, to_core)
    swap_in = move(35, gin, got_in, to_swap)

    def x_pair(k):
        at = chunk((z + zs - 1 - k) % zs)
        return move(46 + k, r_core.at[1, at], xp.at[at], to_x)

    def meet():
        barrier = pltpu.get_barrier_semaphore()
        greet = [to_core, to_y, {"seq": 2 * m + 1 - c, "tensor": 1 - y}, to_x] + [{"dp": (z + i) % zs} for i in range(1, zs)]
        for who in greet:
            pl.semaphore_signal(barrier, inc=1, device_id=who, **mesh_id)
        pl.semaphore_wait(barrier, len(greet))
        late.start()

    def step_z_down(t, p):
        z_down[t - 1][p].wait_recv()
        at = parts[p]
        zd[t - 1, at, :] = (zd[t - 1, at, :].astype(wide) + r_core[0, part(order[t], p), :].astype(wide)).astype(low)
        (z_down[t][p] if t < zs - 1 else x_down[p]).start()

    def end_down(p):
        x_down[p].wait_recv()
        at = parts[p]
        d_out[at, mine] = (zd[2, at, :].astype(wide) + dx[at, :].astype(wide)).astype(low)
        core_down[p].start()

    def step_z_pair(t, p):
        if p == 0:
            x_pair(t).wait_recv()
        at = parts[p]
        term = r_core[2, part(order[t], p), :].astype(wide) + xp[part(order[t], p), :].astype(wide)
        if t:
            z_pair[t - 1][p].wait_recv()
            term = zp[t - 1, at, :].astype(wide) + term
            zp[t - 1, at, :] = term.astype(low)
        else:
            r_core[2, part(order[0], p), :] = term.astype(low)
        if t < zs - 1:
            z_pair[t][p].start()
        else:
            x_pair_back[p].start()
            p_out[m, at, mine] = term.astype(low)
            core_pair[p].start()

    def end_pair(p):
        x_pair_back[p].wait_recv()
        core_pair_back[p].start()

    def step_attn(t):
        @pl.when(c == y)
        def _():
            x_attn[t].wait_recv()
            term = ya[order[t], my_rows, :].astype(wide) + xa[order[t]].astype(wide)
            if t:
                z_attn[t - 1].wait_recv()
                za[t - 1] = (za[t - 1].astype(wide) + term).astype(low)
            else:
                ya[order[0], my_rows, :] = term.astype(low)
            if t < zs - 1:
                z_attn[t].start()
            else:
                a_out[my_rows, :] = za[zs - 2]
                x_attn_back.start()

    hops = [to_core, to_y, to_x, {"dp": z + 1 - 2 * (z % 2)}, {"dp": (z + 2) % zs}]
    exchange = [move(41 + i, sm_src.at[i], sm_in.at[i], who) for i, who in enumerate(hops)]

    def start_sum(i):
        sm_src[i] = small[...]
        exchange[i].start()

    def end_sum(i):
        exchange[i].wait_recv()
        small[...] = sm_src[i] + sm_in[i]

    aside = [
        load(15 + i, src, dst)
        for i, (src, dst) in enumerate(
            ((out_w_h, out_w), (w_t_h, w_t), (qkv_h, qkv), (mixed_h, mixed), (gain2_h, gain2), (gain1_h, gain1))
        )
    ]
    store_in_grad = load(21, gin, gin_h)
    store_down = load(22, d_out, d_out_h)

    def weights(r_buf, l_go, l_gr, l_xo, l_xr, s_buf):
        loads = [
            load(0, hid_h, r_buf.at[0]),
            load(1, go_h, l_go),
            load(2, gr1_h, l_gr.at[:, pl.ds(0, gr1_h.shape[1])]),
            load(3, gr2_h, l_gr.at[:, pl.ds(gr1_h.shape[1], gr2_h.shape[1])]),
            load(4, pair_h.at[1 - m], r_buf.at[1]),
            load(5, xo_h, l_xo),
            load(14, xr_h, l_xr),
        ]
        load_own = load(6, pair_h.at[m], r_buf.at[0])
        for each in loads:
            each.start()
        theirs = side(1 - c, columns)

        def core(i, k):
            at = chunk((z + zs - 1 - k) % zs)
            return move(50 + i * zs + k, s_buf.at[i % 2, at], r_core.at[i, at], to_core)

        def product(left_o, left_r, right, col, at):
            total = dot(left_o[at, :], right[:half_len, col], 1, 0)
            return total + dot(left_r[at, :], right[half_len:, col], 1, 0)

        def send_part(left_o, left_r, right, i, k):
            at = chunk((z + zs - 1 - k) % zs)
            s_buf[i % 2, at, :] = product(left_o, left_r, right, theirs, at).astype(low)
            core(i, k).start()

        def keep_part(left_o, left_r, right, i, k):
            at = chunk((z + zs - 1 - k) % zs)
            total = product(left_o, left_r, right, mine, at)
            core(i, k).wait_recv()
            r_core[i, at, :] = (total + r_core[i, at, :].astype(wide)).astype(low)

        def sent(i):
            def block(k, carry):
                core(i, k).wait_send()
                return carry

            lax.fori_loop(0, zs, block, 0)

        for each in aside:
            each.start()
        down = (l_go, l_gr, r_buf.at[0], 0)
        theirs_first = (l_xo, l_xr, r_buf.at[1], 1)
        own = (l_xo, l_xr, r_buf.at[0], 2)
        meet()
        for each in loads:
            each.wait()

        def first(k, carry):
            @pl.when(k < zs)
            def _():
                send_part(*down, k)
                send_part(*theirs_first, k)

            @pl.when(k > 0)
            def _():
                keep_part(*down, k - 1)

                @pl.when(k == 1)
                def _():
                    for each in z_down[0]:
                        each.start()

                keep_part(*theirs_first, k - 1)
                x_pair(k - 1).start()

            return carry

        lax.fori_loop(0, zs + 1, first, 0)
        load_own.start()
        step_z_down(1, 0)

        @pl.when(c != y)
        def _():
            swap_out.start()

        back_out.start()
        sent(0)
        load_own.wait()

        def second(k, carry):
            @pl.when(k == 2)
            def _():
                step_z_down(1, 1)

            @pl.when(k == zs)
            def _():
                step_z_pair(0, 0)
                step_z_pair(0, 1)
                step_z_down(2, 0)

            @pl.when(k < zs)
            def _():
                send_part(*own, k)

            @pl.when(k > 0)
            def _():
                keep_part(*own, k - 1)

            return carry

        lax.fori_loop(0, zs + 1, second, 0)
        sent(1)
        sent(2)

    hidden = hid_h.shape[1]
    left = pltpu.VMEM((width, half_len), low)
    pl.run_scoped(
        weights,
        pltpu.VMEM((2, length, hidden), low),
        left,
        left,
        left,
        left,
        pltpu.VMEM((2, width, columns), low),
    )

    def attention(gxv, hv, gov, p_buf, k_acc, v_acc, sums, gqkv, gm, xn1, sx, ga):
        loads = [load(7, gx_h, gxv), load(8, hres_h, hv), load(9, go_h, gov), load(10, xn1_h, xn1)]
        load_x = load(11, xin_h, gov)
        for each in loads:
            each.start()

        def probs_load(h, b, slot):
            return load(12 + slot, probs_h.at[h, :, side(b, q_block)], p_buf.at[slot])

        probs_load(0, 0, 0).start()
        lanes = half_len // 128
        piece = 64
        pieces = width // piece

        def fold(a):
            return sum(a[:, i * 128 : (i + 1) * 128] for i in range(lanes))

        def spread(a):
            return jnp.concatenate([a] * lanes, axis=1)

        def norm_backward(values, gain, scale, grad, store, row):
            def first(i, total):
                at = pl.ds(pl.multiple_of(i * piece, piece), piece)
                return total + jnp.sum(values(at) * (spread(gain[at, :]) * grad(at)), axis=0, keepdims=True)

            total = lax.fori_loop(0, pieces, first, jnp.zeros((1, half_len), wide))
            mean = total * scale[...] * (1.0 / width)

            def second(i, carry):
                at = pl.ds(pl.multiple_of(i * piece, piece), piece)
                g = grad(at)
                normed = values(at) * scale[...]
                store(at, scale[...] * (spread(gain[at, :]) * g - normed * mean))
                ga_part[at, :] = fold(g * normed)
                return carry

            lax.fori_loop(0, pieces, second, 0)
            small[row : row + 1, :] = jnp.sum(ga_part[...].T, axis=0, keepdims=True)

        ga_part = sums.at[:width, :128]
        small[...] = jnp.zeros_like(small)
        for each in loads[:3] + aside:
            each.wait()
        late.wait_recv()

        def add_late(i, carry):
            at = pl.ds(pl.multiple_of(i * piece, piece), piece)
            gxv[at, late_from:] += late_in[at, :].astype(wide)
            return carry

        lax.fori_loop(0, pieces, add_late, 0)

        def store_hres(at, back):
            total = gov[at, :].astype(wide) + back
            gxv[at, :] = total
            bf[at, my_half] = total.astype(low)

        norm_backward(lambda at: hv[at, :], gain2, scale2, lambda at: gxv[at, :], store_hres, 0)
        core_branch.start()
        load_x.start()
        step_z_down(2, 1)
        core_branch.wait_recv()
        gm[...] = dot(out_w[...], bf[...], 1, 0).astype(low)

        reach = length - q_block
        blocks = length // q_block
        near_rows = q_block + 2 * band_half
        d = (
            lax.broadcasted_iota(jnp.int32, (near_rows, q_block), 0)
            - lax.broadcasted_iota(jnp.int32, (near_rows, q_block), 1)
            - band_half
        )
        for h in range(heads):
            head = pl.ds(h * dim, dim)
            k_rows = pl.ds((heads + h) * dim, dim)
            v_rows = pl.ds((2 * heads + h) * dim, dim)
            k_acc[...] = jnp.zeros_like(k_acc)
            v_acc[...] = jnp.zeros_like(v_acc)
            sums[...] = jnp.zeros_like(sums)

            def block(b, carry):
                slot = b % 2
                at = side(b, q_block)
                probs_load(h, b, slot).wait()

                @pl.when(b < blocks - 1)
                def _():
                    probs_load(h, b + 1, 1 - slot).start()

                if h < heads - 1:

                    @pl.when(b == blocks - 1)
                    def _():
                        probs_load(h + 1, 0, 1 - slot).start()

                probs = p_buf[slot]
                go = gm[head, at]
                inner = jnp.sum(go.astype(wide) * mixed[head, at].astype(wide), axis=0, keepdims=True)
                scores = probs.astype(wide) * (dot(qkv[v_rows, :], go, 0, 0) - inner)
                first = pl.multiple_of(reach - b * q_block, q_block)
                sums[pl.ds(first, length), :] += scores
                scores = scores.astype(low)
                gqkv[head, at] = dot(qkv[k_rows, :], scores, 1, 0).astype(low)
                k_acc[...] += dot(qkv[head, at], scores, 1, 1)
                v_acc[...] += dot(go, probs, 1, 1)
                return carry

            lax.fori_loop(0, blocks, block, 0)
            gqkv[k_rows, :] = k_acc[...].astype(low)
            gqkv[v_rows, :] = v_acc[...].astype(low)
            near = sums[reach - band_half : reach + q_block + band_half, :]
            n = jnp.abs(d)
            bucket = jnp.zeros((near_rows, q_block), jnp.int32)
            for step in steps_at:
                bucket = bucket + jnp.where(n >= step, 1, 0)
            bucket = bucket + jnp.where(d > 0, 16, 0)
            totals = []
            for b in range(32):
                total = jnp.sum(jnp.where(bucket == b, near, 0.0), axis=0, keepdims=True)
                if b == 15:
                    total = total + jnp.sum(sums[: reach - band_half, :], axis=0, keepdims=True)
                if b == 31:
                    total = total + jnp.sum(sums[reach + q_block + band_half :, :], axis=0, keepdims=True)
                totals.append(total)
            totals = jnp.concatenate(totals, axis=0)
            totals = jnp.concatenate([totals, jnp.zeros((96, q_block), wide)], axis=0)
            line = jnp.sum(totals.T, axis=0, keepdims=True)
            for side_c in range(2):
                row = 8 + side_c * heads + h
                small[row : row + 1, :128] = jnp.where(c == side_c, line, 0.0)
            if h == 0:
                step_z_pair(1, 0)
            if h == 1:
                step_z_down(3, 0)

        def input_grad(half, store):
            def block(i, carry):
                at = chunk(i)
                store(at, dot(w_t[at, :], gqkv[:, half], 1, 0))
                return carry

            lax.fori_loop(0, zs, block, 0)

        def store_sent(at, value):
            sx[at, :] = value.astype(low)

        core_x = move(36, sx, rx, to_core)
        loads[3].wait()
        y_attn = [
            move(37 + k, ga.at[j], ya.at[j], to_y) for k, j in enumerate(order)
        ]
        wide_cols = gqkv.shape[0]

        def weight_part(k):
            j = order[k]
            ga[j, :rows, :wide_cols] = dot(xn1[chunk(j), :], gqkv[...], 1, 1).astype(low)
            ga[j, :rows, wide_cols:] = dot(bf[chunk(j), :], mixed[...], 1, 1).astype(low)
            ga[j, rows:, :] = jnp.zeros((ga.shape[1] - rows, ga.shape[2]), low)
            pl.when(c != y)(y_attn[k].start)

        def store_own(at, value):
            hv[at, :] = value

        def store_in(at, back):
            gin[at, :] = (gxv[at, :] + back).astype(low)

        def step_y_attn(k):
            j = order[k]

            @pl.when(c == y)
            def _():
                y_attn[k].wait_recv()
                ya[j] = (ya[j].astype(wide) + ga[j].astype(wide)).astype(low)
                x_attn[k].start()

        weight_part(0)
        weight_part(1)
        weight_part(2)
        input_grad(other_half, store_sent)
        core_x.start()
        step_z_down(3, 1)
        step_z_pair(2, 0)
        step_z_pair(1, 1)
        input_grad(my_half, store_own)
        end_down(0)
        weight_part(3)
        step_y_attn(0)
        load_x.wait()
        core_x.wait_recv()
        norm_backward(
            lambda at: gov[at, :].astype(wide),
            gain1,
            scale1,
            lambda at: hv[at, :] + rx[at, :].astype(wide),
            store_in,
            1,
        )
        store_in_grad.start()
        start_sum(0)
        end_down(1)
        step_z_pair(3, 0)
        step_y_attn(1)
        end_sum(0)
        start_sum(1)

        @pl.when(c != y)
        def _():
            swap_in.start()

        step_attn(0)
        step_z_pair(2, 1)
        step_y_attn(2)
        end_pair(0)
        step_attn(1)
        step_y_attn(3)
        end_sum(1)
        start_sum(2)
        core_x.wait_send()

        @pl.when(c != y)
        def _():
            for each in y_attn:
                each.wait_send()

    f32 = lambda *shape: pltpu.VMEM(shape, wide)
    b16 = lambda *shape: pltpu.VMEM(shape, low)
    pl.run_scoped(
        attention,
        f32(width, half_len),
        f32(width, half_len),
        b16(width, half_len),
        b16(2, length, q_block),
        f32(dim, length),
        f32(dim, length),
        f32(2 * length - q_block, q_block),
        b16(3 * heads * dim, length),
        b16(heads * dim, length),
        b16(width, length),
        b16(width, half_len),
        b16(*ya.shape),
    )

    step_z_pair(3, 1)
    end_sum(2)
    start_sum(3)
    step_attn(2)
    end_sum(3)
    start_sum(4)
    step_attn(3)
    for each in core_down:
        each.wait()
    store_down.start()
    end_sum(4)
    end_pair(1)

    @pl.when(c == y)
    def _():
        x_attn_back.wait_recv()
        core_attn.start()
        for each in (core_attn, x_attn_back, *x_attn, *z_attn):
            each.wait_send()

    @pl.when(c != y)
    def _():
        core_attn.wait_recv()
        swap_out.wait()
        swap_in.wait()

    back_out.wait()
    for each in core_pair + core_pair_back + [store_in_grad, store_down]:
        each.wait()
    for each in [late, core_branch] + sum(z_down, []) + x_down + sum(z_pair, []) + x_pair_back:
        each.wait_send()
    for each in [x_pair(k) for k in range(zs)] + exchange:
        each.wait_send()


def back_all(
    hid, pair, g_own, g_oth, g_late, x_own, x_oth, gx, hres, x_in, probs, xn_one, out_first, out_oth, late,
    out_w, w_t, qkv, mixed, gain_two, gain_one, scale_two, scale_one, zs,
):
    width, half_len = g_own.shape
    length = 2 * half_len
    rows = width // zs
    columns = hid.shape[1] // 2
    heads = probs.shape[0]
    a_cols = (w_t.shape[1] + out_w.shape[0]) // 2
    a_len = -(-rows // 32) * 32
    hbm = pl.BlockSpec(memory_space=pl.ANY)
    vmem = pl.BlockSpec(memory_space=pltpu.VMEM)
    sds = lambda kind, *shape: jax.ShapeDtypeStruct(shape, kind)
    b16 = lambda *shape: pltpu.VMEM(shape, low)
    return pl.pallas_call(
        back_kernel,
        in_specs=[hbm] * 21 + [vmem] * 2,
        out_specs=[hbm] * 5 + [vmem] * 3,
        out_shape=[
            sds(low, width, half_len),
            sds(low, width, half_len),
            sds(low, width, half_len),
            sds(low, rows, 2 * columns),
            sds(low, width, half_len),
            sds(low, 2, rows, 2 * columns),
            sds(low, a_len, 2 * a_cols),
            sds(wide, 16, width),
        ],
        scratch_shapes=[
            *(pltpu.VMEM(each.shape, each.dtype) for each in (out_w, w_t, qkv, mixed, gain_two, gain_one)),
            b16(rows, 2 * columns),
            b16(width, half_len),
            b16(3, width, columns),
            b16(width, columns),
            b16(zs - 1, rows, columns),
            b16(zs - 1, rows, columns),
            b16(rows, columns),
            b16(width, length),
            b16(width, half_len),
            b16(zs, a_len, 2 * a_cols),
            b16(zs, a_len // 2, 2 * a_cols),
            b16(zs - 1, a_len // 2, 2 * a_cols),
            b16(width, half_len - 128),
            pltpu.VMEM((5, 16, width), wide),
            pltpu.VMEM((5, 16, width), wide),
            pltpu.SemaphoreType.DMA((62,)),
            pltpu.SemaphoreType.DMA((62,)),
            pltpu.SemaphoreType.DMA((23,)),
        ],
        compiler_params=pltpu.CompilerParams(vmem_limit_bytes=61 << 20, collective_id=1, has_side_effects=True),
        cost_estimate=hint,
        name="back_all",
    )(
        hid, pair, g_own, g_oth, g_late, x_own, x_oth, gx, hres, x_in, probs, xn_one, out_first, out_oth, late,
        out_w, w_t, qkv, mixed, gain_two, gain_one, scale_two, scale_one,
    )


def finish_kernel(
    d_h, p_h, a_h, own_in, got_in, own_out, got_out, oth_out, small,
    d_out, g_out, u_out, q_out, k_out, v_out, o_out, in_out, y_out, gain1_out, gain2_out, bias_out,
    w_in, w_out, a_in, i_in, i_out, y_in, sems,
):
    own = lax.axis_index("seq") % 2 == lax.axis_index("tensor")
    rows = w_in.shape[1]
    width = i_in.shape[0]
    copy = lambda k, src, dst: pltpu.make_async_copy(src, dst, sems.at[k])
    loads = [copy(0, d_h, w_in.at[0]), copy(1, p_h.at[0], w_in.at[1]), copy(2, p_h.at[1], w_in.at[2]), copy(3, a_h, a_in)]
    load_y = copy(4, oth_out, y_in.at[1])
    mine = [copy(5, own_in, i_in), copy(6, own_out, y_in.at[0])]
    theirs = [copy(5, got_in, i_in), copy(6, got_out, y_in.at[0])]
    stores = [copy(7 + i, w_out.at[i], out) for i, out in enumerate((d_out, g_out, u_out))]
    store_i = copy(10, i_out, in_out)
    store_y = copy(11, y_in.at[0], y_out)

    def start(which):
        @pl.when(own)
        def _():
            mine[which].start()

        @pl.when(jnp.logical_not(own))
        def _():
            theirs[which].start()

    loads[0].start()
    start(0)
    for each in loads[1:3]:
        each.start()
    start(1)
    load_y.start()
    loads[3].start()

    def piecewise(count, size, run):
        def step(i, carry):
            run(pl.ds(pl.multiple_of(i * size, size), size))
            return carry

        lax.fori_loop(0, count, step, 0)

    def widen(i):
        loads[i].wait()

        def run(at):
            w_out[i, at, :] = w_in[i, at, :].astype(wide)

        piecewise(rows // 16, 16, run)
        stores[i].start()

    widen(0)
    mine[0].wait()

    def run_in(at):
        i_out[at, :] = i_in[at, :].astype(wide)

    piecewise(width // 64, 64, run_in)
    store_i.start()
    widen(1)
    widen(2)
    mine[1].wait()
    load_y.wait()

    def run_y(at):
        y_in[0, at, :] = (y_in[0, at, :].astype(wide) + y_in[1, at, :].astype(wide)).astype(low)

    piecewise(width // 64, 64, run_y)
    store_y.start()
    loads[3].wait()
    inner = q_out.shape[0]
    for i, out in enumerate((q_out, k_out, v_out, o_out)):
        out[...] = a_in[:rows, i * inner : (i + 1) * inner].astype(wide).T
    gain1_out[...] = small[1, :]
    gain2_out[...] = small[0, :]
    bias_out[...] = small[8 : 8 + bias_out.shape[0], : bias_out.shape[1]]
    for each in stores + [store_i, store_y]:
        each.wait()


def finish(d, p, a, own_in, got_in, own_out, got_out, oth_out, small, inner, bias_shape):
    rows, hidden = d.shape
    width, half_len = own_in.shape
    hbm = pl.BlockSpec(memory_space=pl.ANY)
    vmem = pl.BlockSpec(memory_space=pltpu.VMEM)
    sds = lambda kind, *shape: jax.ShapeDtypeStruct(shape, kind)
    return pl.pallas_call(
        finish_kernel,
        in_specs=[hbm] * 8 + [vmem],
        out_specs=[hbm] * 3 + [vmem] * 4 + [hbm] * 2 + [vmem] * 3,
        out_shape=[sds(wide, rows, hidden)] * 3
        + [sds(wide, inner, rows)] * 4
        + [sds(wide, width, half_len), sds(low, width, half_len)]
        + [sds(wide, width)] * 2
        + [sds(wide, *bias_shape)],
        scratch_shapes=[
            pltpu.VMEM((3, rows, hidden), low),
            pltpu.VMEM((3, rows, hidden), wide),
            pltpu.VMEM(a.shape, low),
            pltpu.VMEM((width, half_len), low),
            pltpu.VMEM((width, half_len), wide),
            pltpu.VMEM((2, width, half_len), low),
            pltpu.SemaphoreType.DMA((12,)),
        ],
        compiler_params=pltpu.CompilerParams(vmem_limit_bytes=60 << 20),
        cost_estimate=hint,
        name="finish_all",
    )(d, p, a, own_in, got_in, own_out, got_out, oth_out, small)


def norm_back(values, scale, gain, grad):
    normed = values * scale
    pushed = gain * grad
    mean = jnp.mean(normed * pushed, axis=0, keepdims=True)
    return scale * (pushed - normed * mean), jnp.sum(grad * normed, axis=1)


class Moves:
    def __init__(self, mesh):
        self.nz = mesh.shape["dp"]
        self.nx = mesh.shape["seq"] // 2
        both = [(m, c, y) for m in range(self.nx) for c in range(2) for y in range(2)]
        at = lambda m, c, y: (m * 2 + c) * 2 + y
        self.swap_pairs = [(at(m, c, y), at(m, y, c)) for m, c, y in both if c != y]
        self.second_pairs = [(at(m, c, y), at(m, y, 1 - c)) for m, c, y in both]
        self.back_pairs = [(b, a) for a, b in self.second_pairs]
        self.ring_x = [(m * 2 + c, (m + 1) % self.nx * 2 + c) for m in range(self.nx) for c in range(2)]
        self.y = lax.axis_index("tensor")
        self.z = lax.axis_index("dp")
        s = lax.axis_index("seq")
        self.c = s % 2
        self.m = s // 2

    def swap(self, a):
        got = lax.ppermute(a, ("seq", "tensor"), self.swap_pairs)
        return jnp.where(self.c == self.y, a, got)

    def back(self, a):
        return lax.ppermute(a, ("seq", "tensor"), self.back_pairs)

    def core(self, a):
        return lax.ppermute(a, "seq", [(s, s ^ 1) for s in range(2 * self.nx)])

    def over_y(self, a):
        return lax.ppermute(a, "tensor", [(0, 1), (1, 0)])

    def over_x(self, a):
        return lax.ppermute(a, "seq", self.ring_x)

    def start_x(self, a):
        take = lax.dynamic_index_in_dim(a, (self.m + self.nx - 1) % self.nx, 1, False)
        return a, self.over_x(take)

    def finish_x(self, a, got, *first):
        take = lambda i: lax.dynamic_index_in_dim(a, i % self.nx, 1, False)
        got = after(got, *first)
        held = (got.astype(wide) + take(self.m + 2 * self.nx - 2).astype(wide)).astype(low)
        for t in range(2, self.nx):
            held = (self.over_x(held).astype(wide) + take(self.m + 2 * self.nx - 1 - t).astype(wide)).astype(low)
        return held

    def scatter_x(self, a):
        take = lambda i: lax.dynamic_index_in_dim(a, i % self.nx, 1, False)
        held = take(self.m + self.nx - 1)
        for t in range(1, self.nx):
            held = (self.over_x(held).astype(wide) + take(self.m + 2 * self.nx - 1 - t).astype(wide)).astype(low)
        return held

    def scatter_z(self, a):
        return lax.psum_scatter(a, "dp", scatter_dimension=0, tiled=True)

    def gather_x(self, piece):
        if self.nx == 2:
            over = self.over_x(piece)
            return jnp.where(
                self.m == 0, jnp.concatenate([piece, over], 0), jnp.concatenate([over, piece], 0)
            )
        groups = [[m * 2 + c for m in range(self.nx)] for c in range(2)]
        return lax.all_gather(piece, "seq", axis=0, tiled=True, axis_index_groups=groups)

    def gather_core(self, piece):
        there = self.core(piece)
        return jnp.where(
            self.c == 0, jnp.concatenate([piece, there], 1), jnp.concatenate([there, piece], 1)
        )

    def sum_everywhere(self, a):
        a = a + self.core(a)
        a = a + self.over_y(a)
        step = 1
        while step < self.nx:
            a = a + lax.ppermute(a, "seq", [(s, s ^ (2 * step)) for s in range(2 * self.nx)])
            step *= 2
        step = 1
        while step < self.nz:
            a = a + lax.ppermute(a, "dp", [(z, z ^ step) for z in range(self.nz)])
            step *= 2
        return a


def local(
    mesh,
    layer_in,
    out_grad,
    doc_lengths,
    valid_length,
    gain_attn,
    query_weight,
    key_weight,
    value_weight,
    position_bias,
    output_weight,
    gain_ffn,
    gate_weight,
    up_weight,
    down_weight,
):
    moves = Moves(mesh)
    half_len, _, width = layer_in.shape
    length = 2 * half_len
    heads = position_bias.shape[1]
    inner_width = query_weight.shape[1]
    y, c, m = moves.y, moves.c, moves.m

    flat = lambda a: a.reshape(half_len, width).T
    (
        x_in, g_own, g_oth, g_send, out_w, w_t, xn_one, qkv, mixed, probs, hres, xn_own, scale_one, scale_two, gain_one, gain_two
    ) = front(
        flat(layer_in),
        flat(out_grad),
        (query_weight.T, key_weight.T, value_weight.T, output_weight),
        doc_lengths,
        valid_length,
        position_bias.T,
        gain_attn,
        gain_ffn,
        moves.nx == 2 and moves.nz == 4,
    )
    hid, pair, xn_oth, g_late, out_first, out_oth, gx, late = ffn(
        xn_own, g_own, g_oth, hres, g_send, gate_weight, up_weight, down_weight.T
    )
    if moves.nx == 2 and moves.nz == 4:
        got_first, got_oth, got_in, sum_d, grad_in, sum_p, sums, small = back_all(
            hid, pair, g_own, g_oth, g_late, xn_own, xn_oth, gx, hres, x_in, probs, xn_one, out_first, out_oth, late,
            out_w, w_t, qkv, mixed, gain_two, gain_one, scale_two, scale_one, moves.nz,
        )
        sum_d, sum_g, sum_u, sum_q, sum_k, sum_v, sum_o, grad_in, out_y, gain_one_sum, gain_two_sum, bias_sum = finish(
            sum_d, sum_p, sums, grad_in, got_in, out_first, got_first, got_oth, small,
            inner_width, (2 * heads, position_bias.shape[0]),
        )
        return (
            out_y.T.reshape(half_len, 1, width),
            grad_in.T.reshape(half_len, 1, width),
            gain_one_sum,
            sum_q.T,
            sum_k.T,
            sum_v.T,
            bias_sum.T,
            sum_o,
            gain_two_sum,
            sum_g,
            sum_u,
            sum_d.T,
        )
    grad_gate, grad_up = pair[0], pair[1]
    gx = gx.at[:, 128:].add(moves.over_y(late)[:, 128:].astype(wide))
    g_oth = jnp.concatenate([g_oth, g_late], axis=1)
    qkv_w = w_t.T
    x_wide = x_in.astype(wide)
    gain_one, gain_two = gain_one[:, :1], gain_two[:, :1]

    def both_halves(own):
        other = moves.core(own)
        return jnp.where(
            c == 0, jnp.concatenate([own, other], 1), jnp.concatenate([other, own], 1)
        )

    def my_half(a):
        return lax.dynamic_slice_in_dim(a, c * half_len, half_len, 1)

    def other_half(a):
        return lax.dynamic_slice_in_dim(a, (1 - c) * half_len, half_len, 1)


    columns = hid.shape[1] // 2
    send_d = weight_grad(g_own, g_oth, hid, 1 - c)
    got_d = moves.core(send_d)
    send_g = weight_grad(xn_own, xn_oth, after(grad_gate, send_d), 1 - c)
    got_g = moves.core(send_g)
    send_u = weight_grad(xn_own, xn_oth, after(grad_up, send_g), 1 - c)
    got_u = moves.core(send_u)
    total_d = weight_grad(g_own, g_oth, after(hid, send_u), c, got_d)
    total_g = weight_grad(xn_own, xn_oth, after(grad_gate, total_d), c, got_g)
    total_u = weight_grad(xn_own, xn_oth, after(grad_up, total_g), c, got_u)
    part_d = moves.scatter_z(total_d)
    x_sent = [moves.start_x(t.reshape(moves.nz, moves.nx, -1, columns)) for t in (total_g, total_u)]

    gx = after(gx, total_u)
    out_y = moves.swap(out_first).astype(wide) + moves.back(out_oth).astype(wide)

    back, grad_gain_two = norm_back(hres, scale_two, gain_two, gx)
    grad_hres = g_own.astype(wide) + back
    branch = both_halves(grad_hres.astype(low))

    grad_mixed = dot(out_w, branch, 1, 0).astype(low)
    grad_qkv, grad_bias = attn_backward(qkv, grad_mixed, mixed, probs)

    part_g = moves.finish_x(*x_sent[0], grad_qkv).reshape(-1, columns)
    sent = dot(qkv_w, other_half(after(grad_qkv, part_g)), 0, 0).astype(low)
    part_g = moves.scatter_z(part_g)
    got_x = moves.core(sent)
    grad_attn_w = jnp.concatenate(
        [dot(xn_one, after(grad_qkv, sent), 1, 1).astype(low), dot(branch, mixed, 1, 1).astype(low)], axis=1
    )
    gx = dot(qkv_w, my_half(after(grad_qkv, grad_attn_w)), 0, 0) + got_x.astype(wide)
    back, grad_gain_one = norm_back(x_wide, scale_one, gain_one, gx)
    grad_in = (grad_hres + back).astype(low)
    part_u = moves.scatter_z(moves.finish_x(*x_sent[1], grad_in).reshape(-1, columns))

    a_columns = grad_attn_w.shape[1] // 2
    chunks = grad_attn_w.reshape(moves.nz, moves.nx, -1, 2 * a_columns)

    def scatter_y(a):
        got = moves.over_y(lax.dynamic_slice_in_dim(a, (1 - y) * a_columns, a_columns, a.ndim - 1))
        kept = lax.dynamic_slice_in_dim(a, y * a_columns, a_columns, a.ndim - 1)
        return (kept.astype(wide) + got.astype(wide)).astype(low)

    half_z = moves.nz // 2
    part = jnp.concatenate(
        [moves.scatter_x(scatter_y(chunks[:half_z])), scatter_y(moves.scatter_x(chunks[half_z:]))], 0
    )
    piece = moves.gather_x(moves.scatter_z(part.reshape(-1, a_columns)))
    there = moves.over_y(piece)
    group = jnp.where(y == 0, jnp.concatenate([piece, there], 1), jnp.concatenate([there, piece], 1))
    sums = jnp.where(c == y, group, moves.core(group)).astype(wide)
    sum_q, sum_k, sum_v, sum_o = (
        sums[:, i * inner_width : (i + 1) * inner_width] for i in range(4)
    )
    grad_in = moves.swap(grad_in).astype(wide)

    if moves.nx == 2:
        part_d = (part_d.astype(wide) + moves.over_x(part_d).astype(wide)).astype(low)
    else:
        part_d = moves.gather_x(moves.scatter_x(part_d.reshape(1, moves.nx, -1, columns))[0])
    sum_d = moves.gather_core(part_d).astype(wide)
    sum_g = moves.gather_core(moves.gather_x(part_g)).astype(wide)
    sum_u = moves.gather_core(moves.gather_x(part_u)).astype(wide)

    bias_full = jnp.zeros((grad_bias.shape[0], 2 * heads), wide)
    bias_full = lax.dynamic_update_slice(bias_full, grad_bias, (jnp.int32(0), c * heads))
    early = moves.sum_everywhere(jnp.concatenate([grad_gain_two, bias_full.reshape(-1)]))
    gain_two_sum, bias_sum = early[:width], early[width:].reshape(bias_full.shape)
    gain_one_sum = moves.sum_everywhere(grad_gain_one)
    return (
        out_y.astype(low).T.reshape(half_len, 1, width),
        grad_in.T.reshape(half_len, 1, width),
        gain_one_sum,
        sum_q,
        sum_k,
        sum_v,
        bias_sum,
        sum_o.T,
        gain_two_sum,
        sum_g,
        sum_u,
        sum_d.T,
    )


def solution(mesh):
    rows = P("tensor", ("dp", "seq"), None)
    columns = P(None, "tensor")
    return jax.shard_map(
        functools.partial(local, mesh),
        mesh=mesh,
        in_specs=(
            rows,
            rows,
            P(("dp", "seq"), None),
            P(("dp", "seq")),
            P(),
            columns,
            columns,
            columns,
            columns,
            P("tensor", None),
            P(),
            columns,
            columns,
            P("tensor", None),
        ),
        out_specs=(
            rows,
            rows,
            P(),
            P("dp", "tensor"),
            P("dp", "tensor"),
            P("dp", "tensor"),
            P(),
            P("tensor", "dp"),
            P(),
            P("dp", "tensor"),
            P("dp", "tensor"),
            P("tensor", "dp"),
        ),
        check_vma=False,
    )
```
